32 devices in a mesh: dp: 4 (over y, x), mp: 8 (over z, core).
Axes of the slice: x: 2, y: 2, z: 4, core: 2. Of those that a mesh axis runs over, the one named last changes fastest.
Arguments:
- layer_input: bfloat16 [8192, 2048], P(('dp', 'mp')), may hold values from -6 to 6
- cotangent: bfloat16 [8192, 2048], P(('dp', 'mp')), may hold values from -6 to 6
- lengths: int32 [4], P('dp'), may hold values from 1024 to 2048, as said below
- offsets: int32 [4], P('dp'), may hold values from 0 to 1024, as said below
- step: int32 [1], replicated, may hold values from 2 to 20
- mix_weight: float32 [3, 2048, 2048], P(None, 'dp', 'mp'), may hold values from -0.125 to 0.125
- out_weight: float32 [2048, 2048], P('mp', 'dp'), may hold values from -2 to 2
- up_weight: float32 [2048, 8192], P('dp', 'mp'), may hold values from -0.125 to 0.125
- down_weight: float32 [8192, 2048], P('mp', 'dp'), may hold values from -0.0625 to 0.0625
- mix_first: float32 [3, 2048, 2048], P(None, 'dp', 'mp'), may hold values from -80 to 80
- out_first: float32 [2048, 2048], P('mp', 'dp'), may hold values from -5 to 5
- up_first: float32 [2048, 8192], P('dp', 'mp'), may hold values from -32 to 32
- down_first: float32 [8192, 2048], P('mp', 'dp'), may hold values from -32 to 32
- mix_second: float32 [3, 2048, 2048], P(None, 'dp', 'mp'), may hold values from 6.5536 to 106.496
- out_second: float32 [2048, 2048], P('mp', 'dp'), may hold values from 0.024 to 0.4
- up_second: float32 [2048, 8192], P('dp', 'mp'), may hold values from 1.024 to 16.384
- down_second: float32 [8192, 2048], P('mp', 'dp'), may hold values from 1.024 to 16.384
- mix_bias: float32 [2, 2048], P(None, 'mp'), may hold values from -1.75 to 1.75
- up_bias: float32 [8192], P('mp'), may hold values from -1.75 to 1.75
- norm_gains: float32 [2, 2048], replicated, may hold values from 0.5 to 1.5
- shifts: float32 [4, 2048], replicated, may hold values from -1.25 to 1.25
- mix_bias_first: float32 [2, 2048], P(None, 'mp'), may hold values from -80 to 80
- up_bias_first: float32 [8192], P('mp'), may hold values from -32 to 32
- gains_first: float32 [2, 2048], replicated, may hold values from -96 to 96
- shifts_first: float32 [4, 2048], replicated, may hold values from -96 to 96
- mix_bias_second: float32 [2, 2048], P(None, 'mp'), may hold values from 6.5536 to 106.496
- up_bias_second: float32 [8192], P('mp'), may hold values from 1.024 to 16.384
- gains_second: float32 [2, 2048], replicated, may hold values from 9.0112 to 147.456
- shifts_second: float32 [4, 2048], replicated, may hold values from 9.0112 to 147.456
Outputs:
- layer_output: bfloat16 [8192, 2048], P(('dp', 'mp'))
- input_grad: float32 [8192, 2048], P(('dp', 'mp'))
- mix_updated: float32 [3, 2048, 2048], P(None, 'dp', 'mp')
- mix_first_next: float32 [3, 2048, 2048], P(None, 'dp', 'mp')
- mix_second_next: float32 [3, 2048, 2048], P(None, 'dp', 'mp')
- out_updated: float32 [2048, 2048], P('mp', 'dp')
- out_first_next: float32 [2048, 2048], P('mp', 'dp')
- out_second_next: float32 [2048, 2048], P('mp', 'dp')
- up_updated: float32 [2048, 8192], P('dp', 'mp')
- up_first_next: float32 [2048, 8192], P('dp', 'mp')
- up_second_next: float32 [2048, 8192], P('dp', 'mp')
- down_updated: float32 [8192, 2048], P('mp', 'dp')
- down_first_next: float32 [8192, 2048], P('mp', 'dp')
- down_second_next: float32 [8192, 2048], P('mp', 'dp')
- mix_bias_updated: float32 [2, 2048], P(None, 'mp')
- mix_bias_first_next: float32 [2, 2048], P(None, 'mp')
- mix_bias_second_next: float32 [2, 2048], P(None, 'mp')
- up_bias_updated: float32 [8192], P('mp')
- up_bias_first_next: float32 [8192], P('mp')
- up_bias_second_next: float32 [8192], P('mp')
- gains_updated: float32 [2, 2048], replicated
- gains_first_next: float32 [2, 2048], replicated
- gains_second_next: float32 [2, 2048], replicated
- shifts_updated: float32 [4, 2048], replicated
- shifts_first_next: float32 [4, 2048], replicated
- shifts_second_next: float32 [4, 2048], replicated
- mix_grad: float32 [3, 2048, 2048], P(None, 'dp', 'mp')
- out_weight_grad: float32 [2048, 2048], P('mp', 'dp')
- up_grad: float32 [2048, 8192], P('dp', 'mp')
- down_grad: float32 [8192, 2048], P('mp', 'dp')
- mix_bias_grad: float32 [2, 2048], P(None, 'mp')
- up_bias_grad: float32 [8192], P('mp')
- gains_grad: float32 [2, 2048], replicated
- shifts_grad: float32 [4, 2048], replicated
- mix_copy: bfloat16 [3, 2048, 2048], P(None, 'dp', 'mp')
- out_copy: bfloat16 [2048, 2048], P('mp', 'dp')
- up_copy: bfloat16 [2048, 8192], P('dp', 'mp')
- down_copy: bfloat16 [8192, 2048], P('mp', 'dp')
The draws below stay inside these ranges and needn't reach their ends.
Inputs may be any that keep to these rules, and one draw needn't show every extreme that they name: `lengths`: some slot holds a sequence of exactly 2048 tokens and another one of exactly 1024. offsets[s] + lengths[s] <= 2048 for every slot; the slot of 1024 tokens has its sequence at the slot's end.
All inputs are finite; a program needn't handle non-finite values.
Results may differ from the reference program's by a relative error of at most 0.009.
The reference program's roundings to bfloat16 on the way count: a program that leaves them out, or rounds other values in their place, can miss the bound.
Values may be sent and summed in bfloat16 or wider, within the bound.
A program may use at most 384 MiB of HBM per device.

```python
import math
import jax
import jax.numpy as jnp
from jax import lax

D = 2048
HEADS = 16
HEAD_DIM = 128
FF = 8192
SLOT = 2048
MINLEN = 1024
SLOTS = 4
TOKENS = 8192
OUT_FAN = 7


def slot_layout(key):
    base = jax.random.fold_in(key, 7101)
    length_key, order_key, place_key = jax.random.split(base, 3)
    lengths = jax.random.randint(length_key, (SLOTS,), MINLEN, SLOT + 1, dtype=jnp.int32)
    order = jax.random.permutation(order_key, SLOTS)
    lengths = lengths.at[order[0]].set(SLOT).at[order[1]].set(MINLEN)
    room = SLOT - lengths
    offsets = jax.random.randint(place_key, (SLOTS,), 0, room + 1, dtype=jnp.int32)
    offsets = offsets.at[order[1]].set(SLOT - MINLEN)
    return (lengths, offsets)


def draw_lengths(key, part):
    return slot_layout(key)[0]


def draw_offsets(key, part):
    return slot_layout(key)[1]


def block_scale(rng, shape, cuts, smallest, high):
    def one(position, parts):
        draws = jax.random.uniform(jax.random.fold_in(jax.random.fold_in(rng, 6), position), (parts,), jnp.float32, smallest / len(cuts), high / len(cuts))
        return jnp.repeat(jnp.exp(draws), shape[position] // parts).reshape((-1,) + (1,) * (len(shape) - position - 1))

    level = one(*cuts[0])
    for cut in cuts[1:]:
        level = level * one(*cut)
    return level


def gaussian(own_key, extent, width, most, pieces=(), kind=jnp.bfloat16):
    drawn = jax.random.normal(own_key, extent, jnp.float32) * width
    if len(pieces) > 0:
        drawn = block_scale(own_key, extent, pieces, -0.22, 0.18) * drawn
    return jnp.clip(drawn, min=-most, max=most).astype(kind)


def setup_inputs(seed: int = 0) -> dict:
    key_of = jax.random.split(jax.random.key(seed), 30)
    return {
        "layer_input": gaussian(key_of[0], (TOKENS, D), 1.0, 6.0, ((0, 32),)),
        "cotangent": gaussian(key_of[1], (TOKENS, D), 1.0, 6.0, ((0, 32),)),
        "lengths": draw_lengths(jax.random.fold_in(key_of[29], 71), 0),
        "offsets": draw_offsets(jax.random.fold_in(key_of[29], 71), 0),
        "step": jax.random.randint(key_of[4], (1,), 2, 21).astype(jnp.int32),
        "mix_weight": gaussian(key_of[5], (3, D, D), D ** -0.5, 0.125, ((1, 4), (2, 8)), jnp.float32),
        "out_weight": gaussian(key_of[6], (D, D), OUT_FAN ** -0.5, 2.0, ((0, 8), (1, 4)), jnp.float32),
        "up_weight": gaussian(key_of[7], (D, FF), D ** -0.5, 0.125, ((0, 4), (1, 8)), jnp.float32),
        "down_weight": gaussian(key_of[8], (FF, D), FF ** -0.5, 0.0625, ((0, 8), (1, 4)), jnp.float32),
        "mix_first": gaussian(key_of[9], (3, D, D), (0.15 * TOKENS ** 0.5), 80.0, ((1, 4), (2, 8)), jnp.float32),
        "out_first": gaussian(key_of[10], (D, D), (0.4 * SLOTS ** 0.5), 5.0, ((0, 8), (1, 4)), jnp.float32),
        "up_first": gaussian(key_of[11], (D, FF), (0.055 * TOKENS ** 0.5), 32.0, ((0, 4), (1, 8)), jnp.float32),
        "down_first": gaussian(key_of[12], (FF, D), (0.055 * TOKENS ** 0.5), 32.0, ((0, 8), (1, 4)), jnp.float32),
        "mix_second": jnp.clip(jnp.exp(math.log(106.496) - 2.78809295 * jax.random.uniform(key_of[13], (3, D, D), jnp.float32) ** block_scale(key_of[13], (3, D, D), ((1, 4), (2, 8)), -0.2, 0.2)), 6.5536, 106.496),
        "out_second": jnp.clip(jnp.exp(math.log(0.4) - 2.8134107 * jax.random.uniform(key_of[14], (D, D), jnp.float32) ** block_scale(key_of[14], (D, D), ((0, 8), (1, 4)), -0.2, 0.2)), 0.024, 0.4),
        "up_second": jnp.clip(jnp.exp(math.log(16.384) - 2.7725887 * jax.random.uniform(key_of[15], (D, FF), jnp.float32) ** block_scale(key_of[15], (D, FF), ((0, 4), (1, 8)), -0.2, 0.2)), 1.024, 16.384),
        "down_second": jnp.clip(jnp.exp(math.log(16.384) - 2.7725887 * jax.random.uniform(key_of[16], (FF, D), jnp.float32) ** block_scale(key_of[16], (FF, D), ((0, 8), (1, 4)), -0.2, 0.2)), 1.024, 16.384),
        "mix_bias": gaussian(key_of[17], (2, D), 0.3, 1.75, ((1, 8),), jnp.float32),
        "up_bias": gaussian(key_of[18], (FF,), 0.3, 1.75, ((0, 8),), jnp.float32),
        "norm_gains": jnp.clip(1.0 + 0.1 * jax.random.normal(key_of[19], (2, D), jnp.float32), 0.5, 1.5),
        "shifts": gaussian(key_of[20], (4, D), 0.2, 1.25, (), jnp.float32),
        "mix_bias_first": gaussian(key_of[21], (2, D), (0.15 * TOKENS ** 0.5), 80.0, ((1, 8),), jnp.float32),
        "up_bias_first": gaussian(key_of[22], (FF,), (0.055 * TOKENS ** 0.5), 32.0, ((0, 8),), jnp.float32),
        "gains_first": gaussian(key_of[23], (2, D), (0.17 * TOKENS ** 0.5), 96.0, (), jnp.float32),
        "shifts_first": gaussian(key_of[24], (4, D), (0.17 * TOKENS ** 0.5), 96.0, (), jnp.float32),
        "mix_bias_second": jnp.clip(jnp.exp(math.log(106.496) - 2.78809295 * jax.random.uniform(key_of[25], (2, D), jnp.float32) ** block_scale(key_of[25], (2, D), ((1, 8),), -0.2, 0.2)), 6.5536, 106.496),
        "up_bias_second": jnp.clip(jnp.exp(math.log(16.384) - 2.7725887 * jax.random.uniform(key_of[26], (FF,), jnp.float32) ** block_scale(key_of[26], (FF,), ((0, 8),), -0.2, 0.2)), 1.024, 16.384),
        "gains_second": jnp.clip(jnp.exp(jax.random.uniform(key_of[27], (2, D), jnp.float32, math.log(9.0112), math.log(147.456))), 9.0112, 147.456),
        "shifts_second": jnp.clip(jnp.exp(jax.random.uniform(key_of[28], (4, D), jnp.float32, math.log(9.0112), math.log(147.456))), 9.0112, 147.456),
    }


NORM_EPSILON = 1e-05
ADAM_EPSILON = 1e-08
BETA_FIRST = 0.9
BETA_SECOND = 0.999
MATRIX_DECAY = 0.1
SMALL_RATE = 0.2
MASK_FILL = -1e+30
HIGHEST = lax.Precision.HIGHEST

@jax.custom_vjp
def low(v):
    return lax.optimization_barrier(v.astype(jnp.bfloat16)).astype(jnp.float32)

@jax.custom_vjp
def low_back(v):
    return v

def low_keep(v):
    return (low(v), None)

def low_pass(kept, grad):
    return (grad,)

def back_keep(v):
    return (v, None)

def back_low(kept, grad):
    return (low(grad),)
low.defvjp(low_keep, low_pass)
low_back.defvjp(back_keep, back_low)

def layer_norm(rows, gain, shift):
    center = rows - lax.optimization_barrier(jnp.mean(rows, axis=-1, keepdims=True))
    inverse = lax.rsqrt(lax.optimization_barrier(jnp.mean(center * center, axis=-1, keepdims=True)) + NORM_EPSILON)
    return center * inverse * gain + shift

def product(left, right):
    return jnp.dot(left, right, precision=HIGHEST)

def head_attention(queries, keys, values, allowed):
    scores = low_back(jnp.dot(queries, keys.T, precision=HIGHEST) * HEAD_DIM ** (-0.5))
    probs = low(jax.nn.softmax(jnp.where(allowed, scores, MASK_FILL), axis=-1))
    return jnp.dot(probs, values, precision=HIGHEST)

def slot_forward(weights, slot_rows, live):
    mix_weight, out_weight, up_weight, down_weight, mix_bias, up_bias, norm_gains, shifts = weights
    length = slot_rows.shape[0]
    normed_one = low(layer_norm(slot_rows, norm_gains[0], shifts[0]))
    mixed = jnp.einsum('td,cde->cte', normed_one, low(mix_weight), precision=HIGHEST)
    queries = low(low_back(mixed[0] + mix_bias[0]))
    keys = low(low_back(mixed[1]))
    values = low(low_back(mixed[2] + mix_bias[1]))
    query_heads = queries.reshape(length, HEADS, HEAD_DIM).transpose(1, 0, 2)
    key_heads = keys.reshape(length, HEADS, HEAD_DIM).transpose(1, 0, 2)
    value_heads = values.reshape(length, HEADS, HEAD_DIM).transpose(1, 0, 2)
    positions = jnp.arange(length, dtype=jnp.int32)
    allowed = (positions[None, :] <= positions[:, None]) & (live[:, None] == live[None, :])
    per_head = jax.checkpoint(lambda item: head_attention(item[0], item[1], item[2], allowed))
    attended = lax.map(per_head, (query_heads, key_heads, value_heads))
    attended = low(low_back(attended.transpose(1, 0, 2).reshape(length, D)))
    resid = slot_rows + low_back(product(attended, low(out_weight))) + shifts[1]
    normed_two = low(layer_norm(resid, norm_gains[1], shifts[2]))
    hidden = low_back(product(normed_two, low(up_weight)) + up_bias)
    active = low(jax.nn.gelu(hidden, approximate=True))
    result = resid + low_back(product(active, low(down_weight))) + shifts[3]
    return jnp.where(live[:, None], result, 0.0)

def adam_update(master, grad, first, second, rate, decay, first_fix, second_fix):
    first_next = BETA_FIRST * first + (1.0 - BETA_FIRST) * grad
    second_next = BETA_SECOND * second + (1.0 - BETA_SECOND) * grad * grad
    change = first_next / first_fix / (jnp.sqrt(second_next / second_fix) + ADAM_EPSILON) + decay * master
    return (master - rate * change, first_next, second_next)

def reference(layer_input, cotangent, lengths, offsets, step, mix_weight, out_weight, up_weight, down_weight, mix_first, out_first, up_first, down_first, mix_second, out_second, up_second, down_second, mix_bias, up_bias, norm_gains, shifts, mix_bias_first, up_bias_first, gains_first, shifts_first, mix_bias_second, up_bias_second, gains_second, shifts_second):
    positions = jnp.arange(SLOT, dtype=jnp.int32)
    live = (positions[None, :] >= offsets[:, None]) & (positions[None, :] < (offsets + lengths)[:, None])
    slot_rows = layer_input.astype(jnp.float32).reshape(SLOTS, SLOT, D)
    weights = (mix_weight, out_weight, up_weight, down_weight, mix_bias, up_bias, norm_gains, shifts)
    one_slot = jax.checkpoint(slot_forward)

    def forward(weights, slot_rows):

        def scan_step(carry, item):
            return (carry, one_slot(weights, item[0], item[1]))
        carry, outputs = lax.scan(scan_step, jnp.zeros((), jnp.float32), (slot_rows, live))
        return outputs
    outputs, pullback = jax.vjp(forward, weights, slot_rows)
    weight_grads, input_grad = pullback(cotangent.astype(jnp.float32).reshape(SLOTS, SLOT, D))
    layer_output = outputs.reshape(TOKENS, D).astype(jnp.bfloat16)
    input_grad = input_grad.reshape(TOKENS, D)
    step_count = step[0].astype(jnp.float32)
    first_fix = 1.0 - BETA_FIRST ** step_count
    second_fix = 1.0 - BETA_SECOND ** step_count
    rates = (D ** (-0.5), OUT_FAN ** (-0.5), D ** (-0.5), FF ** (-0.5), SMALL_RATE, SMALL_RATE, SMALL_RATE, SMALL_RATE)
    decays = (MATRIX_DECAY, MATRIX_DECAY, MATRIX_DECAY, MATRIX_DECAY, 0.0, 0.0, 0.0, 0.0)
    firsts = (mix_first, out_first, up_first, down_first, mix_bias_first, up_bias_first, gains_first, shifts_first)
    seconds = (mix_second, out_second, up_second, down_second, mix_bias_second, up_bias_second, gains_second, shifts_second)
    results = []
    for index in range(8):
        results.extend(adam_update(weights[index], weight_grads[index], firsts[index], seconds[index], rates[index], decays[index], first_fix, second_fix))
    return (layer_output, input_grad, results[0], results[1], results[2], results[3], results[4], results[5], results[6], results[7], results[8], results[9], results[10], results[11], results[12], results[13], results[14], results[15], results[16], results[17], results[18], results[19], results[20], results[21], results[22], results[23], weight_grads[0], weight_grads[1], weight_grads[2], weight_grads[3], weight_grads[4], weight_grads[5], weight_grads[6], weight_grads[7], results[0].astype(jnp.bfloat16), results[3].astype(jnp.bfloat16), results[6].astype(jnp.bfloat16), results[9].astype(jnp.bfloat16))
```

```python
import jax
import jax.numpy as jnp
from jax import lax
from jax.sharding import PartitionSpec as P

D = 2048
HEAD_DIM = 128
FF = 8192
BLOCK = 512
OUT_FAN = 7


NORM_EPSILON = 1e-05
ADAM_EPSILON = 1e-08
BETA_FIRST = 0.9
BETA_SECOND = 0.999
MATRIX_DECAY = 0.1
SMALL_RATE = 0.2
MASK_FILL = -1e30


def layer_norm_parts(rows, gain, shift):
    center = rows - jnp.mean(rows, axis=-1, keepdims=True)
    inverse = lax.rsqrt(jnp.mean(center * center, axis=-1, keepdims=True) + NORM_EPSILON)
    normed = center * inverse
    return (normed * gain + shift, normed, inverse)


def layer_norm_back(grad_out, normed, inverse, gain):
    scaled = grad_out * gain
    return inverse * (
        scaled
        - jnp.mean(scaled, axis=-1, keepdims=True)
        - normed * jnp.mean(scaled * normed, axis=-1, keepdims=True)
    )


def tanh_gelu(values):
    return jax.nn.gelu(values, approximate=True)


def own_slice(whole, first_row, count):
    return lax.dynamic_slice_in_dim(whole, first_row, count, 0)


def gather_rows(rows):
    return lax.all_gather(rows, "mp", axis=0, tiled=True)


def scatter_rows(terms):
    low = terms.astype(jnp.bfloat16)
    return lax.psum_scatter(low, "mp", scatter_dimension=0, tiled=True).astype(jnp.float32)


def swap(value, mask):
    size = lax.axis_size("dp")
    return lax.ppermute(value, "dp", [(place, place ^ mask) for place in range(size)])


def gather_shards(shard, axis):
    if lax.axis_size("dp") != 4:
        return lax.all_gather(shard, "dp", axis=axis, tiled=True)
    count = shard.shape[axis]
    me = lax.axis_index("dp")
    from_x = swap(shard, 1)
    from_y = swap(shard, 2)
    half = count // 2
    low = swap(lax.slice_in_dim(from_x, 0, half, axis=axis), 2)
    high = swap(lax.slice_in_dim(from_y, half, count, axis=axis), 1)
    shape = list(shard.shape)
    shape[axis] = 4 * count
    full = jnp.zeros(shape, shard.dtype)
    full = lax.dynamic_update_slice_in_dim(full, shard, me * count, axis)
    full = lax.dynamic_update_slice_in_dim(full, from_x, (me ^ 1) * count, axis)
    full = lax.dynamic_update_slice_in_dim(full, from_y, (me ^ 2) * count, axis)
    full = lax.dynamic_update_slice_in_dim(full, low, (me ^ 3) * count, axis)
    return lax.dynamic_update_slice_in_dim(full, high, (me ^ 3) * count + half, axis)


def scatter_shards(grad, axis):
    if lax.axis_size("dp") != 4:
        return lax.psum_scatter(grad, "dp", scatter_dimension=axis, tiled=True)
    count = grad.shape[axis] // 4
    half = count // 2
    me = lax.axis_index("dp")

    def piece(owner, upper):
        return lax.dynamic_slice_in_dim(grad, owner * count + upper * half, half, axis)

    def one_way(first, second, upper):
        near = swap(piece(me ^ first, upper).astype(jnp.bfloat16), first)
        far = swap(piece(me ^ 3, upper).astype(jnp.bfloat16), first)
        onward = piece(me ^ second, upper) + far.astype(jnp.float32)
        last = swap(onward.astype(jnp.bfloat16), second)
        return piece(me, upper) + near.astype(jnp.float32) + last.astype(jnp.float32)

    return lax.concatenate([one_way(1, 2, 0), one_way(2, 1, 1)], axis)


def tile_scores(query_tile, keys, segment, row_block, col_block):
    key_tile = keys[col_block * BLOCK : (col_block + 1) * BLOCK]
    scale = query_tile.shape[2] ** (-0.5)
    scores = (
        jnp.einsum("qhe,khe->hqk", query_tile, key_tile, preferred_element_type=jnp.float32) * scale
    )
    row_place = row_block * BLOCK + jnp.arange(BLOCK)
    key_place = col_block * BLOCK + jnp.arange(BLOCK)
    row_segment = segment[row_block * BLOCK : (row_block + 1) * BLOCK]
    key_segment = segment[col_block * BLOCK : (col_block + 1) * BLOCK]
    allowed = (key_place[None, :] <= row_place[:, None]) & (
        row_segment[:, None] == key_segment[None, :]
    )
    return (jnp.where(allowed[None], scores, MASK_FILL), allowed)


def attention_forward(queries, keys, values, segment):
    count = queries.shape[0] // BLOCK
    heads = queries.shape[1]
    depth = queries.shape[2]
    outputs = []
    totals = []
    for row_block in range(count):
        query_tile = queries[row_block * BLOCK : (row_block + 1) * BLOCK]
        peak = jnp.full((heads, BLOCK), MASK_FILL, jnp.float32)
        mass = jnp.zeros((heads, BLOCK), jnp.float32)
        for col_block in range(row_block + 1):
            scores, allowed = tile_scores(query_tile, keys, segment, row_block, col_block)
            new_peak = jnp.maximum(peak, jnp.max(scores, axis=-1))
            weights = jnp.where(allowed[None], jnp.exp(scores - new_peak[:, :, None]), 0.0)
            mass = mass * jnp.exp(peak - new_peak) + jnp.sum(weights, axis=-1)
            peak = new_peak
        total = peak + jnp.log(mass)
        gathered = jnp.zeros((BLOCK, heads, depth), jnp.float32)
        for col_block in range(row_block + 1):
            scores, allowed = tile_scores(query_tile, keys, segment, row_block, col_block)
            probs = jnp.where(allowed[None], jnp.exp(scores - total[:, :, None]), 0.0).astype(
                jnp.bfloat16
            )
            value_tile = values[col_block * BLOCK : (col_block + 1) * BLOCK]
            gathered = gathered + jnp.einsum(
                "hqk,khe->qhe", probs, value_tile, preferred_element_type=jnp.float32
            )
        outputs.append(gathered.astype(jnp.bfloat16))
        totals.append(total)
    return (jnp.concatenate(outputs, axis=0), jnp.concatenate(totals, axis=1))


def attention_backward(queries, keys, values, segment, totals, grads):
    count = queries.shape[0] // BLOCK
    heads = queries.shape[1]
    depth = queries.shape[2]
    scale = depth ** (-0.5)
    key_grads = [jnp.zeros((BLOCK, heads, depth), jnp.float32) for index in range(count)]
    value_grads = [jnp.zeros((BLOCK, heads, depth), jnp.float32) for index in range(count)]
    query_grads = []
    for row_block in range(count):
        query_tile = queries[row_block * BLOCK : (row_block + 1) * BLOCK]
        grad_tile = grads[row_block * BLOCK : (row_block + 1) * BLOCK]
        total = totals[:, row_block * BLOCK : (row_block + 1) * BLOCK]
        flows = jnp.zeros((heads, BLOCK), jnp.float32)
        for col_block in range(row_block + 1):
            scores, allowed = tile_scores(query_tile, keys, segment, row_block, col_block)
            probs = jnp.where(allowed[None], jnp.exp(scores - total[:, :, None]), 0.0)
            value_tile = values[col_block * BLOCK : (col_block + 1) * BLOCK]
            prob_grad = jnp.einsum(
                "qhe,khe->hqk", grad_tile, value_tile, preferred_element_type=jnp.float32
            )
            flows = flows + jnp.sum(prob_grad * probs, axis=-1)
            value_grads[col_block] = value_grads[col_block] + jnp.einsum(
                "hqk,qhe->khe",
                probs.astype(jnp.bfloat16),
                grad_tile,
                preferred_element_type=jnp.float32,
            )
        query_sum = jnp.zeros((BLOCK, heads, depth), jnp.float32)
        for col_block in range(row_block + 1):
            scores, allowed = tile_scores(query_tile, keys, segment, row_block, col_block)
            probs = jnp.where(allowed[None], jnp.exp(scores - total[:, :, None]), 0.0)
            value_tile = values[col_block * BLOCK : (col_block + 1) * BLOCK]
            key_tile = keys[col_block * BLOCK : (col_block + 1) * BLOCK]
            prob_grad = jnp.einsum(
                "qhe,khe->hqk", grad_tile, value_tile, preferred_element_type=jnp.float32
            )
            score_grad = (probs * (prob_grad - flows[:, :, None])).astype(jnp.bfloat16)
            query_sum = query_sum + scale * jnp.einsum(
                "hqk,khe->qhe", score_grad, key_tile, preferred_element_type=jnp.float32
            )
            key_grads[col_block] = key_grads[col_block] + scale * jnp.einsum(
                "hqk,qhe->khe", score_grad, query_tile, preferred_element_type=jnp.float32
            )
        query_grads.append(query_sum)
    return (
        jnp.concatenate(query_grads, axis=0).astype(jnp.bfloat16),
        jnp.concatenate(key_grads, axis=0).astype(jnp.bfloat16),
        jnp.concatenate(value_grads, axis=0).astype(jnp.bfloat16),
    )


def adam_update(master, grad, first, second, rate, decay, first_fix, second_fix):
    first_next = BETA_FIRST * first + (1.0 - BETA_FIRST) * grad
    second_next = BETA_SECOND * second + (1.0 - BETA_SECOND) * grad * grad
    change = (
        first_next / first_fix / (jnp.sqrt(second_next / second_fix) + ADAM_EPSILON)
        + decay * master
    )
    return (master - rate * change, first_next, second_next)


def per_device(
    layer_input,
    cotangent,
    lengths,
    offsets,
    step,
    mix_weight,
    out_weight,
    up_weight,
    down_weight,
    mix_first,
    out_first,
    up_first,
    down_first,
    mix_second,
    out_second,
    up_second,
    down_second,
    mix_bias,
    up_bias,
    norm_gains,
    shifts,
    mix_bias_first,
    up_bias_first,
    gains_first,
    shifts_first,
    mix_bias_second,
    up_bias_second,
    gains_second,
    shifts_second,
):
    own_rows = layer_input.shape[0]
    parts = lax.axis_size("mp")
    group_rows = own_rows * parts
    slots_here = lengths.shape[0]
    slot_len = group_rows // slots_here
    local_width = mix_weight.shape[2]
    depth = HEAD_DIM
    heads_here = local_width // depth
    positions = jnp.arange(slot_len, dtype=jnp.int32)
    live = (positions[None, :] >= offsets[:, None]) & (
        positions[None, :] < (offsets + lengths)[:, None]
    )
    segment = live.astype(jnp.int32)
    first_row = lax.axis_index("mp") * own_rows
    own_live = own_slice(live.reshape(-1), first_row, own_rows)[:, None]
    own_input = layer_input.astype(jnp.float32)
    normed_own, hat_one, inv_one = layer_norm_parts(own_input, norm_gains[0], shifts[0])
    normed_one = gather_rows(normed_own.astype(jnp.bfloat16))
    mix_full = gather_shards(mix_weight.astype(jnp.bfloat16), 1)
    out_full = gather_shards(out_weight.astype(jnp.bfloat16), 1)
    up_full = gather_shards(up_weight.astype(jnp.bfloat16), 0)
    down_full = gather_shards(down_weight.astype(jnp.bfloat16), 1)
    out_grad = jnp.where(own_live, cotangent.astype(jnp.float32), 0.0)
    bias_down_grad = jnp.sum(out_grad, axis=0)
    branch_grad = gather_rows(out_grad.astype(jnp.bfloat16))
    mixed = jnp.einsum("td,cde->cte", normed_one, mix_full, preferred_element_type=jnp.float32)
    queries = (
        (mixed[0] + mix_bias[0])
        .astype(jnp.bfloat16)
        .reshape(slots_here, slot_len, heads_here, depth)
    )
    keys = mixed[1].astype(jnp.bfloat16).reshape(slots_here, slot_len, heads_here, depth)
    values = (
        (mixed[2] + mix_bias[1])
        .astype(jnp.bfloat16)
        .reshape(slots_here, slot_len, heads_here, depth)
    )

    def attend(item):
        return attention_forward(item[0], item[1], item[2], item[3])

    attended, totals = lax.map(attend, (queries, keys, values, segment))
    attended_flat = attended.reshape(group_rows, local_width)
    attn_part = jnp.dot(attended_flat, out_full, preferred_element_type=jnp.float32)
    resid_own = own_input + scatter_rows(attn_part) + shifts[1]
    normed_mid, hat_two, inv_two = layer_norm_parts(resid_own, norm_gains[1], shifts[2])
    normed_two = gather_rows(normed_mid.astype(jnp.bfloat16))
    hidden = jnp.dot(normed_two, up_full, preferred_element_type=jnp.float32) + up_bias
    active_value, gelu_pull = jax.vjp(tanh_gelu, hidden)
    active = active_value.astype(jnp.bfloat16)
    active_grad = jnp.einsum(
        "td,fd->tf", branch_grad, down_full, preferred_element_type=jnp.float32
    )
    hidden_grad = gelu_pull(active_grad)[0].astype(jnp.bfloat16)
    two_part = jnp.einsum("tf,df->td", hidden_grad, up_full, preferred_element_type=jnp.float32)
    two_grad = scatter_rows(two_part)
    down_part = jnp.dot(active, down_full, preferred_element_type=jnp.float32)
    down_grad = jnp.einsum("tf,td->fd", active, branch_grad, preferred_element_type=jnp.float32)
    up_bias_grad = jnp.sum(hidden_grad, axis=0, dtype=jnp.float32)
    up_grad = jnp.einsum("td,tf->df", normed_two, hidden_grad, preferred_element_type=jnp.float32)
    resid_grad = out_grad + layer_norm_back(two_grad, hat_two, inv_two, norm_gains[1])
    attn_branch = gather_rows(resid_grad.astype(jnp.bfloat16))
    result_own = resid_own + scatter_rows(down_part) + shifts[3]
    layer_output = jnp.where(own_live, result_own, 0.0).astype(jnp.bfloat16)
    gain_two_grad = jnp.sum(two_grad * hat_two, axis=0)
    shift_two_grad = jnp.sum(two_grad, axis=0)
    bias_out_grad = jnp.sum(resid_grad, axis=0)
    attended_grad = jnp.einsum(
        "td,ed->te", attn_branch, out_full, preferred_element_type=jnp.float32
    ).astype(jnp.bfloat16)
    out_weight_grad = jnp.einsum(
        "te,td->ed", attended_flat, attn_branch, preferred_element_type=jnp.float32
    )

    def attend_back(item):
        return attention_backward(item[0], item[1], item[2], item[3], item[4], item[5])

    query_grad, key_grad, value_grad = lax.map(
        attend_back,
        (
            queries,
            keys,
            values,
            segment,
            totals,
            attended_grad.reshape(slots_here, slot_len, heads_here, depth),
        ),
    )
    stacked = jnp.stack(
        [
            query_grad.reshape(group_rows, local_width),
            key_grad.reshape(group_rows, local_width),
            value_grad.reshape(group_rows, local_width),
        ]
    )
    one_part = jnp.einsum("cte,cde->td", stacked, mix_full, preferred_element_type=jnp.float32)
    one_grad = scatter_rows(one_part)
    mix_grad = jnp.einsum("td,cte->cde", normed_one, stacked, preferred_element_type=jnp.float32)
    mix_bias_grad = jnp.stack(
        [
            jnp.sum(stacked[0], axis=0, dtype=jnp.float32),
            jnp.sum(stacked[2], axis=0, dtype=jnp.float32),
        ]
    )
    mix_owned = scatter_shards(mix_grad, 1)
    out_owned = scatter_shards(out_weight_grad, 1)
    up_owned = scatter_shards(up_grad, 0)
    down_owned = scatter_shards(down_grad, 1)
    input_grad = resid_grad + layer_norm_back(one_grad, hat_one, inv_one, norm_gains[0])
    gain_one_grad = jnp.sum(one_grad * hat_one, axis=0)
    shift_one_grad = jnp.sum(one_grad, axis=0)
    gain_grad = jnp.stack([gain_one_grad, gain_two_grad])
    shift_grad = jnp.stack([shift_one_grad, bias_out_grad, shift_two_grad, bias_down_grad])
    mix_bias_total, up_bias_total = lax.psum((mix_bias_grad, up_bias_grad), "dp")
    gain_total, shift_total = lax.psum((gain_grad, shift_grad), ("dp", "mp"))
    step_count = step[0].astype(jnp.float32)
    first_fix = 1.0 - BETA_FIRST**step_count
    second_fix = 1.0 - BETA_SECOND**step_count
    mix_new = adam_update(
        mix_weight,
        mix_owned,
        mix_first,
        mix_second,
        D ** (-0.5),
        MATRIX_DECAY,
        first_fix,
        second_fix,
    )
    out_new = adam_update(
        out_weight,
        out_owned,
        out_first,
        out_second,
        OUT_FAN ** (-0.5),
        MATRIX_DECAY,
        first_fix,
        second_fix,
    )
    up_new = adam_update(
        up_weight, up_owned, up_first, up_second, D ** (-0.5), MATRIX_DECAY, first_fix, second_fix
    )
    down_new = adam_update(
        down_weight,
        down_owned,
        down_first,
        down_second,
        FF ** (-0.5),
        MATRIX_DECAY,
        first_fix,
        second_fix,
    )
    mix_bias_new = adam_update(
        mix_bias,
        mix_bias_total,
        mix_bias_first,
        mix_bias_second,
        SMALL_RATE,
        0.0,
        first_fix,
        second_fix,
    )
    up_bias_new = adam_update(
        up_bias,
        up_bias_total,
        up_bias_first,
        up_bias_second,
        SMALL_RATE,
        0.0,
        first_fix,
        second_fix,
    )
    gains_new = adam_update(
        norm_gains, gain_total, gains_first, gains_second, SMALL_RATE, 0.0, first_fix, second_fix
    )
    shifts_new = adam_update(
        shifts, shift_total, shifts_first, shifts_second, SMALL_RATE, 0.0, first_fix, second_fix
    )
    return (
        layer_output,
        input_grad,
        mix_new[0],
        mix_new[1],
        mix_new[2],
        out_new[0],
        out_new[1],
        out_new[2],
        up_new[0],
        up_new[1],
        up_new[2],
        down_new[0],
        down_new[1],
        down_new[2],
        mix_bias_new[0],
        mix_bias_new[1],
        mix_bias_new[2],
        up_bias_new[0],
        up_bias_new[1],
        up_bias_new[2],
        gains_new[0],
        gains_new[1],
        gains_new[2],
        shifts_new[0],
        shifts_new[1],
        shifts_new[2],
        mix_owned,
        out_owned,
        up_owned,
        down_owned,
        mix_bias_total,
        up_bias_total,
        gain_total,
        shift_total,
        mix_new[0].astype(jnp.bfloat16),
        out_new[0].astype(jnp.bfloat16),
        up_new[0].astype(jnp.bfloat16),
        down_new[0].astype(jnp.bfloat16),
    )


def solution(mesh):
    placed = (
        P(("dp", "mp"), None),
        P(("dp", "mp"), None),
        P("dp"),
        P("dp"),
        P(),
        P(None, "dp", "mp"),
        P("mp", "dp"),
        P("dp", "mp"),
        P("mp", "dp"),
        P(None, "dp", "mp"),
        P("mp", "dp"),
        P("dp", "mp"),
        P("mp", "dp"),
        P(None, "dp", "mp"),
        P("mp", "dp"),
        P("dp", "mp"),
        P("mp", "dp"),
        P(None, "mp"),
        P("mp"),
        P(),
        P(),
        P(None, "mp"),
        P("mp"),
        P(),
        P(),
        P(None, "mp"),
        P("mp"),
        P(),
        P(),
    )
    return jax.shard_map(
        per_device,
        mesh=mesh,
        in_specs=placed,
        out_specs=(
            P(("dp", "mp"), None),
            P(("dp", "mp"), None),
            P(None, "dp", "mp"),
            P(None, "dp", "mp"),
            P(None, "dp", "mp"),
            P("mp", "dp"),
            P("mp", "dp"),
            P("mp", "dp"),
            P("dp", "mp"),
            P("dp", "mp"),
            P("dp", "mp"),
            P("mp", "dp"),
            P("mp", "dp"),
            P("mp", "dp"),
            P(None, "mp"),
            P(None, "mp"),
            P(None, "mp"),
            P("mp"),
            P("mp"),
            P("mp"),
            P(),
            P(),
            P(),
            P(),
            P(),
            P(),
            P(None, "dp", "mp"),
            P("mp", "dp"),
            P("dp", "mp"),
            P("mp", "dp"),
            P(None, "mp"),
            P("mp"),
            P(),
            P(),
            P(None, "dp", "mp"),
            P("mp", "dp"),
            P("dp", "mp"),
            P("mp", "dp"),
        ),
        check_vma=False,
    )
```

```python
import functools

import jax
import jax.numpy as jnp
from jax import lax
from jax.experimental import pallas as pl
from jax.experimental.pallas import tpu as pltpu
from jax.sharding import PartitionSpec as P

D = 2048
HEAD_DIM = 128
FF = 8192
BLOCK = 512
OUT_FAN = 7


NORM_EPSILON = 1e-05
ADAM_EPSILON = 1e-08
BETA_FIRST = 0.9
BETA_SECOND = 0.999
MATRIX_DECAY = 0.1
SMALL_RATE = 0.2
MASK_FILL = -1e30


def layer_norm_parts(rows, gain, shift):
    center = rows - jnp.mean(rows, axis=-1, keepdims=True)
    inverse = lax.rsqrt(jnp.mean(center * center, axis=-1, keepdims=True) + NORM_EPSILON)
    normed = center * inverse
    return (normed * gain + shift, normed, inverse)


def layer_norm_back(grad_out, normed, inverse, gain):
    scaled = grad_out * gain
    return inverse * (
        scaled
        - jnp.mean(scaled, axis=-1, keepdims=True)
        - normed * jnp.mean(scaled * normed, axis=-1, keepdims=True)
    )


def tanh_gelu(values):
    return jax.nn.gelu(values, approximate=True)


def own_slice(whole, first_row, count):
    return lax.dynamic_slice_in_dim(whole, first_row, count, 0)


def gather_rows(rows):
    return lax.all_gather(rows, "mp", axis=0, tiled=True)


def scatter_rows(terms):
    low = terms.astype(jnp.bfloat16)
    return lax.psum_scatter(low, "mp", scatter_dimension=0, tiled=True).astype(jnp.float32)


def swap(value, mask):
    size = lax.axis_size("dp")
    return lax.ppermute(value, "dp", [(place, place ^ mask) for place in range(size)])


def gather_shards(shard, axis):
    if lax.axis_size("dp") != 4:
        return lax.all_gather(shard, "dp", axis=axis, tiled=True)
    count = shard.shape[axis]
    me = lax.axis_index("dp")
    from_x = swap(shard, 1)
    from_y = swap(shard, 2)
    half = count // 2
    low = swap(lax.slice_in_dim(from_x, 0, half, axis=axis), 2)
    high = swap(lax.slice_in_dim(from_y, half, count, axis=axis), 1)
    shape = list(shard.shape)
    shape[axis] = 4 * count
    full = jnp.zeros(shape, shard.dtype)
    full = lax.dynamic_update_slice_in_dim(full, shard, me * count, axis)
    full = lax.dynamic_update_slice_in_dim(full, from_x, (me ^ 1) * count, axis)
    full = lax.dynamic_update_slice_in_dim(full, from_y, (me ^ 2) * count, axis)
    full = lax.dynamic_update_slice_in_dim(full, low, (me ^ 3) * count, axis)
    return lax.dynamic_update_slice_in_dim(full, high, (me ^ 3) * count + half, axis)


def scatter_shards(grad, axis):
    if lax.axis_size("dp") != 4:
        return lax.psum_scatter(grad, "dp", scatter_dimension=axis, tiled=True)
    count = grad.shape[axis] // 4
    half = count // 2
    me = lax.axis_index("dp")

    def piece(owner, upper):
        return lax.dynamic_slice_in_dim(grad, owner * count + upper * half, half, axis)

    def one_way(first, second, upper):
        near = swap(piece(me ^ first, upper).astype(jnp.bfloat16), first)
        far = swap(piece(me ^ 3, upper).astype(jnp.bfloat16), first)
        onward = piece(me ^ second, upper) + far.astype(jnp.float32)
        last = swap(onward.astype(jnp.bfloat16), second)
        return piece(me, upper) + near.astype(jnp.float32) + last.astype(jnp.float32)

    return lax.concatenate([one_way(1, 2, 0), one_way(2, 1, 1)], axis)


MESH = pl.DeviceIdType.MESH
VMEM_LIMIT = 60 * 1024 * 1024


class Place:
    def __init__(self, chips):
        self.chips = chips
        self.dp = lax.axis_index("dp")
        self.me = lax.axis_index("mp")
        self.chip = self.me // 2
        self.core = self.me % 2
        self.has_up = self.chip < chips - 1
        self.has_down = self.chip > 0
        self.up = (self.dp, jnp.minimum(self.me + 2, 2 * chips - 1))
        self.down = (self.dp, jnp.maximum(self.me - 2, 0))
        self.side = (self.dp, self.me + 1 - 2 * self.core)
        self.x_peer = self.dp + 1 - 2 * (self.dp % 2)
        self.y_peer = (self.dp + 2) % 4
        self.across = 3 - self.dp
        self.x_way = (self.x_peer, self.me)
        self.y_way = (self.y_peer, self.me)

    def greet(self, square):
        barrier = pltpu.get_barrier_semaphore()

        def signal(device):
            pl.semaphore_signal(barrier, inc=1, device_id=device, device_id_type=MESH)

        signal(self.side)
        pl.when(self.has_up)(lambda: signal(self.up))
        pl.when(self.has_down)(lambda: signal(self.down))
        count = 1 + self.has_up.astype(jnp.int32) + self.has_down.astype(jnp.int32)
        if square:
            signal(self.x_way)
            signal(self.y_way)
            count = count + 2
        pl.semaphore_wait(barrier, count)


def remote(source, target, send, recv, device):
    return pltpu.make_async_remote_copy(
        src_ref=source,
        dst_ref=target,
        send_sem=send,
        recv_sem=recv,
        device_id=device,
        device_id_type=MESH,
    )


class LineGather:
    def __init__(self, place, blocks, send, recv):
        self.place, self.blocks, self.send, self.recv = place, blocks, send, recv

    def copy(self, way, chip):
        place = self.place
        block = 2 * chip + place.core
        device = (place.up, place.down, place.side)[way]
        return remote(
            self.blocks.at[block],
            self.blocks.at[block],
            self.send.at[way, chip],
            self.recv.at[block],
            device,
        )

    def arrive(self, chip, core):
        place = self.place
        block = 2 * chip + core
        remote(
            self.blocks.at[block],
            self.blocks.at[block],
            self.send.at[2, chip],
            self.recv.at[block],
            place.side,
        ).wait_recv()

    def begin(self):
        place = self.place
        pl.when(place.has_up)(lambda: self.copy(0, place.chip).start())
        pl.when(place.has_down)(lambda: self.copy(1, place.chip).start())
        self.copy(2, place.chip).start()

    def step(self, distance):
        place = self.place
        low = place.chip - distance
        high = place.chip + distance

        @pl.when(low >= 0)
        def _():
            self.arrive(low, place.core)
            pl.when(place.has_up)(lambda: self.copy(0, low).start())
            self.copy(2, low).start()

        @pl.when(high < place.chips)
        def _():
            self.arrive(high, place.core)
            pl.when(place.has_down)(lambda: self.copy(1, high).start())
            self.copy(2, high).start()

    def finish(self):
        place = self.place

        def drain(chip, carry):
            pl.when(place.has_up & (chip <= place.chip))(lambda: self.copy(0, chip).wait_send())
            pl.when(place.has_down & (chip >= place.chip))(lambda: self.copy(1, chip).wait_send())
            self.copy(2, chip).wait_send()
            return carry

        lax.fori_loop(0, place.chips, drain, 0)


class SquareGather:
    def __init__(self, place, shard, view, half, send, recv):
        self.place, self.shard, self.view, self.half = place, shard, view, half
        self.send, self.recv = send, recv

    def first(self, way):
        place = self.place
        device = (place.x_way, place.y_way)[way]
        return remote(
            self.shard, self.view(place.dp), self.send.at[way], self.recv.at[way], device
        )

    def first_landed(self, way):
        place = self.place
        owner = (place.x_peer, place.y_peer)[way]
        device = (place.x_way, place.y_way)[way]
        remote(
            self.view(owner), self.view(owner), self.send.at[way], self.recv.at[way], device
        ).wait_recv()

    def second(self, way):
        place = self.place
        owner = (place.y_peer, place.x_peer)[way]
        device = (place.x_way, place.y_way)[way]
        part = self.half(owner, 1 - way)
        return remote(part, part, self.send.at[2 + way], self.recv.at[2 + way], device)

    def second_landed(self, way):
        place = self.place
        device = (place.x_way, place.y_way)[way]
        part = self.half(place.across, 1 - way)
        remote(part, part, self.send.at[2 + way], self.recv.at[2 + way], device).wait_recv()

    def begin(self):
        self.first(0).start()
        self.first(1).start()

    def middle(self):
        self.first_landed(0)
        self.second(1).start()
        self.first_landed(1)
        self.second(0).start()

    def end(self):
        self.second_landed(0)
        self.second_landed(1)

    def finish(self):
        self.first(0).wait_send()
        self.first(1).wait_send()
        self.second(0).wait_send()
        self.second(1).wait_send()


def norm_rows(rows, gain, shift):
    normed, hat, inverse = layer_norm_parts(rows, gain, shift)
    return normed


def project_kernel(
    chips,
    rows_ref,
    gain_ref,
    shift_ref,
    mix_ref,
    out_ref,
    bias_ref,
    normed_ref,
    mixed_ref,
    mix_whole,
    out_whole,
    blocks,
    line_send,
    line_recv,
    mix_send,
    mix_recv,
    out_send,
    out_recv,
    own_sem,
    keep_sem,
):
    place = Place(chips)
    count = rows_ref.shape[0]
    place.greet(True)
    mix = SquareGather(
        place,
        mix_ref,
        lambda owner: mix_whole.at[:, owner],
        lambda owner, which: mix_whole.at[:, owner, pl.ds(which * 256, 256)],
        mix_send,
        mix_recv,
    )
    out = SquareGather(
        place,
        out_ref,
        lambda owner: out_whole.at[owner],
        lambda owner, which: out_whole.at[owner, pl.ds(which * 128, 128)],
        out_send,
        out_recv,
    )
    mix.begin()
    own_mix = pltpu.make_async_copy(mix_ref, mix_whole.at[:, place.dp], own_sem.at[0])
    own_out = pltpu.make_async_copy(out_ref, out_whole.at[place.dp], own_sem.at[1])
    own_mix.start()
    own_out.start()
    tile = 64

    def norm(index, carry):
        span = pl.ds(pl.multiple_of(index * tile, tile), tile)
        rows = rows_ref[span, :].astype(jnp.float32)
        normed = norm_rows(rows, gain_ref[...], shift_ref[...])
        blocks[place.me, span, :] = normed.astype(jnp.bfloat16)
        return carry

    lax.fori_loop(0, count // tile, norm, 0)
    line = LineGather(place, blocks, line_send, line_recv)
    line.begin()
    mix.middle()
    out.begin()

    def keep(block):
        span = pl.ds(pl.multiple_of(block * count, count), count)
        return pltpu.make_async_copy(blocks.at[block], normed_ref.at[span], keep_sem.at[block])

    def project(block):
        keep(block).start()
        span = pl.ds(pl.multiple_of(block * count, count), count)
        rows = blocks[block]
        for part in range(3):
            weight = mix_whole[part].reshape(-1, mix_whole.shape[3])
            result = jnp.dot(rows, weight, preferred_element_type=jnp.float32)
            if part == 0:
                result = result + bias_ref[0:1, :]
            if part == 2:
                result = result + bias_ref[1:2, :]
            mixed_ref[part, span, :] = result.astype(jnp.bfloat16)

    def step(distance, carry):
        @pl.when((distance > 0) & (distance < chips))
        def _():
            line.step(distance)

        @pl.when(distance == 1)
        def _():
            mix.end()
            own_mix.wait()
            out.middle()

        def one(index, inner):
            near = distance - 1
            side = index % 2
            core = (place.core + index // 2) % 2
            chip = place.chip + near * (2 * side - 1)

            @pl.when((chip >= 0) & (chip < chips) & ((near > 0) | (side == 0)))
            def _():
                pl.when(index >= 2)(lambda: line.arrive(chip, core))
                project(2 * chip + core)

            return inner

        @pl.when(distance > 0)
        def _():
            lax.fori_loop(0, 4, one, 0)

        return carry

    lax.fori_loop(0, chips + 1, step, 0)
    out.end()
    own_out.wait()
    line.finish()
    mix.finish()
    out.finish()

    def kept(block, carry):
        keep(block).wait()
        return carry

    lax.fori_loop(0, 2 * chips, kept, 0)


def project_call(rows, gain, shift, mix_shard, out_shard, bias, chips):
    count, width = rows.shape
    total = 2 * chips * count
    local = mix_shard.shape[2]
    vmem = pl.BlockSpec(memory_space=pltpu.VMEM)
    dma = pltpu.SemaphoreType.DMA
    flops = 2 * total * width * 3 * local
    return pl.pallas_call(
        functools.partial(project_kernel, chips),
        out_shape=(
            jax.ShapeDtypeStruct((total, width), jnp.bfloat16),
            jax.ShapeDtypeStruct((3, total, local), jnp.bfloat16),
            jax.ShapeDtypeStruct((3, 4, mix_shard.shape[1], local), jnp.bfloat16),
            jax.ShapeDtypeStruct((4,) + out_shard.shape, jnp.bfloat16),
        ),
        in_specs=[vmem] * 6,
        out_specs=(pl.BlockSpec(memory_space=pl.ANY), vmem, vmem, vmem),
        scratch_shapes=[
            pltpu.VMEM((2 * chips, count, width), jnp.bfloat16),
            dma((3, chips)),
            dma((2 * chips,)),
            dma((4,)),
            dma((4,)),
            dma((4,)),
            dma((4,)),
            dma((2,)),
            dma((2 * chips,)),
        ],
        compiler_params=pltpu.CompilerParams(
            collective_id=0, has_side_effects=True, vmem_limit_bytes=VMEM_LIMIT
        ),
        cost_estimate=pl.CostEstimate(flops=flops * 7, bytes_accessed=0, transcendentals=0),
        name="project",
    )(rows, gain, shift, mix_shard, out_shard, bias)


class LineScatter:
    def __init__(self, place, term, tiles, bufs, sems):
        self.place, self.term, self.tiles = place, term, tiles
        self.total, self.side_out, self.side_in, self.line_out, self.line_in = bufs
        self.side_send, self.side_recv, self.line_send, self.line_recv = sems

    def side_copy(self, chip):
        return remote(
            self.side_out.at[chip],
            self.side_in.at[chip],
            self.side_send.at[chip],
            self.side_recv.at[chip],
            self.place.side,
        )

    def line_copy(self, way, chip):
        return remote(
            self.line_out.at[chip],
            self.line_in.at[way, chip],
            self.line_send.at[chip],
            self.line_recv.at[way, chip],
            (self.place.up, self.place.down)[way],
        )

    def each(self, distance, action):
        place = self.place

        def one(index, carry):
            chip = place.chip + distance * (1 - 2 * index)
            valid = (chip >= 0) & (chip < place.chips) & ((distance > 0) | (index == 0))
            pl.when(valid)(lambda: action(chip))
            return carry

        lax.fori_loop(0, 2, one, 0)

    def hand_over(self, chip):
        block = 2 * chip + 1 - self.place.core
        width = self.total.shape[1] // self.tiles
        for tile in range(self.tiles):
            span = slice(tile * width, (tile + 1) * width)
            self.side_out[chip, :, span] = self.term(block, tile).astype(jnp.bfloat16)
        self.side_copy(chip).start()

    def sum_up(self, chip):
        place = self.place
        block = 2 * chip + place.core
        width = self.total.shape[1] // self.tiles
        self.side_copy(chip).wait_recv()
        for tile in range(self.tiles):
            span = slice(tile * width, (tile + 1) * width)
            self.total[:, span] = self.term(block, tile) + self.side_in[chip, :, span].astype(
                jnp.float32
            )
        for way in range(2):
            behind = (place.has_down, place.has_up)[way]
            goes = (chip >= place.chip) if way == 0 else (chip <= place.chip)

            @pl.when(behind & goes)
            def _():
                self.line_copy(way, chip).wait_recv()
                self.total[...] += self.line_in[way, chip].astype(jnp.float32)

        @pl.when(chip != place.chip)
        def _():
            self.line_out[chip] = self.total[...].astype(jnp.bfloat16)
            pl.when(chip > place.chip)(lambda: self.line_copy(0, chip).start())
            pl.when(chip < place.chip)(lambda: self.line_copy(1, chip).start())

    def begin(self):
        self.each(self.place.chips - 1, self.hand_over)

    def step(self, index):
        distance = self.place.chips - 1 - index
        pl.when(distance > 0)(lambda: self.each(distance - 1, self.hand_over))
        self.each(distance, self.sum_up)

    def finish(self):
        place = self.place

        def drain(chip, carry):
            self.side_copy(chip).wait_send()
            pl.when(chip != place.chip)(lambda: self.line_copy(0, chip).wait_send())
            return carry

        lax.fori_loop(0, place.chips, drain, 0)


def scatter_scratch(chips, count, width):
    low = jnp.bfloat16
    dma = pltpu.SemaphoreType.DMA
    return [
        pltpu.VMEM((count, width), jnp.float32),
        pltpu.VMEM((chips, count, width), low),
        pltpu.VMEM((chips, count, width), low),
        pltpu.VMEM((chips, count, width), low),
        pltpu.VMEM((2, chips, count, width), low),
        dma((chips,)),
        dma((chips,)),
        dma((chips,)),
        dma((2, chips)),
    ]


def by_rows(count, tile, action):
    def one(index, carry):
        action(pl.ds(pl.multiple_of(index * tile, tile), tile))
        return carry

    lax.fori_loop(0, count // tile, one, 0)


def attend_out_kernel(
    chips,
    attended_ref,
    out_ref,
    rows_ref,
    branch_ref,
    gain_ref,
    shift_ref,
    bias_ref,
    up_ref,
    down_ref,
    resid_ref,
    normed_ref,
    branch_whole,
    up_whole,
    down_whole,
    blocks,
    line_send,
    line_recv,
    up_send,
    up_recv,
    down_send,
    down_recv,
    own_sem,
    keep_sem,
    *scatter,
):
    place = Place(chips)
    count = rows_ref.shape[0]
    place.greet(True)

    def square(shard, whole, send, recv):
        half = shard.shape[0] // 2
        return SquareGather(
            place,
            shard,
            lambda owner: whole.at[owner],
            lambda owner, which: whole.at[owner, pl.ds(which * half, half)],
            send,
            recv,
        )

    up = square(up_ref, up_whole, up_send, up_recv)
    down = square(down_ref, down_whole, down_send, down_recv)
    up.begin()
    own = [
        pltpu.make_async_copy(up_ref, up_whole.at[place.dp], own_sem.at[0]),
        pltpu.make_async_copy(down_ref, down_whole.at[place.dp], own_sem.at[1]),
    ]
    own[0].start()
    own[1].start()

    def term(block, tile):
        span = pl.ds(pl.multiple_of(block * count, count), count)
        return jnp.dot(attended_ref[span, :], out_ref[tile], preferred_element_type=jnp.float32)

    sums = LineScatter(place, term, 4, scatter[:5], scatter[5:])
    sums.begin()

    def copy_in(span):
        blocks[place.me, span, :] = branch_ref[span, :]

    by_rows(count, 64, copy_in)
    line = LineGather(place, blocks, line_send, line_recv)
    line.begin()

    def keep(block):
        span = pl.ds(pl.multiple_of(block * count, count), count)
        return pltpu.make_async_copy(blocks.at[block], branch_whole.at[span], keep_sem.at[block])

    def step(index, carry):
        sums.step(index)
        pl.when(index < chips - 1)(lambda: line.step(index + 1))

        @pl.when(index == 1)
        def _():
            up.middle()
            down.begin()

        pl.when(index == 2)(down.middle)
        return carry

    lax.fori_loop(0, chips, step, 0)
    total = scatter[0]

    def norm(span):
        resid = rows_ref[span, :].astype(jnp.float32) + total[span, :] + bias_ref[...]
        resid_ref[span, :] = resid
        normed_ref[span, :] = norm_rows(resid, gain_ref[...], shift_ref[...]).astype(jnp.bfloat16)

    by_rows(count, 64, norm)

    def store(block, carry):
        pl.when((block % 2 != place.core))(lambda: line.arrive(block // 2, block % 2))
        keep(block).start()
        return carry

    lax.fori_loop(0, 2 * chips, store, 0)
    sums.finish()
    line.finish()
    up.end()
    down.end()
    up.finish()
    down.finish()
    own[0].wait()
    own[1].wait()

    def kept(block, carry):
        keep(block).wait()
        return carry

    lax.fori_loop(0, 2 * chips, kept, 0)


def attend_out_call(attended, out_whole, rows, branch, gain, shift, bias, up, down, chips):
    count, width = rows.shape
    total = 2 * chips * count
    low = jnp.bfloat16
    vmem = pl.BlockSpec(memory_space=pltpu.VMEM)
    hbm = pl.BlockSpec(memory_space=pl.ANY)
    dma = pltpu.SemaphoreType.DMA
    return pl.pallas_call(
        functools.partial(attend_out_kernel, chips),
        out_shape=(
            jax.ShapeDtypeStruct((count, width), jnp.float32),
            jax.ShapeDtypeStruct((count, width), low),
            jax.ShapeDtypeStruct((total, width), low),
            jax.ShapeDtypeStruct((4,) + up.shape, low),
            jax.ShapeDtypeStruct((4,) + down.shape, low),
        ),
        in_specs=[vmem] * 9,
        out_specs=(vmem, vmem, hbm, vmem, vmem),
        scratch_shapes=[
            pltpu.VMEM((2 * chips, count, width), low),
            dma((3, chips)),
            dma((2 * chips,)),
            dma((4,)),
            dma((4,)),
            dma((4,)),
            dma((4,)),
            dma((2,)),
            dma((2 * chips,)),
        ]
        + scatter_scratch(chips, count, width),
        compiler_params=pltpu.CompilerParams(
            collective_id=1, has_side_effects=True, vmem_limit_bytes=VMEM_LIMIT
        ),
        cost_estimate=pl.CostEstimate(flops=10**11, bytes_accessed=0, transcendentals=0),
        name="attend_out",
    )(attended, out_whole, rows, branch, gain, shift, bias, up, down)


def input_back_kernel(
    chips,
    stacked_ref,
    mix_ref,
    rows_ref,
    resid_grad_ref,
    gain_ref,
    grad_ref,
    gain_grad_ref,
    shift_grad_ref,
    *scatter,
):
    place = Place(chips)
    count = rows_ref.shape[0]
    place.greet(False)

    def term(block, tile):
        span = pl.ds(pl.multiple_of(block * count, count), count)
        result = None
        for part in range(3):
            product = lax.dot_general(
                stacked_ref[part, span, :],
                mix_ref[part, tile],
                (((1,), (1,)), ((), ())),
                preferred_element_type=jnp.float32,
            )
            result = product if result is None else result + product
        return result

    sums = LineScatter(place, term, 4, scatter[:5], scatter[5:])
    sums.begin()

    def step(index, carry):
        sums.step(index)
        return carry

    lax.fori_loop(0, chips, step, 0)
    total = scatter[0]
    gain_grad_ref[...] = jnp.zeros_like(gain_grad_ref)
    shift_grad_ref[...] = jnp.zeros_like(shift_grad_ref)

    def back(span):
        rows = rows_ref[span, :].astype(jnp.float32)
        one_grad = total[span, :]
        _, hat, inverse = layer_norm_parts(rows, gain_ref[...], 0.0)
        grad_ref[span, :] = resid_grad_ref[span, :] + layer_norm_back(
            one_grad, hat, inverse, gain_ref[...]
        )
        gain_grad_ref[...] += jnp.sum(one_grad * hat, axis=0, keepdims=True)
        shift_grad_ref[...] += jnp.sum(one_grad, axis=0, keepdims=True)

    by_rows(count, 64, back)
    sums.finish()


def input_back_call(stacked, mix_whole, rows, resid_grad, gain, chips):
    count, width = rows.shape
    vmem = pl.BlockSpec(memory_space=pltpu.VMEM)
    return pl.pallas_call(
        functools.partial(input_back_kernel, chips),
        out_shape=(
            jax.ShapeDtypeStruct((count, width), jnp.float32),
            jax.ShapeDtypeStruct((1, width), jnp.float32),
            jax.ShapeDtypeStruct((1, width), jnp.float32),
        ),
        in_specs=[vmem] * 5,
        out_specs=(vmem,) * 3,
        scratch_shapes=scatter_scratch(chips, count, width),
        compiler_params=pltpu.CompilerParams(
            collective_id=2, has_side_effects=True, vmem_limit_bytes=VMEM_LIMIT
        ),
        cost_estimate=pl.CostEstimate(flops=10**11, bytes_accessed=0, transcendentals=0),
        name="input_back",
    )(stacked, mix_whole, rows, resid_grad, gain)


def tile_scores(query_tile, keys, segment, row_block, col_block):
    key_tile = keys[col_block * BLOCK : (col_block + 1) * BLOCK]
    scale = query_tile.shape[2] ** (-0.5)
    scores = (
        jnp.einsum("qhe,khe->hqk", query_tile, key_tile, preferred_element_type=jnp.float32) * scale
    )
    row_place = row_block * BLOCK + jnp.arange(BLOCK)
    key_place = col_block * BLOCK + jnp.arange(BLOCK)
    row_segment = segment[row_block * BLOCK : (row_block + 1) * BLOCK]
    key_segment = segment[col_block * BLOCK : (col_block + 1) * BLOCK]
    allowed = (key_place[None, :] <= row_place[:, None]) & (
        row_segment[:, None] == key_segment[None, :]
    )
    return (jnp.where(allowed[None], scores, MASK_FILL), allowed)


def attention_forward(queries, keys, values, segment):
    count = queries.shape[0] // BLOCK
    heads = queries.shape[1]
    depth = queries.shape[2]
    outputs = []
    totals = []
    for row_block in range(count):
        query_tile = queries[row_block * BLOCK : (row_block + 1) * BLOCK]
        peak = jnp.full((heads, BLOCK), MASK_FILL, jnp.float32)
        mass = jnp.zeros((heads, BLOCK), jnp.float32)
        for col_block in range(row_block + 1):
            scores, allowed = tile_scores(query_tile, keys, segment, row_block, col_block)
            new_peak = jnp.maximum(peak, jnp.max(scores, axis=-1))
            weights = jnp.where(allowed[None], jnp.exp(scores - new_peak[:, :, None]), 0.0)
            mass = mass * jnp.exp(peak - new_peak) + jnp.sum(weights, axis=-1)
            peak = new_peak
        total = peak + jnp.log(mass)
        gathered = jnp.zeros((BLOCK, heads, depth), jnp.float32)
        for col_block in range(row_block + 1):
            scores, allowed = tile_scores(query_tile, keys, segment, row_block, col_block)
            probs = jnp.where(allowed[None], jnp.exp(scores - total[:, :, None]), 0.0).astype(
                jnp.bfloat16
            )
            value_tile = values[col_block * BLOCK : (col_block + 1) * BLOCK]
            gathered = gathered + jnp.einsum(
                "hqk,khe->qhe", probs, value_tile, preferred_element_type=jnp.float32
            )
        outputs.append(gathered.astype(jnp.bfloat16))
        totals.append(total)
    return (jnp.concatenate(outputs, axis=0), jnp.concatenate(totals, axis=1))


def attention_backward(queries, keys, values, segment, totals, grads):
    count = queries.shape[0] // BLOCK
    heads = queries.shape[1]
    depth = queries.shape[2]
    scale = depth ** (-0.5)
    key_grads = [jnp.zeros((BLOCK, heads, depth), jnp.float32) for index in range(count)]
    value_grads = [jnp.zeros((BLOCK, heads, depth), jnp.float32) for index in range(count)]
    query_grads = []
    for row_block in range(count):
        query_tile = queries[row_block * BLOCK : (row_block + 1) * BLOCK]
        grad_tile = grads[row_block * BLOCK : (row_block + 1) * BLOCK]
        total = totals[:, row_block * BLOCK : (row_block + 1) * BLOCK]
        flows = jnp.zeros((heads, BLOCK), jnp.float32)
        for col_block in range(row_block + 1):
            scores, allowed = tile_scores(query_tile, keys, segment, row_block, col_block)
            probs = jnp.where(allowed[None], jnp.exp(scores - total[:, :, None]), 0.0)
            value_tile = values[col_block * BLOCK : (col_block + 1) * BLOCK]
            prob_grad = jnp.einsum(
                "qhe,khe->hqk", grad_tile, value_tile, preferred_element_type=jnp.float32
            )
            flows = flows + jnp.sum(prob_grad * probs, axis=-1)
            value_grads[col_block] = value_grads[col_block] + jnp.einsum(
                "hqk,qhe->khe",
                probs.astype(jnp.bfloat16),
                grad_tile,
                preferred_element_type=jnp.float32,
            )
        query_sum = jnp.zeros((BLOCK, heads, depth), jnp.float32)
        for col_block in range(row_block + 1):
            scores, allowed = tile_scores(query_tile, keys, segment, row_block, col_block)
            probs = jnp.where(allowed[None], jnp.exp(scores - total[:, :, None]), 0.0)
            value_tile = values[col_block * BLOCK : (col_block + 1) * BLOCK]
            key_tile = keys[col_block * BLOCK : (col_block + 1) * BLOCK]
            prob_grad = jnp.einsum(
                "qhe,khe->hqk", grad_tile, value_tile, preferred_element_type=jnp.float32
            )
            score_grad = (probs * (prob_grad - flows[:, :, None])).astype(jnp.bfloat16)
            query_sum = query_sum + scale * jnp.einsum(
                "hqk,khe->qhe", score_grad, key_tile, preferred_element_type=jnp.float32
            )
            key_grads[col_block] = key_grads[col_block] + scale * jnp.einsum(
                "hqk,qhe->khe", score_grad, query_tile, preferred_element_type=jnp.float32
            )
        query_grads.append(query_sum)
    return (
        jnp.concatenate(query_grads, axis=0).astype(jnp.bfloat16),
        jnp.concatenate(key_grads, axis=0).astype(jnp.bfloat16),
        jnp.concatenate(value_grads, axis=0).astype(jnp.bfloat16),
    )


def adam_update(master, grad, first, second, rate, decay, first_fix, second_fix):
    first_next = BETA_FIRST * first + (1.0 - BETA_FIRST) * grad
    second_next = BETA_SECOND * second + (1.0 - BETA_SECOND) * grad * grad
    change = (
        first_next / first_fix / (jnp.sqrt(second_next / second_fix) + ADAM_EPSILON)
        + decay * master
    )
    return (master - rate * change, first_next, second_next)


def per_device(
    layer_input,
    cotangent,
    lengths,
    offsets,
    step,
    mix_weight,
    out_weight,
    up_weight,
    down_weight,
    mix_first,
    out_first,
    up_first,
    down_first,
    mix_second,
    out_second,
    up_second,
    down_second,
    mix_bias,
    up_bias,
    norm_gains,
    shifts,
    mix_bias_first,
    up_bias_first,
    gains_first,
    shifts_first,
    mix_bias_second,
    up_bias_second,
    gains_second,
    shifts_second,
):
    own_rows = layer_input.shape[0]
    parts = lax.axis_size("mp")
    group_rows = own_rows * parts
    slots_here = lengths.shape[0]
    slot_len = group_rows // slots_here
    local_width = mix_weight.shape[2]
    depth = HEAD_DIM
    heads_here = local_width // depth
    positions = jnp.arange(slot_len, dtype=jnp.int32)
    live = (positions[None, :] >= offsets[:, None]) & (
        positions[None, :] < (offsets + lengths)[:, None]
    )
    segment = live.astype(jnp.int32)
    first_row = lax.axis_index("mp") * own_rows
    own_live = own_slice(live.reshape(-1), first_row, own_rows)[:, None]
    low = jnp.bfloat16
    normed_one, mixed, mix_whole, out_whole = project_call(
        layer_input,
        norm_gains[0:1],
        shifts[0:1],
        mix_weight.astype(low),
        out_weight.astype(low),
        mix_bias,
        parts // 2,
    )
    out_full = out_whole.transpose(1, 0, 2).reshape(local_width, -1)
    out_grad = jnp.where(own_live, cotangent.astype(jnp.float32), 0.0)
    bias_down_grad = jnp.sum(out_grad, axis=0)
    queries = mixed[0].reshape(slots_here, slot_len, heads_here, depth)
    keys = mixed[1].reshape(slots_here, slot_len, heads_here, depth)
    values = mixed[2].reshape(slots_here, slot_len, heads_here, depth)

    def attend(item):
        return attention_forward(item[0], item[1], item[2], item[3])

    attended, totals = lax.map(attend, (queries, keys, values, segment))
    attended_flat = attended.reshape(group_rows, local_width)
    resid_own, normed_mid, branch_grad, up_whole, down_whole = attend_out_call(
        attended_flat,
        out_whole,
        layer_input,
        out_grad.astype(low),
        norm_gains[1:2],
        shifts[2:3],
        shifts[1:2],
        up_weight.astype(low),
        down_weight.astype(low),
        parts // 2,
    )
    _, hat_two, inv_two = layer_norm_parts(resid_own, norm_gains[1], shifts[2])
    normed_two = gather_rows(normed_mid)
    up_full = up_whole.reshape(-1, up_whole.shape[2])
    down_full = down_whole.transpose(1, 0, 2).reshape(down_whole.shape[1], -1)
    hidden = jnp.dot(normed_two, up_full, preferred_element_type=jnp.float32) + up_bias
    active_value, gelu_pull = jax.vjp(tanh_gelu, hidden)
    active = active_value.astype(jnp.bfloat16)
    active_grad = jnp.einsum(
        "td,fd->tf", branch_grad, down_full, preferred_element_type=jnp.float32
    )
    hidden_grad = gelu_pull(active_grad)[0].astype(jnp.bfloat16)
    two_part = jnp.einsum("tf,df->td", hidden_grad, up_full, preferred_element_type=jnp.float32)
    two_grad = scatter_rows(two_part)
    down_part = jnp.dot(active, down_full, preferred_element_type=jnp.float32)
    down_grad = jnp.einsum("tf,td->fd", active, branch_grad, preferred_element_type=jnp.float32)
    up_bias_grad = jnp.sum(hidden_grad, axis=0, dtype=jnp.float32)
    up_grad = jnp.einsum("td,tf->df", normed_two, hidden_grad, preferred_element_type=jnp.float32)
    resid_grad = out_grad + layer_norm_back(two_grad, hat_two, inv_two, norm_gains[1])
    attn_branch = gather_rows(resid_grad.astype(jnp.bfloat16))
    result_own = resid_own + scatter_rows(down_part) + shifts[3]
    layer_output = jnp.where(own_live, result_own, 0.0).astype(jnp.bfloat16)
    gain_two_grad = jnp.sum(two_grad * hat_two, axis=0)
    shift_two_grad = jnp.sum(two_grad, axis=0)
    bias_out_grad = jnp.sum(resid_grad, axis=0)
    attended_grad = jnp.einsum(
        "td,ed->te", attn_branch, out_full, preferred_element_type=jnp.float32
    ).astype(jnp.bfloat16)
    out_weight_grad = jnp.einsum(
        "te,td->ed", attended_flat, attn_branch, preferred_element_type=jnp.float32
    )

    def attend_back(item):
        return attention_backward(item[0], item[1], item[2], item[3], item[4], item[5])

    query_grad, key_grad, value_grad = lax.map(
        attend_back,
        (
            queries,
            keys,
            values,
            segment,
            totals,
            attended_grad.reshape(slots_here, slot_len, heads_here, depth),
        ),
    )
    stacked = jnp.stack(
        [
            query_grad.reshape(group_rows, local_width),
            key_grad.reshape(group_rows, local_width),
            value_grad.reshape(group_rows, local_width),
        ]
    )
    input_grad, gain_one_grad, shift_one_grad = input_back_call(
        stacked, mix_whole, layer_input, resid_grad, norm_gains[0:1], parts // 2
    )
    gain_one_grad, shift_one_grad = gain_one_grad[0], shift_one_grad[0]
    mix_grad = jnp.einsum("td,cte->cde", normed_one, stacked, preferred_element_type=jnp.float32)
    mix_bias_grad = jnp.stack(
        [
            jnp.sum(stacked[0], axis=0, dtype=jnp.float32),
            jnp.sum(stacked[2], axis=0, dtype=jnp.float32),
        ]
    )
    mix_owned = scatter_shards(mix_grad, 1)
    out_owned = scatter_shards(out_weight_grad, 1)
    up_owned = scatter_shards(up_grad, 0)
    down_owned = scatter_shards(down_grad, 1)
    gain_grad = jnp.stack([gain_one_grad, gain_two_grad])
    shift_grad = jnp.stack([shift_one_grad, bias_out_grad, shift_two_grad, bias_down_grad])
    mix_bias_total, up_bias_total = lax.psum((mix_bias_grad, up_bias_grad), "dp")
    gain_total, shift_total = lax.psum((gain_grad, shift_grad), ("dp", "mp"))
    step_count = step[0].astype(jnp.float32)
    first_fix = 1.0 - BETA_FIRST**step_count
    second_fix = 1.0 - BETA_SECOND**step_count
    mix_new = adam_update(
        mix_weight,
        mix_owned,
        mix_first,
        mix_second,
        D ** (-0.5),
        MATRIX_DECAY,
        first_fix,
        second_fix,
    )
    out_new = adam_update(
        out_weight,
        out_owned,
        out_first,
        out_second,
        OUT_FAN ** (-0.5),
        MATRIX_DECAY,
        first_fix,
        second_fix,
    )
    up_new = adam_update(
        up_weight, up_owned, up_first, up_second, D ** (-0.5), MATRIX_DECAY, first_fix, second_fix
    )
    down_new = adam_update(
        down_weight,
        down_owned,
        down_first,
        down_second,
        FF ** (-0.5),
        MATRIX_DECAY,
        first_fix,
        second_fix,
    )
    mix_bias_new = adam_update(
        mix_bias,
        mix_bias_total,
        mix_bias_first,
        mix_bias_second,
        SMALL_RATE,
        0.0,
        first_fix,
        second_fix,
    )
    up_bias_new = adam_update(
        up_bias,
        up_bias_total,
        up_bias_first,
        up_bias_second,
        SMALL_RATE,
        0.0,
        first_fix,
        second_fix,
    )
    gains_new = adam_update(
        norm_gains, gain_total, gains_first, gains_second, SMALL_RATE, 0.0, first_fix, second_fix
    )
    shifts_new = adam_update(
        shifts, shift_total, shifts_first, shifts_second, SMALL_RATE, 0.0, first_fix, second_fix
    )
    return (
        layer_output,
        input_grad,
        mix_new[0],
        mix_new[1],
        mix_new[2],
        out_new[0],
        out_new[1],
        out_new[2],
        up_new[0],
        up_new[1],
        up_new[2],
        down_new[0],
        down_new[1],
        down_new[2],
        mix_bias_new[0],
        mix_bias_new[1],
        mix_bias_new[2],
        up_bias_new[0],
        up_bias_new[1],
        up_bias_new[2],
        gains_new[0],
        gains_new[1],
        gains_new[2],
        shifts_new[0],
        shifts_new[1],
        shifts_new[2],
        mix_owned,
        out_owned,
        up_owned,
        down_owned,
        mix_bias_total,
        up_bias_total,
        gain_total,
        shift_total,
        mix_new[0].astype(jnp.bfloat16),
        out_new[0].astype(jnp.bfloat16),
        up_new[0].astype(jnp.bfloat16),
        down_new[0].astype(jnp.bfloat16),
    )


def per_device_any(
    layer_input,
    cotangent,
    lengths,
    offsets,
    step,
    mix_weight,
    out_weight,
    up_weight,
    down_weight,
    mix_first,
    out_first,
    up_first,
    down_first,
    mix_second,
    out_second,
    up_second,
    down_second,
    mix_bias,
    up_bias,
    norm_gains,
    shifts,
    mix_bias_first,
    up_bias_first,
    gains_first,
    shifts_first,
    mix_bias_second,
    up_bias_second,
    gains_second,
    shifts_second,
):
    own_rows = layer_input.shape[0]
    parts = lax.axis_size("mp")
    group_rows = own_rows * parts
    slots_here = lengths.shape[0]
    slot_len = group_rows // slots_here
    local_width = mix_weight.shape[2]
    depth = HEAD_DIM
    heads_here = local_width // depth
    positions = jnp.arange(slot_len, dtype=jnp.int32)
    live = (positions[None, :] >= offsets[:, None]) & (
        positions[None, :] < (offsets + lengths)[:, None]
    )
    segment = live.astype(jnp.int32)
    first_row = lax.axis_index("mp") * own_rows
    own_live = own_slice(live.reshape(-1), first_row, own_rows)[:, None]
    own_input = layer_input.astype(jnp.float32)
    normed_own, hat_one, inv_one = layer_norm_parts(own_input, norm_gains[0], shifts[0])
    normed_one = gather_rows(normed_own.astype(jnp.bfloat16))
    mix_full = gather_shards(mix_weight.astype(jnp.bfloat16), 1)
    out_full = gather_shards(out_weight.astype(jnp.bfloat16), 1)
    up_full = gather_shards(up_weight.astype(jnp.bfloat16), 0)
    down_full = gather_shards(down_weight.astype(jnp.bfloat16), 1)
    out_grad = jnp.where(own_live, cotangent.astype(jnp.float32), 0.0)
    bias_down_grad = jnp.sum(out_grad, axis=0)
    branch_grad = gather_rows(out_grad.astype(jnp.bfloat16))
    mixed = jnp.einsum("td,cde->cte", normed_one, mix_full, preferred_element_type=jnp.float32)
    queries = (
        (mixed[0] + mix_bias[0])
        .astype(jnp.bfloat16)
        .reshape(slots_here, slot_len, heads_here, depth)
    )
    keys = mixed[1].astype(jnp.bfloat16).reshape(slots_here, slot_len, heads_here, depth)
    values = (
        (mixed[2] + mix_bias[1])
        .astype(jnp.bfloat16)
        .reshape(slots_here, slot_len, heads_here, depth)
    )

    def attend(item):
        return attention_forward(item[0], item[1], item[2], item[3])

    attended, totals = lax.map(attend, (queries, keys, values, segment))
    attended_flat = attended.reshape(group_rows, local_width)
    attn_part = jnp.dot(attended_flat, out_full, preferred_element_type=jnp.float32)
    resid_own = own_input + scatter_rows(attn_part) + shifts[1]
    normed_mid, hat_two, inv_two = layer_norm_parts(resid_own, norm_gains[1], shifts[2])
    normed_two = gather_rows(normed_mid.astype(jnp.bfloat16))
    hidden = jnp.dot(normed_two, up_full, preferred_element_type=jnp.float32) + up_bias
    active_value, gelu_pull = jax.vjp(tanh_gelu, hidden)
    active = active_value.astype(jnp.bfloat16)
    active_grad = jnp.einsum(
        "td,fd->tf", branch_grad, down_full, preferred_element_type=jnp.float32
    )
    hidden_grad = gelu_pull(active_grad)[0].astype(jnp.bfloat16)
    two_part = jnp.einsum("tf,df->td", hidden_grad, up_full, preferred_element_type=jnp.float32)
    two_grad = scatter_rows(two_part)
    down_part = jnp.dot(active, down_full, preferred_element_type=jnp.float32)
    down_grad = jnp.einsum("tf,td->fd", active, branch_grad, preferred_element_type=jnp.float32)
    up_bias_grad = jnp.sum(hidden_grad, axis=0, dtype=jnp.float32)
    up_grad = jnp.einsum("td,tf->df", normed_two, hidden_grad, preferred_element_type=jnp.float32)
    resid_grad = out_grad + layer_norm_back(two_grad, hat_two, inv_two, norm_gains[1])
    attn_branch = gather_rows(resid_grad.astype(jnp.bfloat16))
    result_own = resid_own + scatter_rows(down_part) + shifts[3]
    layer_output = jnp.where(own_live, result_own, 0.0).astype(jnp.bfloat16)
    gain_two_grad = jnp.sum(two_grad * hat_two, axis=0)
    shift_two_grad = jnp.sum(two_grad, axis=0)
    bias_out_grad = jnp.sum(resid_grad, axis=0)
    attended_grad = jnp.einsum(
        "td,ed->te", attn_branch, out_full, preferred_element_type=jnp.float32
    ).astype(jnp.bfloat16)
    out_weight_grad = jnp.einsum(
        "te,td->ed", attended_flat, attn_branch, preferred_element_type=jnp.float32
    )

    def attend_back(item):
        return attention_backward(item[0], item[1], item[2], item[3], item[4], item[5])

    query_grad, key_grad, value_grad = lax.map(
        attend_back,
        (
            queries,
            keys,
            values,
            segment,
            totals,
            attended_grad.reshape(slots_here, slot_len, heads_here, depth),
        ),
    )
    stacked = jnp.stack(
        [
            query_grad.reshape(group_rows, local_width),
            key_grad.reshape(group_rows, local_width),
            value_grad.reshape(group_rows, local_width),
        ]
    )
    one_part = jnp.einsum("cte,cde->td", stacked, mix_full, preferred_element_type=jnp.float32)
    one_grad = scatter_rows(one_part)
    mix_grad = jnp.einsum("td,cte->cde", normed_one, stacked, preferred_element_type=jnp.float32)
    mix_bias_grad = jnp.stack(
        [
            jnp.sum(stacked[0], axis=0, dtype=jnp.float32),
            jnp.sum(stacked[2], axis=0, dtype=jnp.float32),
        ]
    )
    mix_owned = scatter_shards(mix_grad, 1)
    out_owned = scatter_shards(out_weight_grad, 1)
    up_owned = scatter_shards(up_grad, 0)
    down_owned = scatter_shards(down_grad, 1)
    input_grad = resid_grad + layer_norm_back(one_grad, hat_one, inv_one, norm_gains[0])
    gain_one_grad = jnp.sum(one_grad * hat_one, axis=0)
    shift_one_grad = jnp.sum(one_grad, axis=0)
    gain_grad = jnp.stack([gain_one_grad, gain_two_grad])
    shift_grad = jnp.stack([shift_one_grad, bias_out_grad, shift_two_grad, bias_down_grad])
    mix_bias_total, up_bias_total = lax.psum((mix_bias_grad, up_bias_grad), "dp")
    gain_total, shift_total = lax.psum((gain_grad, shift_grad), ("dp", "mp"))
    step_count = step[0].astype(jnp.float32)
    first_fix = 1.0 - BETA_FIRST**step_count
    second_fix = 1.0 - BETA_SECOND**step_count
    mix_new = adam_update(
        mix_weight,
        mix_owned,
        mix_first,
        mix_second,
        D ** (-0.5),
        MATRIX_DECAY,
        first_fix,
        second_fix,
    )
    out_new = adam_update(
        out_weight,
        out_owned,
        out_first,
        out_second,
        OUT_FAN ** (-0.5),
        MATRIX_DECAY,
        first_fix,
        second_fix,
    )
    up_new = adam_update(
        up_weight, up_owned, up_first, up_second, D ** (-0.5), MATRIX_DECAY, first_fix, second_fix
    )
    down_new = adam_update(
        down_weight,
        down_owned,
        down_first,
        down_second,
        FF ** (-0.5),
        MATRIX_DECAY,
        first_fix,
        second_fix,
    )
    mix_bias_new = adam_update(
        mix_bias,
        mix_bias_total,
        mix_bias_first,
        mix_bias_second,
        SMALL_RATE,
        0.0,
        first_fix,
        second_fix,
    )
    up_bias_new = adam_update(
        up_bias,
        up_bias_total,
        up_bias_first,
        up_bias_second,
        SMALL_RATE,
        0.0,
        first_fix,
        second_fix,
    )
    gains_new = adam_update(
        norm_gains, gain_total, gains_first, gains_second, SMALL_RATE, 0.0, first_fix, second_fix
    )
    shifts_new = adam_update(
        shifts, shift_total, shifts_first, shifts_second, SMALL_RATE, 0.0, first_fix, second_fix
    )
    return (
        layer_output,
        input_grad,
        mix_new[0],
        mix_new[1],
        mix_new[2],
        out_new[0],
        out_new[1],
        out_new[2],
        up_new[0],
        up_new[1],
        up_new[2],
        down_new[0],
        down_new[1],
        down_new[2],
        mix_bias_new[0],
        mix_bias_new[1],
        mix_bias_new[2],
        up_bias_new[0],
        up_bias_new[1],
        up_bias_new[2],
        gains_new[0],
        gains_new[1],
        gains_new[2],
        shifts_new[0],
        shifts_new[1],
        shifts_new[2],
        mix_owned,
        out_owned,
        up_owned,
        down_owned,
        mix_bias_total,
        up_bias_total,
        gain_total,
        shift_total,
        mix_new[0].astype(jnp.bfloat16),
        out_new[0].astype(jnp.bfloat16),
        up_new[0].astype(jnp.bfloat16),
        down_new[0].astype(jnp.bfloat16),
    )


def solution(mesh):
    placed = (
        P(("dp", "mp"), None),
        P(("dp", "mp"), None),
        P("dp"),
        P("dp"),
        P(),
        P(None, "dp", "mp"),
        P("mp", "dp"),
        P("dp", "mp"),
        P("mp", "dp"),
        P(None, "dp", "mp"),
        P("mp", "dp"),
        P("dp", "mp"),
        P("mp", "dp"),
        P(None, "dp", "mp"),
        P("mp", "dp"),
        P("dp", "mp"),
        P("mp", "dp"),
        P(None, "mp"),
        P("mp"),
        P(),
        P(),
        P(None, "mp"),
        P("mp"),
        P(),
        P(),
        P(None, "mp"),
        P("mp"),
        P(),
        P(),
    )
    fits = mesh.shape["dp"] == 4 and mesh.shape["mp"] == 8
    return jax.shard_map(
        per_device if fits else per_device_any,
        mesh=mesh,
        in_specs=placed,
        out_specs=(
            P(("dp", "mp"), None),
            P(("dp", "mp"), None),
            P(None, "dp", "mp"),
            P(None, "dp", "mp"),
            P(None, "dp", "mp"),
            P("mp", "dp"),
            P("mp", "dp"),
            P("mp", "dp"),
            P("dp", "mp"),
            P("dp", "mp"),
            P("dp", "mp"),
            P("mp", "dp"),
            P("mp", "dp"),
            P("mp", "dp"),
            P(None, "mp"),
            P(None, "mp"),
            P(None, "mp"),
            P("mp"),
            P("mp"),
            P("mp"),
            P(),
            P(),
            P(),
            P(),
            P(),
            P(),
            P(None, "dp", "mp"),
            P("mp", "dp"),
            P("dp", "mp"),
            P("mp", "dp"),
            P(None, "mp"),
            P("mp"),
            P(),
            P(),
            P(None, "dp", "mp"),
            P("mp", "dp"),
            P("dp", "mp"),
            P("mp", "dp"),
        ),
        check_vma=False,
    )
```

```python
import functools

import jax
import jax.numpy as jnp
from jax import lax
from jax.experimental import pallas as pl
from jax.experimental.pallas import tpu as pltpu
from jax.sharding import PartitionSpec as P

D = 2048
HEAD_DIM = 128
FF = 8192
BLOCK = 512
OUT_FAN = 7


NORM_EPSILON = 1e-05
ADAM_EPSILON = 1e-08
BETA_FIRST = 0.9
BETA_SECOND = 0.999
MATRIX_DECAY = 0.1
SMALL_RATE = 0.2
MASK_FILL = -1e30


def layer_norm_parts(rows, gain, shift):
    center = rows - jnp.mean(rows, axis=-1, keepdims=True)
    inverse = lax.rsqrt(jnp.mean(center * center, axis=-1, keepdims=True) + NORM_EPSILON)
    normed = center * inverse
    return (normed * gain + shift, normed, inverse)


def layer_norm_back(grad_out, normed, inverse, gain):
    scaled = grad_out * gain
    return inverse * (
        scaled
        - jnp.mean(scaled, axis=-1, keepdims=True)
        - normed * jnp.mean(scaled * normed, axis=-1, keepdims=True)
    )


def tanh_gelu(values):
    return jax.nn.gelu(values, approximate=True)


def own_slice(whole, first_row, count):
    return lax.dynamic_slice_in_dim(whole, first_row, count, 0)


def gather_rows(rows):
    return lax.all_gather(rows, "mp", axis=0, tiled=True)


def scatter_rows(terms):
    low = terms.astype(jnp.bfloat16)
    return lax.psum_scatter(low, "mp", scatter_dimension=0, tiled=True).astype(jnp.float32)


def swap(value, mask):
    size = lax.axis_size("dp")
    return lax.ppermute(value, "dp", [(place, place ^ mask) for place in range(size)])


def gather_shards(shard, axis):
    if lax.axis_size("dp") != 4:
        return lax.all_gather(shard, "dp", axis=axis, tiled=True)
    count = shard.shape[axis]
    me = lax.axis_index("dp")
    from_x = swap(shard, 1)
    from_y = swap(shard, 2)
    half = count // 2
    low = swap(lax.slice_in_dim(from_x, 0, half, axis=axis), 2)
    high = swap(lax.slice_in_dim(from_y, half, count, axis=axis), 1)
    shape = list(shard.shape)
    shape[axis] = 4 * count
    full = jnp.zeros(shape, shard.dtype)
    full = lax.dynamic_update_slice_in_dim(full, shard, me * count, axis)
    full = lax.dynamic_update_slice_in_dim(full, from_x, (me ^ 1) * count, axis)
    full = lax.dynamic_update_slice_in_dim(full, from_y, (me ^ 2) * count, axis)
    full = lax.dynamic_update_slice_in_dim(full, low, (me ^ 3) * count, axis)
    return lax.dynamic_update_slice_in_dim(full, high, (me ^ 3) * count + half, axis)


def scatter_shards(grad, axis):
    if lax.axis_size("dp") != 4:
        return lax.psum_scatter(grad, "dp", scatter_dimension=axis, tiled=True)
    count = grad.shape[axis] // 4
    half = count // 2
    me = lax.axis_index("dp")

    def piece(owner, upper):
        return lax.dynamic_slice_in_dim(grad, owner * count + upper * half, half, axis)

    def one_way(first, second, upper):
        near = swap(piece(me ^ first, upper).astype(jnp.bfloat16), first)
        far = swap(piece(me ^ 3, upper).astype(jnp.bfloat16), first)
        onward = piece(me ^ second, upper) + far.astype(jnp.float32)
        last = swap(onward.astype(jnp.bfloat16), second)
        return piece(me, upper) + near.astype(jnp.float32) + last.astype(jnp.float32)

    return lax.concatenate([one_way(1, 2, 0), one_way(2, 1, 1)], axis)


MESH = pl.DeviceIdType.MESH
VMEM_LIMIT = 60 * 1024 * 1024
TURNED = (((1,), (1,)), ((), ()))
CROSSED = (((0,), (0,)), ((), ()))


class Place:
    def __init__(self, chips):
        self.chips = chips
        self.dp = lax.axis_index("dp")
        self.me = lax.axis_index("mp")
        self.chip = self.me // 2
        self.core = self.me % 2
        self.has_up = self.chip < chips - 1
        self.has_down = self.chip > 0
        self.up = (self.dp, jnp.minimum(self.me + 2, 2 * chips - 1))
        self.down = (self.dp, jnp.maximum(self.me - 2, 0))
        self.side = (self.dp, self.me + 1 - 2 * self.core)
        self.x_peer = self.dp + 1 - 2 * (self.dp % 2)
        self.y_peer = (self.dp + 2) % 4
        self.across = 3 - self.dp
        self.x_way = (self.x_peer, self.me)
        self.y_way = (self.y_peer, self.me)

    def greet(self, square, everyone=False):
        barrier = pltpu.get_barrier_semaphore()

        def signal(device):
            pl.semaphore_signal(barrier, inc=1, device_id=device, device_id_type=MESH)

        signal(self.side)
        pl.when(self.has_up)(lambda: signal(self.up))
        pl.when(self.has_down)(lambda: signal(self.down))
        count = 1 + self.has_up.astype(jnp.int32) + self.has_down.astype(jnp.int32)
        if square:
            signal(self.x_way)
            signal(self.y_way)
            count = count + 2
        if everyone:
            signal((self.across, self.me))
            count = count + 1

            def beyond(chip, carry):
                far = (chip > self.chip + 1) | (chip < self.chip - 1)
                pl.when(far)(lambda: signal((self.dp, 2 * chip + self.core)))
                return carry

            lax.fori_loop(0, self.chips, beyond, 0)
            near = self.has_up.astype(jnp.int32) + self.has_down.astype(jnp.int32)
            count = count + (self.chips - 1) - near
        pl.semaphore_wait(barrier, count)


def remote(source, target, send, recv, device):
    return pltpu.make_async_remote_copy(
        src_ref=source,
        dst_ref=target,
        send_sem=send,
        recv_sem=recv,
        device_id=device,
        device_id_type=MESH,
    )


class LineGather:
    def __init__(self, place, blocks, send, recv, parts=1):
        self.place, self.blocks, self.send, self.recv = place, blocks, send, recv
        self.parts = parts

    def copy(self, way, chip, part=0):
        place = self.place
        piece = chip * self.parts + part
        block = 2 * piece + place.core
        device = (place.up, place.down, place.side)[way]
        return remote(
            self.blocks.at[block],
            self.blocks.at[block],
            self.send.at[way, piece],
            self.recv.at[block],
            device,
        )

    def arrive(self, chip, core, part=0):
        piece = chip * self.parts + part
        block = 2 * piece + core
        remote(
            self.blocks.at[block],
            self.blocks.at[block],
            self.send.at[2, piece],
            self.recv.at[block],
            self.place.side,
        ).wait_recv()

    def begin(self):
        place = self.place
        for part in range(self.parts):
            pl.when(place.has_up)(lambda: self.copy(0, place.chip, part).start())
            pl.when(place.has_down)(lambda: self.copy(1, place.chip, part).start())
            self.copy(2, place.chip, part).start()

    def step(self, distance, part=0):
        place = self.place
        low = place.chip - distance
        high = place.chip + distance

        @pl.when(low >= 0)
        def _():
            self.arrive(low, place.core, part)
            pl.when(place.has_up)(lambda: self.copy(0, low, part).start())
            self.copy(2, low, part).start()

        @pl.when(high < place.chips)
        def _():
            self.arrive(high, place.core, part)
            pl.when(place.has_down)(lambda: self.copy(1, high, part).start())
            self.copy(2, high, part).start()

    def finish(self):
        place = self.place

        def drain(chip, carry):
            for part in range(self.parts):
                pl.when(place.has_up & (chip <= place.chip))(
                    lambda: self.copy(0, chip, part).wait_send()
                )
                pl.when(place.has_down & (chip >= place.chip))(
                    lambda: self.copy(1, chip, part).wait_send()
                )
                self.copy(2, chip, part).wait_send()
            return carry

        lax.fori_loop(0, place.chips, drain, 0)


class SquareGather:
    def __init__(self, place, shard, view, half, send, recv):
        self.place, self.shard, self.view, self.half = place, shard, view, half
        self.send, self.recv = send, recv

    def first(self, way):
        place = self.place
        device = (place.x_way, place.y_way)[way]
        return remote(
            self.shard, self.view(place.dp), self.send.at[way], self.recv.at[way], device
        )

    def first_landed(self, way):
        place = self.place
        owner = (place.x_peer, place.y_peer)[way]
        device = (place.x_way, place.y_way)[way]
        remote(
            self.view(owner), self.view(owner), self.send.at[way], self.recv.at[way], device
        ).wait_recv()

    def second(self, way):
        place = self.place
        owner = (place.y_peer, place.x_peer)[way]
        device = (place.x_way, place.y_way)[way]
        part = self.half(owner, 1 - way)
        return remote(part, part, self.send.at[2 + way], self.recv.at[2 + way], device)

    def second_landed(self, way):
        place = self.place
        device = (place.x_way, place.y_way)[way]
        part = self.half(place.across, 1 - way)
        remote(part, part, self.send.at[2 + way], self.recv.at[2 + way], device).wait_recv()

    def begin(self):
        self.first(0).start()
        self.first(1).start()

    def middle(self):
        self.first_landed(0)
        self.second(1).start()
        self.first_landed(1)
        self.second(0).start()

    def end(self):
        self.second_landed(0)
        self.second_landed(1)

    def finish(self):
        self.first(0).wait_send()
        self.first(1).wait_send()
        self.second(0).wait_send()
        self.second(1).wait_send()


def norm_rows(rows, gain, shift):
    normed, hat, inverse = layer_norm_parts(rows, gain, shift)
    return normed


def project_kernel(
    chips,
    rows_ref,
    gain_ref,
    shift_ref,
    mix_ref,
    out_ref,
    bias_ref,
    normed_ref,
    mixed_ref,
    mix_whole,
    out_whole,
    blocks,
    line_send,
    line_recv,
    mix_send,
    mix_recv,
    out_send,
    out_recv,
    own_sem,
    keep_sem,
):
    place = Place(chips)
    count = rows_ref.shape[0]
    place.greet(True)
    mix = SquareGather(
        place,
        mix_ref,
        lambda owner: mix_whole.at[:, owner],
        lambda owner, which: mix_whole.at[:, owner, pl.ds(which * 256, 256)],
        mix_send,
        mix_recv,
    )
    out = SquareGather(
        place,
        out_ref,
        lambda owner: out_whole.at[owner],
        lambda owner, which: out_whole.at[owner, pl.ds(which * 128, 128)],
        out_send,
        out_recv,
    )
    mix.begin()
    own_mix = pltpu.make_async_copy(mix_ref, mix_whole.at[:, place.dp], own_sem.at[0])
    own_out = pltpu.make_async_copy(out_ref, out_whole.at[place.dp], own_sem.at[1])
    own_mix.start()
    own_out.start()
    tile = 64

    def norm(index, carry):
        span = pl.ds(pl.multiple_of(index * tile, tile), tile)
        rows = rows_ref[span, :].astype(jnp.float32)
        normed = norm_rows(rows, gain_ref[...], shift_ref[...])
        blocks[place.me, span, :] = normed.astype(jnp.bfloat16)
        return carry

    lax.fori_loop(0, count // tile, norm, 0)
    line = LineGather(place, blocks, line_send, line_recv)
    line.begin()
    mix.middle()
    out.begin()

    def keep(block):
        span = pl.ds(pl.multiple_of(block * count, count), count)
        return pltpu.make_async_copy(blocks.at[block], normed_ref.at[span], keep_sem.at[block])

    def project(block):
        keep(block).start()
        span = pl.ds(pl.multiple_of(block * count, count), count)
        rows = blocks[block]
        for part in range(3):
            weight = mix_whole[part].reshape(-1, mix_whole.shape[3])
            result = jnp.dot(rows, weight, preferred_element_type=jnp.float32)
            if part == 0:
                result = result + bias_ref[0:1, :]
            if part == 2:
                result = result + bias_ref[1:2, :]
            mixed_ref[part, span, :] = result.astype(jnp.bfloat16)

    def step(distance, carry):
        @pl.when((distance > 0) & (distance < chips))
        def _():
            line.step(distance)

        @pl.when(distance == 1)
        def _():
            mix.end()
            own_mix.wait()
            out.middle()

        def one(index, inner):
            near = distance - 1
            side = index % 2
            core = (place.core + index // 2) % 2
            chip = place.chip + near * (2 * side - 1)

            @pl.when((chip >= 0) & (chip < chips) & ((near > 0) | (side == 0)))
            def _():
                pl.when(index >= 2)(lambda: line.arrive(chip, core))
                project(2 * chip + core)

            return inner

        @pl.when(distance > 0)
        def _():
            lax.fori_loop(0, 4, one, 0)

        return carry

    lax.fori_loop(0, chips + 1, step, 0)
    out.end()
    own_out.wait()
    line.finish()
    mix.finish()
    out.finish()

    def kept(block, carry):
        keep(block).wait()
        return carry

    lax.fori_loop(0, 2 * chips, kept, 0)


def project_call(rows, gain, shift, mix_shard, out_shard, bias, chips):
    count, width = rows.shape
    total = 2 * chips * count
    local = mix_shard.shape[2]
    vmem = pl.BlockSpec(memory_space=pltpu.VMEM)
    dma = pltpu.SemaphoreType.DMA
    flops = 2 * total * width * 3 * local
    return pl.pallas_call(
        functools.partial(project_kernel, chips),
        out_shape=(
            jax.ShapeDtypeStruct((total, width), jnp.bfloat16),
            jax.ShapeDtypeStruct((3, total, local), jnp.bfloat16),
            jax.ShapeDtypeStruct((3, 4, mix_shard.shape[1], local), jnp.bfloat16),
            jax.ShapeDtypeStruct((4,) + out_shard.shape, jnp.bfloat16),
        ),
        in_specs=[vmem] * 6,
        out_specs=(pl.BlockSpec(memory_space=pl.ANY), vmem, vmem, vmem),
        scratch_shapes=[
            pltpu.VMEM((2 * chips, count, width), jnp.bfloat16),
            dma((3, chips)),
            dma((2 * chips,)),
            dma((4,)),
            dma((4,)),
            dma((4,)),
            dma((4,)),
            dma((2,)),
            dma((2 * chips,)),
        ],
        compiler_params=pltpu.CompilerParams(
            collective_id=0, has_side_effects=True, vmem_limit_bytes=VMEM_LIMIT
        ),
        cost_estimate=pl.CostEstimate(flops=flops * 7, bytes_accessed=0, transcendentals=0),
        name="project",
    )(rows, gain, shift, mix_shard, out_shard, bias)


class LineScatter:
    def __init__(self, place, term, tiles, bufs, sems):
        self.place, self.term, self.tiles = place, term, tiles
        self.total, self.side_out, self.side_in, self.line_in = bufs
        self.side_send, self.side_recv, self.line_send, self.line_recv = sems

    def side_copy(self, chip):
        return remote(
            self.side_out.at[chip],
            self.side_in.at[chip],
            self.side_send.at[chip],
            self.side_recv.at[chip],
            self.place.side,
        )

    def line_copy(self, way, chip):
        place = self.place
        next_chip = place.chip + 1 - 2 * way
        slot = jnp.where((way == 1) & (chip == next_chip), place.chips, chip)
        return remote(
            self.line_in.at[chip],
            self.line_in.at[slot],
            self.line_send.at[chip],
            self.line_recv.at[slot],
            (place.up, place.down)[way],
        )

    def landed(self, way, chip):
        place = self.place
        slot = jnp.where((way == 1) & (chip == place.chip), place.chips, chip)
        remote(
            self.line_in.at[slot],
            self.line_in.at[slot],
            self.line_send.at[chip],
            self.line_recv.at[slot],
            (place.up, place.down)[way],
        ).wait_recv()
        return slot

    def each(self, distance, action):
        place = self.place

        def one(index, carry):
            chip = place.chip + distance * (1 - 2 * index)
            valid = (chip >= 0) & (chip < place.chips) & ((distance > 0) | (index == 0))
            pl.when(valid)(lambda: action(chip))
            return carry

        lax.fori_loop(0, 2, one, 0)

    def hand_over(self, chip):
        block = 2 * chip + 1 - self.place.core
        width = self.total.shape[1] // self.tiles
        for tile in range(self.tiles):
            span = slice(tile * width, (tile + 1) * width)
            self.side_out[chip, :, span] = self.term(block, tile).astype(jnp.bfloat16)
        self.side_copy(chip).start()

    def sum_up(self, chip):
        place = self.place
        block = 2 * chip + place.core
        width = self.total.shape[1] // self.tiles
        self.side_copy(chip).wait_recv()
        for tile in range(self.tiles):
            span = slice(tile * width, (tile + 1) * width)
            self.total[:, span] = self.term(block, tile) + self.side_in[chip, :, span].astype(
                jnp.float32
            )
        for way in range(2):
            behind = (place.has_down, place.has_up)[way]
            goes = (chip >= place.chip) if way == 0 else (chip <= place.chip)

            @pl.when(behind & goes)
            def _():
                slot = self.landed(way, chip)
                self.total[...] += self.line_in[slot].astype(jnp.float32)

        @pl.when(chip != place.chip)
        def _():
            self.line_in[chip] = self.total[...].astype(jnp.bfloat16)
            pl.when(chip > place.chip)(lambda: self.line_copy(0, chip).start())
            pl.when(chip < place.chip)(lambda: self.line_copy(1, chip).start())

    def begin(self):
        self.each(self.place.chips - 1, self.hand_over)

    def step(self, index):
        distance = self.place.chips - 1 - index
        pl.when(distance > 0)(lambda: self.each(distance - 1, self.hand_over))
        self.each(distance, self.sum_up)

    def finish(self):
        place = self.place

        def drain(chip, carry):
            self.side_copy(chip).wait_send()
            pl.when(chip != place.chip)(lambda: self.line_copy(0, chip).wait_send())
            return carry

        lax.fori_loop(0, place.chips, drain, 0)


class SquareScatter:
    def __init__(self, place, piece, owned, bufs, sems):
        self.place, self.piece, self.owned = place, piece, owned
        self.out, self.arrived = bufs
        self.send, self.recv = sems

    def copy(self, kind, way):
        place = self.place
        turn = way if kind < 2 else 1 - way
        peer = place.x_peer + turn * (place.y_peer - place.x_peer)
        return remote(
            self.out.at[kind, way],
            self.arrived.at[kind, way],
            self.send.at[kind, way],
            self.recv.at[kind, way],
            (peer, place.me),
        )

    def stage(self, kind):
        place = self.place

        def one(way, carry):
            near = place.x_peer + way * (place.y_peer - place.x_peer)
            other = place.y_peer + way * (place.x_peer - place.y_peer)
            owner = (place.across, near, other, place.dp)[kind]
            value = self.piece(owner, way)
            if kind == 2:
                self.copy(0, way).wait_recv()
                value = value + self.arrived[0, way].astype(jnp.float32)
            if kind < 3:
                self.out[kind, way] = value.astype(jnp.bfloat16)
                self.copy(kind, way).start()
            else:
                self.owned[way] = value
            return carry

        lax.fori_loop(0, 2, one, 0)

    def end(self):
        def one(way, carry):
            self.copy(1, way).wait_recv()
            self.copy(2, way).wait_recv()
            self.owned[way] = (
                self.owned[way]
                + self.arrived[1, way].astype(jnp.float32)
                + self.arrived[2, way].astype(jnp.float32)
            )
            for kind in range(3):
                self.copy(kind, way).wait_send()
            return carry

        lax.fori_loop(0, 2, one, 0)


def square_scratch(half):
    dma = pltpu.SemaphoreType.DMA
    return [
        pltpu.VMEM((3, 2) + half, jnp.bfloat16),
        pltpu.VMEM((3, 2) + half, jnp.bfloat16),
        dma((3, 2)),
        dma((3, 2)),
    ]


class SmallSum:
    def __init__(self, place, rows, alone, bufs, sems):
        self.place, self.rows, self.alone = place, rows, alone
        self.side_buf, self.line_buf, self.square_buf = bufs
        self.send, self.recv = sems

    def side_copy(self):
        place = self.place
        return remote(
            self.rows,
            self.side_buf,
            self.send.at[0],
            self.recv.at[0],
            place.side,
        )

    def line_copy(self, hop):
        place = self.place
        chip = (place.chip + hop) % place.chips
        return remote(
            self.rows,
            self.line_buf.at[place.chip],
            self.send.at[hop],
            self.recv.at[hop],
            (place.dp, 2 * chip + place.core),
        )

    def line_landed(self, hop):
        place = self.place
        chip = (place.chip + place.chips - hop) % place.chips
        remote(
            self.rows,
            self.line_buf.at[chip],
            self.send.at[hop],
            self.recv.at[hop],
            (place.dp, 2 * chip + place.core),
        ).wait_recv()

    def square_copy(self, hop):
        place = self.place
        target = (place.dp + hop) % 4
        at = place.chips + hop
        return remote(
            self.rows,
            self.square_buf.at[place.dp],
            self.send.at[at],
            self.recv.at[at],
            (target, place.me),
        )

    def square_landed(self, hop):
        place = self.place
        source = (place.dp + 4 - hop) % 4
        at = place.chips + hop
        remote(
            self.rows,
            self.square_buf.at[source],
            self.send.at[at],
            self.recv.at[at],
            (source, place.me),
        ).wait_recv()

    def put(self, value):
        if self.alone < self.rows.shape[0]:
            index = lax.broadcasted_iota(jnp.int32, value.shape, 0)
            value = jnp.where(index < self.alone, value, self.rows[...])
        self.rows[...] = value

    def begin(self):
        self.side_copy().start()

    def middle(self):
        self.side_copy().wait()
        self.put(self.rows[...] + self.side_buf[...])
        self.line_buf[self.place.chip] = self.rows[...]
        for hop in range(1, self.place.chips):
            self.line_copy(hop).start()

    def late(self):
        place = self.place
        for hop in range(1, place.chips):
            self.line_copy(hop).wait_send()
            self.line_landed(hop)
        value = self.line_buf[0]
        for chip in range(1, place.chips):
            value = value + self.line_buf[chip]
        self.put(value)
        self.square_buf[place.dp] = self.rows[...]
        for hop in range(1, 4):
            self.square_copy(hop).start()

    def end(self):
        for hop in range(1, 4):
            self.square_copy(hop).wait_send()
            self.square_landed(hop)
        value = self.square_buf[0]
        for device in range(1, 4):
            value = value + self.square_buf[device]
        self.rows[...] = value


def small_scratch(chips, rows, width):
    dma = pltpu.SemaphoreType.DMA
    return [
        pltpu.VMEM((rows, width), jnp.float32),
        pltpu.VMEM((chips, rows, width), jnp.float32),
        pltpu.VMEM((4, rows, width), jnp.float32),
        dma((chips + 4,)),
        dma((chips + 4,)),
    ]


def scatter_scratch(chips, count, width):
    low = jnp.bfloat16
    dma = pltpu.SemaphoreType.DMA
    return [
        pltpu.VMEM((count, width), jnp.float32),
        pltpu.VMEM((chips, count, width), low),
        pltpu.VMEM((chips, count, width), low),
        pltpu.VMEM((chips + 1, count, width), low),
        dma((chips,)),
        dma((chips,)),
        dma((chips,)),
        dma((chips + 1,)),
    ]


def by_rows(count, tile, action):
    def one(index, carry):
        action(pl.ds(pl.multiple_of(index * tile, tile), tile))
        return carry

    lax.fori_loop(0, count // tile, one, 0)


def attend_out_kernel(
    chips,
    attended_ref,
    out_ref,
    rows_ref,
    branch_ref,
    gain_ref,
    shift_ref,
    bias_ref,
    up_ref,
    down_ref,
    resid_ref,
    normed_ref,
    branch_whole,
    up_whole,
    down_whole,
    blocks,
    line_send,
    line_recv,
    up_send,
    up_recv,
    down_send,
    down_recv,
    own_sem,
    keep_sem,
    *scatter,
):
    place = Place(chips)
    count = rows_ref.shape[0]
    place.greet(True)

    def square(shard, whole, send, recv):
        half = shard.shape[0] // 2
        return SquareGather(
            place,
            shard,
            lambda owner: whole.at[owner],
            lambda owner, which: whole.at[owner, pl.ds(which * half, half)],
            send,
            recv,
        )

    up = square(up_ref, up_whole, up_send, up_recv)
    down = square(down_ref, down_whole, down_send, down_recv)
    up.begin()
    own = [
        pltpu.make_async_copy(up_ref, up_whole.at[place.dp], own_sem.at[0]),
        pltpu.make_async_copy(down_ref, down_whole.at[place.dp], own_sem.at[1]),
    ]
    own[0].start()
    own[1].start()

    def term(block, tile):
        span = pl.ds(pl.multiple_of(block * count, count), count)
        return jnp.dot(attended_ref[span, :], out_ref[tile], preferred_element_type=jnp.float32)

    sums = LineScatter(place, term, 4, scatter[:4], scatter[4:8])
    sums.begin()

    def copy_in(span):
        blocks[place.me, span, :] = branch_ref[span, :]

    by_rows(count, 64, copy_in)
    line = LineGather(place, blocks, line_send, line_recv)
    line.begin()

    def keep(block, part):
        half = count // 2
        place_of = ((block // 2 * 2 + part) * 2 + block % 2) * half
        span = pl.ds(pl.multiple_of(place_of, half), half)
        source = blocks.at[block, pl.ds(part * half, half)]
        return pltpu.make_async_copy(source, branch_whole.at[span], keep_sem.at[block, part])

    def step(index, carry):
        sums.step(index)
        pl.when(index < chips - 1)(lambda: line.step(index + 1))

        @pl.when(index == 1)
        def _():
            up.middle()
            down.begin()

        pl.when(index == 2)(down.middle)
        return carry

    lax.fori_loop(0, chips, step, 0)
    total = scatter[0]

    def norm(span):
        resid = rows_ref[span, :].astype(jnp.float32) + total[span, :] + bias_ref[...]
        resid_ref[span, :] = resid
        normed_ref[span, :] = norm_rows(resid, gain_ref[...], shift_ref[...]).astype(jnp.bfloat16)

    by_rows(count, 64, norm)

    def store(block, carry):
        pl.when((block % 2 != place.core))(lambda: line.arrive(block // 2, block % 2))
        keep(block, 0).start()
        keep(block, 1).start()
        return carry

    lax.fori_loop(0, 2 * chips, store, 0)
    sums.finish()
    line.finish()
    up.end()
    down.end()
    up.finish()
    down.finish()
    own[0].wait()
    own[1].wait()

    def kept(block, carry):
        keep(block, 0).wait()
        keep(block, 1).wait()
        return carry

    lax.fori_loop(0, 2 * chips, kept, 0)


def attend_out_call(attended, out_whole, rows, branch, gain, shift, bias, up, down, chips):
    count, width = rows.shape
    total = 2 * chips * count
    low = jnp.bfloat16
    vmem = pl.BlockSpec(memory_space=pltpu.VMEM)
    hbm = pl.BlockSpec(memory_space=pl.ANY)
    dma = pltpu.SemaphoreType.DMA
    return pl.pallas_call(
        functools.partial(attend_out_kernel, chips),
        out_shape=(
            jax.ShapeDtypeStruct((count, width), jnp.float32),
            jax.ShapeDtypeStruct((count, width), low),
            jax.ShapeDtypeStruct((total, width), low),
            jax.ShapeDtypeStruct((4,) + up.shape, low),
            jax.ShapeDtypeStruct((4,) + down.shape, low),
        ),
        in_specs=[vmem] * 9,
        out_specs=(vmem, vmem, hbm, vmem, vmem),
        scratch_shapes=[
            pltpu.VMEM((2 * chips, count, width), low),
            dma((3, chips)),
            dma((2 * chips,)),
            dma((4,)),
            dma((4,)),
            dma((4,)),
            dma((4,)),
            dma((2,)),
            dma((2 * chips, 2)),
        ]
        + scatter_scratch(chips, count, width),
        compiler_params=pltpu.CompilerParams(
            collective_id=1, has_side_effects=True, vmem_limit_bytes=VMEM_LIMIT
        ),
        cost_estimate=pl.CostEstimate(flops=10**11, bytes_accessed=0, transcendentals=0),
        name="attend_out",
    )(attended, out_whole, rows, branch, gain, shift, bias, up, down)


def input_back_kernel(
    chips,
    stacked_ref,
    mix_ref,
    rows_ref,
    resid_grad_ref,
    gain_ref,
    early_ref,
    hidden_ref,
    normed_one_ref,
    normed_two_ref,
    grad_ref,
    late_out_ref,
    early_out_ref,
    mix_grad_ref,
    up_grad_ref,
    columns_buf,
    columns_sem,
    *scatter,
):
    place = Place(chips)
    count = rows_ref.shape[0]
    place.greet(True, True)
    early_out_ref[...] = early_ref[...]
    early = SmallSum(place, early_out_ref, 4, scatter[16:19], scatter[19:21])
    late = SmallSum(place, late_out_ref, late_out_ref.shape[0], scatter[21:24], scatter[24:26])

    def term(block, tile):
        span = pl.ds(pl.multiple_of(block * count, count), count)
        result = None
        for part in range(3):
            product = lax.dot_general(
                stacked_ref[part, span, :],
                mix_ref[part, tile],
                TURNED,
                preferred_element_type=jnp.float32,
            )
            result = product if result is None else result + product
        return result

    sums = LineScatter(place, term, 4, scatter[:4], scatter[4:8])
    sums.begin()
    early.begin()
    half_columns = columns_buf.shape[1]

    def load(source, owner, half):
        start = pl.multiple_of((2 * owner + half) * half_columns, half_columns)
        copy = pltpu.make_async_copy(
            source.at[:, pl.ds(start, half_columns)], columns_buf, columns_sem
        )
        copy.start()
        copy.wait()

    def mix_piece(owner, half):
        load(normed_one_ref, owner, half)
        return jnp.stack(
            [
                lax.dot_general(
                    columns_buf[...],
                    stacked_ref[part],
                    CROSSED,
                    preferred_element_type=jnp.float32,
                )
                for part in range(3)
            ]
        )

    def up_piece(owner, half):
        load(normed_two_ref, owner, half)
        return lax.dot_general(
            columns_buf[...], hidden_ref[...], CROSSED, preferred_element_type=jnp.float32
        )

    mix = SquareScatter(place, mix_piece, mix_grad_ref, scatter[8:10], scatter[10:12])
    up = SquareScatter(place, up_piece, up_grad_ref, scatter[12:14], scatter[14:16])

    def step(index, carry):
        sums.step(index)
        for kind in range(4):

            @pl.when(index == kind)
            def _():
                up.stage(kind)
                mix.stage(kind)
                if kind == 1:
                    early.middle()
                if kind == 2:
                    early.late()

        return carry

    lax.fori_loop(0, chips, step, 0)
    total = scatter[0]
    late_out_ref[...] = jnp.zeros_like(late_out_ref)

    def back(span):
        rows = rows_ref[span, :].astype(jnp.float32)
        one_grad = total[span, :]
        _, hat, inverse = layer_norm_parts(rows, gain_ref[...], 0.0)
        grad_ref[span, :] = resid_grad_ref[span, :] + layer_norm_back(
            one_grad, hat, inverse, gain_ref[...]
        )
        late_out_ref[0:1, :] += jnp.sum(one_grad * hat, axis=0, keepdims=True)
        late_out_ref[1:2, :] += jnp.sum(one_grad, axis=0, keepdims=True)

    by_rows(count, 64, back)
    late.begin()
    early.end()
    up.end()
    late.middle()
    mix.end()
    late.late()
    sums.finish()
    late.end()


def input_back_call(
    stacked, mix_whole, rows, resid_grad, gain, early, hidden, normed_one, normed_two, chips
):
    count, width = rows.shape
    total, units = hidden.shape
    local = stacked.shape[2]
    half = width // 8
    vmem = pl.BlockSpec(memory_space=pltpu.VMEM)
    hbm = pl.BlockSpec(memory_space=pl.ANY)
    return pl.pallas_call(
        functools.partial(input_back_kernel, chips),
        out_shape=(
            jax.ShapeDtypeStruct((count, width), jnp.float32),
            jax.ShapeDtypeStruct((2, width), jnp.float32),
            jax.ShapeDtypeStruct(early.shape, jnp.float32),
            jax.ShapeDtypeStruct((2, 3, half, local), jnp.float32),
            jax.ShapeDtypeStruct((2, half, units), jnp.float32),
        ),
        in_specs=[vmem] * 7 + [hbm] * 2,
        out_specs=(vmem,) * 5,
        scratch_shapes=[
            pltpu.VMEM((total, half), jnp.bfloat16),
            pltpu.SemaphoreType.DMA,
        ]
        + scatter_scratch(chips, count, width)
        + square_scratch((3, half, local))
        + square_scratch((half, units))
        + small_scratch(chips, early.shape[0], width)
        + small_scratch(chips, 2, width),
        compiler_params=pltpu.CompilerParams(
            collective_id=2, has_side_effects=True, vmem_limit_bytes=VMEM_LIMIT
        ),
        cost_estimate=pl.CostEstimate(flops=10**11, bytes_accessed=0, transcendentals=0),
        name="input_back",
    )(stacked, mix_whole, rows, resid_grad, gain, early, hidden, normed_one, normed_two)


GELU_SLOPE = 0.7978845608028654
GELU_CUBE = 0.044715


def gelu_parts(hidden):
    square = hidden * hidden
    bend = jnp.tanh(GELU_SLOPE * hidden * (1.0 + GELU_CUBE * square))
    lift = 0.5 * (1.0 + bend)
    slope = lift + 0.5 * hidden * (1.0 - bend * bend) * (
        GELU_SLOPE * (1.0 + 3.0 * GELU_CUBE * square)
    )
    return hidden * lift, slope


def feed_kernel(
    chips,
    parts,
    normed_ref,
    branch_ref,
    up_ref,
    down_ref,
    bias_ref,
    resid_ref,
    own_branch_ref,
    gain_ref,
    normed_whole,
    active_ref,
    hidden_ref,
    grad_ref,
    grad_low_ref,
    sums_ref,
    bias_grad_ref,
    blocks,
    branch_buf,
    work,
    hold,
    side_out,
    side_in,
    line_in,
    line_send,
    line_recv,
    keep_sem,
    load_sem,
    side_send,
    side_recv,
    out_send,
    out_recv,
):
    place = Place(chips)
    count = normed_ref.shape[0]
    rows = count // parts
    pair = 2 * rows
    last = chips - 1
    place.greet(False)

    def fill(part, carry):
        block = 2 * (place.chip * parts + part) + place.core
        blocks[block] = normed_ref[pl.ds(pl.multiple_of(part * rows, rows), rows), :]
        return carry

    lax.fori_loop(0, parts, fill, 0)
    line = LineGather(place, blocks, line_send, line_recv, parts)
    line.begin()
    bias_grad_ref[...] = jnp.zeros_like(bias_grad_ref)

    def piece_span(piece):
        return pl.ds(pl.multiple_of(piece * pair, pair), pair)

    def load(piece, slot):
        return pltpu.make_async_copy(
            branch_ref.at[piece_span(piece)], branch_buf.at[slot], load_sem.at[slot]
        )

    def keep(piece, core):
        span = pl.ds(pl.multiple_of(piece * pair + core * rows, rows), rows)
        return pltpu.make_async_copy(
            blocks.at[2 * piece + core], normed_whole.at[span], keep_sem.at[piece, core]
        )

    def side_copy(piece):
        return remote(
            side_out.at[piece],
            side_in.at[piece],
            side_send.at[piece],
            side_recv.at[piece],
            place.side,
        )

    def line_copy(way, chip, part):
        piece = chip * parts + part
        next_chip = place.chip + 1 - 2 * way
        slot = jnp.where((way == 1) & (chip == next_chip), chips * parts + part, piece)
        return remote(
            line_in.at[piece],
            line_in.at[slot],
            out_send.at[piece],
            out_recv.at[slot],
            (place.up, place.down)[way],
        )

    def line_landed(way, chip, part):
        piece = chip * parts + part
        slot = jnp.where((way == 1) & (chip == place.chip), chips * parts + part, piece)
        remote(
            line_in.at[slot],
            line_in.at[slot],
            out_send.at[piece],
            out_recv.at[slot],
            (place.up, place.down)[way],
        ).wait_recv()
        return slot

    width = 256
    tiles = up_ref.shape[2] // width

    def compute(chip, part):
        piece = chip * parts + part
        load(piece, 0).start()
        keep(piece, 0).start()
        keep(piece, 1).start()
        span = piece_span(piece)
        own_rows = blocks[pl.ds(2 * piece, 2)].reshape(pair, -1)
        load(piece, 0).wait()

        def tile(index, carry):
            units = pl.ds(pl.multiple_of(index * width, width), width)
            hidden = jnp.dot(
                own_rows,
                up_ref[:, :, units].reshape(-1, width),
                preferred_element_type=jnp.float32,
            )
            active, slope = gelu_parts(hidden + bias_ref[:, units])
            active_ref[span, units] = active.astype(jnp.bfloat16)
            grad = None
            for owner in range(4):
                columns = down_ref.shape[2]
                product = lax.dot_general(
                    branch_buf[0, :, owner * columns : (owner + 1) * columns],
                    down_ref[owner, units, :],
                    TURNED,
                    preferred_element_type=jnp.float32,
                )
                grad = product if grad is None else grad + product
            low = (grad * slope).astype(jnp.bfloat16)
            hidden_ref[span, units] = low
            bias_grad_ref[:, units] += jnp.sum(low.astype(jnp.float32), axis=0, keepdims=True)
            return carry

        lax.fori_loop(0, tiles, tile, 0)
        low = hidden_ref[span, :]
        depth = up_ref.shape[1]
        for owner in range(4):
            columns = slice(owner * depth, (owner + 1) * depth)
            product = lax.dot_general(
                low, up_ref[owner], TURNED, preferred_element_type=jnp.float32
            )
            work[:, :, columns] = product.reshape(2, rows, depth)
        side_out[piece] = work[1 - place.core].astype(jnp.bfloat16)
        side_copy(piece).start()
        hold[piece] = work[place.core]

    def pass_on(way, chip, part):
        piece = chip * parts + part
        side_copy(piece).wait_recv()
        total = hold[piece] + side_in[piece].astype(jnp.float32)
        behind = (place.has_down, place.has_up)[way]

        @pl.when(behind)
        def _():
            slot = line_landed(way, chip, part)
            line_in[piece] = (total + line_in[slot].astype(jnp.float32)).astype(jnp.bfloat16)

        @pl.when(jnp.logical_not(behind))
        def _():
            line_in[piece] = total.astype(jnp.bfloat16)

        line_copy(way, chip, part).start()

    def turn(index, carry):
        distance = index // parts
        part = index % parts

        @pl.when(distance < chips)
        def _():
            pl.when(distance > 0)(lambda: line.step(distance, part))

            def one(side, inner):
                chip = place.chip + distance * (2 * side - 1)

                @pl.when((chip >= 0) & (chip < chips) & ((distance > 0) | (side == 0)))
                def _():
                    line.arrive(chip, 1 - place.core, part)
                    compute(chip, part)

                return inner

            lax.fori_loop(0, 2, one, 0)

        upward = index - place.chip

        @pl.when((upward >= 0) & (upward // parts > place.chip) & (upward // parts < chips))
        def _():
            pass_on(0, upward // parts, upward % parts)

        downward = index - (last - place.chip)
        target = last - downward // parts

        @pl.when((downward >= 0) & (target >= 0) & (target < place.chip))
        def _():
            pass_on(1, target, downward % parts)

        return carry

    lax.fori_loop(0, parts * chips + last, turn, 0)
    sums_ref[...] = jnp.zeros_like(sums_ref)

    def own_part(part, carry):
        piece = place.chip * parts + part
        side_copy(piece).wait_recv()
        hold[piece] += side_in[piece].astype(jnp.float32)

        @pl.when(place.has_down)
        def _():
            slot = line_landed(0, place.chip, part)
            hold[piece] += line_in[slot].astype(jnp.float32)

        @pl.when(place.has_up)
        def _():
            slot = line_landed(1, place.chip, part)
            hold[piece] += line_in[slot].astype(jnp.float32)

        tile = 64

        def back(index, inner):
            here = pl.ds(pl.multiple_of(index * tile, tile), tile)
            span = pl.ds(pl.multiple_of(part * rows + index * tile, tile), tile)
            two_grad = hold[piece, here, :]
            _, hat, inverse = layer_norm_parts(resid_ref[span, :], gain_ref[...], 0.0)
            grad = own_branch_ref[span, :].astype(jnp.float32) + layer_norm_back(
                two_grad, hat, inverse, gain_ref[...]
            )
            grad_ref[span, :] = grad
            grad_low_ref[span, :] = grad.astype(jnp.bfloat16)
            sums_ref[0:1, :] += jnp.sum(two_grad * hat, axis=0, keepdims=True)
            sums_ref[1:2, :] += jnp.sum(two_grad, axis=0, keepdims=True)
            sums_ref[2:3, :] += jnp.sum(grad, axis=0, keepdims=True)
            return inner

        lax.fori_loop(0, rows // tile, back, 0)
        return carry

    lax.fori_loop(0, parts, own_part, 0)
    line.finish()

    def drain(piece, carry):
        side_copy(piece).wait_send()
        keep(piece, 0).wait()
        keep(piece, 1).wait()
        pl.when(piece // parts != place.chip)(
            lambda: line_copy(0, piece // parts, piece % parts).wait_send()
        )
        return carry

    lax.fori_loop(0, chips * parts, drain, 0)


def feed_call(normed, branch, up_whole, down_whole, bias, resid, own_branch, gain, chips):
    count, width = normed.shape
    total = 2 * chips * count
    units = up_whole.shape[2]
    parts = 2
    rows = count // parts
    low = jnp.bfloat16
    vmem = pl.BlockSpec(memory_space=pltpu.VMEM)
    hbm = pl.BlockSpec(memory_space=pl.ANY)
    dma = pltpu.SemaphoreType.DMA
    pieces = chips * parts
    return pl.pallas_call(
        functools.partial(feed_kernel, chips, parts),
        out_shape=(
            jax.ShapeDtypeStruct((total, width), low),
            jax.ShapeDtypeStruct((total, units), low),
            jax.ShapeDtypeStruct((total, units), low),
            jax.ShapeDtypeStruct((count, width), jnp.float32),
            jax.ShapeDtypeStruct((count, width), low),
            jax.ShapeDtypeStruct((3, width), jnp.float32),
            jax.ShapeDtypeStruct((1, units), jnp.float32),
        ),
        in_specs=[vmem, hbm] + [vmem] * 6,
        out_specs=(hbm,) + (vmem,) * 6,
        scratch_shapes=[
            pltpu.VMEM((2 * pieces, rows, width), low),
            pltpu.VMEM((1, 2 * rows, width), low),
            pltpu.VMEM((2, rows, width), jnp.float32),
            pltpu.VMEM((pieces, rows, width), jnp.float32),
            pltpu.VMEM((pieces, rows, width), low),
            pltpu.VMEM((pieces, rows, width), low),
            pltpu.VMEM((pieces + parts, rows, width), low),
            dma((3, pieces)),
            dma((2 * pieces,)),
            dma((pieces, 2)),
            dma((1,)),
            dma((pieces,)),
            dma((pieces,)),
            dma((pieces,)),
            dma((pieces + parts,)),
        ],
        compiler_params=pltpu.CompilerParams(
            collective_id=3, has_side_effects=True, vmem_limit_bytes=VMEM_LIMIT
        ),
        cost_estimate=pl.CostEstimate(flops=10**11, bytes_accessed=0, transcendentals=0),
        name="feed",
    )(normed, branch, up_whole, down_whole, bias, resid, own_branch, gain)


def branch_back_kernel(
    chips,
    parts,
    branch_ref,
    active_ref,
    down_ref,
    attended_ref,
    out_ref,
    resid_ref,
    shift_ref,
    live_ref,
    cotangent_ref,
    attended_grad_ref,
    down_grad_ref,
    out_owned_ref,
    output_ref,
    blocks,
    out_grad_ref,
    columns_buf,
    line_send,
    line_recv,
    columns_sem,
    *scatter,
):
    place = Place(chips)
    count = branch_ref.shape[0]
    rows = count // parts
    place.greet(True)

    def copy_in(span):
        blocks[place.me, span, :] = branch_ref[span, :]

    by_rows(count, 64, copy_in)
    line = LineGather(place, blocks, line_send, line_recv)
    line.begin()

    def term(block, tile):
        chip, core = block // 2, block % 2
        taken = []
        for part in range(parts):
            start = ((chip * parts + part) * 2 + core) * rows
            taken.append(active_ref[pl.ds(pl.multiple_of(start, rows), rows), :])
        return jnp.dot(
            jnp.concatenate(taken, axis=0), down_ref[tile], preferred_element_type=jnp.float32
        )

    sums = LineScatter(place, term, 4, scatter[:4], scatter[4:8])
    sums.begin()
    out_grad_ref[...] = jnp.zeros_like(out_grad_ref)
    down_units = down_ref.shape[1] // 2
    down_columns = down_ref.shape[2]

    def down_piece(owner, half):
        load = pltpu.make_async_copy(
            cotangent_ref.at[:, pl.ds(pl.multiple_of(owner * down_columns, 128), down_columns)],
            columns_buf,
            columns_sem,
        )
        load.start()
        load.wait()
        units = pl.ds(pl.multiple_of(half * down_units, down_units), down_units)
        return lax.dot_general(
            active_ref[:, units], columns_buf[...], CROSSED, preferred_element_type=jnp.float32
        )

    down = SquareScatter(place, down_piece, down_grad_ref, scatter[8:10], scatter[10:12])
    out_units = out_ref.shape[1] // 2

    def out_piece(owner, half):
        units = pl.ds(pl.multiple_of(half * out_units, out_units), out_units)
        columns = pl.ds(pl.multiple_of(owner * down_columns, 128), down_columns)
        return out_grad_ref[units, columns]

    out = SquareScatter(place, out_piece, out_owned_ref, scatter[12:14], scatter[14:16])

    def take(block):
        span = pl.ds(pl.multiple_of(block * count, count), count)
        columns = out_ref.shape[2]
        result = None
        for owner in range(4):
            here = blocks[block, :, owner * columns : (owner + 1) * columns]
            product = lax.dot_general(
                here, out_ref[owner], TURNED, preferred_element_type=jnp.float32
            )
            result = product if result is None else result + product
            out_grad_ref[:, owner * columns : (owner + 1) * columns] += lax.dot_general(
                attended_ref[span, :],
                here,
                (((0,), (0,)), ((), ())),
                preferred_element_type=jnp.float32,
            )
        attended_grad_ref[span, :] = result.astype(jnp.bfloat16)

    def step(index, carry):
        def one(side, inner):
            chip = place.chip + index * (2 * (side % 2) - 1)
            core = (place.core + side // 2) % 2

            @pl.when((chip >= 0) & (chip < chips) & ((index > 0) | (side % 2 == 0)))
            def _():
                pl.when(side >= 2)(lambda: line.arrive(chip, core))
                take(2 * chip + core)

            return inner

        lax.fori_loop(0, 4, one, 0)
        sums.step(index)
        pl.when(index < chips - 1)(lambda: line.step(index + 1))
        for kind in range(4):
            pl.when(index == kind)(lambda: down.stage(kind))
        return carry

    lax.fori_loop(0, chips, step, 0)
    out.stage(0)
    out.stage(1)
    total = scatter[0]

    def emit(span):
        result = resid_ref[span, :] + total[span, :] + shift_ref[...]
        output_ref[span, :] = jnp.where(live_ref[span, :] > 0, result, 0.0).astype(jnp.bfloat16)

    by_rows(count, 64, emit)
    down.end()
    out.stage(2)
    out.stage(3)
    sums.finish()
    line.finish()
    out.end()


def branch_back_call(
    branch, active, down_whole, attended, out_whole, resid, shift, live, cotangent, chips
):
    count, width = branch.shape
    total, local = attended.shape
    _, units, columns = down_whole.shape
    low = jnp.bfloat16
    vmem = pl.BlockSpec(memory_space=pltpu.VMEM)
    hbm = pl.BlockSpec(memory_space=pl.ANY)
    dma = pltpu.SemaphoreType.DMA
    return pl.pallas_call(
        functools.partial(branch_back_kernel, chips, 2),
        out_shape=(
            jax.ShapeDtypeStruct((total, local), low),
            jax.ShapeDtypeStruct((2, units // 2, columns), jnp.float32),
            jax.ShapeDtypeStruct((2, local // 2, columns), jnp.float32),
            jax.ShapeDtypeStruct((count, width), low),
        ),
        in_specs=[vmem] * 8 + [hbm],
        out_specs=(vmem,) * 4,
        scratch_shapes=[
            pltpu.VMEM((2 * chips, count, width), low),
            pltpu.VMEM((local, width), jnp.float32),
            pltpu.VMEM((total, columns), low),
            dma((3, chips)),
            dma((2 * chips,)),
            dma,
        ]
        + scatter_scratch(chips, count, width)
        + square_scratch((units // 2, columns))
        + square_scratch((local // 2, columns)),
        compiler_params=pltpu.CompilerParams(
            collective_id=4, has_side_effects=True, vmem_limit_bytes=VMEM_LIMIT
        ),
        cost_estimate=pl.CostEstimate(flops=10**11, bytes_accessed=0, transcendentals=0),
        name="branch_back",
    )(branch, active, down_whole, attended, out_whole, resid, shift, live, cotangent)


ATTEND_ROWS = 256
ATTEND_KEYS = 512


def tile_mask(row_block, key_block, seg_col_ref, seg_row_ref):
    rows = lax.broadcasted_iota(jnp.int32, (ATTEND_ROWS, ATTEND_KEYS), 0)
    keys = lax.broadcasted_iota(jnp.int32, (ATTEND_ROWS, ATTEND_KEYS), 1)
    causal = keys - rows <= row_block * ATTEND_ROWS - key_block * ATTEND_KEYS
    row_span = pl.ds(pl.multiple_of(row_block * ATTEND_ROWS, ATTEND_ROWS), ATTEND_ROWS)
    key_span = pl.ds(pl.multiple_of(key_block * ATTEND_KEYS, ATTEND_KEYS), ATTEND_KEYS)
    return causal & (seg_col_ref[row_span, :] == seg_row_ref[:, key_span])


def attention_kernel(mixed_ref, seg_col_ref, seg_row_ref, attended_ref, lse_ref, score_ref):
    length = mixed_ref.shape[1]
    heads = mixed_ref.shape[2] // HEAD_DIM
    row_blocks = length // ATTEND_ROWS
    scale = HEAD_DIM ** (-0.5)

    def one(index, carry):
        head = index // row_blocks
        row_block = index % row_blocks
        lanes = pl.ds(pl.multiple_of(head * HEAD_DIM, HEAD_DIM), HEAD_DIM)
        row_span = pl.ds(pl.multiple_of(row_block * ATTEND_ROWS, ATTEND_ROWS), ATTEND_ROWS)
        count = (row_block * ATTEND_ROWS) // ATTEND_KEYS + 1
        query = mixed_ref[0, row_span, lanes]

        def score(key_block, peak):
            key_span = pl.ds(pl.multiple_of(key_block * ATTEND_KEYS, ATTEND_KEYS), ATTEND_KEYS)
            scores = lax.dot_general(
                query, mixed_ref[1, key_span, lanes], TURNED, preferred_element_type=jnp.float32
            )
            mask = tile_mask(row_block, key_block, seg_col_ref, seg_row_ref)
            scores = jnp.where(mask, scores * scale, MASK_FILL)
            score_ref[:, key_span] = scores
            for part in range(ATTEND_KEYS // 128):
                peak = jnp.maximum(peak, scores[:, part * 128 : (part + 1) * 128])
            return peak

        peak = lax.fori_loop(
            0, count, score, jnp.full((ATTEND_ROWS, 128), MASK_FILL, jnp.float32)
        )
        peak = jnp.max(peak, axis=1, keepdims=True)

        def weigh(key_block, mass):
            key_span = pl.ds(pl.multiple_of(key_block * ATTEND_KEYS, ATTEND_KEYS), ATTEND_KEYS)
            weights = jnp.exp(score_ref[:, key_span] - peak)
            score_ref[:, key_span] = weights
            for part in range(ATTEND_KEYS // 128):
                mass = mass + weights[:, part * 128 : (part + 1) * 128]
            return mass

        mass = lax.fori_loop(0, count, weigh, jnp.zeros((ATTEND_ROWS, 128), jnp.float32))
        mass = jnp.sum(mass, axis=1, keepdims=True)
        inverse = 1.0 / mass
        lse_ref[head, row_span, :] = peak + jnp.log(mass)

        def gather(key_block, total):
            key_span = pl.ds(pl.multiple_of(key_block * ATTEND_KEYS, ATTEND_KEYS), ATTEND_KEYS)
            probs = (score_ref[:, key_span] * inverse).astype(jnp.bfloat16)
            return total + jnp.dot(
                probs, mixed_ref[2, key_span, lanes], preferred_element_type=jnp.float32
            )

        total = lax.fori_loop(
            0, count, gather, jnp.zeros((ATTEND_ROWS, HEAD_DIM), jnp.float32)
        )
        attended_ref[row_span, lanes] = total.astype(jnp.bfloat16)
        return carry

    lax.fori_loop(0, heads * row_blocks, one, 0)


def attention_call(mixed, seg_col, seg_row):
    _, length, width = mixed.shape
    heads = width // HEAD_DIM
    vmem = pl.BlockSpec(memory_space=pltpu.VMEM)
    return pl.pallas_call(
        attention_kernel,
        out_shape=(
            jax.ShapeDtypeStruct((length, width), jnp.bfloat16),
            jax.ShapeDtypeStruct((heads, length, 1), jnp.float32),
        ),
        in_specs=[vmem] * 3,
        out_specs=(vmem,) * 2,
        scratch_shapes=[pltpu.VMEM((ATTEND_ROWS, length), jnp.float32)],
        compiler_params=pltpu.CompilerParams(vmem_limit_bytes=VMEM_LIMIT),
        cost_estimate=pl.CostEstimate(flops=10**10, bytes_accessed=0, transcendentals=0),
        name="attention",
    )(mixed, seg_col, seg_row)


def attention_back_kernel(
    mixed_ref,
    seg_col_ref,
    seg_row_ref,
    lse_ref,
    grad_ref,
    stacked_ref,
    bias_grad_ref,
    probs_ref,
    flow_ref,
    key_sum,
    value_sum,
):
    length = mixed_ref.shape[1]
    heads = mixed_ref.shape[2] // HEAD_DIM
    row_blocks = length // ATTEND_ROWS
    scale = HEAD_DIM ** (-0.5)

    def one_head(head, carry):
        lanes = pl.ds(pl.multiple_of(head * HEAD_DIM, HEAD_DIM), HEAD_DIM)
        key_sum[...] = jnp.zeros_like(key_sum)
        value_sum[...] = jnp.zeros_like(value_sum)

        def one(row_block, bias_sum):
            row_span = pl.ds(pl.multiple_of(row_block * ATTEND_ROWS, ATTEND_ROWS), ATTEND_ROWS)
            count = (row_block * ATTEND_ROWS) // ATTEND_KEYS + 1
            query = mixed_ref[0, row_span, lanes]
            grad = grad_ref[row_span, lanes]
            lse = lse_ref[head, row_span, :]

            def first(key_block, delta):
                key_span = pl.ds(pl.multiple_of(key_block * ATTEND_KEYS, ATTEND_KEYS), ATTEND_KEYS)
                scores = lax.dot_general(
                    query,
                    mixed_ref[1, key_span, lanes],
                    TURNED,
                    preferred_element_type=jnp.float32,
                )
                flow = lax.dot_general(
                    grad,
                    mixed_ref[2, key_span, lanes],
                    TURNED,
                    preferred_element_type=jnp.float32,
                )
                mask = tile_mask(row_block, key_block, seg_col_ref, seg_row_ref)
                probs = jnp.exp(jnp.where(mask, scores * scale, MASK_FILL) - lse)
                probs_ref[:, key_span] = probs
                flow_ref[:, key_span] = flow
                product = probs * flow
                for part in range(ATTEND_KEYS // 128):
                    delta = delta + product[:, part * 128 : (part + 1) * 128]
                value_sum[key_span, :] += lax.dot_general(
                    probs.astype(jnp.bfloat16), grad, CROSSED, preferred_element_type=jnp.float32
                )
                return delta

            delta = lax.fori_loop(
                0, count, first, jnp.zeros((ATTEND_ROWS, 128), jnp.float32)
            )
            delta = jnp.sum(delta, axis=1, keepdims=True)

            def second(key_block, total):
                key_span = pl.ds(pl.multiple_of(key_block * ATTEND_KEYS, ATTEND_KEYS), ATTEND_KEYS)
                low = (probs_ref[:, key_span] * (flow_ref[:, key_span] - delta)).astype(
                    jnp.bfloat16
                )
                key_sum[key_span, :] += lax.dot_general(
                    low, query, CROSSED, preferred_element_type=jnp.float32
                )
                return total + jnp.dot(
                    low, mixed_ref[1, key_span, lanes], preferred_element_type=jnp.float32
                )

            total = lax.fori_loop(
                0, count, second, jnp.zeros((ATTEND_ROWS, HEAD_DIM), jnp.float32)
            )
            query_grad = (total * scale).astype(jnp.bfloat16)
            stacked_ref[0, row_span, lanes] = query_grad
            return bias_sum + jnp.sum(query_grad.astype(jnp.float32), axis=0, keepdims=True)

        bias_sum = lax.fori_loop(0, row_blocks, one, jnp.zeros((1, HEAD_DIM), jnp.float32))
        bias_grad_ref[0:1, lanes] = bias_sum
        stacked_ref[1, :, lanes] = (key_sum[...] * scale).astype(jnp.bfloat16)
        value_grad = value_sum[...].astype(jnp.bfloat16)
        stacked_ref[2, :, lanes] = value_grad
        bias_grad_ref[1:2, lanes] = jnp.sum(
            value_grad.astype(jnp.float32), axis=0, keepdims=True
        )
        return carry

    lax.fori_loop(0, heads, one_head, 0)


def attention_back_call(mixed, seg_col, seg_row, lse, grad):
    _, length, width = mixed.shape
    vmem = pl.BlockSpec(memory_space=pltpu.VMEM)
    return pl.pallas_call(
        attention_back_kernel,
        out_shape=(
            jax.ShapeDtypeStruct((3, length, width), jnp.bfloat16),
            jax.ShapeDtypeStruct((2, width), jnp.float32),
        ),
        in_specs=[vmem] * 5,
        out_specs=(vmem,) * 2,
        scratch_shapes=[
            pltpu.VMEM((ATTEND_ROWS, length), jnp.float32),
            pltpu.VMEM((ATTEND_ROWS, length), jnp.float32),
            pltpu.VMEM((length, HEAD_DIM), jnp.float32),
            pltpu.VMEM((length, HEAD_DIM), jnp.float32),
        ],
        compiler_params=pltpu.CompilerParams(vmem_limit_bytes=VMEM_LIMIT),
        cost_estimate=pl.CostEstimate(flops=3 * 10**10, bytes_accessed=0, transcendentals=0),
        name="attention_back",
    )(mixed, seg_col, seg_row, lse, grad)


def tile_scores(query_tile, keys, segment, row_block, col_block):
    key_tile = keys[col_block * BLOCK : (col_block + 1) * BLOCK]
    scale = query_tile.shape[2] ** (-0.5)
    scores = (
        jnp.einsum("qhe,khe->hqk", query_tile, key_tile, preferred_element_type=jnp.float32) * scale
    )
    row_place = row_block * BLOCK + jnp.arange(BLOCK)
    key_place = col_block * BLOCK + jnp.arange(BLOCK)
    row_segment = segment[row_block * BLOCK : (row_block + 1) * BLOCK]
    key_segment = segment[col_block * BLOCK : (col_block + 1) * BLOCK]
    allowed = (key_place[None, :] <= row_place[:, None]) & (
        row_segment[:, None] == key_segment[None, :]
    )
    return (jnp.where(allowed[None], scores, MASK_FILL), allowed)


def attention_forward(queries, keys, values, segment):
    count = queries.shape[0] // BLOCK
    heads = queries.shape[1]
    depth = queries.shape[2]
    outputs = []
    totals = []
    for row_block in range(count):
        query_tile = queries[row_block * BLOCK : (row_block + 1) * BLOCK]
        peak = jnp.full((heads, BLOCK), MASK_FILL, jnp.float32)
        mass = jnp.zeros((heads, BLOCK), jnp.float32)
        for col_block in range(row_block + 1):
            scores, allowed = tile_scores(query_tile, keys, segment, row_block, col_block)
            new_peak = jnp.maximum(peak, jnp.max(scores, axis=-1))
            weights = jnp.where(allowed[None], jnp.exp(scores - new_peak[:, :, None]), 0.0)
            mass = mass * jnp.exp(peak - new_peak) + jnp.sum(weights, axis=-1)
            peak = new_peak
        total = peak + jnp.log(mass)
        gathered = jnp.zeros((BLOCK, heads, depth), jnp.float32)
        for col_block in range(row_block + 1):
            scores, allowed = tile_scores(query_tile, keys, segment, row_block, col_block)
            probs = jnp.where(allowed[None], jnp.exp(scores - total[:, :, None]), 0.0).astype(
                jnp.bfloat16
            )
            value_tile = values[col_block * BLOCK : (col_block + 1) * BLOCK]
            gathered = gathered + jnp.einsum(
                "hqk,khe->qhe", probs, value_tile, preferred_element_type=jnp.float32
            )
        outputs.append(gathered.astype(jnp.bfloat16))
        totals.append(total)
    return (jnp.concatenate(outputs, axis=0), jnp.concatenate(totals, axis=1))


def attention_backward(queries, keys, values, segment, totals, grads):
    count = queries.shape[0] // BLOCK
    heads = queries.shape[1]
    depth = queries.shape[2]
    scale = depth ** (-0.5)
    key_grads = [jnp.zeros((BLOCK, heads, depth), jnp.float32) for index in range(count)]
    value_grads = [jnp.zeros((BLOCK, heads, depth), jnp.float32) for index in range(count)]
    query_grads = []
    for row_block in range(count):
        query_tile = queries[row_block * BLOCK : (row_block + 1) * BLOCK]
        grad_tile = grads[row_block * BLOCK : (row_block + 1) * BLOCK]
        total = totals[:, row_block * BLOCK : (row_block + 1) * BLOCK]
        flows = jnp.zeros((heads, BLOCK), jnp.float32)
        for col_block in range(row_block + 1):
            scores, allowed = tile_scores(query_tile, keys, segment, row_block, col_block)
            probs = jnp.where(allowed[None], jnp.exp(scores - total[:, :, None]), 0.0)
            value_tile = values[col_block * BLOCK : (col_block + 1) * BLOCK]
            prob_grad = jnp.einsum(
                "qhe,khe->hqk", grad_tile, value_tile, preferred_element_type=jnp.float32
            )
            flows = flows + jnp.sum(prob_grad * probs, axis=-1)
            value_grads[col_block] = value_grads[col_block] + jnp.einsum(
                "hqk,qhe->khe",
                probs.astype(jnp.bfloat16),
                grad_tile,
                preferred_element_type=jnp.float32,
            )
        query_sum = jnp.zeros((BLOCK, heads, depth), jnp.float32)
        for col_block in range(row_block + 1):
            scores, allowed = tile_scores(query_tile, keys, segment, row_block, col_block)
            probs = jnp.where(allowed[None], jnp.exp(scores - total[:, :, None]), 0.0)
            value_tile = values[col_block * BLOCK : (col_block + 1) * BLOCK]
            key_tile = keys[col_block * BLOCK : (col_block + 1) * BLOCK]
            prob_grad = jnp.einsum(
                "qhe,khe->hqk", grad_tile, value_tile, preferred_element_type=jnp.float32
            )
            score_grad = (probs * (prob_grad - flows[:, :, None])).astype(jnp.bfloat16)
            query_sum = query_sum + scale * jnp.einsum(
                "hqk,khe->qhe", score_grad, key_tile, preferred_element_type=jnp.float32
            )
            key_grads[col_block] = key_grads[col_block] + scale * jnp.einsum(
                "hqk,qhe->khe", score_grad, query_tile, preferred_element_type=jnp.float32
            )
        query_grads.append(query_sum)
    return (
        jnp.concatenate(query_grads, axis=0).astype(jnp.bfloat16),
        jnp.concatenate(key_grads, axis=0).astype(jnp.bfloat16),
        jnp.concatenate(value_grads, axis=0).astype(jnp.bfloat16),
    )


def adam_update(master, grad, first, second, rate, decay, first_fix, second_fix):
    first_next = BETA_FIRST * first + (1.0 - BETA_FIRST) * grad
    second_next = BETA_SECOND * second + (1.0 - BETA_SECOND) * grad * grad
    change = (
        first_next / first_fix / (jnp.sqrt(second_next / second_fix) + ADAM_EPSILON)
        + decay * master
    )
    return (master - rate * change, first_next, second_next)


def per_device(
    layer_input,
    cotangent,
    lengths,
    offsets,
    step,
    mix_weight,
    out_weight,
    up_weight,
    down_weight,
    mix_first,
    out_first,
    up_first,
    down_first,
    mix_second,
    out_second,
    up_second,
    down_second,
    mix_bias,
    up_bias,
    norm_gains,
    shifts,
    mix_bias_first,
    up_bias_first,
    gains_first,
    shifts_first,
    mix_bias_second,
    up_bias_second,
    gains_second,
    shifts_second,
):
    own_rows = layer_input.shape[0]
    parts = lax.axis_size("mp")
    group_rows = own_rows * parts
    slots_here = lengths.shape[0]
    slot_len = group_rows // slots_here
    local_width = mix_weight.shape[2]
    positions = jnp.arange(slot_len, dtype=jnp.int32)
    live = (positions[None, :] >= offsets[:, None]) & (
        positions[None, :] < (offsets + lengths)[:, None]
    )
    first_row = lax.axis_index("mp") * own_rows
    own_live = own_slice(live.reshape(-1), first_row, own_rows)[:, None]
    low = jnp.bfloat16
    normed_one, mixed, mix_whole, out_whole = project_call(
        layer_input,
        norm_gains[0:1],
        shifts[0:1],
        mix_weight.astype(low),
        out_weight.astype(low),
        mix_bias,
        parts // 2,
    )
    out_grad = jnp.where(own_live, cotangent.astype(jnp.float32), 0.0)
    bias_down_grad = jnp.sum(out_grad, axis=0)
    seg_col = live.reshape(-1, 1).astype(jnp.float32)
    seg_row = live.reshape(1, -1).astype(jnp.float32)
    attended_flat, lse = attention_call(mixed, seg_col, seg_row)
    resid_own, normed_mid, branch_grad, up_whole, down_whole = attend_out_call(
        attended_flat,
        out_whole,
        layer_input,
        out_grad.astype(low),
        norm_gains[1:2],
        shifts[2:3],
        shifts[1:2],
        up_weight.astype(low),
        down_weight.astype(low),
        parts // 2,
    )
    own_branch = out_grad.astype(low)
    normed_two, active, hidden_grad, resid_grad, resid_low, row_sums, up_bias_grad = feed_call(
        normed_mid,
        branch_grad,
        up_whole,
        down_whole,
        up_bias[None],
        resid_own,
        own_branch,
        norm_gains[1:2],
        parts // 2,
    )
    up_bias_grad = up_bias_grad[0]
    attended_grad, down_pieces, out_pieces, layer_output = branch_back_call(
        resid_low,
        active,
        down_whole,
        attended_flat,
        out_whole,
        resid_own,
        shifts[3:4],
        own_live.astype(jnp.float32),
        branch_grad,
        parts // 2,
    )
    stacked, mix_bias_grad = attention_back_call(mixed, seg_col, seg_row, lse, attended_grad)
    early = jnp.concatenate(
        [
            row_sums,
            bias_down_grad[None],
            jnp.pad(
                jnp.concatenate([mix_bias_grad.reshape(-1), up_bias_grad]),
                (0, row_sums.shape[1] - 2 * local_width - up_bias_grad.shape[0]),
            )[None]
        ],
        axis=0,
    )
    input_grad, late, early, mix_pieces, up_pieces = input_back_call(
        stacked,
        mix_whole,
        layer_input,
        resid_grad,
        norm_gains[0:1],
        early,
        hidden_grad,
        normed_one,
        normed_two,
        parts // 2,
    )
    mix_owned = mix_pieces.transpose(1, 0, 2, 3).reshape(mix_weight.shape)
    up_owned = up_pieces.reshape(up_weight.shape)
    down_owned = down_pieces.reshape(down_weight.shape)
    out_owned = out_pieces.reshape(out_weight.shape)
    mix_bias_total = early[4, : 2 * local_width].reshape(2, local_width)
    up_bias_total = early[4, 2 * local_width : 2 * local_width + up_bias.shape[0]]
    gain_total = jnp.stack([late[0], early[0]])
    shift_total = jnp.stack([late[1], early[2], early[1], early[3]])
    step_count = step[0].astype(jnp.float32)
    first_fix = 1.0 - BETA_FIRST**step_count
    second_fix = 1.0 - BETA_SECOND**step_count
    mix_new = adam_update(
        mix_weight,
        mix_owned,
        mix_first,
        mix_second,
        D ** (-0.5),
        MATRIX_DECAY,
        first_fix,
        second_fix,
    )
    out_new = adam_update(
        out_weight,
        out_owned,
        out_first,
        out_second,
        OUT_FAN ** (-0.5),
        MATRIX_DECAY,
        first_fix,
        second_fix,
    )
    up_new = adam_update(
        up_weight, up_owned, up_first, up_second, D ** (-0.5), MATRIX_DECAY, first_fix, second_fix
    )
    down_new = adam_update(
        down_weight,
        down_owned,
        down_first,
        down_second,
        FF ** (-0.5),
        MATRIX_DECAY,
        first_fix,
        second_fix,
    )
    mix_bias_new = adam_update(
        mix_bias,
        mix_bias_total,
        mix_bias_first,
        mix_bias_second,
        SMALL_RATE,
        0.0,
        first_fix,
        second_fix,
    )
    up_bias_new = adam_update(
        up_bias,
        up_bias_total,
        up_bias_first,
        up_bias_second,
        SMALL_RATE,
        0.0,
        first_fix,
        second_fix,
    )
    gains_new = adam_update(
        norm_gains, gain_total, gains_first, gains_second, SMALL_RATE, 0.0, first_fix, second_fix
    )
    shifts_new = adam_update(
        shifts, shift_total, shifts_first, shifts_second, SMALL_RATE, 0.0, first_fix, second_fix
    )
    return (
        layer_output,
        input_grad,
        mix_new[0],
        mix_new[1],
        mix_new[2],
        out_new[0],
        out_new[1],
        out_new[2],
        up_new[0],
        up_new[1],
        up_new[2],
        down_new[0],
        down_new[1],
        down_new[2],
        mix_bias_new[0],
        mix_bias_new[1],
        mix_bias_new[2],
        up_bias_new[0],
        up_bias_new[1],
        up_bias_new[2],
        gains_new[0],
        gains_new[1],
        gains_new[2],
        shifts_new[0],
        shifts_new[1],
        shifts_new[2],
        mix_owned,
        out_owned,
        up_owned,
        down_owned,
        mix_bias_total,
        up_bias_total,
        gain_total,
        shift_total,
        mix_new[0].astype(jnp.bfloat16),
        out_new[0].astype(jnp.bfloat16),
        up_new[0].astype(jnp.bfloat16),
        down_new[0].astype(jnp.bfloat16),
    )


def per_device_any(
    layer_input,
    cotangent,
    lengths,
    offsets,
    step,
    mix_weight,
    out_weight,
    up_weight,
    down_weight,
    mix_first,
    out_first,
    up_first,
    down_first,
    mix_second,
    out_second,
    up_second,
    down_second,
    mix_bias,
    up_bias,
    norm_gains,
    shifts,
    mix_bias_first,
    up_bias_first,
    gains_first,
    shifts_first,
    mix_bias_second,
    up_bias_second,
    gains_second,
    shifts_second,
):
    own_rows = layer_input.shape[0]
    parts = lax.axis_size("mp")
    group_rows = own_rows * parts
    slots_here = lengths.shape[0]
    slot_len = group_rows // slots_here
    local_width = mix_weight.shape[2]
    depth = HEAD_DIM
    heads_here = local_width // depth
    positions = jnp.arange(slot_len, dtype=jnp.int32)
    live = (positions[None, :] >= offsets[:, None]) & (
        positions[None, :] < (offsets + lengths)[:, None]
    )
    segment = live.astype(jnp.int32)
    first_row = lax.axis_index("mp") * own_rows
    own_live = own_slice(live.reshape(-1), first_row, own_rows)[:, None]
    own_input = layer_input.astype(jnp.float32)
    normed_own, hat_one, inv_one = layer_norm_parts(own_input, norm_gains[0], shifts[0])
    normed_one = gather_rows(normed_own.astype(jnp.bfloat16))
    mix_full = gather_shards(mix_weight.astype(jnp.bfloat16), 1)
    out_full = gather_shards(out_weight.astype(jnp.bfloat16), 1)
    up_full = gather_shards(up_weight.astype(jnp.bfloat16), 0)
    down_full = gather_shards(down_weight.astype(jnp.bfloat16), 1)
    out_grad = jnp.where(own_live, cotangent.astype(jnp.float32), 0.0)
    bias_down_grad = jnp.sum(out_grad, axis=0)
    branch_grad = gather_rows(out_grad.astype(jnp.bfloat16))
    mixed = jnp.einsum("td,cde->cte", normed_one, mix_full, preferred_element_type=jnp.float32)
    queries = (
        (mixed[0] + mix_bias[0])
        .astype(jnp.bfloat16)
        .reshape(slots_here, slot_len, heads_here, depth)
    )
    keys = mixed[1].astype(jnp.bfloat16).reshape(slots_here, slot_len, heads_here, depth)
    values = (
        (mixed[2] + mix_bias[1])
        .astype(jnp.bfloat16)
        .reshape(slots_here, slot_len, heads_here, depth)
    )

    def attend(item):
        return attention_forward(item[0], item[1], item[2], item[3])

    attended, totals = lax.map(attend, (queries, keys, values, segment))
    attended_flat = attended.reshape(group_rows, local_width)
    attn_part = jnp.dot(attended_flat, out_full, preferred_element_type=jnp.float32)
    resid_own = own_input + scatter_rows(attn_part) + shifts[1]
    normed_mid, hat_two, inv_two = layer_norm_parts(resid_own, norm_gains[1], shifts[2])
    normed_two = gather_rows(normed_mid.astype(jnp.bfloat16))
    hidden = jnp.dot(normed_two, up_full, preferred_element_type=jnp.float32) + up_bias
    active_value, gelu_pull = jax.vjp(tanh_gelu, hidden)
    active = active_value.astype(jnp.bfloat16)
    active_grad = jnp.einsum(
        "td,fd->tf", branch_grad, down_full, preferred_element_type=jnp.float32
    )
    hidden_grad = gelu_pull(active_grad)[0].astype(jnp.bfloat16)
    two_part = jnp.einsum("tf,df->td", hidden_grad, up_full, preferred_element_type=jnp.float32)
    two_grad = scatter_rows(two_part)
    down_part = jnp.dot(active, down_full, preferred_element_type=jnp.float32)
    down_grad = jnp.einsum("tf,td->fd", active, branch_grad, preferred_element_type=jnp.float32)
    up_bias_grad = jnp.sum(hidden_grad, axis=0, dtype=jnp.float32)
    up_grad = jnp.einsum("td,tf->df", normed_two, hidden_grad, preferred_element_type=jnp.float32)
    resid_grad = out_grad + layer_norm_back(two_grad, hat_two, inv_two, norm_gains[1])
    attn_branch = gather_rows(resid_grad.astype(jnp.bfloat16))
    result_own = resid_own + scatter_rows(down_part) + shifts[3]
    layer_output = jnp.where(own_live, result_own, 0.0).astype(jnp.bfloat16)
    gain_two_grad = jnp.sum(two_grad * hat_two, axis=0)
    shift_two_grad = jnp.sum(two_grad, axis=0)
    bias_out_grad = jnp.sum(resid_grad, axis=0)
    attended_grad = jnp.einsum(
        "td,ed->te", attn_branch, out_full, preferred_element_type=jnp.float32
    ).astype(jnp.bfloat16)
    out_weight_grad = jnp.einsum(
        "te,td->ed", attended_flat, attn_branch, preferred_element_type=jnp.float32
    )

    def attend_back(item):
        return attention_backward(item[0], item[1], item[2], item[3], item[4], item[5])

    query_grad, key_grad, value_grad = lax.map(
        attend_back,
        (
            queries,
            keys,
            values,
            segment,
            totals,
            attended_grad.reshape(slots_here, slot_len, heads_here, depth),
        ),
    )
    stacked = jnp.stack(
        [
            query_grad.reshape(group_rows, local_width),
            key_grad.reshape(group_rows, local_width),
            value_grad.reshape(group_rows, local_width),
        ]
    )
    one_part = jnp.einsum("cte,cde->td", stacked, mix_full, preferred_element_type=jnp.float32)
    one_grad = scatter_rows(one_part)
    mix_grad = jnp.einsum("td,cte->cde", normed_one, stacked, preferred_element_type=jnp.float32)
    mix_bias_grad = jnp.stack(
        [
            jnp.sum(stacked[0], axis=0, dtype=jnp.float32),
            jnp.sum(stacked[2], axis=0, dtype=jnp.float32),
        ]
    )
    mix_owned = scatter_shards(mix_grad, 1)
    out_owned = scatter_shards(out_weight_grad, 1)
    up_owned = scatter_shards(up_grad, 0)
    down_owned = scatter_shards(down_grad, 1)
    input_grad = resid_grad + layer_norm_back(one_grad, hat_one, inv_one, norm_gains[0])
    gain_one_grad = jnp.sum(one_grad * hat_one, axis=0)
    shift_one_grad = jnp.sum(one_grad, axis=0)
    gain_grad = jnp.stack([gain_one_grad, gain_two_grad])
    shift_grad = jnp.stack([shift_one_grad, bias_out_grad, shift_two_grad, bias_down_grad])
    mix_bias_total, up_bias_total = lax.psum((mix_bias_grad, up_bias_grad), "dp")
    gain_total, shift_total = lax.psum((gain_grad, shift_grad), ("dp", "mp"))
    step_count = step[0].astype(jnp.float32)
    first_fix = 1.0 - BETA_FIRST**step_count
    second_fix = 1.0 - BETA_SECOND**step_count
    mix_new = adam_update(
        mix_weight,
        mix_owned,
        mix_first,
        mix_second,
        D ** (-0.5),
        MATRIX_DECAY,
        first_fix,
        second_fix,
    )
    out_new = adam_update(
        out_weight,
        out_owned,
        out_first,
        out_second,
        OUT_FAN ** (-0.5),
        MATRIX_DECAY,
        first_fix,
        second_fix,
    )
    up_new = adam_update(
        up_weight, up_owned, up_first, up_second, D ** (-0.5), MATRIX_DECAY, first_fix, second_fix
    )
    down_new = adam_update(
        down_weight,
        down_owned,
        down_first,
        down_second,
        FF ** (-0.5),
        MATRIX_DECAY,
        first_fix,
        second_fix,
    )
    mix_bias_new = adam_update(
        mix_bias,
        mix_bias_total,
        mix_bias_first,
        mix_bias_second,
        SMALL_RATE,
        0.0,
        first_fix,
        second_fix,
    )
    up_bias_new = adam_update(
        up_bias,
        up_bias_total,
        up_bias_first,
        up_bias_second,
        SMALL_RATE,
        0.0,
        first_fix,
        second_fix,
    )
    gains_new = adam_update(
        norm_gains, gain_total, gains_first, gains_second, SMALL_RATE, 0.0, first_fix, second_fix
    )
    shifts_new = adam_update(
        shifts, shift_total, shifts_first, shifts_second, SMALL_RATE, 0.0, first_fix, second_fix
    )
    return (
        layer_output,
        input_grad,
        mix_new[0],
        mix_new[1],
        mix_new[2],
        out_new[0],
        out_new[1],
        out_new[2],
        up_new[0],
        up_new[1],
        up_new[2],
        down_new[0],
        down_new[1],
        down_new[2],
        mix_bias_new[0],
        mix_bias_new[1],
        mix_bias_new[2],
        up_bias_new[0],
        up_bias_new[1],
        up_bias_new[2],
        gains_new[0],
        gains_new[1],
        gains_new[2],
        shifts_new[0],
        shifts_new[1],
        shifts_new[2],
        mix_owned,
        out_owned,
        up_owned,
        down_owned,
        mix_bias_total,
        up_bias_total,
        gain_total,
        shift_total,
        mix_new[0].astype(jnp.bfloat16),
        out_new[0].astype(jnp.bfloat16),
        up_new[0].astype(jnp.bfloat16),
        down_new[0].astype(jnp.bfloat16),
    )


def solution(mesh):
    placed = (
        P(("dp", "mp"), None),
        P(("dp", "mp"), None),
        P("dp"),
        P("dp"),
        P(),
        P(None, "dp", "mp"),
        P("mp", "dp"),
        P("dp", "mp"),
        P("mp", "dp"),
        P(None, "dp", "mp"),
        P("mp", "dp"),
        P("dp", "mp"),
        P("mp", "dp"),
        P(None, "dp", "mp"),
        P("mp", "dp"),
        P("dp", "mp"),
        P("mp", "dp"),
        P(None, "mp"),
        P("mp"),
        P(),
        P(),
        P(None, "mp"),
        P("mp"),
        P(),
        P(),
        P(None, "mp"),
        P("mp"),
        P(),
        P(),
    )
    fits = mesh.shape["dp"] == 4 and mesh.shape["mp"] == 8
    return jax.shard_map(
        per_device if fits else per_device_any,
        mesh=mesh,
        in_specs=placed,
        out_specs=(
            P(("dp", "mp"), None),
            P(("dp", "mp"), None),
            P(None, "dp", "mp"),
            P(None, "dp", "mp"),
            P(None, "dp", "mp"),
            P("mp", "dp"),
            P("mp", "dp"),
            P("mp", "dp"),
            P("dp", "mp"),
            P("dp", "mp"),
            P("dp", "mp"),
            P("mp", "dp"),
            P("mp", "dp"),
            P("mp", "dp"),
            P(None, "mp"),
            P(None, "mp"),
            P(None, "mp"),
            P("mp"),
            P("mp"),
            P("mp"),
            P(),
            P(),
            P(),
            P(),
            P(),
            P(),
            P(None, "dp", "mp"),
            P("mp", "dp"),
            P("dp", "mp"),
            P("mp", "dp"),
            P(None, "mp"),
            P("mp"),
            P(),
            P(),
            P(None, "dp", "mp"),
            P("mp", "dp"),
            P("dp", "mp"),
            P("mp", "dp"),
        ),
        check_vma=False,
    )
```

```python
import functools

import jax
import jax.numpy as jnp
from jax import lax
from jax.experimental import pallas as pl
from jax.experimental.pallas import tpu as pltpu
from jax.sharding import PartitionSpec as P

D = 2048
HEAD_DIM = 128
FF = 8192
BLOCK = 512
OUT_FAN = 7


NORM_EPSILON = 1e-05
ADAM_EPSILON = 1e-08
BETA_FIRST = 0.9
BETA_SECOND = 0.999
MATRIX_DECAY = 0.1
SMALL_RATE = 0.2
MASK_FILL = -1e30


def layer_norm_parts(rows, gain, shift):
    center = rows - jnp.mean(rows, axis=-1, keepdims=True)
    inverse = lax.rsqrt(jnp.mean(center * center, axis=-1, keepdims=True) + NORM_EPSILON)
    normed = center * inverse
    return (normed * gain + shift, normed, inverse)


def layer_norm_back(grad_out, normed, inverse, gain):
    scaled = grad_out * gain
    return inverse * (
        scaled
        - jnp.mean(scaled, axis=-1, keepdims=True)
        - normed * jnp.mean(scaled * normed, axis=-1, keepdims=True)
    )


def tanh_gelu(values):
    return jax.nn.gelu(values, approximate=True)


def own_slice(whole, first_row, count):
    return lax.dynamic_slice_in_dim(whole, first_row, count, 0)


def gather_rows(rows):
    return lax.all_gather(rows, "mp", axis=0, tiled=True)


def scatter_rows(terms):
    low = terms.astype(jnp.bfloat16)
    return lax.psum_scatter(low, "mp", scatter_dimension=0, tiled=True).astype(jnp.float32)


def swap(value, mask):
    size = lax.axis_size("dp")
    return lax.ppermute(value, "dp", [(place, place ^ mask) for place in range(size)])


def gather_shards(shard, axis):
    if lax.axis_size("dp") != 4:
        return lax.all_gather(shard, "dp", axis=axis, tiled=True)
    count = shard.shape[axis]
    me = lax.axis_index("dp")
    from_x = swap(shard, 1)
    from_y = swap(shard, 2)
    half = count // 2
    low = swap(lax.slice_in_dim(from_x, 0, half, axis=axis), 2)
    high = swap(lax.slice_in_dim(from_y, half, count, axis=axis), 1)
    shape = list(shard.shape)
    shape[axis] = 4 * count
    full = jnp.zeros(shape, shard.dtype)
    full = lax.dynamic_update_slice_in_dim(full, shard, me * count, axis)
    full = lax.dynamic_update_slice_in_dim(full, from_x, (me ^ 1) * count, axis)
    full = lax.dynamic_update_slice_in_dim(full, from_y, (me ^ 2) * count, axis)
    full = lax.dynamic_update_slice_in_dim(full, low, (me ^ 3) * count, axis)
    return lax.dynamic_update_slice_in_dim(full, high, (me ^ 3) * count + half, axis)


def scatter_shards(grad, axis):
    if lax.axis_size("dp") != 4:
        return lax.psum_scatter(grad, "dp", scatter_dimension=axis, tiled=True)
    count = grad.shape[axis] // 4
    half = count // 2
    me = lax.axis_index("dp")

    def piece(owner, upper):
        return lax.dynamic_slice_in_dim(grad, owner * count + upper * half, half, axis)

    def one_way(first, second, upper):
        near = swap(piece(me ^ first, upper).astype(jnp.bfloat16), first)
        far = swap(piece(me ^ 3, upper).astype(jnp.bfloat16), first)
        onward = piece(me ^ second, upper) + far.astype(jnp.float32)
        last = swap(onward.astype(jnp.bfloat16), second)
        return piece(me, upper) + near.astype(jnp.float32) + last.astype(jnp.float32)

    return lax.concatenate([one_way(1, 2, 0), one_way(2, 1, 1)], axis)


MESH = pl.DeviceIdType.MESH
VMEM_LIMIT = 62 * 1024 * 1024
TURNED = (((1,), (1,)), ((), ()))
CROSSED = (((0,), (0,)), ((), ()))


class Place:
    def __init__(self, chips):
        self.chips = chips
        self.dp = lax.axis_index("dp")
        self.me = lax.axis_index("mp")
        self.chip = self.me // 2
        self.core = self.me % 2
        self.has_up = self.chip < chips - 1
        self.has_down = self.chip > 0
        self.up = (self.dp, jnp.minimum(self.me + 2, 2 * chips - 1))
        self.down = (self.dp, jnp.maximum(self.me - 2, 0))
        self.side = (self.dp, self.me + 1 - 2 * self.core)
        self.x_peer = self.dp + 1 - 2 * (self.dp % 2)
        self.y_peer = (self.dp + 2) % 4
        self.across = 3 - self.dp
        self.x_way = (self.x_peer, self.me)
        self.y_way = (self.y_peer, self.me)

    def greet(self, square, everyone=False):
        barrier = pltpu.get_barrier_semaphore()

        def signal(device):
            pl.semaphore_signal(barrier, inc=1, device_id=device, device_id_type=MESH)

        signal(self.side)
        pl.when(self.has_up)(lambda: signal(self.up))
        pl.when(self.has_down)(lambda: signal(self.down))
        count = 1 + self.has_up.astype(jnp.int32) + self.has_down.astype(jnp.int32)
        if square:
            signal(self.x_way)
            signal(self.y_way)
            count = count + 2
        if everyone:
            signal((self.across, self.me))
            count = count + 1

            def beyond(chip, carry):
                far = (chip > self.chip + 1) | (chip < self.chip - 1)
                pl.when(far)(lambda: signal((self.dp, 2 * chip + self.core)))
                return carry

            lax.fori_loop(0, self.chips, beyond, 0)
            near = self.has_up.astype(jnp.int32) + self.has_down.astype(jnp.int32)
            count = count + (self.chips - 1) - near
        pl.semaphore_wait(barrier, count)


def remote(source, target, send, recv, device):
    return pltpu.make_async_remote_copy(
        src_ref=source,
        dst_ref=target,
        send_sem=send,
        recv_sem=recv,
        device_id=device,
        device_id_type=MESH,
    )


def fetch(pairs, sems):
    copies = [
        pltpu.make_async_copy(source, target, sems.at[index])
        for index, (source, target) in enumerate(pairs)
    ]
    for copy in copies:
        copy.start()
    return copies


class LineGather:
    def __init__(self, place, blocks, send, recv, parts=1, own=None):
        self.place, self.blocks, self.send, self.recv = place, blocks, send, recv
        self.parts, self.own = parts, own

    def copy(self, way, chip, part=0, own=None):
        place = self.place
        piece = chip * self.parts + part
        block = 2 * piece + place.core
        device = (place.up, place.down, place.side)[way]
        return remote(
            self.blocks.at[block] if own is None else own,
            self.blocks.at[block],
            self.send.at[way, piece],
            self.recv.at[block],
            device,
        )

    def arrive(self, chip, core, part=0):
        piece = chip * self.parts + part
        block = 2 * piece + core
        remote(
            self.blocks.at[block],
            self.blocks.at[block],
            self.send.at[2, piece],
            self.recv.at[block],
            self.place.side,
        ).wait_recv()

    def begin(self):
        place = self.place
        for part in range(self.parts):
            pl.when(place.has_up)(lambda: self.copy(0, place.chip, part, self.own).start())
            pl.when(place.has_down)(lambda: self.copy(1, place.chip, part, self.own).start())
            self.copy(2, place.chip, part, self.own).start()

    def step(self, distance, part=0):
        place = self.place
        low = place.chip - distance
        high = place.chip + distance

        @pl.when(low >= 0)
        def _():
            self.arrive(low, place.core, part)
            pl.when(place.has_up)(lambda: self.copy(0, low, part).start())
            self.copy(2, low, part).start()

        @pl.when(high < place.chips)
        def _():
            self.arrive(high, place.core, part)
            pl.when(place.has_down)(lambda: self.copy(1, high, part).start())
            self.copy(2, high, part).start()

    def finish(self):
        place = self.place

        def drain(chip, carry):
            for part in range(self.parts):
                pl.when(place.has_up & (chip <= place.chip))(
                    lambda: self.copy(0, chip, part).wait_send()
                )
                pl.when(place.has_down & (chip >= place.chip))(
                    lambda: self.copy(1, chip, part).wait_send()
                )
                self.copy(2, chip, part).wait_send()
            return carry

        lax.fori_loop(0, place.chips, drain, 0)


class SquareGather:
    def __init__(self, place, shard, view, half, send, recv):
        self.place, self.shard, self.view, self.half = place, shard, view, half
        self.send, self.recv = send, recv

    def first(self, way):
        place = self.place
        device = (place.x_way, place.y_way)[way]
        return remote(
            self.shard, self.view(place.dp), self.send.at[way], self.recv.at[way], device
        )

    def first_landed(self, way):
        place = self.place
        owner = (place.x_peer, place.y_peer)[way]
        device = (place.x_way, place.y_way)[way]
        remote(
            self.view(owner), self.view(owner), self.send.at[way], self.recv.at[way], device
        ).wait_recv()

    def second(self, way):
        place = self.place
        owner = (place.y_peer, place.x_peer)[way]
        device = (place.x_way, place.y_way)[way]
        part = self.half(owner, 1 - way)
        return remote(part, part, self.send.at[2 + way], self.recv.at[2 + way], device)

    def second_landed(self, way):
        place = self.place
        device = (place.x_way, place.y_way)[way]
        part = self.half(place.across, 1 - way)
        remote(part, part, self.send.at[2 + way], self.recv.at[2 + way], device).wait_recv()

    def begin(self):
        self.first(0).start()
        self.first(1).start()

    def middle(self):
        self.first_landed(0)
        self.second(1).start()
        self.first_landed(1)
        self.second(0).start()

    def end(self):
        self.second_landed(0)
        self.second_landed(1)

    def finish(self):
        self.first(0).wait_send()
        self.first(1).wait_send()
        self.second(0).wait_send()
        self.second(1).wait_send()


def norm_rows(rows, gain, shift):
    normed, hat, inverse = layer_norm_parts(rows, gain, shift)
    return normed


def project_kernel(
    chips,
    rows_ref,
    gain_ref,
    shift_ref,
    mix_weight_ref,
    out_weight_ref,
    bias_ref,
    up_weight_ref,
    down_weight_ref,
    cotangent_ref,
    bounds_ref,
    normed_ref,
    mixed_hbm,
    mix_hbm,
    out_whole,
    up_ref,
    down_ref,
    branch_ref,
    branch_sum_ref,
    mix_ref,
    out_ref,
    mixed_ref,
    mix_whole,
    emit_sem,
    blocks,
    line_send,
    line_recv,
    mix_send,
    mix_recv,
    out_send,
    out_recv,
    own_sem,
    keep_sem,
):
    place = Place(chips)
    count = rows_ref.shape[0]
    place.greet(True)
    mix = SquareGather(
        place,
        mix_ref,
        lambda owner: mix_whole.at[:, owner],
        lambda owner, which: mix_whole.at[:, owner, pl.ds(which * 256, 256)],
        mix_send,
        mix_recv,
    )
    out = SquareGather(
        place,
        out_ref,
        lambda owner: out_whole.at[owner],
        lambda owner, which: out_whole.at[owner, pl.ds(which * 128, 128)],
        out_send,
        out_recv,
    )

    def lower(source, target):
        def one(span):
            target[span, :] = source[span, :].astype(jnp.bfloat16)

        by_rows(source.shape[0], 64, one)

    for part in range(3):
        lower(mix_weight_ref.at[part], mix_ref.at[part])
    lower(out_weight_ref, out_ref)
    mix.begin()
    own_mix = pltpu.make_async_copy(mix_ref, mix_whole.at[:, place.dp], own_sem.at[0])
    own_out = pltpu.make_async_copy(out_ref, out_whole.at[place.dp], own_sem.at[1])
    own_mix.start()
    own_out.start()
    tile = 64

    def norm(index, carry):
        span = pl.ds(pl.multiple_of(index * tile, tile), tile)
        rows = rows_ref[span, :].astype(jnp.float32)
        normed = norm_rows(rows, gain_ref[...], shift_ref[...])
        blocks[place.me, span, :] = normed.astype(jnp.bfloat16)
        return carry

    lax.fori_loop(0, count // tile, norm, 0)
    line = LineGather(place, blocks, line_send, line_recv)
    line.begin()
    branch_sum_ref[...] = jnp.zeros_like(branch_sum_ref)

    def branch(span):
        live = alive((64, 1), 0, place.me * count + span.start, bounds_ref)
        grad = jnp.where(live > 0, cotangent_ref[span, :].astype(jnp.float32), 0.0)
        branch_ref[span, :] = grad.astype(jnp.bfloat16)
        branch_sum_ref[...] += jnp.sum(grad, axis=0, keepdims=True)

    by_rows(count, 64, branch)
    lower(up_weight_ref, up_ref)
    lower(down_weight_ref, down_ref)
    mix.middle()
    out.begin()

    def keep(block):
        span = pl.ds(pl.multiple_of(block * count, count), count)
        return pltpu.make_async_copy(blocks.at[block], normed_ref.at[span], keep_sem.at[block])

    def emit(block):
        span = pl.ds(pl.multiple_of(block * count, count), count)
        return pltpu.make_async_copy(
            mixed_ref.at[:, span], mixed_hbm.at[:, span], emit_sem.at[block]
        )

    keep_mix = pltpu.make_async_copy(mix_whole, mix_hbm, emit_sem.at[2 * chips])

    def project(block):
        keep(block).start()
        span = pl.ds(pl.multiple_of(block * count, count), count)
        rows = blocks[block]
        for part in range(3):
            weight = mix_whole[part].reshape(-1, mix_whole.shape[3])
            result = jnp.dot(rows, weight, preferred_element_type=jnp.float32)
            if part == 0:
                result = result + bias_ref[0:1, :]
            if part == 2:
                result = result + bias_ref[1:2, :]
            mixed_ref[part, span, :] = result.astype(jnp.bfloat16)
        emit(block).start()

    def step(distance, carry):
        @pl.when((distance > 0) & (distance < chips))
        def _():
            line.step(distance)

        @pl.when(distance == 1)
        def _():
            mix.end()
            own_mix.wait()
            keep_mix.start()
            out.middle()

        def one(index, inner):
            near = distance - 1
            side = index % 2
            core = (place.core + index // 2) % 2
            chip = place.chip + near * (2 * side - 1)

            @pl.when((chip >= 0) & (chip < chips) & ((near > 0) | (side == 0)))
            def _():
                pl.when(index >= 2)(lambda: line.arrive(chip, core))
                project(2 * chip + core)

            return inner

        @pl.when(distance > 0)
        def _():
            lax.fori_loop(0, 4, one, 0)

        return carry

    lax.fori_loop(0, chips + 1, step, 0)
    out.end()
    own_out.wait()
    line.finish()
    mix.finish()
    out.finish()

    def kept(block, carry):
        keep(block).wait()
        emit(block).wait()
        return carry

    lax.fori_loop(0, 2 * chips, kept, 0)
    keep_mix.wait()


def project_call(
    rows, gain, shift, mix_shard, out_shard, bias, up, down, cotangent, bounds, chips
):
    count, width = rows.shape
    total = 2 * chips * count
    local = mix_shard.shape[2]
    vmem = pl.BlockSpec(memory_space=pltpu.VMEM)
    dma = pltpu.SemaphoreType.DMA
    flops = 2 * total * width * 3 * local
    return pl.pallas_call(
        functools.partial(project_kernel, chips),
        out_shape=(
            jax.ShapeDtypeStruct((total, width), jnp.bfloat16),
            jax.ShapeDtypeStruct((3, total, local), jnp.bfloat16),
            jax.ShapeDtypeStruct((3, 4, mix_shard.shape[1], local), jnp.bfloat16),
            jax.ShapeDtypeStruct((4,) + out_shard.shape, jnp.bfloat16),
            jax.ShapeDtypeStruct(up.shape, jnp.bfloat16),
            jax.ShapeDtypeStruct(down.shape, jnp.bfloat16),
            jax.ShapeDtypeStruct((count, width), jnp.bfloat16),
            jax.ShapeDtypeStruct((1, width), jnp.float32),
        ),
        in_specs=[vmem] * 9 + [pl.BlockSpec(memory_space=pltpu.SMEM)],
        out_specs=(pl.BlockSpec(memory_space=pl.ANY),) * 4 + (vmem,) * 4,
        scratch_shapes=[
            pltpu.VMEM(mix_shard.shape, jnp.bfloat16),
            pltpu.VMEM(out_shard.shape, jnp.bfloat16),
            pltpu.VMEM((3, total, local), jnp.bfloat16),
            pltpu.VMEM((3, 4, mix_shard.shape[1], local), jnp.bfloat16),
            dma((2 * chips + 1,)),
            pltpu.VMEM((2 * chips, count, width), jnp.bfloat16),
            dma((3, chips)),
            dma((2 * chips,)),
            dma((4,)),
            dma((4,)),
            dma((4,)),
            dma((4,)),
            dma((2,)),
            dma((2 * chips,)),
        ],
        compiler_params=pltpu.CompilerParams(
            collective_id=0, has_side_effects=True, vmem_limit_bytes=VMEM_LIMIT
        ),
        cost_estimate=pl.CostEstimate(flops=flops * 7, bytes_accessed=0, transcendentals=0),
        name="project",
    )(rows, gain, shift, mix_shard, out_shard, bias, up, down, cotangent, bounds)


class LineScatter:
    def __init__(self, place, term, tiles, bufs, sems, prepare=lambda chip: None):
        self.place, self.term, self.tiles, self.prepare = place, term, tiles, prepare
        self.total, self.side_out, self.side_in, self.line_in = bufs
        self.side_send, self.side_recv, self.line_send, self.line_recv = sems

    def side_copy(self, chip):
        return remote(
            self.side_out.at[chip],
            self.side_in.at[chip],
            self.side_send.at[chip],
            self.side_recv.at[chip],
            self.place.side,
        )

    def span(self, tile):
        width = self.total.shape[1] // self.tiles
        return slice(tile * width, (tile + 1) * width)

    def line_copy(self, way, chip, tile):
        place = self.place
        next_chip = place.chip + 1 - 2 * way
        slot = jnp.where((way == 1) & (chip == next_chip), place.chips, chip)
        return remote(
            self.line_in.at[chip, :, self.span(tile)],
            self.line_in.at[slot, :, self.span(tile)],
            self.line_send.at[chip, tile],
            self.line_recv.at[slot, tile],
            (place.up, place.down)[way],
        )

    def landed(self, way, chip, tile):
        place = self.place
        slot = jnp.where((way == 1) & (chip == place.chip), place.chips, chip)
        remote(
            self.line_in.at[slot, :, self.span(tile)],
            self.line_in.at[slot, :, self.span(tile)],
            self.line_send.at[chip, tile],
            self.line_recv.at[slot, tile],
            (place.up, place.down)[way],
        ).wait_recv()
        return slot

    def each(self, distance, action):
        place = self.place

        def one(index, carry):
            chip = place.chip + distance * (1 - 2 * index)
            valid = (chip >= 0) & (chip < place.chips) & ((distance > 0) | (index == 0))
            pl.when(valid)(lambda: action(chip))
            return carry

        lax.fori_loop(0, 2, one, 0)

    def hand_over(self, chip):
        self.prepare(chip)
        block = 2 * chip + 1 - self.place.core
        for tile in range(self.tiles):
            self.side_out[chip, :, self.span(tile)] = self.term(block, tile).astype(jnp.bfloat16)
        self.side_copy(chip).start()

    def sum_up(self, chip):
        place = self.place
        block = 2 * chip + place.core
        self.side_copy(chip).wait_recv()
        for tile in range(self.tiles):
            span = self.span(tile)
            self.total[:, span] = self.term(block, tile) + self.side_in[chip, :, span].astype(
                jnp.float32
            )
            for way in range(2):
                behind = (place.has_down, place.has_up)[way]
                goes = (chip >= place.chip) if way == 0 else (chip <= place.chip)

                @pl.when(behind & goes)
                def _():
                    slot = self.landed(way, chip, tile)
                    self.total[:, span] += self.line_in[slot, :, span].astype(jnp.float32)

            @pl.when(chip != place.chip)
            def _():
                self.line_in[chip, :, span] = self.total[:, span].astype(jnp.bfloat16)
                pl.when(chip > place.chip)(lambda: self.line_copy(0, chip, tile).start())
                pl.when(chip < place.chip)(lambda: self.line_copy(1, chip, tile).start())

    def begin(self):
        self.each(self.place.chips - 1, self.hand_over)

    def step(self, index):
        distance = self.place.chips - 1 - index
        pl.when(distance > 0)(lambda: self.each(distance - 1, self.hand_over))
        self.each(distance, self.sum_up)

    def finish(self):
        place = self.place

        def drain(chip, carry):
            self.side_copy(chip).wait_send()
            for tile in range(self.tiles):
                pl.when(chip != place.chip)(lambda: self.line_copy(0, chip, tile).wait_send())
            return carry

        lax.fori_loop(0, place.chips, drain, 0)


class SquareScatter:
    def __init__(self, place, piece, owned, bufs, sems):
        self.place, self.piece, self.owned = place, piece, owned
        self.out, self.arrived = bufs
        self.send, self.recv = sems

    def copy(self, kind, way):
        place = self.place
        turn = way if kind < 2 else 1 - way
        peer = place.x_peer + turn * (place.y_peer - place.x_peer)
        return remote(
            self.out.at[kind, way],
            self.arrived.at[kind, way],
            self.send.at[kind, way],
            self.recv.at[kind, way],
            (peer, place.me),
        )

    def owner(self, kind, way):
        place = self.place
        near = place.x_peer + way * (place.y_peer - place.x_peer)
        other = place.y_peer + way * (place.x_peer - place.y_peer)
        return (place.across, near, other, place.dp)[kind]

    def following(self, kind, way):
        after = self.owner(kind, 1) if kind == 3 else self.owner(kind + 1, 0)
        return jnp.where(way == 0, self.owner(kind, 1), after), 1 - way

    def one(self, kind, way):
        value = self.piece(self.owner(kind, way), way)
        if kind == 2:
            self.copy(0, way).wait_recv()
            value = value + self.arrived[0, way].astype(jnp.float32)
        if kind < 3:
            self.out[kind, way] = value.astype(jnp.bfloat16)
            self.copy(kind, way).start()
        else:
            self.owned[way] = value

    def stage(self, kind):
        def one(way, carry):
            self.one(kind, way)
            return carry

        lax.fori_loop(0, 2, one, 0)

    def end(self):
        def one(way, carry):
            self.copy(1, way).wait_recv()
            self.copy(2, way).wait_recv()
            self.owned[way] = (
                self.owned[way]
                + self.arrived[1, way].astype(jnp.float32)
                + self.arrived[2, way].astype(jnp.float32)
            )
            for kind in range(3):
                self.copy(kind, way).wait_send()
            return carry

        lax.fori_loop(0, 2, one, 0)


def square_scratch(half):
    dma = pltpu.SemaphoreType.DMA
    return [
        pltpu.VMEM((3, 2) + half, jnp.bfloat16),
        pltpu.VMEM((3, 2) + half, jnp.bfloat16),
        dma((3, 2)),
        dma((3, 2)),
    ]


class SmallSum:
    def __init__(self, place, rows, alone, bufs, sems):
        self.place, self.rows, self.alone = place, rows, alone
        self.side_buf, self.line_buf, self.square_buf = bufs
        self.send, self.recv = sems

    def side_copy(self):
        place = self.place
        return remote(
            self.rows,
            self.side_buf,
            self.send.at[0],
            self.recv.at[0],
            place.side,
        )

    def line_copy(self, hop):
        place = self.place
        chip = (place.chip + hop) % place.chips
        return remote(
            self.rows,
            self.line_buf.at[place.chip],
            self.send.at[hop],
            self.recv.at[hop],
            (place.dp, 2 * chip + place.core),
        )

    def line_landed(self, hop):
        place = self.place
        chip = (place.chip + place.chips - hop) % place.chips
        remote(
            self.rows,
            self.line_buf.at[chip],
            self.send.at[hop],
            self.recv.at[hop],
            (place.dp, 2 * chip + place.core),
        ).wait_recv()

    def square_copy(self, hop):
        place = self.place
        target = (place.dp + hop) % 4
        at = place.chips + hop
        return remote(
            self.rows,
            self.square_buf.at[place.dp],
            self.send.at[at],
            self.recv.at[at],
            (target, place.me),
        )

    def square_landed(self, hop):
        place = self.place
        source = (place.dp + 4 - hop) % 4
        at = place.chips + hop
        remote(
            self.rows,
            self.square_buf.at[source],
            self.send.at[at],
            self.recv.at[at],
            (source, place.me),
        ).wait_recv()

    def put(self, value):
        if self.alone < self.rows.shape[0]:
            index = lax.broadcasted_iota(jnp.int32, value.shape, 0)
            value = jnp.where(index < self.alone, value, self.rows[...])
        self.rows[...] = value

    def begin(self):
        self.side_copy().start()

    def middle(self):
        self.side_copy().wait()
        self.put(self.rows[...] + self.side_buf[...])
        self.line_buf[self.place.chip] = self.rows[...]
        for hop in range(1, self.place.chips):
            self.line_copy(hop).start()

    def late(self):
        place = self.place
        for hop in range(1, place.chips):
            self.line_copy(hop).wait_send()
            self.line_landed(hop)
        value = self.line_buf[0]
        for chip in range(1, place.chips):
            value = value + self.line_buf[chip]
        self.put(value)
        self.square_buf[place.dp] = self.rows[...]
        for hop in range(1, 4):
            self.square_copy(hop).start()

    def end(self):
        for hop in range(1, 4):
            self.square_copy(hop).wait_send()
            self.square_landed(hop)
        value = self.square_buf[0]
        for device in range(1, 4):
            value = value + self.square_buf[device]
        self.rows[...] = value


def small_scratch(chips, rows, width):
    dma = pltpu.SemaphoreType.DMA
    return [
        pltpu.VMEM((rows, width), jnp.float32),
        pltpu.VMEM((chips, rows, width), jnp.float32),
        pltpu.VMEM((4, rows, width), jnp.float32),
        dma((chips + 4,)),
        dma((chips + 4,)),
    ]


def scatter_scratch(chips, count, width):
    low = jnp.bfloat16
    dma = pltpu.SemaphoreType.DMA
    return [
        pltpu.VMEM((count, width), jnp.float32),
        pltpu.VMEM((chips, count, width), low),
        pltpu.VMEM((chips, count, width), low),
        pltpu.VMEM((chips + 1, count, width), low),
        dma((chips,)),
        dma((chips,)),
        dma((chips, 4)),
        dma((chips + 1, 4)),
    ]


def alive(shape, axis, start, bounds_ref):
    place = lax.broadcasted_iota(jnp.int32, shape, axis) + start
    return jnp.where((place >= bounds_ref[0]) & (place < bounds_ref[1]), 1.0, 0.0)


def by_rows(count, tile, action):
    def one(index, carry):
        action(pl.ds(pl.multiple_of(index * tile, tile), tile))
        return carry

    lax.fori_loop(0, count // tile, one, 0)


def attend_out_kernel(
    chips,
    mixed_hbm,
    bounds_ref,
    out_hbm,
    rows_hbm,
    branch_ref,
    gain_ref,
    shift_ref,
    bias_ref,
    up_ref,
    down_ref,
    attended_ref,
    lse_ref,
    resid_ref,
    normed_ref,
    branch_whole,
    up_whole,
    down_whole,
    mixed_ref,
    out_ref,
    rows_ref,
    fetch_sem,
    seg_col_ref,
    seg_row_ref,
    score_ref,
    blocks,
    line_send,
    line_recv,
    up_send,
    up_recv,
    down_send,
    down_recv,
    own_sem,
    keep_sem,
    *scatter,
):
    place = Place(chips)
    count = rows_ref.shape[0]
    fetched = fetch(
        [(mixed_hbm, mixed_ref), (out_hbm, out_ref), (rows_hbm, rows_ref)], fetch_sem
    )
    place.greet(True)

    def square(shard, whole, send, recv):
        half = shard.shape[0] // 2
        return SquareGather(
            place,
            shard,
            lambda owner: whole.at[owner],
            lambda owner, which: whole.at[owner, pl.ds(which * half, half)],
            send,
            recv,
        )

    up = square(up_ref, up_whole, up_send, up_recv)
    down = square(down_ref, down_whole, down_send, down_recv)
    up.begin()
    own = [
        pltpu.make_async_copy(up_ref, up_whole.at[place.dp], own_sem.at[0]),
        pltpu.make_async_copy(down_ref, down_whole.at[place.dp], own_sem.at[1]),
    ]
    own[0].start()
    own[1].start()

    def term(block, tile):
        span = pl.ds(pl.multiple_of(block * count, count), count)
        return jnp.dot(attended_ref[span, :], out_ref[tile], preferred_element_type=jnp.float32)

    def prepare(chip):
        def one(index, carry):
            for head in range(mixed_ref.shape[2] // HEAD_DIM):
                attend_rows(
                    head,
                    chip * (2 * count // ATTEND_ROWS) + index,
                    mixed_ref,
                    seg_col_ref,
                    seg_row_ref,
                    attended_ref,
                    lse_ref,
                    score_ref,
                )
            return carry

        lax.fori_loop(0, 2 * count // ATTEND_ROWS, one, 0)

    def copy_in(span):
        blocks[place.me, span, :] = branch_ref[span, :]

    by_rows(count, 64, copy_in)
    line = LineGather(place, blocks, line_send, line_recv)
    line.begin()
    seg_row_ref[...] = alive(seg_row_ref.shape, 1, 0, bounds_ref)

    def column(span):
        seg_col_ref[span, :] = alive((64, 1), 0, span.start, bounds_ref)

    by_rows(seg_col_ref.shape[0], 64, column)
    for copy in fetched:
        copy.wait()
    sums = LineScatter(place, term, 4, scatter[:4], scatter[4:8], prepare)
    sums.begin()

    def keep(block, part):
        half = count // 2
        place_of = ((block // 2 * 2 + part) * 2 + block % 2) * half
        span = pl.ds(pl.multiple_of(place_of, half), half)
        source = blocks.at[block, pl.ds(part * half, half)]
        return pltpu.make_async_copy(source, branch_whole.at[span], keep_sem.at[block, part])

    def step(index, carry):
        sums.step(index)
        pl.when(index < chips - 1)(lambda: line.step(index + 1))

        @pl.when(index == 1)
        def _():
            up.middle()
            down.begin()

        pl.when(index == 2)(down.middle)
        return carry

    lax.fori_loop(0, chips, step, 0)
    total = scatter[0]

    def norm(span):
        resid = rows_ref[span, :].astype(jnp.float32) + total[span, :] + bias_ref[...]
        resid_ref[span, :] = resid
        normed_ref[span, :] = norm_rows(resid, gain_ref[...], shift_ref[...]).astype(jnp.bfloat16)

    by_rows(count, 64, norm)

    def store(block, carry):
        pl.when((block % 2 != place.core))(lambda: line.arrive(block // 2, block % 2))
        keep(block, 0).start()
        keep(block, 1).start()
        return carry

    lax.fori_loop(0, 2 * chips, store, 0)
    sums.finish()
    line.finish()
    up.end()
    down.end()
    up.finish()
    down.finish()
    own[0].wait()
    own[1].wait()

    def kept(block, carry):
        keep(block, 0).wait()
        keep(block, 1).wait()
        return carry

    lax.fori_loop(0, 2 * chips, kept, 0)


def attend_out_call(
    mixed, bounds, out_whole, rows, branch, gain, shift, bias, up, down, chips
):
    count, width = rows.shape
    local = mixed.shape[2]
    total = 2 * chips * count
    low = jnp.bfloat16
    vmem = pl.BlockSpec(memory_space=pltpu.VMEM)
    hbm = pl.BlockSpec(memory_space=pl.ANY)
    dma = pltpu.SemaphoreType.DMA
    return pl.pallas_call(
        functools.partial(attend_out_kernel, chips),
        out_shape=(
            jax.ShapeDtypeStruct((total, local), low),
            jax.ShapeDtypeStruct((total, 1 + local // HEAD_DIM), jnp.float32),
            jax.ShapeDtypeStruct((count, width), jnp.float32),
            jax.ShapeDtypeStruct((count, width), low),
            jax.ShapeDtypeStruct((total, width), low),
            jax.ShapeDtypeStruct((4,) + up.shape, low),
            jax.ShapeDtypeStruct((4,) + down.shape, low),
        ),
        in_specs=[hbm, pl.BlockSpec(memory_space=pltpu.SMEM), hbm, hbm] + [vmem] * 6,
        out_specs=(vmem, vmem, vmem, vmem, hbm, hbm, hbm),
        scratch_shapes=[
            pltpu.VMEM(mixed.shape, low),
            pltpu.VMEM(out_whole.shape, low),
            pltpu.VMEM(rows.shape, low),
            dma((3,)),
            pltpu.VMEM((total, 1), jnp.float32),
            pltpu.VMEM((1, total), jnp.float32),
            pltpu.VMEM((ATTEND_ROWS, total), jnp.float32),
            pltpu.VMEM((2 * chips, count, width), low),
            dma((3, chips)),
            dma((2 * chips,)),
            dma((4,)),
            dma((4,)),
            dma((4,)),
            dma((4,)),
            dma((2,)),
            dma((2 * chips, 2)),
        ]
        + scatter_scratch(chips, count, width),
        compiler_params=pltpu.CompilerParams(
            collective_id=1, has_side_effects=True, vmem_limit_bytes=VMEM_LIMIT
        ),
        cost_estimate=pl.CostEstimate(flops=10**11, bytes_accessed=0, transcendentals=0),
        name="attend_out",
    )(mixed, bounds, out_whole, rows, branch, gain, shift, bias, up, down)


def input_back_kernel(
    chips,
    stacked_hbm,
    mix_hbm,
    rows_hbm,
    resid_grad_hbm,
    gain_ref,
    early_ref,
    hidden_hbm,
    out_grad_hbm,
    normed_one_ref,
    normed_two_ref,
    grad_ref,
    late_out_ref,
    early_out_ref,
    mix_grad_ref,
    up_grad_ref,
    out_owned_ref,
    stacked_ref,
    mix_ref,
    rows_ref,
    resid_grad_ref,
    hidden_ref,
    out_grad_ref,
    fetch_sem,
    columns_buf,
    columns_sem,
    *scatter,
):
    place = Place(chips)
    count = rows_ref.shape[0]
    fetched = fetch(
        [
            (stacked_hbm, stacked_ref),
            (mix_hbm, mix_ref),
            (hidden_hbm, hidden_ref),
            (out_grad_hbm, out_grad_ref),
            (rows_hbm, rows_ref),
            (resid_grad_hbm, resid_grad_ref),
        ],
        fetch_sem,
    )
    place.greet(True, True)
    fetched[0].wait()
    fetched[1].wait()
    early_out_ref[...] = early_ref[...]
    early = SmallSum(place, early_out_ref, 4, scatter[16:19], scatter[19:21])
    late = SmallSum(place, late_out_ref, late_out_ref.shape[0], scatter[21:24], scatter[24:26])

    def term(block, tile):
        span = pl.ds(pl.multiple_of(block * count, count), count)
        result = None
        for part in range(3):
            product = lax.dot_general(
                stacked_ref[part, span, :],
                mix_ref[part, tile],
                TURNED,
                preferred_element_type=jnp.float32,
            )
            result = product if result is None else result + product
        return result

    sums = LineScatter(place, term, 4, scatter[:4], scatter[4:8])
    sums.begin()
    early.begin()
    half_columns = columns_buf.shape[2]

    def load(which, owner, half):
        start = pl.multiple_of((2 * owner + half) * half_columns, half_columns)
        source = (normed_one_ref, normed_two_ref)[which]
        return pltpu.make_async_copy(
            source.at[:, pl.ds(start, half_columns)], columns_buf.at[which], columns_sem.at[which]
        )

    def mix_piece(owner, half):
        load(0, owner, half).wait()
        return jnp.stack(
            [
                lax.dot_general(
                    columns_buf[0],
                    stacked_ref[part],
                    CROSSED,
                    preferred_element_type=jnp.float32,
                )
                for part in range(3)
            ]
        )

    def up_piece(owner, half):
        load(1, owner, half).wait()
        return lax.dot_general(
            columns_buf[1], hidden_ref[...], CROSSED, preferred_element_type=jnp.float32
        )

    out_units = out_grad_ref.shape[0] // 2
    out_columns = out_grad_ref.shape[1] // 4

    def out_piece(owner, half):
        units = pl.ds(pl.multiple_of(half * out_units, out_units), out_units)
        columns = pl.ds(pl.multiple_of(owner * out_columns, 128), out_columns)
        return out_grad_ref[units, columns]

    out = SquareScatter(place, out_piece, out_owned_ref, scatter[26:28], scatter[28:30])
    mix = SquareScatter(place, mix_piece, mix_grad_ref, scatter[8:10], scatter[10:12])
    up = SquareScatter(place, up_piece, up_grad_ref, scatter[12:14], scatter[14:16])

    load(1, place.across, 0).start()
    load(0, place.across, 0).start()

    def stage(kind):
        def one(way, carry):
            for which, matrix in ((1, up), (0, mix)):
                matrix.one(kind, way)
                owner, half = matrix.following(kind, way)
                more = (way == 0) | (kind < 3)
                pl.when(more)(lambda: load(which, owner, half).start())
            out.one(kind, way)
            return carry

        lax.fori_loop(0, 2, one, 0)

    for copy in fetched[2:]:
        copy.wait()

    def step(index, carry):
        pl.when(index == 3)(lambda: stage(3))
        sums.step(index)
        for kind in range(3):

            @pl.when(index == kind)
            def _():
                stage(kind)
                if kind == 1:
                    early.middle()
                if kind == 2:
                    early.late()

        return carry

    lax.fori_loop(0, chips, step, 0)
    total = scatter[0]
    late_out_ref[...] = jnp.zeros_like(late_out_ref)

    def columns(span):
        one_grad = total[span, :]
        _, hat, _ = layer_norm_parts(rows_ref[span, :].astype(jnp.float32), gain_ref[...], 0.0)
        late_out_ref[0:1, :] += jnp.sum(one_grad * hat, axis=0, keepdims=True)
        late_out_ref[1:2, :] += jnp.sum(one_grad, axis=0, keepdims=True)

    def back(span):
        rows = rows_ref[span, :].astype(jnp.float32)
        _, hat, inverse = layer_norm_parts(rows, gain_ref[...], 0.0)
        grad_ref[span, :] = resid_grad_ref[span, :] + layer_norm_back(
            total[span, :], hat, inverse, gain_ref[...]
        )

    by_rows(count, 64, columns)
    late.begin()
    up.end()
    late.middle()
    by_rows(count, 64, back)
    late.late()
    early.end()
    mix.end()
    out.end()
    sums.finish()
    late.end()


def input_back_call(
    stacked, mix_whole, rows, resid_grad, gain, early, hidden, out_grad, normed_one, normed_two, chips
):
    count, width = rows.shape
    total, units = hidden.shape
    local = stacked.shape[2]
    half = width // 8
    vmem = pl.BlockSpec(memory_space=pltpu.VMEM)
    hbm = pl.BlockSpec(memory_space=pl.ANY)
    return pl.pallas_call(
        functools.partial(input_back_kernel, chips),
        out_shape=(
            jax.ShapeDtypeStruct((count, width), jnp.float32),
            jax.ShapeDtypeStruct((2, width), jnp.float32),
            jax.ShapeDtypeStruct(early.shape, jnp.float32),
            jax.ShapeDtypeStruct((2, 3, half, local), jnp.float32),
            jax.ShapeDtypeStruct((2, half, units), jnp.float32),
            jax.ShapeDtypeStruct((2, local // 2, width // 4), jnp.float32),
        ),
        in_specs=[hbm] * 4 + [vmem] * 2 + [hbm] * 4,
        out_specs=(vmem,) * 6,
        scratch_shapes=[
            pltpu.VMEM(stacked.shape, jnp.bfloat16),
            pltpu.VMEM(mix_whole.shape, jnp.bfloat16),
            pltpu.VMEM(rows.shape, jnp.bfloat16),
            pltpu.VMEM(resid_grad.shape, jnp.float32),
            pltpu.VMEM(hidden.shape, jnp.bfloat16),
            pltpu.VMEM(out_grad.shape, jnp.float32),
            pltpu.SemaphoreType.DMA((6,)),
            pltpu.VMEM((2, total, half), jnp.bfloat16),
            pltpu.SemaphoreType.DMA((2,)),
        ]
        + scatter_scratch(chips, count, width)
        + square_scratch((3, half, local))
        + square_scratch((half, units))
        + small_scratch(chips, early.shape[0], width)
        + small_scratch(chips, 2, width)
        + square_scratch((local // 2, width // 4)),
        compiler_params=pltpu.CompilerParams(
            collective_id=2, has_side_effects=True, vmem_limit_bytes=VMEM_LIMIT
        ),
        cost_estimate=pl.CostEstimate(flops=10**11, bytes_accessed=0, transcendentals=0),
        name="input_back",
    )(stacked, mix_whole, rows, resid_grad, gain, early, hidden, out_grad, normed_one, normed_two)


GELU_SLOPE = 0.7978845608028654
GELU_CUBE = 0.044715


def gelu_parts(hidden):
    square = hidden * hidden
    bend = jnp.tanh(GELU_SLOPE * hidden * (1.0 + GELU_CUBE * square))
    lift = 0.5 * (1.0 + bend)
    slope = lift + 0.5 * hidden * (1.0 - bend * bend) * (
        GELU_SLOPE * (1.0 + 3.0 * GELU_CUBE * square)
    )
    return hidden * lift, slope


def feed_kernel(
    chips,
    parts,
    normed_ref,
    branch_ref,
    up_hbm,
    down_hbm,
    bias_ref,
    resid_hbm,
    own_branch_hbm,
    gain_ref,
    normed_whole,
    active_hbm,
    hidden_hbm,
    grad_ref,
    grad_low_ref,
    sums_ref,
    bias_grad_ref,
    up_ref,
    down_ref,
    resid_ref,
    own_branch_ref,
    active_ref,
    hidden_ref,
    fetch_sem,
    emit_sem,
    blocks,
    branch_buf,
    work,
    hold,
    side_out,
    side_in,
    line_in,
    line_send,
    line_recv,
    keep_sem,
    load_sem,
    side_send,
    side_recv,
    out_send,
    out_recv,
):
    place = Place(chips)
    count = normed_ref.shape[0]
    rows = count // parts
    pair = 2 * rows
    last = chips - 1
    fetched = fetch(
        [
            (up_hbm, up_ref),
            (down_hbm, down_ref),
            (resid_hbm, resid_ref),
            (own_branch_hbm, own_branch_ref),
        ],
        fetch_sem,
    )
    place.greet(False)

    def fill(part, carry):
        block = 2 * (place.chip * parts + part) + place.core
        blocks[block] = normed_ref[pl.ds(pl.multiple_of(part * rows, rows), rows), :]
        return carry

    lax.fori_loop(0, parts, fill, 0)
    line = LineGather(place, blocks, line_send, line_recv, parts)
    line.begin()
    bias_grad_ref[...] = jnp.zeros_like(bias_grad_ref)

    def piece_span(piece):
        return pl.ds(pl.multiple_of(piece * pair, pair), pair)

    def load(piece, slot):
        return pltpu.make_async_copy(
            branch_ref.at[piece_span(piece)], branch_buf.at[slot], load_sem.at[slot]
        )

    def keep(piece, core):
        span = pl.ds(pl.multiple_of(piece * pair + core * rows, rows), rows)
        return pltpu.make_async_copy(
            blocks.at[2 * piece + core], normed_whole.at[span], keep_sem.at[piece, core]
        )

    def side_copy(piece):
        return remote(
            side_out.at[piece],
            side_in.at[piece],
            side_send.at[piece],
            side_recv.at[piece],
            place.side,
        )

    chunk = normed_ref.shape[1] // 4

    def line_copy(way, chip, part, tile):
        piece = chip * parts + part
        next_chip = place.chip + 1 - 2 * way
        slot = jnp.where((way == 1) & (chip == next_chip), chips * parts + part, piece)
        span = slice(tile * chunk, (tile + 1) * chunk)
        return remote(
            line_in.at[piece, :, span],
            line_in.at[slot, :, span],
            out_send.at[piece, tile],
            out_recv.at[slot, tile],
            (place.up, place.down)[way],
        )

    def line_landed(way, chip, part, tile):
        piece = chip * parts + part
        slot = jnp.where((way == 1) & (chip == place.chip), chips * parts + part, piece)
        span = slice(tile * chunk, (tile + 1) * chunk)
        remote(
            line_in.at[slot, :, span],
            line_in.at[slot, :, span],
            out_send.at[piece, tile],
            out_recv.at[slot, tile],
            (place.up, place.down)[way],
        ).wait_recv()
        return slot

    def emit(piece):
        span = piece_span(piece)
        return [
            pltpu.make_async_copy(active_ref.at[span], active_hbm.at[span], emit_sem.at[piece, 0]),
            pltpu.make_async_copy(hidden_ref.at[span], hidden_hbm.at[span], emit_sem.at[piece, 1]),
        ]

    width = 512
    tiles = up_ref.shape[2] // width

    def compute(chip, part):
        piece = chip * parts + part
        load(piece, 0).start()
        keep(piece, 0).start()
        keep(piece, 1).start()
        span = piece_span(piece)
        own_rows = blocks[pl.ds(2 * piece, 2)].reshape(pair, -1)
        load(piece, 0).wait()

        def tile(index, carry):
            units = pl.ds(pl.multiple_of(index * width, width), width)
            hidden = jnp.dot(
                own_rows,
                up_ref[:, :, units].reshape(-1, width),
                preferred_element_type=jnp.float32,
            )
            active, slope = gelu_parts(hidden + bias_ref[:, units])
            active_ref[span, units] = active.astype(jnp.bfloat16)
            grad = None
            for owner in range(4):
                columns = down_ref.shape[2]
                product = lax.dot_general(
                    branch_buf[0, :, owner * columns : (owner + 1) * columns],
                    down_ref[owner, units, :],
                    TURNED,
                    preferred_element_type=jnp.float32,
                )
                grad = product if grad is None else grad + product
            low = (grad * slope).astype(jnp.bfloat16)
            hidden_ref[span, units] = low
            bias_grad_ref[:, units] += jnp.sum(low.astype(jnp.float32), axis=0, keepdims=True)
            return carry

        lax.fori_loop(0, tiles, tile, 0)
        low = hidden_ref[span, :]
        depth = up_ref.shape[1]
        for owner in range(4):
            columns = slice(owner * depth, (owner + 1) * depth)
            product = lax.dot_general(
                low, up_ref[owner], TURNED, preferred_element_type=jnp.float32
            )
            work[:, :, columns] = product.reshape(2, rows, depth)
        side_out[piece] = work[1 - place.core].astype(jnp.bfloat16)
        side_copy(piece).start()
        hold[piece] = work[place.core]
        for copy in emit(piece):
            copy.start()

    def pass_on(way, chip, part):
        piece = chip * parts + part
        side_copy(piece).wait_recv()
        behind = (place.has_down, place.has_up)[way]
        for tile in range(4):
            span = slice(tile * chunk, (tile + 1) * chunk)
            total = hold[piece, :, span] + side_in[piece, :, span].astype(jnp.float32)

            @pl.when(behind)
            def _():
                slot = line_landed(way, chip, part, tile)
                line_in[piece, :, span] = (
                    total + line_in[slot, :, span].astype(jnp.float32)
                ).astype(jnp.bfloat16)

            @pl.when(jnp.logical_not(behind))
            def _():
                line_in[piece, :, span] = total.astype(jnp.bfloat16)

            line_copy(way, chip, part, tile).start()

    def turn(index, carry):
        distance = index // parts
        part = index % parts

        @pl.when(distance < chips)
        def _():
            pl.when(distance > 0)(lambda: line.step(distance, part))

            def one(side, inner):
                chip = place.chip + distance * (2 * side - 1)

                @pl.when((chip >= 0) & (chip < chips) & ((distance > 0) | (side == 0)))
                def _():
                    line.arrive(chip, 1 - place.core, part)
                    compute(chip, part)

                return inner

            lax.fori_loop(0, 2, one, 0)

        upward = index - place.chip

        @pl.when((upward >= 0) & (upward // parts > place.chip) & (upward // parts < chips))
        def _():
            pass_on(0, upward // parts, upward % parts)

        downward = index - (last - place.chip)
        target = last - downward // parts

        @pl.when((downward >= 0) & (target >= 0) & (target < place.chip))
        def _():
            pass_on(1, target, downward % parts)

        return carry

    fetched[0].wait()
    fetched[1].wait()
    lax.fori_loop(0, parts * chips + last, turn, 0)
    sums_ref[...] = jnp.zeros_like(sums_ref)
    fetched[2].wait()
    fetched[3].wait()

    def own_part(part, carry):
        piece = place.chip * parts + part
        side_copy(piece).wait_recv()
        hold[piece] += side_in[piece].astype(jnp.float32)

        for tile in range(4):

            @pl.when(place.has_down)
            def _():
                line_landed(0, place.chip, part, tile)

            @pl.when(place.has_up)
            def _():
                line_landed(1, place.chip, part, tile)

        pieces_end = chips * parts

        @pl.when(place.has_down)
        def _():
            hold[piece] += line_in[piece].astype(jnp.float32)

        @pl.when(place.has_up)
        def _():
            hold[piece] += line_in[pieces_end + part].astype(jnp.float32)

        tile = 64

        def back(index, inner):
            here = pl.ds(pl.multiple_of(index * tile, tile), tile)
            span = pl.ds(pl.multiple_of(part * rows + index * tile, tile), tile)
            two_grad = hold[piece, here, :]
            _, hat, inverse = layer_norm_parts(resid_ref[span, :], gain_ref[...], 0.0)
            grad = own_branch_ref[span, :].astype(jnp.float32) + layer_norm_back(
                two_grad, hat, inverse, gain_ref[...]
            )
            grad_ref[span, :] = grad
            grad_low_ref[span, :] = grad.astype(jnp.bfloat16)
            sums_ref[0:1, :] += jnp.sum(two_grad * hat, axis=0, keepdims=True)
            sums_ref[1:2, :] += jnp.sum(two_grad, axis=0, keepdims=True)
            sums_ref[2:3, :] += jnp.sum(grad, axis=0, keepdims=True)
            return inner

        lax.fori_loop(0, rows // tile, back, 0)
        return carry

    lax.fori_loop(0, parts, own_part, 0)
    line.finish()

    def drain(piece, carry):
        side_copy(piece).wait_send()
        keep(piece, 0).wait()
        keep(piece, 1).wait()
        for copy in emit(piece):
            copy.wait()
        for tile in range(4):
            pl.when(piece // parts != place.chip)(
                lambda: line_copy(0, piece // parts, piece % parts, tile).wait_send()
            )
        return carry

    lax.fori_loop(0, chips * parts, drain, 0)


def feed_call(normed, branch, up_whole, down_whole, bias, resid, own_branch, gain, chips):
    count, width = normed.shape
    total = 2 * chips * count
    units = up_whole.shape[2]
    parts = 2
    rows = count // parts
    low = jnp.bfloat16
    vmem = pl.BlockSpec(memory_space=pltpu.VMEM)
    hbm = pl.BlockSpec(memory_space=pl.ANY)
    dma = pltpu.SemaphoreType.DMA
    pieces = chips * parts
    return pl.pallas_call(
        functools.partial(feed_kernel, chips, parts),
        out_shape=(
            jax.ShapeDtypeStruct((total, width), low),
            jax.ShapeDtypeStruct((total, units), low),
            jax.ShapeDtypeStruct((total, units), low),
            jax.ShapeDtypeStruct((count, width), jnp.float32),
            jax.ShapeDtypeStruct((count, width), low),
            jax.ShapeDtypeStruct((3, width), jnp.float32),
            jax.ShapeDtypeStruct((1, units), jnp.float32),
        ),
        in_specs=[vmem, hbm, hbm, hbm, vmem, hbm, hbm, vmem],
        out_specs=(hbm,) * 3 + (vmem,) * 4,
        scratch_shapes=[
            pltpu.VMEM(up_whole.shape, low),
            pltpu.VMEM(down_whole.shape, low),
            pltpu.VMEM(resid.shape, jnp.float32),
            pltpu.VMEM(own_branch.shape, low),
            pltpu.VMEM((total, units), low),
            pltpu.VMEM((total, units), low),
            dma((4,)),
            dma((pieces, 2)),
            pltpu.VMEM((2 * pieces, rows, width), low),
            pltpu.VMEM((1, 2 * rows, width), low),
            pltpu.VMEM((2, rows, width), jnp.float32),
            pltpu.VMEM((pieces, rows, width), jnp.float32),
            pltpu.VMEM((pieces, rows, width), low),
            pltpu.VMEM((pieces, rows, width), low),
            pltpu.VMEM((pieces + parts, rows, width), low),
            dma((3, pieces)),
            dma((2 * pieces,)),
            dma((pieces, 2)),
            dma((1,)),
            dma((pieces,)),
            dma((pieces,)),
            dma((pieces, 4)),
            dma((pieces + parts, 4)),
        ],
        compiler_params=pltpu.CompilerParams(
            collective_id=3, has_side_effects=True, vmem_limit_bytes=VMEM_LIMIT
        ),
        cost_estimate=pl.CostEstimate(flops=10**11, bytes_accessed=0, transcendentals=0),
        name="feed",
    )(normed, branch, up_whole, down_whole, bias, resid, own_branch, gain)


def branch_back_kernel(
    chips,
    parts,
    branch_ref,
    active_hbm,
    down_hbm,
    attended_hbm,
    out_hbm,
    shift_ref,
    bounds_ref,
    mixed_hbm,
    aux_hbm,
    resid_ref,
    cotangent_ref,
    stacked_ref,
    bias_sum_ref,
    down_grad_ref,
    out_grad_ref,
    output_ref,
    blocks,
    active_ref,
    down_ref,
    attended_ref,
    out_ref,
    mixed_ref,
    aux_ref,
    fetch_sem,
    seg_row_ref,
    block_buf,
    columns_buf,
    probs_ref,
    flow_ref,
    key_sum,
    value_sum,
    line_send,
    line_recv,
    columns_sem,
    block_sem,
    *scatter,
):
    place = Place(chips)
    count = branch_ref.shape[0]
    rows = count // parts
    fetched = fetch(
        [
            (active_hbm, active_ref),
            (down_hbm, down_ref),
            (attended_hbm, attended_ref),
            (out_hbm, out_ref),
            (mixed_hbm, mixed_ref),
            (aux_hbm, aux_ref),
        ],
        fetch_sem,
    )
    place.greet(True)
    line = LineGather(place, blocks, line_send, line_recv, 1, branch_ref)
    line.begin()

    def term(block, tile):
        chip, core = block // 2, block % 2
        taken = []
        for part in range(parts):
            start = ((chip * parts + part) * 2 + core) * rows
            taken.append(active_ref[pl.ds(pl.multiple_of(start, rows), rows), :])
        return jnp.dot(
            jnp.concatenate(taken, axis=0), down_ref[tile], preferred_element_type=jnp.float32
        )

    fetched[0].wait()
    fetched[1].wait()
    sums = LineScatter(place, term, 4, scatter[:4], scatter[4:8])
    sums.begin()
    seg_row_ref[...] = alive(seg_row_ref.shape, 1, 0, bounds_ref)
    out_grad_ref[...] = jnp.zeros_like(out_grad_ref)
    key_sum[...] = jnp.zeros_like(key_sum)
    value_sum[...] = jnp.zeros_like(value_sum)
    bias_sum_ref[...] = jnp.zeros_like(bias_sum_ref)
    down_units = down_ref.shape[1] // 2
    down_columns = down_ref.shape[2]

    def load_columns(owner):
        return pltpu.make_async_copy(
            cotangent_ref.at[:, pl.ds(pl.multiple_of(owner * down_columns, 128), down_columns)],
            columns_buf,
            columns_sem,
        )

    load_columns(place.across).start()

    def down_piece(owner, half):
        units = pl.ds(pl.multiple_of(half * down_units, down_units), down_units)
        return lax.dot_general(
            active_ref[:, units], columns_buf[...], CROSSED, preferred_element_type=jnp.float32
        )

    down = SquareScatter(place, down_piece, down_grad_ref, scatter[8:10], scatter[10:12])
    def down_stage(kind):
        def one(way, carry):
            fresh = (way == 0) if kind in (0, 3) else ((way >= 0) if kind == 1 else (way == 1))
            pl.when(fresh)(lambda: load_columns(place.dp).wait())
            down.one(kind, way)
            owner, _ = down.following(kind, way)
            more = (way == 1) if kind == 0 else ((way == 0) if kind == 1 else (way >= 0))
            if kind < 3:
                pl.when(more)(lambda: load_columns(owner).start())
            return carry

        lax.fori_loop(0, 2, one, 0)

    def load_part(source, owner):
        columns = out_ref.shape[2]
        span = slice(owner * columns, (owner + 1) * columns)
        return pltpu.make_async_copy(source.at[:, span], block_buf.at[:, span], block_sem.at[owner])

    def load_block(block):
        mine = block == place.me

        @pl.when(mine)
        def _():
            for owner in range(4):
                load_part(branch_ref, owner).start()

        @pl.when(jnp.logical_not(mine))
        def _():
            for owner in range(4):
                load_part(blocks.at[block], owner).start()

    def take(block):
        span = pl.ds(pl.multiple_of(block * count, count), count)
        columns = out_ref.shape[2]
        load_block(block)
        result = None
        for owner in range(4):
            load_part(branch_ref, owner).wait()
            here = block_buf[:, owner * columns : (owner + 1) * columns]
            product = lax.dot_general(
                here, out_ref[owner], TURNED, preferred_element_type=jnp.float32
            )
            result = product if result is None else result + product
            out_grad_ref[:, owner * columns : (owner + 1) * columns] += lax.dot_general(
                attended_ref[span, :], here, CROSSED, preferred_element_type=jnp.float32
            )
        grad = result.astype(jnp.bfloat16)
        for head in range(mixed_ref.shape[2] // HEAD_DIM):
            attend_back_rows(
                head,
                block,
                grad[:, head * HEAD_DIM : (head + 1) * HEAD_DIM],
                mixed_ref,
                aux_ref,
                seg_row_ref,
                stacked_ref,
                probs_ref,
                flow_ref,
                key_sum,
                value_sum,
                bias_sum_ref,
            )

    for copy in fetched[2:]:
        copy.wait()

    def step(index, carry):
        def one(side, inner):
            chip = place.chip + index * (2 * (side % 2) - 1)
            core = (place.core + side // 2) % 2

            @pl.when((chip >= 0) & (chip < chips) & ((index > 0) | (side % 2 == 0)))
            def _():
                pl.when(side >= 2)(lambda: line.arrive(chip, core))
                take(2 * chip + core)

            return inner

        lax.fori_loop(0, 4, one, 0)
        for kind in range(4):
            pl.when(index == kind)(lambda: down_stage(kind))
        pl.when(index < chips - 1)(lambda: line.step(index + 1))
        sums.step(index)
        return carry

    lax.fori_loop(0, chips, step, 0)
    resid = pltpu.make_async_copy(resid_ref, probs_ref, columns_sem)
    resid.start()
    stacked_ref[1] = (key_sum[...] * HEAD_DIM ** (-0.5)).astype(jnp.bfloat16)
    value_grad = value_sum[...].astype(jnp.bfloat16)
    stacked_ref[2] = value_grad
    bias_sum_ref[1:2, :] = jnp.sum(value_grad.astype(jnp.float32), axis=0, keepdims=True)
    down.end()
    total = scatter[0]
    resid.wait()

    def emit(span):
        result = probs_ref[span, :] + total[span, :] + shift_ref[...]
        live = alive((64, 1), 0, place.me * count + span.start, bounds_ref)
        output_ref[span, :] = jnp.where(live > 0, result, 0.0).astype(jnp.bfloat16)

    by_rows(count, 64, emit)
    sums.finish()
    line.finish()


def branch_back_call(
    branch,
    active,
    down_whole,
    attended,
    out_whole,
    shift,
    bounds,
    mixed,
    aux,
    resid,
    cotangent,
    chips,
):
    count, width = branch.shape
    total, local = attended.shape
    _, units, columns = down_whole.shape
    low = jnp.bfloat16
    vmem = pl.BlockSpec(memory_space=pltpu.VMEM)
    hbm = pl.BlockSpec(memory_space=pl.ANY)
    dma = pltpu.SemaphoreType.DMA
    return pl.pallas_call(
        functools.partial(branch_back_kernel, chips, 2),
        out_shape=(
            jax.ShapeDtypeStruct((3, total, local), low),
            jax.ShapeDtypeStruct((2, local), jnp.float32),
            jax.ShapeDtypeStruct((2, units // 2, columns), jnp.float32),
            jax.ShapeDtypeStruct((local, width), jnp.float32),
            jax.ShapeDtypeStruct((count, width), low),
            jax.ShapeDtypeStruct((2 * chips, count, width), low),
        ),
        in_specs=[hbm] * 5 + [vmem, pl.BlockSpec(memory_space=pltpu.SMEM)] + [hbm] * 4,
        out_specs=(vmem,) * 5 + (hbm,),
        scratch_shapes=[
            pltpu.VMEM(active.shape, low),
            pltpu.VMEM(down_whole.shape, low),
            pltpu.VMEM(attended.shape, low),
            pltpu.VMEM(out_whole.shape, low),
            pltpu.VMEM(mixed.shape, low),
            pltpu.VMEM(aux.shape, jnp.float32),
            dma((6,)),
            pltpu.VMEM((1, total), jnp.float32),
            pltpu.VMEM((count, width), low),
            pltpu.VMEM((total, columns), low),
            pltpu.VMEM((ATTEND_ROWS, total), jnp.float32),
            pltpu.VMEM((ATTEND_ROWS, total), jnp.float32),
            pltpu.VMEM((total, local), jnp.float32),
            pltpu.VMEM((total, local), jnp.float32),
            dma((3, chips)),
            dma((2 * chips,)),
            dma,
            dma((4,)),
        ]
        + scatter_scratch(chips, count, width)
        + square_scratch((units // 2, columns)),
        compiler_params=pltpu.CompilerParams(
            collective_id=4, has_side_effects=True, vmem_limit_bytes=VMEM_LIMIT
        ),
        cost_estimate=pl.CostEstimate(flops=10**11, bytes_accessed=0, transcendentals=0),
        name="branch_back",
    )(
        branch,
        active,
        down_whole,
        attended,
        out_whole,
        shift,
        bounds,
        mixed,
        aux,
        resid,
        cotangent,
    )


ATTEND_ROWS = 256
ATTEND_KEYS = 512


def tile_mask(row_block, key_block, seg_col_ref, seg_row_ref):
    rows = lax.broadcasted_iota(jnp.int32, (ATTEND_ROWS, ATTEND_KEYS), 0)
    keys = lax.broadcasted_iota(jnp.int32, (ATTEND_ROWS, ATTEND_KEYS), 1)
    causal = keys - rows <= row_block * ATTEND_ROWS - key_block * ATTEND_KEYS
    row_span = pl.ds(pl.multiple_of(row_block * ATTEND_ROWS, ATTEND_ROWS), ATTEND_ROWS)
    key_span = pl.ds(pl.multiple_of(key_block * ATTEND_KEYS, ATTEND_KEYS), ATTEND_KEYS)
    return causal & (seg_col_ref[row_span, 0:1] == seg_row_ref[:, key_span])


def attend_rows(head, row_block, mixed_ref, seg_col_ref, seg_row_ref, attended_ref, lse_ref, score_ref):
    scale = HEAD_DIM ** (-0.5)
    lanes = slice(head * HEAD_DIM, (head + 1) * HEAD_DIM)
    row_span = pl.ds(pl.multiple_of(row_block * ATTEND_ROWS, ATTEND_ROWS), ATTEND_ROWS)
    count = (row_block * ATTEND_ROWS) // ATTEND_KEYS + 1
    query = mixed_ref[0, row_span, lanes]

    def score(key_block, peak):
        key_span = pl.ds(pl.multiple_of(key_block * ATTEND_KEYS, ATTEND_KEYS), ATTEND_KEYS)
        scores = lax.dot_general(
            query, mixed_ref[1, key_span, lanes], TURNED, preferred_element_type=jnp.float32
        )
        mask = tile_mask(row_block, key_block, seg_col_ref, seg_row_ref)
        scores = jnp.where(mask, scores * scale, MASK_FILL)
        score_ref[:, key_span] = scores
        for part in range(ATTEND_KEYS // 128):
            peak = jnp.maximum(peak, scores[:, part * 128 : (part + 1) * 128])
        return peak

    peak = lax.fori_loop(0, count, score, jnp.full((ATTEND_ROWS, 128), MASK_FILL, jnp.float32))
    peak = jnp.max(peak, axis=1, keepdims=True)

    def weigh(key_block, mass):
        key_span = pl.ds(pl.multiple_of(key_block * ATTEND_KEYS, ATTEND_KEYS), ATTEND_KEYS)
        weights = jnp.exp(score_ref[:, key_span] - peak)
        score_ref[:, key_span] = weights
        for part in range(ATTEND_KEYS // 128):
            mass = mass + weights[:, part * 128 : (part + 1) * 128]
        return mass

    mass = lax.fori_loop(0, count, weigh, jnp.zeros((ATTEND_ROWS, 128), jnp.float32))
    mass = jnp.sum(mass, axis=1, keepdims=True)
    inverse = 1.0 / mass
    lse_ref[row_span, head + 1 : head + 2] = peak + jnp.log(mass)
    if head == 0:
        lse_ref[row_span, 0:1] = seg_col_ref[row_span, :]

    def gather(key_block, total):
        key_span = pl.ds(pl.multiple_of(key_block * ATTEND_KEYS, ATTEND_KEYS), ATTEND_KEYS)
        probs = (score_ref[:, key_span] * inverse).astype(jnp.bfloat16)
        return total + jnp.dot(
            probs, mixed_ref[2, key_span, lanes], preferred_element_type=jnp.float32
        )

    total = lax.fori_loop(0, count, gather, jnp.zeros((ATTEND_ROWS, HEAD_DIM), jnp.float32))
    attended_ref[row_span, lanes] = total.astype(jnp.bfloat16)


def attend_back_rows(
    head,
    row_block,
    grad,
    mixed_ref,
    aux_ref,
    seg_row_ref,
    stacked_ref,
    probs_ref,
    flow_ref,
    key_sum,
    value_sum,
    bias_sum,
):
    scale = HEAD_DIM ** (-0.5)
    lanes = slice(head * HEAD_DIM, (head + 1) * HEAD_DIM)
    row_span = pl.ds(pl.multiple_of(row_block * ATTEND_ROWS, ATTEND_ROWS), ATTEND_ROWS)
    count = (row_block * ATTEND_ROWS) // ATTEND_KEYS + 1
    query = mixed_ref[0, row_span, lanes]
    lse = aux_ref[row_span, head + 1 : head + 2]

    def first(key_block, delta):
        key_span = pl.ds(pl.multiple_of(key_block * ATTEND_KEYS, ATTEND_KEYS), ATTEND_KEYS)
        scores = lax.dot_general(
            query, mixed_ref[1, key_span, lanes], TURNED, preferred_element_type=jnp.float32
        )
        flow = lax.dot_general(
            grad, mixed_ref[2, key_span, lanes], TURNED, preferred_element_type=jnp.float32
        )
        mask = tile_mask(row_block, key_block, aux_ref, seg_row_ref)
        probs = jnp.exp(jnp.where(mask, scores * scale, MASK_FILL) - lse)
        probs_ref[:, key_span] = probs
        flow_ref[:, key_span] = flow
        product = probs * flow
        for part in range(ATTEND_KEYS // 128):
            delta = delta + product[:, part * 128 : (part + 1) * 128]
        value_sum[key_span, lanes] += lax.dot_general(
            probs.astype(jnp.bfloat16), grad, CROSSED, preferred_element_type=jnp.float32
        )
        return delta

    delta = lax.fori_loop(0, count, first, jnp.zeros((ATTEND_ROWS, 128), jnp.float32))
    delta = jnp.sum(delta, axis=1, keepdims=True)

    def second(key_block, total):
        key_span = pl.ds(pl.multiple_of(key_block * ATTEND_KEYS, ATTEND_KEYS), ATTEND_KEYS)
        low = (probs_ref[:, key_span] * (flow_ref[:, key_span] - delta)).astype(jnp.bfloat16)
        key_sum[key_span, lanes] += lax.dot_general(
            low, query, CROSSED, preferred_element_type=jnp.float32
        )
        return total + jnp.dot(
            low, mixed_ref[1, key_span, lanes], preferred_element_type=jnp.float32
        )

    total = lax.fori_loop(0, count, second, jnp.zeros((ATTEND_ROWS, HEAD_DIM), jnp.float32))
    query_grad = (total * scale).astype(jnp.bfloat16)
    stacked_ref[0, row_span, lanes] = query_grad
    bias_sum[0:1, lanes] += jnp.sum(query_grad.astype(jnp.float32), axis=0, keepdims=True)


def tile_scores(query_tile, keys, segment, row_block, col_block):
    key_tile = keys[col_block * BLOCK : (col_block + 1) * BLOCK]
    scale = query_tile.shape[2] ** (-0.5)
    scores = (
        jnp.einsum("qhe,khe->hqk", query_tile, key_tile, preferred_element_type=jnp.float32) * scale
    )
    row_place = row_block * BLOCK + jnp.arange(BLOCK)
    key_place = col_block * BLOCK + jnp.arange(BLOCK)
    row_segment = segment[row_block * BLOCK : (row_block + 1) * BLOCK]
    key_segment = segment[col_block * BLOCK : (col_block + 1) * BLOCK]
    allowed = (key_place[None, :] <= row_place[:, None]) & (
        row_segment[:, None] == key_segment[None, :]
    )
    return (jnp.where(allowed[None], scores, MASK_FILL), allowed)


def attention_forward(queries, keys, values, segment):
    count = queries.shape[0] // BLOCK
    heads = queries.shape[1]
    depth = queries.shape[2]
    outputs = []
    totals = []
    for row_block in range(count):
        query_tile = queries[row_block * BLOCK : (row_block + 1) * BLOCK]
        peak = jnp.full((heads, BLOCK), MASK_FILL, jnp.float32)
        mass = jnp.zeros((heads, BLOCK), jnp.float32)
        for col_block in range(row_block + 1):
            scores, allowed = tile_scores(query_tile, keys, segment, row_block, col_block)
            new_peak = jnp.maximum(peak, jnp.max(scores, axis=-1))
            weights = jnp.where(allowed[None], jnp.exp(scores - new_peak[:, :, None]), 0.0)
            mass = mass * jnp.exp(peak - new_peak) + jnp.sum(weights, axis=-1)
            peak = new_peak
        total = peak + jnp.log(mass)
        gathered = jnp.zeros((BLOCK, heads, depth), jnp.float32)
        for col_block in range(row_block + 1):
            scores, allowed = tile_scores(query_tile, keys, segment, row_block, col_block)
            probs = jnp.where(allowed[None], jnp.exp(scores - total[:, :, None]), 0.0).astype(
                jnp.bfloat16
            )
            value_tile = values[col_block * BLOCK : (col_block + 1) * BLOCK]
            gathered = gathered + jnp.einsum(
                "hqk,khe->qhe", probs, value_tile, preferred_element_type=jnp.float32
            )
        outputs.append(gathered.astype(jnp.bfloat16))
        totals.append(total)
    return (jnp.concatenate(outputs, axis=0), jnp.concatenate(totals, axis=1))


def attention_backward(queries, keys, values, segment, totals, grads):
    count = queries.shape[0] // BLOCK
    heads = queries.shape[1]
    depth = queries.shape[2]
    scale = depth ** (-0.5)
    key_grads = [jnp.zeros((BLOCK, heads, depth), jnp.float32) for index in range(count)]
    value_grads = [jnp.zeros((BLOCK, heads, depth), jnp.float32) for index in range(count)]
    query_grads = []
    for row_block in range(count):
        query_tile = queries[row_block * BLOCK : (row_block + 1) * BLOCK]
        grad_tile = grads[row_block * BLOCK : (row_block + 1) * BLOCK]
        total = totals[:, row_block * BLOCK : (row_block + 1) * BLOCK]
        flows = jnp.zeros((heads, BLOCK), jnp.float32)
        for col_block in range(row_block + 1):
            scores, allowed = tile_scores(query_tile, keys, segment, row_block, col_block)
            probs = jnp.where(allowed[None], jnp.exp(scores - total[:, :, None]), 0.0)
            value_tile = values[col_block * BLOCK : (col_block + 1) * BLOCK]
            prob_grad = jnp.einsum(
                "qhe,khe->hqk", grad_tile, value_tile, preferred_element_type=jnp.float32
            )
            flows = flows + jnp.sum(prob_grad * probs, axis=-1)
            value_grads[col_block] = value_grads[col_block] + jnp.einsum(
                "hqk,qhe->khe",
                probs.astype(jnp.bfloat16),
                grad_tile,
                preferred_element_type=jnp.float32,
            )
        query_sum = jnp.zeros((BLOCK, heads, depth), jnp.float32)
        for col_block in range(row_block + 1):
            scores, allowed = tile_scores(query_tile, keys, segment, row_block, col_block)
            probs = jnp.where(allowed[None], jnp.exp(scores - total[:, :, None]), 0.0)
            value_tile = values[col_block * BLOCK : (col_block + 1) * BLOCK]
            key_tile = keys[col_block * BLOCK : (col_block + 1) * BLOCK]
            prob_grad = jnp.einsum(
                "qhe,khe->hqk", grad_tile, value_tile, preferred_element_type=jnp.float32
            )
            score_grad = (probs * (prob_grad - flows[:, :, None])).astype(jnp.bfloat16)
            query_sum = query_sum + scale * jnp.einsum(
                "hqk,khe->qhe", score_grad, key_tile, preferred_element_type=jnp.float32
            )
            key_grads[col_block] = key_grads[col_block] + scale * jnp.einsum(
                "hqk,qhe->khe", score_grad, query_tile, preferred_element_type=jnp.float32
            )
        query_grads.append(query_sum)
    return (
        jnp.concatenate(query_grads, axis=0).astype(jnp.bfloat16),
        jnp.concatenate(key_grads, axis=0).astype(jnp.bfloat16),
        jnp.concatenate(value_grads, axis=0).astype(jnp.bfloat16),
    )


def adam_update(master, grad, first, second, rate, decay, first_fix, second_fix):
    first_next = BETA_FIRST * first + (1.0 - BETA_FIRST) * grad
    second_next = BETA_SECOND * second + (1.0 - BETA_SECOND) * grad * grad
    change = (
        first_next / first_fix / (jnp.sqrt(second_next / second_fix) + ADAM_EPSILON)
        + decay * master
    )
    return (master - rate * change, first_next, second_next)


def adam_step(master, grad, first, second, rate, decay, fixes):
    first_next = BETA_FIRST * first + (1.0 - BETA_FIRST) * grad
    second_next = BETA_SECOND * second + (1.0 - BETA_SECOND) * grad * grad
    change = (
        first_next / fixes[0] / (jnp.sqrt(second_next / fixes[1]) + ADAM_EPSILON)
        + decay * master
    )
    return master - rate * change, first_next, second_next


def adam_kernel(rates, fix_ref, late_ref, early_ref, *refs):
    fixes = (fix_ref[0], fix_ref[1])
    smalls = 4
    matrix_inputs, small_inputs = refs[: 4 * len(rates)], refs[4 * len(rates) :][: 3 * smalls]
    outputs = refs[4 * len(rates) + 3 * smalls :]
    for index, rate in enumerate(rates):
        master, grad, first, second = matrix_inputs[4 * index : 4 * index + 4]
        updated, first_out, second_out, grad_out, low_out = outputs[5 * index : 5 * index + 5]
        value = grad[...].reshape(master.shape)
        fresh = adam_step(
            master[...], value, first[...], second[...], rate, MATRIX_DECAY, fixes
        )
        updated[...], first_out[...], second_out[...] = fresh
        grad_out[...] = value
        low_out[...] = fresh[0].astype(jnp.bfloat16)

    @pl.when(pl.program_id(0) == 0)
    def _():
        local = small_inputs[0].shape[1]
        units = small_inputs[3].shape[1]
        early = early_ref
        pieces = (
            [early[4:5, :local], early[4:5, local : 2 * local]],
            [early[4:5, 2 * local : 2 * local + units]],
            [late_ref[0:1, :], early[0:1, :]],
            [late_ref[1:2, :], early[2:3, :], early[1:2, :], early[3:4, :]],
        )
        for index in range(smalls):
            master, first, second = small_inputs[3 * index : 3 * index + 3]
            to = 5 * len(rates) + 4 * index
            updated, first_out, second_out, grad_out = outputs[to : to + 4]
            for row, value in enumerate(pieces[index]):
                here = slice(row, row + 1)
                fresh = adam_step(
                    master[here, :], value, first[here, :], second[here, :], SMALL_RATE, 0.0, fixes
                )
                updated[here, :], first_out[here, :], second_out[here, :] = fresh
                grad_out[here, :] = value


ADAM_STEPS = 8


def adam_call(matrices, smalls, late, early, fixes):
    in_specs = [pl.BlockSpec(memory_space=pltpu.SMEM)] + [
        pl.BlockSpec(rows.shape, lambda i: (0, 0)) for rows in (late, early)
    ]
    out_specs, out_shape, operands, rates = [], [], [fixes, late, early], []
    for master, grad, first, second, rate in matrices:
        lead = master.shape[:-2]
        rows, columns = master.shape[-2] // ADAM_STEPS, master.shape[-1]
        zeros = (0,) * len(lead)
        whole = pl.BlockSpec(lead + (rows, columns), lambda i, z=zeros: z + (i, 0))
        half = pl.BlockSpec(
            (1,) + lead + (rows, columns),
            lambda i, z=zeros: (i // (ADAM_STEPS // 2),) + z + (i % (ADAM_STEPS // 2), 0),
        )
        in_specs += [whole, half, whole, whole]
        operands += [master, grad, first, second]
        shape = jax.ShapeDtypeStruct(master.shape, jnp.float32)
        out_specs += [whole] * 5
        out_shape += [shape] * 4 + [jax.ShapeDtypeStruct(master.shape, jnp.bfloat16)]
        rates.append(rate)
    for group in smalls:
        spec = pl.BlockSpec(group[0].shape, lambda i: (0, 0))
        in_specs += [spec] * 3
        operands += list(group)
        out_specs += [spec] * 4
        out_shape += [jax.ShapeDtypeStruct(group[0].shape, jnp.float32)] * 4
    return pl.pallas_call(
        functools.partial(adam_kernel, tuple(rates)),
        grid=(ADAM_STEPS,),
        in_specs=in_specs,
        out_specs=out_specs,
        out_shape=out_shape,
        compiler_params=pltpu.CompilerParams(vmem_limit_bytes=VMEM_LIMIT),
        name="adam",
    )(*operands)


def per_device(
    layer_input,
    cotangent,
    lengths,
    offsets,
    step,
    mix_weight,
    out_weight,
    up_weight,
    down_weight,
    mix_first,
    out_first,
    up_first,
    down_first,
    mix_second,
    out_second,
    up_second,
    down_second,
    mix_bias,
    up_bias,
    norm_gains,
    shifts,
    mix_bias_first,
    up_bias_first,
    gains_first,
    shifts_first,
    mix_bias_second,
    up_bias_second,
    gains_second,
    shifts_second,
):
    parts = lax.axis_size("mp")
    local_width = mix_weight.shape[2]
    bounds = jnp.concatenate([offsets, offsets + lengths])
    (
        normed_one,
        mixed,
        mix_whole,
        out_whole,
        up_low,
        down_low,
        own_branch,
        bias_down_grad,
    ) = project_call(
        layer_input,
        norm_gains[0:1],
        shifts[0:1],
        mix_weight,
        out_weight,
        mix_bias,
        up_weight,
        down_weight,
        cotangent,
        bounds,
        parts // 2,
    )
    (
        attended_flat,
        aux,
        resid_own,
        normed_mid,
        branch_grad,
        up_whole,
        down_whole,
    ) = attend_out_call(
        mixed,
        bounds,
        out_whole,
        layer_input,
        own_branch,
        norm_gains[1:2],
        shifts[2:3],
        shifts[1:2],
        up_low,
        down_low,
        parts // 2,
    )
    normed_two, active, hidden_grad, resid_grad, resid_low, row_sums, up_bias_grad = feed_call(
        normed_mid,
        branch_grad,
        up_whole,
        down_whole,
        up_bias[None],
        resid_own,
        own_branch,
        norm_gains[1:2],
        parts // 2,
    )
    up_bias_grad = up_bias_grad[0]
    stacked, mix_bias_grad, down_pieces, out_grad, layer_output, _ = branch_back_call(
        resid_low,
        active,
        down_whole,
        attended_flat,
        out_whole,
        shifts[3:4],
        bounds,
        mixed,
        aux,
        resid_own,
        branch_grad,
        parts // 2,
    )
    early = jnp.concatenate(
        [
            row_sums,
            bias_down_grad,
            jnp.pad(
                jnp.concatenate([mix_bias_grad.reshape(-1), up_bias_grad]),
                (0, row_sums.shape[1] - 2 * local_width - up_bias_grad.shape[0]),
            )[None]
        ],
        axis=0,
    )
    input_grad, late, early, mix_pieces, up_pieces, out_pieces = input_back_call(
        stacked,
        mix_whole,
        layer_input,
        resid_grad,
        norm_gains[0:1],
        early,
        hidden_grad,
        out_grad,
        normed_one,
        normed_two,
        parts // 2,
    )
    step_count = step[0].astype(jnp.float32)
    fixes = jnp.stack([1.0 - BETA_FIRST**step_count, 1.0 - BETA_SECOND**step_count])
    news = adam_call(
        [
            (mix_weight, mix_pieces, mix_first, mix_second, D ** (-0.5)),
            (out_weight, out_pieces, out_first, out_second, OUT_FAN ** (-0.5)),
            (up_weight, up_pieces, up_first, up_second, D ** (-0.5)),
            (down_weight, down_pieces, down_first, down_second, FF ** (-0.5)),
        ],
        [
            (mix_bias, mix_bias_first, mix_bias_second),
            (up_bias[None], up_bias_first[None], up_bias_second[None]),
            (norm_gains, gains_first, gains_second),
            (shifts, shifts_first, shifts_second),
        ],
        late,
        early,
        fixes,
    )
    mix, out, up, down = (news[5 * index : 5 * index + 5] for index in range(4))
    biases, unit_biases, gains, moves = (
        news[20 + 4 * index : 24 + 4 * index] for index in range(4)
    )
    unit_biases = [value[0] for value in unit_biases]
    return (
        layer_output,
        input_grad,
        *mix[:3],
        *out[:3],
        *up[:3],
        *down[:3],
        *biases[:3],
        *unit_biases[:3],
        *gains[:3],
        *moves[:3],
        mix[3],
        out[3],
        up[3],
        down[3],
        biases[3],
        unit_biases[3],
        gains[3],
        moves[3],
        mix[4],
        out[4],
        up[4],
        down[4],
    )


def per_device_any(
    layer_input,
    cotangent,
    lengths,
    offsets,
    step,
    mix_weight,
    out_weight,
    up_weight,
    down_weight,
    mix_first,
    out_first,
    up_first,
    down_first,
    mix_second,
    out_second,
    up_second,
    down_second,
    mix_bias,
    up_bias,
    norm_gains,
    shifts,
    mix_bias_first,
    up_bias_first,
    gains_first,
    shifts_first,
    mix_bias_second,
    up_bias_second,
    gains_second,
    shifts_second,
):
    own_rows = layer_input.shape[0]
    parts = lax.axis_size("mp")
    group_rows = own_rows * parts
    slots_here = lengths.shape[0]
    slot_len = group_rows // slots_here
    local_width = mix_weight.shape[2]
    depth = HEAD_DIM
    heads_here = local_width // depth
    positions = jnp.arange(slot_len, dtype=jnp.int32)
    live = (positions[None, :] >= offsets[:, None]) & (
        positions[None, :] < (offsets + lengths)[:, None]
    )
    segment = live.astype(jnp.int32)
    first_row = lax.axis_index("mp") * own_rows
    own_live = own_slice(live.reshape(-1), first_row, own_rows)[:, None]
    own_input = layer_input.astype(jnp.float32)
    normed_own, hat_one, inv_one = layer_norm_parts(own_input, norm_gains[0], shifts[0])
    normed_one = gather_rows(normed_own.astype(jnp.bfloat16))
    mix_full = gather_shards(mix_weight.astype(jnp.bfloat16), 1)
    out_full = gather_shards(out_weight.astype(jnp.bfloat16), 1)
    up_full = gather_shards(up_weight.astype(jnp.bfloat16), 0)
    down_full = gather_shards(down_weight.astype(jnp.bfloat16), 1)
    out_grad = jnp.where(own_live, cotangent.astype(jnp.float32), 0.0)
    bias_down_grad = jnp.sum(out_grad, axis=0)
    branch_grad = gather_rows(out_grad.astype(jnp.bfloat16))
    mixed = jnp.einsum("td,cde->cte", normed_one, mix_full, preferred_element_type=jnp.float32)
    queries = (
        (mixed[0] + mix_bias[0])
        .astype(jnp.bfloat16)
        .reshape(slots_here, slot_len, heads_here, depth)
    )
    keys = mixed[1].astype(jnp.bfloat16).reshape(slots_here, slot_len, heads_here, depth)
    values = (
        (mixed[2] + mix_bias[1])
        .astype(jnp.bfloat16)
        .reshape(slots_here, slot_len, heads_here, depth)
    )

    def attend(item):
        return attention_forward(item[0], item[1], item[2], item[3])

    attended, totals = lax.map(attend, (queries, keys, values, segment))
    attended_flat = attended.reshape(group_rows, local_width)
    attn_part = jnp.dot(attended_flat, out_full, preferred_element_type=jnp.float32)
    resid_own = own_input + scatter_rows(attn_part) + shifts[1]
    normed_mid, hat_two, inv_two = layer_norm_parts(resid_own, norm_gains[1], shifts[2])
    normed_two = gather_rows(normed_mid.astype(jnp.bfloat16))
    hidden = jnp.dot(normed_two, up_full, preferred_element_type=jnp.float32) + up_bias
    active_value, gelu_pull = jax.vjp(tanh_gelu, hidden)
    active = active_value.astype(jnp.bfloat16)
    active_grad = jnp.einsum(
        "td,fd->tf", branch_grad, down_full, preferred_element_type=jnp.float32
    )
    hidden_grad = gelu_pull(active_grad)[0].astype(jnp.bfloat16)
    two_part = jnp.einsum("tf,df->td", hidden_grad, up_full, preferred_element_type=jnp.float32)
    two_grad = scatter_rows(two_part)
    down_part = jnp.dot(active, down_full, preferred_element_type=jnp.float32)
    down_grad = jnp.einsum("tf,td->fd", active, branch_grad, preferred_element_type=jnp.float32)
    up_bias_grad = jnp.sum(hidden_grad, axis=0, dtype=jnp.float32)
    up_grad = jnp.einsum("td,tf->df", normed_two, hidden_grad, preferred_element_type=jnp.float32)
    resid_grad = out_grad + layer_norm_back(two_grad, hat_two, inv_two, norm_gains[1])
    attn_branch = gather_rows(resid_grad.astype(jnp.bfloat16))
    result_own = resid_own + scatter_rows(down_part) + shifts[3]
    layer_output = jnp.where(own_live, result_own, 0.0).astype(jnp.bfloat16)
    gain_two_grad = jnp.sum(two_grad * hat_two, axis=0)
    shift_two_grad = jnp.sum(two_grad, axis=0)
    bias_out_grad = jnp.sum(resid_grad, axis=0)
    attended_grad = jnp.einsum(
        "td,ed->te", attn_branch, out_full, preferred_element_type=jnp.float32
    ).astype(jnp.bfloat16)
    out_weight_grad = jnp.einsum(
        "te,td->ed", attended_flat, attn_branch, preferred_element_type=jnp.float32
    )

    def attend_back(item):
        return attention_backward(item[0], item[1], item[2], item[3], item[4], item[5])

    query_grad, key_grad, value_grad = lax.map(
        attend_back,
        (
            queries,
            keys,
            values,
            segment,
            totals,
            attended_grad.reshape(slots_here, slot_len, heads_here, depth),
        ),
    )
    stacked = jnp.stack(
        [
            query_grad.reshape(group_rows, local_width),
            key_grad.reshape(group_rows, local_width),
            value_grad.reshape(group_rows, local_width),
        ]
    )
    one_part = jnp.einsum("cte,cde->td", stacked, mix_full, preferred_element_type=jnp.float32)
    one_grad = scatter_rows(one_part)
    mix_grad = jnp.einsum("td,cte->cde", normed_one, stacked, preferred_element_type=jnp.float32)
    mix_bias_grad = jnp.stack(
        [
            jnp.sum(stacked[0], axis=0, dtype=jnp.float32),
            jnp.sum(stacked[2], axis=0, dtype=jnp.float32),
        ]
    )
    mix_owned = scatter_shards(mix_grad, 1)
    out_owned = scatter_shards(out_weight_grad, 1)
    up_owned = scatter_shards(up_grad, 0)
    down_owned = scatter_shards(down_grad, 1)
    input_grad = resid_grad + layer_norm_back(one_grad, hat_one, inv_one, norm_gains[0])
    gain_one_grad = jnp.sum(one_grad * hat_one, axis=0)
    shift_one_grad = jnp.sum(one_grad, axis=0)
    gain_grad = jnp.stack([gain_one_grad, gain_two_grad])
    shift_grad = jnp.stack([shift_one_grad, bias_out_grad, shift_two_grad, bias_down_grad])
    mix_bias_total, up_bias_total = lax.psum((mix_bias_grad, up_bias_grad), "dp")
    gain_total, shift_total = lax.psum((gain_grad, shift_grad), ("dp", "mp"))
    step_count = step[0].astype(jnp.float32)
    first_fix = 1.0 - BETA_FIRST**step_count
    second_fix = 1.0 - BETA_SECOND**step_count
    mix_new = adam_update(
        mix_weight,
        mix_owned,
        mix_first,
        mix_second,
        D ** (-0.5),
        MATRIX_DECAY,
        first_fix,
        second_fix,
    )
    out_new = adam_update(
        out_weight,
        out_owned,
        out_first,
        out_second,
        OUT_FAN ** (-0.5),
        MATRIX_DECAY,
        first_fix,
        second_fix,
    )
    up_new = adam_update(
        up_weight, up_owned, up_first, up_second, D ** (-0.5), MATRIX_DECAY, first_fix, second_fix
    )
    down_new = adam_update(
        down_weight,
        down_owned,
        down_first,
        down_second,
        FF ** (-0.5),
        MATRIX_DECAY,
        first_fix,
        second_fix,
    )
    mix_bias_new = adam_update(
        mix_bias,
        mix_bias_total,
        mix_bias_first,
        mix_bias_second,
        SMALL_RATE,
        0.0,
        first_fix,
        second_fix,
    )
    up_bias_new = adam_update(
        up_bias,
        up_bias_total,
        up_bias_first,
        up_bias_second,
        SMALL_RATE,
        0.0,
        first_fix,
        second_fix,
    )
    gains_new = adam_update(
        norm_gains, gain_total, gains_first, gains_second, SMALL_RATE, 0.0, first_fix, second_fix
    )
    shifts_new = adam_update(
        shifts, shift_total, shifts_first, shifts_second, SMALL_RATE, 0.0, first_fix, second_fix
    )
    return (
        layer_output,
        input_grad,
        mix_new[0],
        mix_new[1],
        mix_new[2],
        out_new[0],
        out_new[1],
        out_new[2],
        up_new[0],
        up_new[1],
        up_new[2],
        down_new[0],
        down_new[1],
        down_new[2],
        mix_bias_new[0],
        mix_bias_new[1],
        mix_bias_new[2],
        up_bias_new[0],
        up_bias_new[1],
        up_bias_new[2],
        gains_new[0],
        gains_new[1],
        gains_new[2],
        shifts_new[0],
        shifts_new[1],
        shifts_new[2],
        mix_owned,
        out_owned,
        up_owned,
        down_owned,
        mix_bias_total,
        up_bias_total,
        gain_total,
        shift_total,
        mix_new[0].astype(jnp.bfloat16),
        out_new[0].astype(jnp.bfloat16),
        up_new[0].astype(jnp.bfloat16),
        down_new[0].astype(jnp.bfloat16),
    )


def solution(mesh):
    placed = (
        P(("dp", "mp"), None),
        P(("dp", "mp"), None),
        P("dp"),
        P("dp"),
        P(),
        P(None, "dp", "mp"),
        P("mp", "dp"),
        P("dp", "mp"),
        P("mp", "dp"),
        P(None, "dp", "mp"),
        P("mp", "dp"),
        P("dp", "mp"),
        P("mp", "dp"),
        P(None, "dp", "mp"),
        P("mp", "dp"),
        P("dp", "mp"),
        P("mp", "dp"),
        P(None, "mp"),
        P("mp"),
        P(),
        P(),
        P(None, "mp"),
        P("mp"),
        P(),
        P(),
        P(None, "mp"),
        P("mp"),
        P(),
        P(),
    )
    fits = mesh.shape["dp"] == 4 and mesh.shape["mp"] == 8
    return jax.shard_map(
        per_device if fits else per_device_any,
        mesh=mesh,
        in_specs=placed,
        out_specs=(
            P(("dp", "mp"), None),
            P(("dp", "mp"), None),
            P(None, "dp", "mp"),
            P(None, "dp", "mp"),
            P(None, "dp", "mp"),
            P("mp", "dp"),
            P("mp", "dp"),
            P("mp", "dp"),
            P("dp", "mp"),
            P("dp", "mp"),
            P("dp", "mp"),
            P("mp", "dp"),
            P("mp", "dp"),
            P("mp", "dp"),
            P(None, "mp"),
            P(None, "mp"),
            P(None, "mp"),
            P("mp"),
            P("mp"),
            P("mp"),
            P(),
            P(),
            P(),
            P(),
            P(),
            P(),
            P(None, "dp", "mp"),
            P("mp", "dp"),
            P("dp", "mp"),
            P("mp", "dp"),
            P(None, "mp"),
            P("mp"),
            P(),
            P(),
            P(None, "dp", "mp"),
            P("mp", "dp"),
            P("dp", "mp"),
            P("mp", "dp"),
        ),
        check_vma=False,
    )
```

```python
import functools

import jax
import jax.numpy as jnp
from jax import lax
from jax.experimental import pallas as pl
from jax.experimental.pallas import tpu as pltpu
from jax.sharding import PartitionSpec as P

D = 2048
HEAD_DIM = 128
FF = 8192
BLOCK = 512
OUT_FAN = 7


NORM_EPSILON = 1e-05
ADAM_EPSILON = 1e-08
BETA_FIRST = 0.9
BETA_SECOND = 0.999
MATRIX_DECAY = 0.1
SMALL_RATE = 0.2
MASK_FILL = -1e30


def layer_norm_parts(rows, gain, shift):
    center = rows - jnp.mean(rows, axis=-1, keepdims=True)
    inverse = lax.rsqrt(jnp.mean(center * center, axis=-1, keepdims=True) + NORM_EPSILON)
    normed = center * inverse
    return (normed * gain + shift, normed, inverse)


def layer_norm_back(grad_out, normed, inverse, gain):
    scaled = grad_out * gain
    return inverse * (
        scaled
        - jnp.mean(scaled, axis=-1, keepdims=True)
        - normed * jnp.mean(scaled * normed, axis=-1, keepdims=True)
    )


def tanh_gelu(values):
    return jax.nn.gelu(values, approximate=True)


def own_slice(whole, first_row, count):
    return lax.dynamic_slice_in_dim(whole, first_row, count, 0)


def gather_rows(rows):
    return lax.all_gather(rows, "mp", axis=0, tiled=True)


def scatter_rows(terms):
    low = terms.astype(jnp.bfloat16)
    return lax.psum_scatter(low, "mp", scatter_dimension=0, tiled=True).astype(jnp.float32)


def swap(value, mask):
    size = lax.axis_size("dp")
    return lax.ppermute(value, "dp", [(place, place ^ mask) for place in range(size)])


def gather_shards(shard, axis):
    if lax.axis_size("dp") != 4:
        return lax.all_gather(shard, "dp", axis=axis, tiled=True)
    count = shard.shape[axis]
    me = lax.axis_index("dp")
    from_x = swap(shard, 1)
    from_y = swap(shard, 2)
    half = count // 2
    low = swap(lax.slice_in_dim(from_x, 0, half, axis=axis), 2)
    high = swap(lax.slice_in_dim(from_y, half, count, axis=axis), 1)
    shape = list(shard.shape)
    shape[axis] = 4 * count
    full = jnp.zeros(shape, shard.dtype)
    full = lax.dynamic_update_slice_in_dim(full, shard, me * count, axis)
    full = lax.dynamic_update_slice_in_dim(full, from_x, (me ^ 1) * count, axis)
    full = lax.dynamic_update_slice_in_dim(full, from_y, (me ^ 2) * count, axis)
    full = lax.dynamic_update_slice_in_dim(full, low, (me ^ 3) * count, axis)
    return lax.dynamic_update_slice_in_dim(full, high, (me ^ 3) * count + half, axis)


def scatter_shards(grad, axis):
    if lax.axis_size("dp") != 4:
        return lax.psum_scatter(grad, "dp", scatter_dimension=axis, tiled=True)
    count = grad.shape[axis] // 4
    half = count // 2
    me = lax.axis_index("dp")

    def piece(owner, upper):
        return lax.dynamic_slice_in_dim(grad, owner * count + upper * half, half, axis)

    def one_way(first, second, upper):
        near = swap(piece(me ^ first, upper).astype(jnp.bfloat16), first)
        far = swap(piece(me ^ 3, upper).astype(jnp.bfloat16), first)
        onward = piece(me ^ second, upper) + far.astype(jnp.float32)
        last = swap(onward.astype(jnp.bfloat16), second)
        return piece(me, upper) + near.astype(jnp.float32) + last.astype(jnp.float32)

    return lax.concatenate([one_way(1, 2, 0), one_way(2, 1, 1)], axis)


MESH = pl.DeviceIdType.MESH
VMEM_LIMIT = 62 * 1024 * 1024
TURNED = (((1,), (1,)), ((), ()))
CROSSED = (((0,), (0,)), ((), ()))


class Place:
    def __init__(self, chips):
        self.chips = chips
        self.dp = lax.axis_index("dp")
        self.me = lax.axis_index("mp")
        self.chip = self.me // 2
        self.core = self.me % 2
        self.has_up = self.chip < chips - 1
        self.has_down = self.chip > 0
        self.up = (self.dp, jnp.minimum(self.me + 2, 2 * chips - 1))
        self.down = (self.dp, jnp.maximum(self.me - 2, 0))
        self.side = (self.dp, self.me + 1 - 2 * self.core)
        self.x_peer = self.dp + 1 - 2 * (self.dp % 2)
        self.y_peer = (self.dp + 2) % 4
        self.across = 3 - self.dp
        self.x_way = (self.x_peer, self.me)
        self.y_way = (self.y_peer, self.me)

    def greet(self, square, everyone=False):
        barrier = pltpu.get_barrier_semaphore()

        def signal(device):
            pl.semaphore_signal(barrier, inc=1, device_id=device, device_id_type=MESH)

        signal(self.side)
        pl.when(self.has_up)(lambda: signal(self.up))
        pl.when(self.has_down)(lambda: signal(self.down))
        count = 1 + self.has_up.astype(jnp.int32) + self.has_down.astype(jnp.int32)
        if square:
            signal(self.x_way)
            signal(self.y_way)
            count = count + 2
        if everyone:
            signal((self.across, self.me))
            count = count + 1

            def beyond(chip, carry):
                far = (chip > self.chip + 1) | (chip < self.chip - 1)
                pl.when(far)(lambda: signal((self.dp, 2 * chip + self.core)))
                return carry

            lax.fori_loop(0, self.chips, beyond, 0)
            near = self.has_up.astype(jnp.int32) + self.has_down.astype(jnp.int32)
            count = count + (self.chips - 1) - near
        pl.semaphore_wait(barrier, count)


def remote(source, target, send, recv, device):
    return pltpu.make_async_remote_copy(
        src_ref=source,
        dst_ref=target,
        send_sem=send,
        recv_sem=recv,
        device_id=device,
        device_id_type=MESH,
    )


def fetch(pairs, sems):
    copies = [
        pltpu.make_async_copy(source, target, sems.at[index])
        for index, (source, target) in enumerate(pairs)
    ]
    for copy in copies:
        copy.start()
    return copies


class LineGather:
    def __init__(self, place, blocks, send, recv, parts=1, own=None):
        self.place, self.blocks, self.send, self.recv = place, blocks, send, recv
        self.parts, self.own = parts, own

    def copy(self, way, chip, part=0, own=None):
        place = self.place
        piece = chip * self.parts + part
        block = 2 * piece + place.core
        device = (place.up, place.down, place.side)[way]
        return remote(
            self.blocks.at[block] if own is None else own,
            self.blocks.at[block],
            self.send.at[way, piece],
            self.recv.at[block],
            device,
        )

    def arrive(self, chip, core, part=0):
        piece = chip * self.parts + part
        block = 2 * piece + core
        remote(
            self.blocks.at[block],
            self.blocks.at[block],
            self.send.at[2, piece],
            self.recv.at[block],
            self.place.side,
        ).wait_recv()

    def begin_part(self, part):
        place = self.place
        pl.when(place.has_up)(lambda: self.copy(0, place.chip, part, self.own).start())
        pl.when(place.has_down)(lambda: self.copy(1, place.chip, part, self.own).start())
        self.copy(2, place.chip, part, self.own).start()

    def begin(self):
        for part in range(self.parts):
            self.begin_part(part)

    def step(self, distance, part=0):
        place = self.place
        low = place.chip - distance
        high = place.chip + distance

        @pl.when(low >= 0)
        def _():
            self.arrive(low, place.core, part)
            pl.when(place.has_up)(lambda: self.copy(0, low, part).start())
            self.copy(2, low, part).start()

        @pl.when(high < place.chips)
        def _():
            self.arrive(high, place.core, part)
            pl.when(place.has_down)(lambda: self.copy(1, high, part).start())
            self.copy(2, high, part).start()

    def finish(self):
        place = self.place

        def drain(chip, carry):
            for part in range(self.parts):
                pl.when(place.has_up & (chip <= place.chip))(
                    lambda: self.copy(0, chip, part).wait_send()
                )
                pl.when(place.has_down & (chip >= place.chip))(
                    lambda: self.copy(1, chip, part).wait_send()
                )
                self.copy(2, chip, part).wait_send()
            return carry

        lax.fori_loop(0, place.chips, drain, 0)


class SquareGather:
    def __init__(self, place, shard, view, half, send, recv):
        self.place, self.shard, self.view, self.half = place, shard, view, half
        self.send, self.recv = send, recv

    def first(self, way):
        place = self.place
        device = (place.x_way, place.y_way)[way]
        return remote(
            self.shard, self.view(place.dp), self.send.at[way], self.recv.at[way], device
        )

    def first_landed(self, way):
        place = self.place
        owner = (place.x_peer, place.y_peer)[way]
        device = (place.x_way, place.y_way)[way]
        remote(
            self.view(owner), self.view(owner), self.send.at[way], self.recv.at[way], device
        ).wait_recv()

    def second(self, way):
        place = self.place
        owner = (place.y_peer, place.x_peer)[way]
        device = (place.x_way, place.y_way)[way]
        part = self.half(owner, 1 - way)
        return remote(part, part, self.send.at[2 + way], self.recv.at[2 + way], device)

    def second_landed(self, way):
        place = self.place
        device = (place.x_way, place.y_way)[way]
        part = self.half(place.across, 1 - way)
        remote(part, part, self.send.at[2 + way], self.recv.at[2 + way], device).wait_recv()

    def begin(self):
        self.first(0).start()
        self.first(1).start()

    def middle(self):
        self.first_landed(0)
        self.second(1).start()
        self.first_landed(1)
        self.second(0).start()

    def end(self):
        self.second_landed(0)
        self.second_landed(1)

    def finish(self):
        self.first(0).wait_send()
        self.first(1).wait_send()
        self.second(0).wait_send()
        self.second(1).wait_send()


def norm_rows(rows, gain, shift):
    normed, hat, inverse = layer_norm_parts(rows, gain, shift)
    return normed


def project_kernel(
    chips,
    parts,
    rows_ref,
    gain_ref,
    shift_ref,
    mix_weight_hbm,
    out_weight_hbm,
    bias_ref,
    up_weight_hbm,
    down_weight_hbm,
    cotangent_hbm,
    bounds_ref,
    normed_ref,
    mixed_hbm,
    mix_hbm,
    out_whole,
    up_ref,
    down_ref,
    branch_ref,
    branch_sum_ref,
    mix_weight_ref,
    out_weight_ref,
    up_weight_ref,
    down_weight_ref,
    cotangent_ref,
    fetch_sem,
    mix_ref,
    out_ref,
    mixed_ref,
    mix_whole,
    emit_sem,
    blocks,
    line_send,
    line_recv,
    mix_send,
    mix_recv,
    out_send,
    out_recv,
    own_sem,
    keep_sem,
):
    place = Place(chips)
    count = rows_ref.shape[0]
    rows = count // parts
    fetched = fetch(
        [
            (mix_weight_hbm, mix_weight_ref),
            (out_weight_hbm, out_weight_ref),
            (cotangent_hbm, cotangent_ref),
            (up_weight_hbm, up_weight_ref),
            (down_weight_hbm, down_weight_ref),
        ],
        fetch_sem,
    )
    line = LineGather(place, blocks, line_send, line_recv, parts)

    def norm(part):
        def one(span):
            own = rows_ref[pl.ds(part * rows + span.start, 64), :].astype(jnp.float32)
            normed = norm_rows(own, gain_ref[...], shift_ref[...])
            blocks[2 * (place.chip * parts + part) + place.core, span, :] = normed.astype(
                jnp.bfloat16
            )

        by_rows(rows, 64, one)

    norm(0)
    place.greet(True)
    line.begin_part(0)
    for part in range(1, parts):
        norm(part)
        line.begin_part(part)
    mix = SquareGather(
        place,
        mix_ref,
        lambda owner: mix_whole.at[:, owner],
        lambda owner, which: mix_whole.at[:, owner, pl.ds(which * 256, 256)],
        mix_send,
        mix_recv,
    )
    out = SquareGather(
        place,
        out_ref,
        lambda owner: out_whole.at[owner],
        lambda owner, which: out_whole.at[owner, pl.ds(which * 128, 128)],
        out_send,
        out_recv,
    )

    def lower(source, target):
        def one(span):
            target[span, :] = source[span, :].astype(jnp.bfloat16)

        by_rows(source.shape[0], 64, one)

    fetched[0].wait()
    for part in range(3):
        lower(mix_weight_ref.at[part], mix_ref.at[part])
    mix.begin()
    own_mix = pltpu.make_async_copy(mix_ref, mix_whole.at[:, place.dp], own_sem.at[0])
    own_mix.start()
    fetched[1].wait()
    lower(out_weight_ref, out_ref)
    own_out = pltpu.make_async_copy(out_ref, out_whole.at[place.dp], own_sem.at[1])
    own_out.start()
    branch_sum_ref[...] = jnp.zeros_like(branch_sum_ref)

    def branch(span):
        live = alive((64, 1), 0, place.me * count + span.start, bounds_ref)
        grad = jnp.where(live > 0, cotangent_ref[span, :].astype(jnp.float32), 0.0)
        branch_ref[span, :] = grad.astype(jnp.bfloat16)
        branch_sum_ref[...] += jnp.sum(grad, axis=0, keepdims=True)

    fetched[2].wait()
    by_rows(count, 64, branch)
    fetched[3].wait()
    lower(up_weight_ref, up_ref)
    fetched[4].wait()
    lower(down_weight_ref, down_ref)

    def span_of(chip, core, part):
        start = (2 * chip + core) * count + part * rows
        return pl.ds(pl.multiple_of(start, rows), rows)

    def copies(chip, part):
        piece = chip * parts + part
        taken = []
        for core in range(2):
            span = span_of(chip, core, part)
            taken.append(
                pltpu.make_async_copy(
                    blocks.at[2 * piece + core], normed_ref.at[span], keep_sem.at[piece, core]
                )
            )
            taken.append(
                pltpu.make_async_copy(
                    mixed_ref.at[:, span], mixed_hbm.at[:, span], emit_sem.at[piece, core]
                )
            )
        return taken

    keep_mix = pltpu.make_async_copy(mix_whole, mix_hbm, own_sem.at[2])

    def project(chip, part):
        piece = chip * parts + part
        line.arrive(chip, 1 - place.core, part)
        pair = blocks[pl.ds(2 * piece, 2)].reshape(2 * rows, -1)
        for kind in range(3):
            weight = mix_whole[kind].reshape(-1, mix_whole.shape[3])
            result = jnp.dot(pair, weight, preferred_element_type=jnp.float32)
            if kind == 0:
                result = result + bias_ref[0:1, :]
            if kind == 2:
                result = result + bias_ref[1:2, :]
            low = result.astype(jnp.bfloat16)
            for core in range(2):
                mixed_ref[kind, span_of(chip, core, part), :] = low[
                    core * rows : (core + 1) * rows
                ]
        for copy in copies(chip, part):
            copy.start()

    def turn(index, carry):
        distance = index // parts
        part = index % parts

        @pl.when(distance > 0)
        def _():
            line.step(distance, part)

        @pl.when(index == parts)
        def _():
            mix.middle()
            out.begin()
            mix.end()
            own_mix.wait()
            keep_mix.start()
            out.middle()

        first = jnp.where(index == parts, 0, index)

        def one(order, inner):
            each = order // 2
            side = order % 2
            near = each // parts
            chip = place.chip + near * (2 * side - 1)

            @pl.when((chip >= 0) & (chip < chips) & ((near > 0) | (side == 0)))
            def _():
                project(chip, each % parts)

            return inner

        @pl.when(index >= parts)
        def _():
            lax.fori_loop(2 * first, 2 * index + 2, one, 0)

        return carry

    lax.fori_loop(0, chips * parts, turn, 0)
    out.end()
    own_out.wait()
    line.finish()
    mix.finish()
    out.finish()

    def kept(piece, carry):
        for copy in copies(piece // parts, piece % parts):
            copy.wait()
        return carry

    lax.fori_loop(0, parts * chips, kept, 0)
    keep_mix.wait()


def project_call(
    rows, gain, shift, mix_shard, out_shard, bias, up, down, cotangent, bounds, chips
):
    count, width = rows.shape
    total = 2 * chips * count
    local = mix_shard.shape[2]
    parts = 2
    vmem = pl.BlockSpec(memory_space=pltpu.VMEM)
    hbm = pl.BlockSpec(memory_space=pl.ANY)
    dma = pltpu.SemaphoreType.DMA
    flops = 2 * total * width * 3 * local
    return pl.pallas_call(
        functools.partial(project_kernel, chips, parts),
        out_shape=(
            jax.ShapeDtypeStruct((total, width), jnp.bfloat16),
            jax.ShapeDtypeStruct((3, total, local), jnp.bfloat16),
            jax.ShapeDtypeStruct((3, 4, mix_shard.shape[1], local), jnp.bfloat16),
            jax.ShapeDtypeStruct((4,) + out_shard.shape, jnp.bfloat16),
            jax.ShapeDtypeStruct(up.shape, jnp.bfloat16),
            jax.ShapeDtypeStruct(down.shape, jnp.bfloat16),
            jax.ShapeDtypeStruct((count, width), jnp.bfloat16),
            jax.ShapeDtypeStruct((1, width), jnp.float32),
        ),
        in_specs=[vmem] * 3
        + [hbm] * 2
        + [vmem]
        + [hbm] * 3
        + [pl.BlockSpec(memory_space=pltpu.SMEM)],
        out_specs=(hbm,) * 4 + (vmem,) * 4,
        scratch_shapes=[
            pltpu.VMEM(mix_shard.shape, jnp.float32),
            pltpu.VMEM(out_shard.shape, jnp.float32),
            pltpu.VMEM(up.shape, jnp.float32),
            pltpu.VMEM(down.shape, jnp.float32),
            pltpu.VMEM(cotangent.shape, jnp.bfloat16),
            dma((5,)),
            pltpu.VMEM(mix_shard.shape, jnp.bfloat16),
            pltpu.VMEM(out_shard.shape, jnp.bfloat16),
            pltpu.VMEM((3, total, local), jnp.bfloat16),
            pltpu.VMEM((3, 4, mix_shard.shape[1], local), jnp.bfloat16),
            dma((parts * chips, 2)),
            pltpu.VMEM((2 * chips * parts, count // parts, width), jnp.bfloat16),
            dma((3, chips * parts)),
            dma((2 * chips * parts,)),
            dma((4,)),
            dma((4,)),
            dma((4,)),
            dma((4,)),
            dma((3,)),
            dma((parts * chips, 2)),
        ],
        compiler_params=pltpu.CompilerParams(
            collective_id=0, has_side_effects=True, vmem_limit_bytes=VMEM_LIMIT
        ),
        cost_estimate=pl.CostEstimate(flops=flops * 7, bytes_accessed=0, transcendentals=0),
        name="project",
    )(rows, gain, shift, mix_shard, out_shard, bias, up, down, cotangent, bounds)


class LineScatter:
    def __init__(self, place, term, tiles, bufs, sems, prepare=lambda chip: None):
        self.place, self.term, self.tiles, self.prepare = place, term, tiles, prepare
        self.total, self.side_out, self.side_in, self.line_in = bufs
        self.side_send, self.side_recv, self.line_send, self.line_recv = sems

    def side_copy(self, chip):
        return remote(
            self.side_out.at[chip],
            self.side_in.at[chip],
            self.side_send.at[chip],
            self.side_recv.at[chip],
            self.place.side,
        )

    def span(self, tile):
        width = self.total.shape[1] // self.tiles
        return slice(tile * width, (tile + 1) * width)

    def line_copy(self, way, chip, tile):
        place = self.place
        next_chip = place.chip + 1 - 2 * way
        slot = jnp.where((way == 1) & (chip == next_chip), place.chips, chip)
        return remote(
            self.line_in.at[chip, :, self.span(tile)],
            self.line_in.at[slot, :, self.span(tile)],
            self.line_send.at[chip, tile],
            self.line_recv.at[slot, tile],
            (place.up, place.down)[way],
        )

    def landed(self, way, chip, tile):
        place = self.place
        slot = jnp.where((way == 1) & (chip == place.chip), place.chips, chip)
        remote(
            self.line_in.at[slot, :, self.span(tile)],
            self.line_in.at[slot, :, self.span(tile)],
            self.line_send.at[chip, tile],
            self.line_recv.at[slot, tile],
            (place.up, place.down)[way],
        ).wait_recv()
        return slot

    def each(self, distance, action):
        place = self.place

        def one(index, carry):
            chip = place.chip + distance * (1 - 2 * index)
            valid = (chip >= 0) & (chip < place.chips) & ((distance > 0) | (index == 0))
            pl.when(valid)(lambda: action(chip))
            return carry

        lax.fori_loop(0, 2, one, 0)

    def hand_over(self, chip):
        self.prepare(chip)
        block = 2 * chip + 1 - self.place.core
        for tile in range(self.tiles):
            self.side_out[chip, :, self.span(tile)] = self.term(block, tile).astype(jnp.bfloat16)
        self.side_copy(chip).start()

    def sum_up(self, chip):
        place = self.place
        block = 2 * chip + place.core
        self.side_copy(chip).wait_recv()
        for tile in range(self.tiles):
            span = self.span(tile)
            self.total[:, span] = self.term(block, tile) + self.side_in[chip, :, span].astype(
                jnp.float32
            )
            for way in range(2):
                behind = (place.has_down, place.has_up)[way]
                goes = (chip >= place.chip) if way == 0 else (chip <= place.chip)

                @pl.when(behind & goes)
                def _():
                    slot = self.landed(way, chip, tile)
                    self.total[:, span] += self.line_in[slot, :, span].astype(jnp.float32)

            @pl.when(chip != place.chip)
            def _():
                self.line_in[chip, :, span] = self.total[:, span].astype(jnp.bfloat16)
                pl.when(chip > place.chip)(lambda: self.line_copy(0, chip, tile).start())
                pl.when(chip < place.chip)(lambda: self.line_copy(1, chip, tile).start())

    def begin(self):
        self.each(self.place.chips - 1, self.hand_over)

    def step(self, index, early=False):
        distance = self.place.chips - 1 - index
        ahead = (index > 0) if early else (index < 0)
        pl.when(ahead & (distance > 0))(lambda: self.each(distance - 1, self.hand_over))
        self.each(distance, self.sum_up)
        behind = (index == 0) if early else (index >= 0)
        pl.when(behind & (distance > 0))(lambda: self.each(distance - 1, self.hand_over))

    def finish(self):
        place = self.place

        def drain(chip, carry):
            self.side_copy(chip).wait_send()
            for tile in range(self.tiles):
                pl.when(chip != place.chip)(lambda: self.line_copy(0, chip, tile).wait_send())
            return carry

        lax.fori_loop(0, place.chips, drain, 0)


class SquareScatter:
    def __init__(self, place, piece, owned, bufs, sems):
        self.place, self.piece, self.owned = place, piece, owned
        self.out, self.arrived = bufs
        self.send, self.recv = sems

    def copy(self, kind, way):
        place = self.place
        turn = way if kind < 2 else 1 - way
        peer = place.x_peer + turn * (place.y_peer - place.x_peer)
        return remote(
            self.out.at[kind, way],
            self.arrived.at[kind, way],
            self.send.at[kind, way],
            self.recv.at[kind, way],
            (peer, place.me),
        )

    def owner(self, kind, way):
        place = self.place
        near = place.x_peer + way * (place.y_peer - place.x_peer)
        other = place.y_peer + way * (place.x_peer - place.y_peer)
        return (place.across, near, other, place.dp)[kind]

    def following(self, kind, way):
        after = self.owner(kind, 1) if kind == 3 else self.owner(kind + 1, 0)
        return jnp.where(way == 0, self.owner(kind, 1), after), 1 - way

    def one(self, kind, way):
        value = self.piece(self.owner(kind, way), way)
        if kind == 2:
            self.copy(0, way).wait_recv()
            value = value + self.arrived[0, way].astype(jnp.float32)
        if kind < 3:
            self.out[kind, way] = value.astype(jnp.bfloat16)
            self.copy(kind, way).start()
        else:
            self.owned[way] = value

    def stage(self, kind):
        def one(way, carry):
            self.one(kind, way)
            return carry

        lax.fori_loop(0, 2, one, 0)

    def end(self):
        def one(way, carry):
            self.copy(1, way).wait_recv()
            self.copy(2, way).wait_recv()
            self.owned[way] = (
                self.owned[way]
                + self.arrived[1, way].astype(jnp.float32)
                + self.arrived[2, way].astype(jnp.float32)
            )
            for kind in range(3):
                self.copy(kind, way).wait_send()
            return carry

        lax.fori_loop(0, 2, one, 0)


def square_scratch(half):
    dma = pltpu.SemaphoreType.DMA
    return [
        pltpu.VMEM((3, 2) + half, jnp.bfloat16),
        pltpu.VMEM((3, 2) + half, jnp.bfloat16),
        dma((3, 2)),
        dma((3, 2)),
    ]


class SmallSum:
    def __init__(self, place, rows, alone, bufs, sems):
        self.place, self.rows, self.alone = place, rows, alone
        self.side_buf, self.line_buf, self.square_buf = bufs
        self.send, self.recv = sems

    def side_copy(self):
        place = self.place
        return remote(
            self.rows,
            self.side_buf,
            self.send.at[0],
            self.recv.at[0],
            place.side,
        )

    def line_copy(self, hop):
        place = self.place
        chip = (place.chip + hop) % place.chips
        return remote(
            self.rows,
            self.line_buf.at[place.chip],
            self.send.at[hop],
            self.recv.at[hop],
            (place.dp, 2 * chip + place.core),
        )

    def line_landed(self, hop):
        place = self.place
        chip = (place.chip + place.chips - hop) % place.chips
        remote(
            self.rows,
            self.line_buf.at[chip],
            self.send.at[hop],
            self.recv.at[hop],
            (place.dp, 2 * chip + place.core),
        ).wait_recv()

    def square_copy(self, hop):
        place = self.place
        target = (place.dp + hop) % 4
        at = place.chips + hop
        return remote(
            self.rows,
            self.square_buf.at[place.dp],
            self.send.at[at],
            self.recv.at[at],
            (target, place.me),
        )

    def square_landed(self, hop):
        place = self.place
        source = (place.dp + 4 - hop) % 4
        at = place.chips + hop
        remote(
            self.rows,
            self.square_buf.at[source],
            self.send.at[at],
            self.recv.at[at],
            (source, place.me),
        ).wait_recv()

    def put(self, value):
        if self.alone < self.rows.shape[0]:
            index = lax.broadcasted_iota(jnp.int32, value.shape, 0)
            value = jnp.where(index < self.alone, value, self.rows[...])
        self.rows[...] = value

    def begin(self):
        self.side_copy().start()

    def middle(self):
        self.side_copy().wait()
        self.put(self.rows[...] + self.side_buf[...])
        self.line_buf[self.place.chip] = self.rows[...]
        for hop in range(1, self.place.chips):
            self.line_copy(hop).start()

    def late(self):
        place = self.place
        for hop in range(1, place.chips):
            self.line_copy(hop).wait_send()
            self.line_landed(hop)
        value = self.line_buf[0]
        for chip in range(1, place.chips):
            value = value + self.line_buf[chip]
        self.put(value)
        self.square_buf[place.dp] = self.rows[...]
        for hop in range(1, 4):
            self.square_copy(hop).start()

    def end(self):
        for hop in range(1, 4):
            self.square_copy(hop).wait_send()
            self.square_landed(hop)
        value = self.square_buf[0]
        for device in range(1, 4):
            value = value + self.square_buf[device]
        self.rows[...] = value


def small_scratch(chips, rows, width):
    dma = pltpu.SemaphoreType.DMA
    return [
        pltpu.VMEM((rows, width), jnp.float32),
        pltpu.VMEM((chips, rows, width), jnp.float32),
        pltpu.VMEM((4, rows, width), jnp.float32),
        dma((chips + 4,)),
        dma((chips + 4,)),
    ]


def scatter_scratch(chips, count, width):
    low = jnp.bfloat16
    dma = pltpu.SemaphoreType.DMA
    return [
        pltpu.VMEM((count, width), jnp.float32),
        pltpu.VMEM((chips, count, width), low),
        pltpu.VMEM((chips, count, width), low),
        pltpu.VMEM((chips + 1, count, width), low),
        dma((chips,)),
        dma((chips,)),
        dma((chips, 4)),
        dma((chips + 1, 4)),
    ]


def alive(shape, axis, start, bounds_ref):
    place = lax.broadcasted_iota(jnp.int32, shape, axis) + start
    return jnp.where((place >= bounds_ref[0]) & (place < bounds_ref[1]), 1.0, 0.0)


def by_rows(count, tile, action):
    def one(index, carry):
        action(pl.ds(pl.multiple_of(index * tile, tile), tile))
        return carry

    lax.fori_loop(0, count // tile, one, 0)


def attend_out_kernel(
    chips,
    mixed_hbm,
    bounds_ref,
    out_hbm,
    rows_hbm,
    branch_ref,
    gain_ref,
    shift_ref,
    bias_ref,
    up_ref,
    down_ref,
    attended_ref,
    lse_ref,
    resid_ref,
    normed_ref,
    branch_whole,
    up_whole,
    down_whole,
    mixed_ref,
    out_ref,
    rows_ref,
    fetch_sem,
    seg_col_ref,
    seg_row_ref,
    score_ref,
    blocks,
    line_send,
    line_recv,
    up_send,
    up_recv,
    down_send,
    down_recv,
    own_sem,
    keep_sem,
    *scatter,
):
    place = Place(chips)
    count = rows_ref.shape[0]
    fetched = fetch(
        [(mixed_hbm, mixed_ref), (out_hbm, out_ref), (rows_hbm, rows_ref)], fetch_sem
    )
    place.greet(True)

    def square(shard, whole, send, recv):
        half = shard.shape[0] // 2
        return SquareGather(
            place,
            shard,
            lambda owner: whole.at[owner],
            lambda owner, which: whole.at[owner, pl.ds(which * half, half)],
            send,
            recv,
        )

    up = square(up_ref, up_whole, up_send, up_recv)
    down = square(down_ref, down_whole, down_send, down_recv)
    up.begin()
    own = [
        pltpu.make_async_copy(up_ref, up_whole.at[place.dp], own_sem.at[0]),
        pltpu.make_async_copy(down_ref, down_whole.at[place.dp], own_sem.at[1]),
    ]
    own[0].start()
    own[1].start()

    def term(block, tile):
        span = pl.ds(pl.multiple_of(block * count, count), count)
        return jnp.dot(attended_ref[span, :], out_ref[tile], preferred_element_type=jnp.float32)

    def prepare(chip):
        def one(index, carry):
            attend_rows(
                chip * (2 * count // ATTEND_ROWS) + index,
                mixed_ref,
                seg_col_ref,
                seg_row_ref,
                attended_ref,
                lse_ref,
                score_ref,
            )
            return carry

        lax.fori_loop(0, 2 * count // ATTEND_ROWS, one, 0)

    def copy_in(span):
        blocks[place.me, span, :] = branch_ref[span, :]

    by_rows(count, 64, copy_in)
    line = LineGather(place, blocks, line_send, line_recv)
    line.begin()
    seg_row_ref[...] = alive(seg_row_ref.shape, 1, 0, bounds_ref)

    def column(span):
        seg_col_ref[span, :] = alive((64, 1), 0, span.start, bounds_ref)

    by_rows(seg_col_ref.shape[0], 64, column)
    for copy in fetched:
        copy.wait()
    sums = LineScatter(place, term, 4, scatter[:4], scatter[4:8], prepare)
    sums.begin()

    def keep(block, part):
        half = count // 2
        place_of = ((block // 2 * 2 + part) * 2 + block % 2) * half
        span = pl.ds(pl.multiple_of(place_of, half), half)
        source = blocks.at[block, pl.ds(part * half, half)]
        return pltpu.make_async_copy(source, branch_whole.at[span], keep_sem.at[block, part])

    def step(index, carry):
        sums.step(index, True)
        pl.when(index < chips - 1)(lambda: line.step(index + 1))

        @pl.when(index == 1)
        def _():
            up.middle()
            down.begin()

        pl.when(index == 2)(down.middle)
        return carry

    lax.fori_loop(0, chips, step, 0)
    total = scatter[0]

    def norm(span):
        resid = rows_ref[span, :].astype(jnp.float32) + total[span, :] + bias_ref[...]
        resid_ref[span, :] = resid
        normed_ref[span, :] = norm_rows(resid, gain_ref[...], shift_ref[...]).astype(jnp.bfloat16)

    by_rows(count, 64, norm)

    def store(block, carry):
        pl.when((block % 2 != place.core))(lambda: line.arrive(block // 2, block % 2))
        keep(block, 0).start()
        keep(block, 1).start()
        return carry

    lax.fori_loop(0, 2 * chips, store, 0)
    sums.finish()
    line.finish()
    up.end()
    down.end()
    up.finish()
    down.finish()
    own[0].wait()
    own[1].wait()

    def kept(block, carry):
        keep(block, 0).wait()
        keep(block, 1).wait()
        return carry

    lax.fori_loop(0, 2 * chips, kept, 0)


def attend_out_call(
    mixed, bounds, out_whole, rows, branch, gain, shift, bias, up, down, chips
):
    count, width = rows.shape
    local = mixed.shape[2]
    total = 2 * chips * count
    low = jnp.bfloat16
    vmem = pl.BlockSpec(memory_space=pltpu.VMEM)
    hbm = pl.BlockSpec(memory_space=pl.ANY)
    dma = pltpu.SemaphoreType.DMA
    return pl.pallas_call(
        functools.partial(attend_out_kernel, chips),
        out_shape=(
            jax.ShapeDtypeStruct((total, local), low),
            jax.ShapeDtypeStruct((total, 1 + local // HEAD_DIM), jnp.float32),
            jax.ShapeDtypeStruct((count, width), jnp.float32),
            jax.ShapeDtypeStruct((count, width), low),
            jax.ShapeDtypeStruct((total, width), low),
            jax.ShapeDtypeStruct((4,) + up.shape, low),
            jax.ShapeDtypeStruct((4,) + down.shape, low),
        ),
        in_specs=[hbm, pl.BlockSpec(memory_space=pltpu.SMEM), hbm, hbm] + [vmem] * 6,
        out_specs=(vmem, vmem, vmem, vmem, hbm, hbm, hbm),
        scratch_shapes=[
            pltpu.VMEM(mixed.shape, low),
            pltpu.VMEM(out_whole.shape, low),
            pltpu.VMEM(rows.shape, low),
            dma((3,)),
            pltpu.VMEM((total, 1), jnp.float32),
            pltpu.VMEM((1, total), jnp.float32),
            pltpu.VMEM((local // HEAD_DIM, ATTEND_ROWS, total), jnp.float32),
            pltpu.VMEM((2 * chips, count, width), low),
            dma((3, chips)),
            dma((2 * chips,)),
            dma((4,)),
            dma((4,)),
            dma((4,)),
            dma((4,)),
            dma((2,)),
            dma((2 * chips, 2)),
        ]
        + scatter_scratch(chips, count, width),
        compiler_params=pltpu.CompilerParams(
            collective_id=1, has_side_effects=True, vmem_limit_bytes=VMEM_LIMIT
        ),
        cost_estimate=pl.CostEstimate(flops=10**11, bytes_accessed=0, transcendentals=0),
        name="attend_out",
    )(mixed, bounds, out_whole, rows, branch, gain, shift, bias, up, down)


def input_back_kernel(
    chips,
    stacked_hbm,
    mix_hbm,
    rows_hbm,
    resid_grad_hbm,
    gain_ref,
    early_ref,
    hidden_hbm,
    out_grad_hbm,
    normed_one_ref,
    normed_two_ref,
    grad_ref,
    late_out_ref,
    early_out_ref,
    mix_grad_ref,
    up_grad_ref,
    out_owned_ref,
    stacked_ref,
    mix_ref,
    rows_ref,
    resid_grad_ref,
    hidden_ref,
    out_grad_ref,
    fetch_sem,
    columns_buf,
    columns_sem,
    *scatter,
):
    place = Place(chips)
    count = rows_ref.shape[0]
    fetched = fetch(
        [
            (stacked_hbm, stacked_ref),
            (mix_hbm, mix_ref),
            (hidden_hbm, hidden_ref),
            (out_grad_hbm, out_grad_ref),
            (rows_hbm, rows_ref),
            (resid_grad_hbm, resid_grad_ref),
        ],
        fetch_sem,
    )
    place.greet(True, True)
    fetched[0].wait()
    fetched[1].wait()
    early_out_ref[...] = early_ref[...]
    early = SmallSum(place, early_out_ref, 4, scatter[16:19], scatter[19:21])
    late = SmallSum(place, late_out_ref, late_out_ref.shape[0], scatter[21:24], scatter[24:26])

    def term(block, tile):
        span = pl.ds(pl.multiple_of(block * count, count), count)
        result = None
        for part in range(3):
            product = lax.dot_general(
                stacked_ref[part, span, :],
                mix_ref[part, tile],
                TURNED,
                preferred_element_type=jnp.float32,
            )
            result = product if result is None else result + product
        return result

    sums = LineScatter(place, term, 4, scatter[:4], scatter[4:8])
    sums.begin()
    early.begin()
    half_columns = columns_buf.shape[2]

    def load(which, owner, half):
        start = pl.multiple_of((2 * owner + half) * half_columns, half_columns)
        source = (normed_one_ref, normed_two_ref)[which]
        return pltpu.make_async_copy(
            source.at[:, pl.ds(start, half_columns)], columns_buf.at[which], columns_sem.at[which]
        )

    def mix_piece(owner, half):
        load(0, owner, half).wait()
        return jnp.stack(
            [
                lax.dot_general(
                    columns_buf[0],
                    stacked_ref[part],
                    CROSSED,
                    preferred_element_type=jnp.float32,
                )
                for part in range(3)
            ]
        )

    def up_piece(owner, half):
        load(1, owner, half).wait()
        return lax.dot_general(
            columns_buf[1], hidden_ref[...], CROSSED, preferred_element_type=jnp.float32
        )

    out_units = out_grad_ref.shape[0] // 2
    out_columns = out_grad_ref.shape[1] // 4

    def out_piece(owner, half):
        units = pl.ds(pl.multiple_of(half * out_units, out_units), out_units)
        columns = pl.ds(pl.multiple_of(owner * out_columns, 128), out_columns)
        return out_grad_ref[units, columns]

    out = SquareScatter(place, out_piece, out_owned_ref, scatter[26:28], scatter[28:30])
    mix = SquareScatter(place, mix_piece, mix_grad_ref, scatter[8:10], scatter[10:12])
    up = SquareScatter(place, up_piece, up_grad_ref, scatter[12:14], scatter[14:16])

    load(1, place.across, 0).start()
    load(0, place.across, 0).start()

    def stage(kind):
        def one(way, carry):
            for which, matrix in ((1, up), (0, mix)):
                matrix.one(kind, way)
                owner, half = matrix.following(kind, way)
                more = (way == 0) | (kind < 3)
                pl.when(more)(lambda: load(which, owner, half).start())
            out.one(kind, way)
            return carry

        lax.fori_loop(0, 2, one, 0)

    for copy in fetched[2:]:
        copy.wait()

    def step(index, carry):
        pl.when(index == 3)(lambda: stage(3))
        sums.step(index)
        for kind in range(3):

            @pl.when(index == kind)
            def _():
                stage(kind)
                if kind == 1:
                    early.middle()
                if kind == 2:
                    early.late()

        return carry

    lax.fori_loop(0, chips, step, 0)
    total = scatter[0]
    late_out_ref[...] = jnp.zeros_like(late_out_ref)

    def columns(span):
        one_grad = total[span, :]
        _, hat, _ = layer_norm_parts(rows_ref[span, :].astype(jnp.float32), gain_ref[...], 0.0)
        late_out_ref[0:1, :] += jnp.sum(one_grad * hat, axis=0, keepdims=True)
        late_out_ref[1:2, :] += jnp.sum(one_grad, axis=0, keepdims=True)

    def back(span):
        rows = rows_ref[span, :].astype(jnp.float32)
        _, hat, inverse = layer_norm_parts(rows, gain_ref[...], 0.0)
        grad_ref[span, :] = resid_grad_ref[span, :] + layer_norm_back(
            total[span, :], hat, inverse, gain_ref[...]
        )

    by_rows(count, 64, columns)
    late.begin()
    up.end()
    late.middle()
    by_rows(count, 64, back)
    late.late()
    early.end()
    mix.end()
    out.end()
    sums.finish()
    late.end()


def input_back_call(
    stacked, mix_whole, rows, resid_grad, gain, early, hidden, out_grad, normed_one, normed_two, chips
):
    count, width = rows.shape
    total, units = hidden.shape
    local = stacked.shape[2]
    half = width // 8
    vmem = pl.BlockSpec(memory_space=pltpu.VMEM)
    hbm = pl.BlockSpec(memory_space=pl.ANY)
    return pl.pallas_call(
        functools.partial(input_back_kernel, chips),
        out_shape=(
            jax.ShapeDtypeStruct((count, width), jnp.float32),
            jax.ShapeDtypeStruct((2, width), jnp.float32),
            jax.ShapeDtypeStruct(early.shape, jnp.float32),
            jax.ShapeDtypeStruct((2, 3, half, local), jnp.float32),
            jax.ShapeDtypeStruct((2, half, units), jnp.float32),
            jax.ShapeDtypeStruct((2, local // 2, width // 4), jnp.float32),
        ),
        in_specs=[hbm] * 4 + [vmem] * 2 + [hbm] * 4,
        out_specs=(vmem,) * 6,
        scratch_shapes=[
            pltpu.VMEM(stacked.shape, jnp.bfloat16),
            pltpu.VMEM(mix_whole.shape, jnp.bfloat16),
            pltpu.VMEM(rows.shape, jnp.bfloat16),
            pltpu.VMEM(resid_grad.shape, jnp.float32),
            pltpu.VMEM(hidden.shape, jnp.bfloat16),
            pltpu.VMEM(out_grad.shape, jnp.float32),
            pltpu.SemaphoreType.DMA((6,)),
            pltpu.VMEM((2, total, half), jnp.bfloat16),
            pltpu.SemaphoreType.DMA((2,)),
        ]
        + scatter_scratch(chips, count, width)
        + square_scratch((3, half, local))
        + square_scratch((half, units))
        + small_scratch(chips, early.shape[0], width)
        + small_scratch(chips, 2, width)
        + square_scratch((local // 2, width // 4)),
        compiler_params=pltpu.CompilerParams(
            collective_id=2, has_side_effects=True, vmem_limit_bytes=VMEM_LIMIT
        ),
        cost_estimate=pl.CostEstimate(flops=10**11, bytes_accessed=0, transcendentals=0),
        name="input_back",
    )(stacked, mix_whole, rows, resid_grad, gain, early, hidden, out_grad, normed_one, normed_two)


GELU_SLOPE = 0.7978845608028654
GELU_CUBE = 0.044715


def gelu_parts(hidden):
    square = hidden * hidden
    bend = jnp.tanh(GELU_SLOPE * hidden * (1.0 + GELU_CUBE * square))
    lift = 0.5 * (1.0 + bend)
    slope = lift + 0.5 * hidden * (1.0 - bend * bend) * (
        GELU_SLOPE * (1.0 + 3.0 * GELU_CUBE * square)
    )
    return hidden * lift, slope


def feed_kernel(
    chips,
    parts,
    normed_ref,
    branch_ref,
    up_hbm,
    down_hbm,
    bias_ref,
    resid_hbm,
    own_branch_hbm,
    gain_ref,
    normed_whole,
    active_hbm,
    hidden_hbm,
    grad_ref,
    grad_low_ref,
    sums_ref,
    bias_grad_ref,
    up_ref,
    down_ref,
    resid_ref,
    own_branch_ref,
    active_ref,
    hidden_ref,
    fetch_sem,
    emit_sem,
    blocks,
    branch_buf,
    work,
    hold,
    side_out,
    side_in,
    line_in,
    line_send,
    line_recv,
    keep_sem,
    load_sem,
    side_send,
    side_recv,
    out_send,
    out_recv,
):
    place = Place(chips)
    count = normed_ref.shape[0]
    rows = count // parts
    pair = 2 * rows
    last = chips - 1
    fetched = fetch(
        [
            (up_hbm, up_ref),
            (down_hbm, down_ref),
            (resid_hbm, resid_ref),
            (own_branch_hbm, own_branch_ref),
        ],
        fetch_sem,
    )
    place.greet(False)

    def fill(part, carry):
        block = 2 * (place.chip * parts + part) + place.core
        blocks[block] = normed_ref[pl.ds(pl.multiple_of(part * rows, rows), rows), :]
        return carry

    lax.fori_loop(0, parts, fill, 0)
    line = LineGather(place, blocks, line_send, line_recv, parts)
    line.begin_part(0)
    line.copy(2, place.chip, 1).start()
    pl.when(place.has_up & jnp.logical_not(place.has_down))(
        lambda: line.copy(0, place.chip, 1).start()
    )
    pl.when(place.has_down & jnp.logical_not(place.has_up))(
        lambda: line.copy(1, place.chip, 1).start()
    )
    bias_grad_ref[...] = jnp.zeros_like(bias_grad_ref)

    def piece_span(piece):
        return pl.ds(pl.multiple_of(piece * pair, pair), pair)

    def load(piece, slot):
        return pltpu.make_async_copy(
            branch_ref.at[piece_span(piece)], branch_buf.at[slot], load_sem.at[slot]
        )

    def keep(piece, core):
        span = pl.ds(pl.multiple_of(piece * pair + core * rows, rows), rows)
        return pltpu.make_async_copy(
            blocks.at[2 * piece + core], normed_whole.at[span], keep_sem.at[piece, core]
        )

    def side_copy(piece):
        return remote(
            side_out.at[piece],
            side_in.at[piece],
            side_send.at[piece],
            side_recv.at[piece],
            place.side,
        )

    chunk = normed_ref.shape[1] // 4

    def line_copy(way, chip, part, tile):
        piece = chip * parts + part
        next_chip = place.chip + 1 - 2 * way
        slot = jnp.where((way == 1) & (chip == next_chip), chips * parts + part, piece)
        span = slice(tile * chunk, (tile + 1) * chunk)
        return remote(
            line_in.at[piece, :, span],
            line_in.at[slot, :, span],
            out_send.at[piece, tile],
            out_recv.at[slot, tile],
            (place.up, place.down)[way],
        )

    def line_landed(way, chip, part, tile):
        piece = chip * parts + part
        slot = jnp.where((way == 1) & (chip == place.chip), chips * parts + part, piece)
        span = slice(tile * chunk, (tile + 1) * chunk)
        remote(
            line_in.at[slot, :, span],
            line_in.at[slot, :, span],
            out_send.at[piece, tile],
            out_recv.at[slot, tile],
            (place.up, place.down)[way],
        ).wait_recv()
        return slot

    def emit(piece):
        span = piece_span(piece)
        return [
            pltpu.make_async_copy(active_ref.at[span], active_hbm.at[span], emit_sem.at[piece, 0]),
            pltpu.make_async_copy(hidden_ref.at[span], hidden_hbm.at[span], emit_sem.at[piece, 1]),
        ]

    width = 512
    tiles = up_ref.shape[2] // width

    def compute(chip, part, side):
        piece = chip * parts + part
        keep(piece, 0).start()
        keep(piece, 1).start()
        span = piece_span(piece)
        own_rows = blocks[pl.ds(2 * piece, 2)].reshape(pair, -1)
        load(piece, side).wait()

        def tile(index, carry):
            units = pl.ds(pl.multiple_of(index * width, width), width)
            hidden = jnp.dot(
                own_rows,
                up_ref[:, :, units].reshape(-1, width),
                preferred_element_type=jnp.float32,
            )
            active, slope = gelu_parts(hidden + bias_ref[:, units])
            active_ref[span, units] = active.astype(jnp.bfloat16)
            grad = None
            for owner in range(4):
                columns = down_ref.shape[2]
                product = lax.dot_general(
                    branch_buf[side, :, owner * columns : (owner + 1) * columns],
                    down_ref[owner, units, :],
                    TURNED,
                    preferred_element_type=jnp.float32,
                )
                grad = product if grad is None else grad + product
            low = (grad * slope).astype(jnp.bfloat16)
            hidden_ref[span, units] = low
            bias_grad_ref[:, units] += jnp.sum(low.astype(jnp.float32), axis=0, keepdims=True)
            return carry

        lax.fori_loop(0, tiles, tile, 0)
        low = hidden_ref[span, :]
        depth = up_ref.shape[1]
        for owner in range(4):
            columns = slice(owner * depth, (owner + 1) * depth)
            product = lax.dot_general(
                low, up_ref[owner], TURNED, preferred_element_type=jnp.float32
            )
            work[:, :, columns] = product.reshape(2, rows, depth)
        side_out[piece] = work[1 - place.core].astype(jnp.bfloat16)
        side_copy(piece).start()
        hold[piece] = work[place.core]
        for copy in emit(piece):
            copy.start()

    def pass_on(way, chip, part):
        piece = chip * parts + part
        side_copy(piece).wait_recv()
        behind = (place.has_down, place.has_up)[way]
        for tile in range(4):
            span = slice(tile * chunk, (tile + 1) * chunk)
            total = hold[piece, :, span] + side_in[piece, :, span].astype(jnp.float32)

            @pl.when(behind)
            def _():
                slot = line_landed(way, chip, part, tile)
                line_in[piece, :, span] = (
                    total + line_in[slot, :, span].astype(jnp.float32)
                ).astype(jnp.bfloat16)

            @pl.when(jnp.logical_not(behind))
            def _():
                line_in[piece, :, span] = total.astype(jnp.bfloat16)

            line_copy(way, chip, part, tile).start()

    def coming(index, side):
        count_beyond = jnp.where(side == 0, place.chip, last - place.chip)
        early = index <= count_beyond
        distance = jnp.where(early, index, 2 * count_beyond + 1 - index)
        valid = (index == 0) | (index <= 2 * count_beyond)
        chip = jnp.where(index == 0, place.chip, place.chip + distance * (2 * side - 1))
        part = jnp.where(index == 0, side, jnp.where(early, 0, 1))
        return valid, chip, part, count_beyond

    def turn(index, carry):
        def ahead(side, inner):
            valid, chip, part, _ = coming(index, side)
            pl.when(valid)(lambda: load(chip * parts + part, side).start())
            return inner

        lax.fori_loop(0, 2, ahead, 0)

        @pl.when(index > 0)
        def _():
            for side in range(2):
                valid, chip, part, count_beyond = coming(index, side)
                onward = (place.has_up, place.has_down)[side]

                @pl.when(valid)
                def _():
                    line.arrive(chip, place.core, part)
                    pl.when(onward)(lambda: line.copy(side, chip, part).start())
                    pl.when(onward & (index == 2 * count_beyond))(
                        lambda: line.copy(side, place.chip, 1).start()
                    )
                    line.copy(2, chip, part).start()

        def one(side, inner):
            valid, chip, part, _ = coming(index, side)

            @pl.when(valid)
            def _():
                line.arrive(chip, 1 - place.core, part)
                compute(chip, part, side)

            return inner

        lax.fori_loop(0, 2, one, 0)
        mirrored = last - place.chip
        for part in range(2):
            reach = index - place.chip if part == 0 else 2 * last + 1 + place.chip - index

            @pl.when((reach > place.chip) & (reach < chips))
            def _():
                pass_on(0, reach, part)

            back = index - mirrored if part == 0 else 2 * last + 1 + mirrored - index

            @pl.when((back > mirrored) & (back < chips))
            def _():
                pass_on(1, last - back, part)

        return carry

    fetched[0].wait()
    fetched[1].wait()
    lax.fori_loop(0, 2 * last + 1, turn, 0)
    sums_ref[...] = jnp.zeros_like(sums_ref)
    fetched[2].wait()
    fetched[3].wait()

    def own_part(part, carry):
        piece = place.chip * parts + part
        side_copy(piece).wait_recv()
        hold[piece] += side_in[piece].astype(jnp.float32)

        for tile in range(4):

            @pl.when(place.has_down)
            def _():
                line_landed(0, place.chip, part, tile)

            @pl.when(place.has_up)
            def _():
                line_landed(1, place.chip, part, tile)

        pieces_end = chips * parts

        @pl.when(place.has_down)
        def _():
            hold[piece] += line_in[piece].astype(jnp.float32)

        @pl.when(place.has_up)
        def _():
            hold[piece] += line_in[pieces_end + part].astype(jnp.float32)

        tile = 64

        def back(index, inner):
            here = pl.ds(pl.multiple_of(index * tile, tile), tile)
            span = pl.ds(pl.multiple_of(part * rows + index * tile, tile), tile)
            two_grad = hold[piece, here, :]
            _, hat, inverse = layer_norm_parts(resid_ref[span, :], gain_ref[...], 0.0)
            grad = own_branch_ref[span, :].astype(jnp.float32) + layer_norm_back(
                two_grad, hat, inverse, gain_ref[...]
            )
            grad_ref[span, :] = grad
            grad_low_ref[span, :] = grad.astype(jnp.bfloat16)
            sums_ref[0:1, :] += jnp.sum(two_grad * hat, axis=0, keepdims=True)
            sums_ref[1:2, :] += jnp.sum(two_grad, axis=0, keepdims=True)
            sums_ref[2:3, :] += jnp.sum(grad, axis=0, keepdims=True)
            return inner

        lax.fori_loop(0, rows // tile, back, 0)
        return carry

    lax.fori_loop(0, parts, own_part, 0)
    line.finish()

    def drain(piece, carry):
        side_copy(piece).wait_send()
        keep(piece, 0).wait()
        keep(piece, 1).wait()
        for copy in emit(piece):
            copy.wait()
        for tile in range(4):
            pl.when(piece // parts != place.chip)(
                lambda: line_copy(0, piece // parts, piece % parts, tile).wait_send()
            )
        return carry

    lax.fori_loop(0, chips * parts, drain, 0)


def feed_call(normed, branch, up_whole, down_whole, bias, resid, own_branch, gain, chips):
    count, width = normed.shape
    total = 2 * chips * count
    units = up_whole.shape[2]
    parts = 2
    rows = count // parts
    low = jnp.bfloat16
    vmem = pl.BlockSpec(memory_space=pltpu.VMEM)
    hbm = pl.BlockSpec(memory_space=pl.ANY)
    dma = pltpu.SemaphoreType.DMA
    pieces = chips * parts
    return pl.pallas_call(
        functools.partial(feed_kernel, chips, parts),
        out_shape=(
            jax.ShapeDtypeStruct((total, width), low),
            jax.ShapeDtypeStruct((total, units), low),
            jax.ShapeDtypeStruct((total, units), low),
            jax.ShapeDtypeStruct((count, width), jnp.float32),
            jax.ShapeDtypeStruct((count, width), low),
            jax.ShapeDtypeStruct((3, width), jnp.float32),
            jax.ShapeDtypeStruct((1, units), jnp.float32),
        ),
        in_specs=[vmem, hbm, hbm, hbm, vmem, hbm, hbm, vmem],
        out_specs=(hbm,) * 3 + (vmem,) * 4,
        scratch_shapes=[
            pltpu.VMEM(up_whole.shape, low),
            pltpu.VMEM(down_whole.shape, low),
            pltpu.VMEM(resid.shape, jnp.float32),
            pltpu.VMEM(own_branch.shape, low),
            pltpu.VMEM((total, units), low),
            pltpu.VMEM((total, units), low),
            dma((4,)),
            dma((pieces, 2)),
            pltpu.VMEM((2 * pieces, rows, width), low),
            pltpu.VMEM((2, 2 * rows, width), low),
            pltpu.VMEM((2, rows, width), jnp.float32),
            pltpu.VMEM((pieces, rows, width), jnp.float32),
            pltpu.VMEM((pieces, rows, width), low),
            pltpu.VMEM((pieces, rows, width), low),
            pltpu.VMEM((pieces + parts, rows, width), low),
            dma((3, pieces)),
            dma((2 * pieces,)),
            dma((pieces, 2)),
            dma((2,)),
            dma((pieces,)),
            dma((pieces,)),
            dma((pieces, 4)),
            dma((pieces + parts, 4)),
        ],
        compiler_params=pltpu.CompilerParams(
            collective_id=3, has_side_effects=True, vmem_limit_bytes=VMEM_LIMIT
        ),
        cost_estimate=pl.CostEstimate(flops=10**11, bytes_accessed=0, transcendentals=0),
        name="feed",
    )(normed, branch, up_whole, down_whole, bias, resid, own_branch, gain)


def branch_back_kernel(
    chips,
    parts,
    branch_ref,
    active_hbm,
    down_hbm,
    attended_hbm,
    out_hbm,
    shift_ref,
    bounds_ref,
    mixed_hbm,
    aux_hbm,
    resid_ref,
    cotangent_ref,
    stacked_ref,
    bias_sum_ref,
    down_grad_ref,
    out_grad_ref,
    output_ref,
    blocks,
    active_ref,
    down_ref,
    attended_ref,
    out_ref,
    mixed_ref,
    aux_ref,
    fetch_sem,
    seg_row_ref,
    block_buf,
    columns_buf,
    resid_buf,
    key_sum,
    value_sum,
    line_send,
    line_recv,
    columns_sem,
    block_sem,
    *scatter,
):
    place = Place(chips)
    count = branch_ref.shape[0]
    rows = count // parts
    fetched = fetch(
        [
            (active_hbm, active_ref),
            (down_hbm, down_ref),
            (attended_hbm, attended_ref),
            (out_hbm, out_ref),
            (mixed_hbm, mixed_ref),
            (aux_hbm, aux_ref),
        ],
        fetch_sem,
    )
    place.greet(True)
    line = LineGather(place, blocks, line_send, line_recv, 1, branch_ref)
    line.begin()

    def term(block, tile):
        chip, core = block // 2, block % 2
        taken = []
        for part in range(parts):
            start = ((chip * parts + part) * 2 + core) * rows
            taken.append(active_ref[pl.ds(pl.multiple_of(start, rows), rows), :])
        return jnp.dot(
            jnp.concatenate(taken, axis=0), down_ref[tile], preferred_element_type=jnp.float32
        )

    fetched[0].wait()
    fetched[1].wait()
    sums = LineScatter(place, term, 4, scatter[:4], scatter[4:8])
    sums.begin()
    seg_row_ref[...] = alive(seg_row_ref.shape, 1, 0, bounds_ref)
    out_grad_ref[...] = jnp.zeros_like(out_grad_ref)
    key_sum[...] = jnp.zeros_like(key_sum)
    value_sum[...] = jnp.zeros_like(value_sum)
    bias_sum_ref[...] = jnp.zeros_like(bias_sum_ref)
    down_units = down_ref.shape[1] // 2
    down_columns = down_ref.shape[2]

    def load_columns(owner):
        return pltpu.make_async_copy(
            cotangent_ref.at[:, pl.ds(pl.multiple_of(owner * down_columns, 128), down_columns)],
            columns_buf,
            columns_sem,
        )

    load_columns(place.across).start()

    def down_piece(owner, half):
        units = pl.ds(pl.multiple_of(half * down_units, down_units), down_units)
        return lax.dot_general(
            active_ref[:, units], columns_buf[...], CROSSED, preferred_element_type=jnp.float32
        )

    down = SquareScatter(place, down_piece, down_grad_ref, scatter[8:10], scatter[10:12])
    def down_stage(kind):
        def one(way, carry):
            fresh = (way == 0) if kind in (0, 3) else ((way >= 0) if kind == 1 else (way == 1))
            pl.when(fresh)(lambda: load_columns(place.dp).wait())
            down.one(kind, way)
            owner, _ = down.following(kind, way)
            more = (way == 1) if kind == 0 else ((way == 0) if kind == 1 else (way >= 0))
            if kind < 3:
                pl.when(more)(lambda: load_columns(owner).start())
            return carry

        lax.fori_loop(0, 2, one, 0)

    def load_part(source, owner):
        columns = out_ref.shape[2]
        span = slice(owner * columns, (owner + 1) * columns)
        return pltpu.make_async_copy(source.at[:, span], block_buf.at[:, span], block_sem.at[owner])

    def load_block(block):
        mine = block == place.me

        @pl.when(mine)
        def _():
            for owner in range(4):
                load_part(branch_ref, owner).start()

        @pl.when(jnp.logical_not(mine))
        def _():
            for owner in range(4):
                load_part(blocks.at[block], owner).start()

    def take(block):
        span = pl.ds(pl.multiple_of(block * count, count), count)
        columns = out_ref.shape[2]
        load_block(block)
        result = None
        for owner in range(4):
            load_part(branch_ref, owner).wait()
            here = block_buf[:, owner * columns : (owner + 1) * columns]
            product = lax.dot_general(
                here, out_ref[owner], TURNED, preferred_element_type=jnp.float32
            )
            result = product if result is None else result + product
            out_grad_ref[:, owner * columns : (owner + 1) * columns] += lax.dot_general(
                attended_ref[span, :], here, CROSSED, preferred_element_type=jnp.float32
            )
        grad = result.astype(jnp.bfloat16)
        attend_back_rows(
            block,
            grad,
            attended_ref,
            mixed_ref,
            aux_ref,
            seg_row_ref,
            stacked_ref,
            key_sum,
            value_sum,
            bias_sum_ref,
        )

    for copy in fetched[2:]:
        copy.wait()

    def step(index, carry):
        def one(side, inner):
            chip = place.chip + index * (2 * (side % 2) - 1)
            core = (place.core + side // 2) % 2

            @pl.when((chip >= 0) & (chip < chips) & ((index > 0) | (side % 2 == 0)))
            def _():
                pl.when(side >= 2)(lambda: line.arrive(chip, core))
                take(2 * chip + core)

            return inner

        lax.fori_loop(0, 4, one, 0)
        for kind in range(4):
            pl.when(index == kind)(lambda: down_stage(kind))
        pl.when(index < chips - 1)(lambda: line.step(index + 1))
        sums.step(index)
        return carry

    lax.fori_loop(0, chips, step, 0)
    resid = pltpu.make_async_copy(resid_ref, resid_buf, columns_sem)
    resid.start()
    stacked_ref[1] = (key_sum[...] * HEAD_DIM ** (-0.5)).astype(jnp.bfloat16)
    value_grad = value_sum[...].astype(jnp.bfloat16)
    stacked_ref[2] = value_grad
    bias_sum_ref[1:2, :] = jnp.sum(value_grad.astype(jnp.float32), axis=0, keepdims=True)
    down.end()
    total = scatter[0]
    resid.wait()

    def emit(span):
        result = resid_buf[span, :] + total[span, :] + shift_ref[...]
        live = alive((64, 1), 0, place.me * count + span.start, bounds_ref)
        output_ref[span, :] = jnp.where(live > 0, result, 0.0).astype(jnp.bfloat16)

    by_rows(count, 64, emit)
    sums.finish()
    line.finish()


def branch_back_call(
    branch,
    active,
    down_whole,
    attended,
    out_whole,
    shift,
    bounds,
    mixed,
    aux,
    resid,
    cotangent,
    chips,
):
    count, width = branch.shape
    total, local = attended.shape
    _, units, columns = down_whole.shape
    low = jnp.bfloat16
    vmem = pl.BlockSpec(memory_space=pltpu.VMEM)
    hbm = pl.BlockSpec(memory_space=pl.ANY)
    dma = pltpu.SemaphoreType.DMA
    return pl.pallas_call(
        functools.partial(branch_back_kernel, chips, 2),
        out_shape=(
            jax.ShapeDtypeStruct((3, total, local), low),
            jax.ShapeDtypeStruct((2, local), jnp.float32),
            jax.ShapeDtypeStruct((2, units // 2, columns), jnp.float32),
            jax.ShapeDtypeStruct((local, width), jnp.float32),
            jax.ShapeDtypeStruct((count, width), low),
            jax.ShapeDtypeStruct((2 * chips, count, width), low),
        ),
        in_specs=[hbm] * 5 + [vmem, pl.BlockSpec(memory_space=pltpu.SMEM)] + [hbm] * 4,
        out_specs=(vmem,) * 5 + (hbm,),
        scratch_shapes=[
            pltpu.VMEM(active.shape, low),
            pltpu.VMEM(down_whole.shape, low),
            pltpu.VMEM(attended.shape, low),
            pltpu.VMEM(out_whole.shape, low),
            pltpu.VMEM(mixed.shape, low),
            pltpu.VMEM(aux.shape, jnp.float32),
            dma((6,)),
            pltpu.VMEM((1, total), jnp.float32),
            pltpu.VMEM((count, width), low),
            pltpu.VMEM((total, columns), low),
            pltpu.VMEM((count, width), jnp.float32),
            pltpu.VMEM((total, local), jnp.float32),
            pltpu.VMEM((total, local), jnp.float32),
            dma((3, chips)),
            dma((2 * chips,)),
            dma,
            dma((4,)),
        ]
        + scatter_scratch(chips, count, width)
        + square_scratch((units // 2, columns)),
        compiler_params=pltpu.CompilerParams(
            collective_id=4, has_side_effects=True, vmem_limit_bytes=VMEM_LIMIT
        ),
        cost_estimate=pl.CostEstimate(flops=10**11, bytes_accessed=0, transcendentals=0),
        name="branch_back",
    )(
        branch,
        active,
        down_whole,
        attended,
        out_whole,
        shift,
        bounds,
        mixed,
        aux,
        resid,
        cotangent,
    )


ATTEND_ROWS = 256
ATTEND_KEYS = 512


def tile_mask(row_block, key_block, seg_col_ref, seg_row_ref):
    rows = lax.broadcasted_iota(jnp.int32, (ATTEND_ROWS, ATTEND_KEYS), 0)
    keys = lax.broadcasted_iota(jnp.int32, (ATTEND_ROWS, ATTEND_KEYS), 1)
    causal = keys - rows <= row_block * ATTEND_ROWS - key_block * ATTEND_KEYS
    row_span = pl.ds(pl.multiple_of(row_block * ATTEND_ROWS, ATTEND_ROWS), ATTEND_ROWS)
    key_span = pl.ds(pl.multiple_of(key_block * ATTEND_KEYS, ATTEND_KEYS), ATTEND_KEYS)
    return causal & (seg_col_ref[row_span, 0:1] == seg_row_ref[:, key_span])


def attend_rows(
    row_block, mixed_ref, seg_col_ref, seg_row_ref, attended_ref, lse_ref, score_ref
):
    scale = HEAD_DIM ** (-0.5)
    heads = range(mixed_ref.shape[2] // HEAD_DIM)
    lanes = [slice(head * HEAD_DIM, (head + 1) * HEAD_DIM) for head in heads]
    row_span = pl.ds(pl.multiple_of(row_block * ATTEND_ROWS, ATTEND_ROWS), ATTEND_ROWS)
    count = (row_block * ATTEND_ROWS) // ATTEND_KEYS + 1
    queries = [mixed_ref[0, row_span, lanes[head]] for head in heads]

    def span_of(key_block):
        return pl.ds(pl.multiple_of(key_block * ATTEND_KEYS, ATTEND_KEYS), ATTEND_KEYS)

    def score(key_block, peaks):
        key_span = span_of(key_block)
        mask = tile_mask(row_block, key_block, seg_col_ref, seg_row_ref)
        results = []
        for head in heads:
            scores = lax.dot_general(
                queries[head],
                mixed_ref[1, key_span, lanes[head]],
                TURNED,
                preferred_element_type=jnp.float32,
            )
            scores = jnp.where(mask, scores * scale, MASK_FILL)
            score_ref[head, :, key_span] = scores
            peak = peaks[head]
            for part in range(ATTEND_KEYS // 128):
                peak = jnp.maximum(peak, scores[:, part * 128 : (part + 1) * 128])
            results.append(peak)
        return tuple(results)

    filled = jnp.full((ATTEND_ROWS, 128), MASK_FILL, jnp.float32)
    peaks = lax.fori_loop(0, count, score, (filled,) * len(heads))
    peaks = [jnp.max(peak, axis=1, keepdims=True) for peak in peaks]

    def weigh(key_block, masses):
        key_span = span_of(key_block)
        results = []
        for head in heads:
            weights = jnp.exp(score_ref[head, :, key_span] - peaks[head])
            score_ref[head, :, key_span] = weights
            mass = masses[head]
            for part in range(ATTEND_KEYS // 128):
                mass = mass + weights[:, part * 128 : (part + 1) * 128]
            results.append(mass)
        return tuple(results)

    nothing = jnp.zeros((ATTEND_ROWS, 128), jnp.float32)
    masses = lax.fori_loop(0, count, weigh, (nothing,) * len(heads))
    masses = [jnp.sum(mass, axis=1, keepdims=True) for mass in masses]
    inverses = [1.0 / mass for mass in masses]
    lse_ref[row_span, 0:1] = seg_col_ref[row_span, :]
    for head in heads:
        lse_ref[row_span, head + 1 : head + 2] = peaks[head] + jnp.log(masses[head])

    def gather(key_block, totals):
        key_span = span_of(key_block)
        results = []
        for head in heads:
            probs = (score_ref[head, :, key_span] * inverses[head]).astype(jnp.bfloat16)
            results.append(
                totals[head]
                + jnp.dot(
                    probs,
                    mixed_ref[2, key_span, lanes[head]],
                    preferred_element_type=jnp.float32,
                )
            )
        return tuple(results)

    empty = jnp.zeros((ATTEND_ROWS, HEAD_DIM), jnp.float32)
    totals = lax.fori_loop(0, count, gather, (empty,) * len(heads))
    for head in heads:
        attended_ref[row_span, lanes[head]] = totals[head].astype(jnp.bfloat16)


def attend_back_rows(
    row_block,
    grads,
    attended_ref,
    mixed_ref,
    aux_ref,
    seg_row_ref,
    stacked_ref,
    key_sum,
    value_sum,
    bias_sum,
):
    scale = HEAD_DIM ** (-0.5)
    row_span = pl.ds(pl.multiple_of(row_block * ATTEND_ROWS, ATTEND_ROWS), ATTEND_ROWS)
    count = (row_block * ATTEND_ROWS) // ATTEND_KEYS + 1
    row_live = seg_row_ref[:, row_span]
    heads = []
    for head in range(mixed_ref.shape[2] // HEAD_DIM):
        lanes = slice(head * HEAD_DIM, (head + 1) * HEAD_DIM)
        grad = grads[:, lanes]
        product = grad.astype(jnp.float32) * attended_ref[row_span, lanes].astype(jnp.float32)
        delta = jnp.sum(product, axis=1, keepdims=True).reshape(1, ATTEND_ROWS)
        lse = aux_ref[row_span, head + 1 : head + 2].reshape(1, ATTEND_ROWS)
        heads.append((lanes, mixed_ref[0, row_span, lanes], grad, lse, delta))

    def one(key_block, totals):
        key_span = pl.ds(pl.multiple_of(key_block * ATTEND_KEYS, ATTEND_KEYS), ATTEND_KEYS)
        keys = lax.broadcasted_iota(jnp.int32, (ATTEND_KEYS, ATTEND_ROWS), 0)
        rows = lax.broadcasted_iota(jnp.int32, (ATTEND_KEYS, ATTEND_ROWS), 1)
        allowed = (keys - rows <= row_block * ATTEND_ROWS - key_block * ATTEND_KEYS) & (
            aux_ref[key_span, 0:1] == row_live
        )
        results = []
        for (lanes, query, grad, lse, delta), total in zip(heads, totals):
            key = mixed_ref[1, key_span, lanes]
            scores = lax.dot_general(key, query, TURNED, preferred_element_type=jnp.float32)
            flow = lax.dot_general(
                mixed_ref[2, key_span, lanes], grad, TURNED, preferred_element_type=jnp.float32
            )
            probs = jnp.exp(jnp.where(allowed, scores * scale, MASK_FILL) - lse)
            value_sum[key_span, lanes] += jnp.dot(
                probs.astype(jnp.bfloat16), grad, preferred_element_type=jnp.float32
            )
            low = (probs * (flow - delta)).astype(jnp.bfloat16)
            key_sum[key_span, lanes] += jnp.dot(low, query, preferred_element_type=jnp.float32)
            results.append(
                total + lax.dot_general(low, key, CROSSED, preferred_element_type=jnp.float32)
            )
        return tuple(results)

    totals = lax.fori_loop(
        0, count, one, (jnp.zeros((ATTEND_ROWS, HEAD_DIM), jnp.float32),) * len(heads)
    )
    for (lanes, _, _, _, _), total in zip(heads, totals):
        query_grad = (total * scale).astype(jnp.bfloat16)
        stacked_ref[0, row_span, lanes] = query_grad
        bias_sum[0:1, lanes] += jnp.sum(query_grad.astype(jnp.float32), axis=0, keepdims=True)


def tile_scores(query_tile, keys, segment, row_block, col_block):
    key_tile = keys[col_block * BLOCK : (col_block + 1) * BLOCK]
    scale = query_tile.shape[2] ** (-0.5)
    scores = (
        jnp.einsum("qhe,khe->hqk", query_tile, key_tile, preferred_element_type=jnp.float32) * scale
    )
    row_place = row_block * BLOCK + jnp.arange(BLOCK)
    key_place = col_block * BLOCK + jnp.arange(BLOCK)
    row_segment = segment[row_block * BLOCK : (row_block + 1) * BLOCK]
    key_segment = segment[col_block * BLOCK : (col_block + 1) * BLOCK]
    allowed = (key_place[None, :] <= row_place[:, None]) & (
        row_segment[:, None] == key_segment[None, :]
    )
    return (jnp.where(allowed[None], scores, MASK_FILL), allowed)


def attention_forward(queries, keys, values, segment):
    count = queries.shape[0] // BLOCK
    heads = queries.shape[1]
    depth = queries.shape[2]
    outputs = []
    totals = []
    for row_block in range(count):
        query_tile = queries[row_block * BLOCK : (row_block + 1) * BLOCK]
        peak = jnp.full((heads, BLOCK), MASK_FILL, jnp.float32)
        mass = jnp.zeros((heads, BLOCK), jnp.float32)
        for col_block in range(row_block + 1):
            scores, allowed = tile_scores(query_tile, keys, segment, row_block, col_block)
            new_peak = jnp.maximum(peak, jnp.max(scores, axis=-1))
            weights = jnp.where(allowed[None], jnp.exp(scores - new_peak[:, :, None]), 0.0)
            mass = mass * jnp.exp(peak - new_peak) + jnp.sum(weights, axis=-1)
            peak = new_peak
        total = peak + jnp.log(mass)
        gathered = jnp.zeros((BLOCK, heads, depth), jnp.float32)
        for col_block in range(row_block + 1):
            scores, allowed = tile_scores(query_tile, keys, segment, row_block, col_block)
            probs = jnp.where(allowed[None], jnp.exp(scores - total[:, :, None]), 0.0).astype(
                jnp.bfloat16
            )
            value_tile = values[col_block * BLOCK : (col_block + 1) * BLOCK]
            gathered = gathered + jnp.einsum(
                "hqk,khe->qhe", probs, value_tile, preferred_element_type=jnp.float32
            )
        outputs.append(gathered.astype(jnp.bfloat16))
        totals.append(total)
    return (jnp.concatenate(outputs, axis=0), jnp.concatenate(totals, axis=1))


def attention_backward(queries, keys, values, segment, totals, grads):
    count = queries.shape[0] // BLOCK
    heads = queries.shape[1]
    depth = queries.shape[2]
    scale = depth ** (-0.5)
    key_grads = [jnp.zeros((BLOCK, heads, depth), jnp.float32) for index in range(count)]
    value_grads = [jnp.zeros((BLOCK, heads, depth), jnp.float32) for index in range(count)]
    query_grads = []
    for row_block in range(count):
        query_tile = queries[row_block * BLOCK : (row_block + 1) * BLOCK]
        grad_tile = grads[row_block * BLOCK : (row_block + 1) * BLOCK]
        total = totals[:, row_block * BLOCK : (row_block + 1) * BLOCK]
        flows = jnp.zeros((heads, BLOCK), jnp.float32)
        for col_block in range(row_block + 1):
            scores, allowed = tile_scores(query_tile, keys, segment, row_block, col_block)
            probs = jnp.where(allowed[None], jnp.exp(scores - total[:, :, None]), 0.0)
            value_tile = values[col_block * BLOCK : (col_block + 1) * BLOCK]
            prob_grad = jnp.einsum(
                "qhe,khe->hqk", grad_tile, value_tile, preferred_element_type=jnp.float32
            )
            flows = flows + jnp.sum(prob_grad * probs, axis=-1)
            value_grads[col_block] = value_grads[col_block] + jnp.einsum(
                "hqk,qhe->khe",
                probs.astype(jnp.bfloat16),
                grad_tile,
                preferred_element_type=jnp.float32,
            )
        query_sum = jnp.zeros((BLOCK, heads, depth), jnp.float32)
        for col_block in range(row_block + 1):
            scores, allowed = tile_scores(query_tile, keys, segment, row_block, col_block)
            probs = jnp.where(allowed[None], jnp.exp(scores - total[:, :, None]), 0.0)
            value_tile = values[col_block * BLOCK : (col_block + 1) * BLOCK]
            key_tile = keys[col_block * BLOCK : (col_block + 1) * BLOCK]
            prob_grad = jnp.einsum(
                "qhe,khe->hqk", grad_tile, value_tile, preferred_element_type=jnp.float32
            )
            score_grad = (probs * (prob_grad - flows[:, :, None])).astype(jnp.bfloat16)
            query_sum = query_sum + scale * jnp.einsum(
                "hqk,khe->qhe", score_grad, key_tile, preferred_element_type=jnp.float32
            )
            key_grads[col_block] = key_grads[col_block] + scale * jnp.einsum(
                "hqk,qhe->khe", score_grad, query_tile, preferred_element_type=jnp.float32
            )
        query_grads.append(query_sum)
    return (
        jnp.concatenate(query_grads, axis=0).astype(jnp.bfloat16),
        jnp.concatenate(key_grads, axis=0).astype(jnp.bfloat16),
        jnp.concatenate(value_grads, axis=0).astype(jnp.bfloat16),
    )


def adam_update(master, grad, first, second, rate, decay, first_fix, second_fix):
    first_next = BETA_FIRST * first + (1.0 - BETA_FIRST) * grad
    second_next = BETA_SECOND * second + (1.0 - BETA_SECOND) * grad * grad
    change = (
        first_next / first_fix / (jnp.sqrt(second_next / second_fix) + ADAM_EPSILON)
        + decay * master
    )
    return (master - rate * change, first_next, second_next)


def adam_step(master, grad, first, second, rate, decay, fixes):
    first_next = BETA_FIRST * first + (1.0 - BETA_FIRST) * grad
    second_next = BETA_SECOND * second + (1.0 - BETA_SECOND) * grad * grad
    change = (
        first_next / fixes[0] / (jnp.sqrt(second_next / fixes[1]) + ADAM_EPSILON)
        + decay * master
    )
    return master - rate * change, first_next, second_next


def adam_kernel(rates, fix_ref, late_ref, early_ref, *refs):
    fixes = (fix_ref[0], fix_ref[1])
    smalls = 4
    matrix_inputs, small_inputs = refs[: 4 * len(rates)], refs[4 * len(rates) :][: 3 * smalls]
    outputs = refs[4 * len(rates) + 3 * smalls :]
    for index, rate in enumerate(rates):
        master, grad, first, second = matrix_inputs[4 * index : 4 * index + 4]
        updated, first_out, second_out, grad_out, low_out = outputs[5 * index : 5 * index + 5]
        value = grad[...].reshape(master.shape)
        fresh = adam_step(
            master[...], value, first[...], second[...], rate, MATRIX_DECAY, fixes
        )
        updated[...], first_out[...], second_out[...] = fresh
        grad_out[...] = value
        low_out[...] = fresh[0].astype(jnp.bfloat16)

    @pl.when(pl.program_id(0) == 0)
    def _():
        local = small_inputs[0].shape[1]
        units = small_inputs[3].shape[1]
        early = early_ref
        pieces = (
            [early[4:5, :local], early[4:5, local : 2 * local]],
            [early[4:5, 2 * local : 2 * local + units]],
            [late_ref[0:1, :], early[0:1, :]],
            [late_ref[1:2, :], early[2:3, :], early[1:2, :], early[3:4, :]],
        )
        for index in range(smalls):
            master, first, second = small_inputs[3 * index : 3 * index + 3]
            to = 5 * len(rates) + 4 * index
            updated, first_out, second_out, grad_out = outputs[to : to + 4]
            for row, value in enumerate(pieces[index]):
                here = slice(row, row + 1)
                fresh = adam_step(
                    master[here, :], value, first[here, :], second[here, :], SMALL_RATE, 0.0, fixes
                )
                updated[here, :], first_out[here, :], second_out[here, :] = fresh
                grad_out[here, :] = value


ADAM_STEPS = 4


def adam_call(matrices, smalls, late, early, fixes):
    in_specs = [pl.BlockSpec(memory_space=pltpu.SMEM)] + [
        pl.BlockSpec(rows.shape, lambda i: (0, 0)) for rows in (late, early)
    ]
    out_specs, out_shape, operands, rates = [], [], [fixes, late, early], []
    for master, grad, first, second, rate in matrices:
        lead = master.shape[:-2]
        rows, columns = master.shape[-2] // ADAM_STEPS, master.shape[-1]
        zeros = (0,) * len(lead)
        whole = pl.BlockSpec(lead + (rows, columns), lambda i, z=zeros: z + (i, 0))
        half = pl.BlockSpec(
            (1,) + lead + (rows, columns),
            lambda i, z=zeros: (i // (ADAM_STEPS // 2),) + z + (i % (ADAM_STEPS // 2), 0),
        )
        in_specs += [whole, half, whole, whole]
        operands += [master, grad, first, second]
        shape = jax.ShapeDtypeStruct(master.shape, jnp.float32)
        out_specs += [whole] * 5
        out_shape += [shape] * 4 + [jax.ShapeDtypeStruct(master.shape, jnp.bfloat16)]
        rates.append(rate)
    for group in smalls:
        spec = pl.BlockSpec(group[0].shape, lambda i: (0, 0))
        in_specs += [spec] * 3
        operands += list(group)
        out_specs += [spec] * 4
        out_shape += [jax.ShapeDtypeStruct(group[0].shape, jnp.float32)] * 4
    return pl.pallas_call(
        functools.partial(adam_kernel, tuple(rates)),
        grid=(ADAM_STEPS,),
        in_specs=in_specs,
        out_specs=out_specs,
        out_shape=out_shape,
        compiler_params=pltpu.CompilerParams(vmem_limit_bytes=VMEM_LIMIT),
        name="adam",
    )(*operands)


def per_device(
    layer_input,
    cotangent,
    lengths,
    offsets,
    step,
    mix_weight,
    out_weight,
    up_weight,
    down_weight,
    mix_first,
    out_first,
    up_first,
    down_first,
    mix_second,
    out_second,
    up_second,
    down_second,
    mix_bias,
    up_bias,
    norm_gains,
    shifts,
    mix_bias_first,
    up_bias_first,
    gains_first,
    shifts_first,
    mix_bias_second,
    up_bias_second,
    gains_second,
    shifts_second,
):
    parts = lax.axis_size("mp")
    local_width = mix_weight.shape[2]
    bounds = jnp.concatenate([offsets, offsets + lengths])
    (
        normed_one,
        mixed,
        mix_whole,
        out_whole,
        up_low,
        down_low,
        own_branch,
        bias_down_grad,
    ) = project_call(
        layer_input,
        norm_gains[0:1],
        shifts[0:1],
        mix_weight,
        out_weight,
        mix_bias,
        up_weight,
        down_weight,
        cotangent,
        bounds,
        parts // 2,
    )
    (
        attended_flat,
        aux,
        resid_own,
        normed_mid,
        branch_grad,
        up_whole,
        down_whole,
    ) = attend_out_call(
        mixed,
        bounds,
        out_whole,
        layer_input,
        own_branch,
        norm_gains[1:2],
        shifts[2:3],
        shifts[1:2],
        up_low,
        down_low,
        parts // 2,
    )
    normed_two, active, hidden_grad, resid_grad, resid_low, row_sums, up_bias_grad = feed_call(
        normed_mid,
        branch_grad,
        up_whole,
        down_whole,
        up_bias[None],
        resid_own,
        own_branch,
        norm_gains[1:2],
        parts // 2,
    )
    up_bias_grad = up_bias_grad[0]
    stacked, mix_bias_grad, down_pieces, out_grad, layer_output, _ = branch_back_call(
        resid_low,
        active,
        down_whole,
        attended_flat,
        out_whole,
        shifts[3:4],
        bounds,
        mixed,
        aux,
        resid_own,
        branch_grad,
        parts // 2,
    )
    early = jnp.concatenate(
        [
            row_sums,
            bias_down_grad,
            jnp.pad(
                jnp.concatenate([mix_bias_grad.reshape(-1), up_bias_grad]),
                (0, row_sums.shape[1] - 2 * local_width - up_bias_grad.shape[0]),
            )[None]
        ],
        axis=0,
    )
    input_grad, late, early, mix_pieces, up_pieces, out_pieces = input_back_call(
        stacked,
        mix_whole,
        layer_input,
        resid_grad,
        norm_gains[0:1],
        early,
        hidden_grad,
        out_grad,
        normed_one,
        normed_two,
        parts // 2,
    )
    step_count = step[0].astype(jnp.float32)
    fixes = jnp.stack([1.0 - BETA_FIRST**step_count, 1.0 - BETA_SECOND**step_count])
    news = adam_call(
        [
            (mix_weight, mix_pieces, mix_first, mix_second, D ** (-0.5)),
            (out_weight, out_pieces, out_first, out_second, OUT_FAN ** (-0.5)),
            (up_weight, up_pieces, up_first, up_second, D ** (-0.5)),
            (down_weight, down_pieces, down_first, down_second, FF ** (-0.5)),
        ],
        [
            (mix_bias, mix_bias_first, mix_bias_second),
            (up_bias[None], up_bias_first[None], up_bias_second[None]),
            (norm_gains, gains_first, gains_second),
            (shifts, shifts_first, shifts_second),
        ],
        late,
        early,
        fixes,
    )
    mix, out, up, down = (news[5 * index : 5 * index + 5] for index in range(4))
    biases, unit_biases, gains, moves = (
        news[20 + 4 * index : 24 + 4 * index] for index in range(4)
    )
    unit_biases = [value[0] for value in unit_biases]
    return (
        layer_output,
        input_grad,
        *mix[:3],
        *out[:3],
        *up[:3],
        *down[:3],
        *biases[:3],
        *unit_biases[:3],
        *gains[:3],
        *moves[:3],
        mix[3],
        out[3],
        up[3],
        down[3],
        biases[3],
        unit_biases[3],
        gains[3],
        moves[3],
        mix[4],
        out[4],
        up[4],
        down[4],
    )


def per_device_any(
    layer_input,
    cotangent,
    lengths,
    offsets,
    step,
    mix_weight,
    out_weight,
    up_weight,
    down_weight,
    mix_first,
    out_first,
    up_first,
    down_first,
    mix_second,
    out_second,
    up_second,
    down_second,
    mix_bias,
    up_bias,
    norm_gains,
    shifts,
    mix_bias_first,
    up_bias_first,
    gains_first,
    shifts_first,
    mix_bias_second,
    up_bias_second,
    gains_second,
    shifts_second,
):
    own_rows = layer_input.shape[0]
    parts = lax.axis_size("mp")
    group_rows = own_rows * parts
    slots_here = lengths.shape[0]
    slot_len = group_rows // slots_here
    local_width = mix_weight.shape[2]
    depth = HEAD_DIM
    heads_here = local_width // depth
    positions = jnp.arange(slot_len, dtype=jnp.int32)
    live = (positions[None, :] >= offsets[:, None]) & (
        positions[None, :] < (offsets + lengths)[:, None]
    )
    segment = live.astype(jnp.int32)
    first_row = lax.axis_index("mp") * own_rows
    own_live = own_slice(live.reshape(-1), first_row, own_rows)[:, None]
    own_input = layer_input.astype(jnp.float32)
    normed_own, hat_one, inv_one = layer_norm_parts(own_input, norm_gains[0], shifts[0])
    normed_one = gather_rows(normed_own.astype(jnp.bfloat16))
    mix_full = gather_shards(mix_weight.astype(jnp.bfloat16), 1)
    out_full = gather_shards(out_weight.astype(jnp.bfloat16), 1)
    up_full = gather_shards(up_weight.astype(jnp.bfloat16), 0)
    down_full = gather_shards(down_weight.astype(jnp.bfloat16), 1)
    out_grad = jnp.where(own_live, cotangent.astype(jnp.float32), 0.0)
    bias_down_grad = jnp.sum(out_grad, axis=0)
    branch_grad = gather_rows(out_grad.astype(jnp.bfloat16))
    mixed = jnp.einsum("td,cde->cte", normed_one, mix_full, preferred_element_type=jnp.float32)
    queries = (
        (mixed[0] + mix_bias[0])
        .astype(jnp.bfloat16)
        .reshape(slots_here, slot_len, heads_here, depth)
    )
    keys = mixed[1].astype(jnp.bfloat16).reshape(slots_here, slot_len, heads_here, depth)
    values = (
        (mixed[2] + mix_bias[1])
        .astype(jnp.bfloat16)
        .reshape(slots_here, slot_len, heads_here, depth)
    )

    def attend(item):
        return attention_forward(item[0], item[1], item[2], item[3])

    attended, totals = lax.map(attend, (queries, keys, values, segment))
    attended_flat = attended.reshape(group_rows, local_width)
    attn_part = jnp.dot(attended_flat, out_full, preferred_element_type=jnp.float32)
    resid_own = own_input + scatter_rows(attn_part) + shifts[1]
    normed_mid, hat_two, inv_two = layer_norm_parts(resid_own, norm_gains[1], shifts[2])
    normed_two = gather_rows(normed_mid.astype(jnp.bfloat16))
    hidden = jnp.dot(normed_two, up_full, preferred_element_type=jnp.float32) + up_bias
    active_value, gelu_pull = jax.vjp(tanh_gelu, hidden)
    active = active_value.astype(jnp.bfloat16)
    active_grad = jnp.einsum(
        "td,fd->tf", branch_grad, down_full, preferred_element_type=jnp.float32
    )
    hidden_grad = gelu_pull(active_grad)[0].astype(jnp.bfloat16)
    two_part = jnp.einsum("tf,df->td", hidden_grad, up_full, preferred_element_type=jnp.float32)
    two_grad = scatter_rows(two_part)
    down_part = jnp.dot(active, down_full, preferred_element_type=jnp.float32)
    down_grad = jnp.einsum("tf,td->fd", active, branch_grad, preferred_element_type=jnp.float32)
    up_bias_grad = jnp.sum(hidden_grad, axis=0, dtype=jnp.float32)
    up_grad = jnp.einsum("td,tf->df", normed_two, hidden_grad, preferred_element_type=jnp.float32)
    resid_grad = out_grad + layer_norm_back(two_grad, hat_two, inv_two, norm_gains[1])
    attn_branch = gather_rows(resid_grad.astype(jnp.bfloat16))
    result_own = resid_own + scatter_rows(down_part) + shifts[3]
    layer_output = jnp.where(own_live, result_own, 0.0).astype(jnp.bfloat16)
    gain_two_grad = jnp.sum(two_grad * hat_two, axis=0)
    shift_two_grad = jnp.sum(two_grad, axis=0)
    bias_out_grad = jnp.sum(resid_grad, axis=0)
    attended_grad = jnp.einsum(
        "td,ed->te", attn_branch, out_full, preferred_element_type=jnp.float32
    ).astype(jnp.bfloat16)
    out_weight_grad = jnp.einsum(
        "te,td->ed", attended_flat, attn_branch, preferred_element_type=jnp.float32
    )

    def attend_back(item):
        return attention_backward(item[0], item[1], item[2], item[3], item[4], item[5])

    query_grad, key_grad, value_grad = lax.map(
        attend_back,
        (
            queries,
            keys,
            values,
            segment,
            totals,
            attended_grad.reshape(slots_here, slot_len, heads_here, depth),
        ),
    )
    stacked = jnp.stack(
        [
            query_grad.reshape(group_rows, local_width),
            key_grad.reshape(group_rows, local_width),
            value_grad.reshape(group_rows, local_width),
        ]
    )
    one_part = jnp.einsum("cte,cde->td", stacked, mix_full, preferred_element_type=jnp.float32)
    one_grad = scatter_rows(one_part)
    mix_grad = jnp.einsum("td,cte->cde", normed_one, stacked, preferred_element_type=jnp.float32)
    mix_bias_grad = jnp.stack(
        [
            jnp.sum(stacked[0], axis=0, dtype=jnp.float32),
            jnp.sum(stacked[2], axis=0, dtype=jnp.float32),
        ]
    )
    mix_owned = scatter_shards(mix_grad, 1)
    out_owned = scatter_shards(out_weight_grad, 1)
    up_owned = scatter_shards(up_grad, 0)
    down_owned = scatter_shards(down_grad, 1)
    input_grad = resid_grad + layer_norm_back(one_grad, hat_one, inv_one, norm_gains[0])
    gain_one_grad = jnp.sum(one_grad * hat_one, axis=0)
    shift_one_grad = jnp.sum(one_grad, axis=0)
    gain_grad = jnp.stack([gain_one_grad, gain_two_grad])
    shift_grad = jnp.stack([shift_one_grad, bias_out_grad, shift_two_grad, bias_down_grad])
    mix_bias_total, up_bias_total = lax.psum((mix_bias_grad, up_bias_grad), "dp")
    gain_total, shift_total = lax.psum((gain_grad, shift_grad), ("dp", "mp"))
    step_count = step[0].astype(jnp.float32)
    first_fix = 1.0 - BETA_FIRST**step_count
    second_fix = 1.0 - BETA_SECOND**step_count
    mix_new = adam_update(
        mix_weight,
        mix_owned,
        mix_first,
        mix_second,
        D ** (-0.5),
        MATRIX_DECAY,
        first_fix,
        second_fix,
    )
    out_new = adam_update(
        out_weight,
        out_owned,
        out_first,
        out_second,
        OUT_FAN ** (-0.5),
        MATRIX_DECAY,
        first_fix,
        second_fix,
    )
    up_new = adam_update(
        up_weight, up_owned, up_first, up_second, D ** (-0.5), MATRIX_DECAY, first_fix, second_fix
    )
    down_new = adam_update(
        down_weight,
        down_owned,
        down_first,
        down_second,
        FF ** (-0.5),
        MATRIX_DECAY,
        first_fix,
        second_fix,
    )
    mix_bias_new = adam_update(
        mix_bias,
        mix_bias_total,
        mix_bias_first,
        mix_bias_second,
        SMALL_RATE,
        0.0,
        first_fix,
        second_fix,
    )
    up_bias_new = adam_update(
        up_bias,
        up_bias_total,
        up_bias_first,
        up_bias_second,
        SMALL_RATE,
        0.0,
        first_fix,
        second_fix,
    )
    gains_new = adam_update(
        norm_gains, gain_total, gains_first, gains_second, SMALL_RATE, 0.0, first_fix, second_fix
    )
    shifts_new = adam_update(
        shifts, shift_total, shifts_first, shifts_second, SMALL_RATE, 0.0, first_fix, second_fix
    )
    return (
        layer_output,
        input_grad,
        mix_new[0],
        mix_new[1],
        mix_new[2],
        out_new[0],
        out_new[1],
        out_new[2],
        up_new[0],
        up_new[1],
        up_new[2],
        down_new[0],
        down_new[1],
        down_new[2],
        mix_bias_new[0],
        mix_bias_new[1],
        mix_bias_new[2],
        up_bias_new[0],
        up_bias_new[1],
        up_bias_new[2],
        gains_new[0],
        gains_new[1],
        gains_new[2],
        shifts_new[0],
        shifts_new[1],
        shifts_new[2],
        mix_owned,
        out_owned,
        up_owned,
        down_owned,
        mix_bias_total,
        up_bias_total,
        gain_total,
        shift_total,
        mix_new[0].astype(jnp.bfloat16),
        out_new[0].astype(jnp.bfloat16),
        up_new[0].astype(jnp.bfloat16),
        down_new[0].astype(jnp.bfloat16),
    )


def solution(mesh):
    placed = (
        P(("dp", "mp"), None),
        P(("dp", "mp"), None),
        P("dp"),
        P("dp"),
        P(),
        P(None, "dp", "mp"),
        P("mp", "dp"),
        P("dp", "mp"),
        P("mp", "dp"),
        P(None, "dp", "mp"),
        P("mp", "dp"),
        P("dp", "mp"),
        P("mp", "dp"),
        P(None, "dp", "mp"),
        P("mp", "dp"),
        P("dp", "mp"),
        P("mp", "dp"),
        P(None, "mp"),
        P("mp"),
        P(),
        P(),
        P(None, "mp"),
        P("mp"),
        P(),
        P(),
        P(None, "mp"),
        P("mp"),
        P(),
        P(),
    )
    fits = mesh.shape["dp"] == 4 and mesh.shape["mp"] == 8
    return jax.shard_map(
        per_device if fits else per_device_any,
        mesh=mesh,
        in_specs=placed,
        out_specs=(
            P(("dp", "mp"), None),
            P(("dp", "mp"), None),
            P(None, "dp", "mp"),
            P(None, "dp", "mp"),
            P(None, "dp", "mp"),
            P("mp", "dp"),
            P("mp", "dp"),
            P("mp", "dp"),
            P("dp", "mp"),
            P("dp", "mp"),
            P("dp", "mp"),
            P("mp", "dp"),
            P("mp", "dp"),
            P("mp", "dp"),
            P(None, "mp"),
            P(None, "mp"),
            P(None, "mp"),
            P("mp"),
            P("mp"),
            P("mp"),
            P(),
            P(),
            P(),
            P(),
            P(),
            P(),
            P(None, "dp", "mp"),
            P("mp", "dp"),
            P("dp", "mp"),
            P("mp", "dp"),
            P(None, "mp"),
            P("mp"),
            P(),
            P(),
            P(None, "dp", "mp"),
            P("mp", "dp"),
            P("dp", "mp"),
            P("mp", "dp"),
        ),
        check_vma=False,
    )
```

```python
import functools

import jax
import jax.numpy as jnp
from jax import lax
from jax.experimental import pallas as pl
from jax.experimental.pallas import tpu as pltpu
from jax.sharding import PartitionSpec as P

D = 2048
HEAD_DIM = 128
FF = 8192
BLOCK = 512
OUT_FAN = 7


NORM_EPSILON = 1e-05
ADAM_EPSILON = 1e-08
BETA_FIRST = 0.9
BETA_SECOND = 0.999
MATRIX_DECAY = 0.1
SMALL_RATE = 0.2
MASK_FILL = -1e30


def layer_norm_parts(rows, gain, shift):
    center = rows - jnp.mean(rows, axis=-1, keepdims=True)
    inverse = lax.rsqrt(jnp.mean(center * center, axis=-1, keepdims=True) + NORM_EPSILON)
    normed = center * inverse
    return (normed * gain + shift, normed, inverse)


def layer_norm_back(grad_out, normed, inverse, gain):
    scaled = grad_out * gain
    return inverse * (
        scaled
        - jnp.mean(scaled, axis=-1, keepdims=True)
        - normed * jnp.mean(scaled * normed, axis=-1, keepdims=True)
    )


def tanh_gelu(values):
    return jax.nn.gelu(values, approximate=True)


def own_slice(whole, first_row, count):
    return lax.dynamic_slice_in_dim(whole, first_row, count, 0)


def gather_rows(rows):
    return lax.all_gather(rows, "mp", axis=0, tiled=True)


def scatter_rows(terms):
    low = terms.astype(jnp.bfloat16)
    return lax.psum_scatter(low, "mp", scatter_dimension=0, tiled=True).astype(jnp.float32)


def swap(value, mask):
    size = lax.axis_size("dp")
    return lax.ppermute(value, "dp", [(place, place ^ mask) for place in range(size)])


def gather_shards(shard, axis):
    if lax.axis_size("dp") != 4:
        return lax.all_gather(shard, "dp", axis=axis, tiled=True)
    count = shard.shape[axis]
    me = lax.axis_index("dp")
    from_x = swap(shard, 1)
    from_y = swap(shard, 2)
    half = count // 2
    low = swap(lax.slice_in_dim(from_x, 0, half, axis=axis), 2)
    high = swap(lax.slice_in_dim(from_y, half, count, axis=axis), 1)
    shape = list(shard.shape)
    shape[axis] = 4 * count
    full = jnp.zeros(shape, shard.dtype)
    full = lax.dynamic_update_slice_in_dim(full, shard, me * count, axis)
    full = lax.dynamic_update_slice_in_dim(full, from_x, (me ^ 1) * count, axis)
    full = lax.dynamic_update_slice_in_dim(full, from_y, (me ^ 2) * count, axis)
    full = lax.dynamic_update_slice_in_dim(full, low, (me ^ 3) * count, axis)
    return lax.dynamic_update_slice_in_dim(full, high, (me ^ 3) * count + half, axis)


def scatter_shards(grad, axis):
    if lax.axis_size("dp") != 4:
        return lax.psum_scatter(grad, "dp", scatter_dimension=axis, tiled=True)
    count = grad.shape[axis] // 4
    half = count // 2
    me = lax.axis_index("dp")

    def piece(owner, upper):
        return lax.dynamic_slice_in_dim(grad, owner * count + upper * half, half, axis)

    def one_way(first, second, upper):
        near = swap(piece(me ^ first, upper).astype(jnp.bfloat16), first)
        far = swap(piece(me ^ 3, upper).astype(jnp.bfloat16), first)
        onward = piece(me ^ second, upper) + far.astype(jnp.float32)
        last = swap(onward.astype(jnp.bfloat16), second)
        return piece(me, upper) + near.astype(jnp.float32) + last.astype(jnp.float32)

    return lax.concatenate([one_way(1, 2, 0), one_way(2, 1, 1)], axis)


MESH = pl.DeviceIdType.MESH
VMEM_LIMIT = 62 * 1024 * 1024
TURNED = (((1,), (1,)), ((), ()))
CROSSED = (((0,), (0,)), ((), ()))


class Place:
    def __init__(self, chips):
        self.chips = chips
        self.dp = lax.axis_index("dp")
        self.me = lax.axis_index("mp")
        self.chip = self.me // 2
        self.core = self.me % 2
        self.has_up = self.chip < chips - 1
        self.has_down = self.chip > 0
        self.up = (self.dp, jnp.minimum(self.me + 2, 2 * chips - 1))
        self.down = (self.dp, jnp.maximum(self.me - 2, 0))
        self.side = (self.dp, self.me + 1 - 2 * self.core)
        self.x_peer = self.dp + 1 - 2 * (self.dp % 2)
        self.y_peer = (self.dp + 2) % 4
        self.across = 3 - self.dp
        self.x_way = (self.x_peer, self.me)
        self.y_way = (self.y_peer, self.me)

    def greet(self, square, everyone=False):
        barrier = pltpu.get_barrier_semaphore()

        def signal(device):
            pl.semaphore_signal(barrier, inc=1, device_id=device, device_id_type=MESH)

        signal(self.side)
        pl.when(self.has_up)(lambda: signal(self.up))
        pl.when(self.has_down)(lambda: signal(self.down))
        count = 1 + self.has_up.astype(jnp.int32) + self.has_down.astype(jnp.int32)
        if square:
            signal(self.x_way)
            signal(self.y_way)
            count = count + 2
        if everyone:
            signal((self.across, self.me))
            count = count + 1

            def beyond(chip, carry):
                far = (chip > self.chip + 1) | (chip < self.chip - 1)
                pl.when(far)(lambda: signal((self.dp, 2 * chip + self.core)))
                return carry

            lax.fori_loop(0, self.chips, beyond, 0)
            near = self.has_up.astype(jnp.int32) + self.has_down.astype(jnp.int32)
            count = count + (self.chips - 1) - near
        pl.semaphore_wait(barrier, count)


def remote(source, target, send, recv, device):
    return pltpu.make_async_remote_copy(
        src_ref=source,
        dst_ref=target,
        send_sem=send,
        recv_sem=recv,
        device_id=device,
        device_id_type=MESH,
    )


def fetch(pairs, sems):
    copies = [
        pltpu.make_async_copy(source, target, sems.at[index])
        for index, (source, target) in enumerate(pairs)
    ]
    for copy in copies:
        copy.start()
    return copies


class LineGather:
    def __init__(self, place, blocks, send, recv, parts=1, own=None):
        self.place, self.blocks, self.send, self.recv = place, blocks, send, recv
        self.parts, self.own = parts, own

    def copy(self, way, chip, part=0, own=None):
        place = self.place
        piece = chip * self.parts + part
        block = 2 * piece + place.core
        device = (place.up, place.down, place.side)[way]
        return remote(
            self.blocks.at[block] if own is None else own,
            self.blocks.at[block],
            self.send.at[way, piece],
            self.recv.at[block],
            device,
        )

    def arrive(self, chip, core, part=0):
        piece = chip * self.parts + part
        block = 2 * piece + core
        remote(
            self.blocks.at[block],
            self.blocks.at[block],
            self.send.at[2, piece],
            self.recv.at[block],
            self.place.side,
        ).wait_recv()

    def begin_part(self, part):
        place = self.place
        pl.when(place.has_up)(lambda: self.copy(0, place.chip, part, self.own).start())
        pl.when(place.has_down)(lambda: self.copy(1, place.chip, part, self.own).start())
        self.copy(2, place.chip, part, self.own).start()

    def begin(self):
        for part in range(self.parts):
            self.begin_part(part)

    def step(self, distance, part=0):
        place = self.place
        low = place.chip - distance
        high = place.chip + distance

        @pl.when(low >= 0)
        def _():
            self.arrive(low, place.core, part)
            pl.when(place.has_up)(lambda: self.copy(0, low, part).start())
            self.copy(2, low, part).start()

        @pl.when(high < place.chips)
        def _():
            self.arrive(high, place.core, part)
            pl.when(place.has_down)(lambda: self.copy(1, high, part).start())
            self.copy(2, high, part).start()

    def finish(self):
        place = self.place

        def drain(chip, carry):
            for part in range(self.parts):
                pl.when(place.has_up & (chip <= place.chip))(
                    lambda: self.copy(0, chip, part).wait_send()
                )
                pl.when(place.has_down & (chip >= place.chip))(
                    lambda: self.copy(1, chip, part).wait_send()
                )
                self.copy(2, chip, part).wait_send()
            return carry

        lax.fori_loop(0, place.chips, drain, 0)


class SquareGather:
    def __init__(self, place, shard, view, half, send, recv):
        self.place, self.shard, self.view, self.half = place, shard, view, half
        self.send, self.recv = send, recv

    def first(self, way):
        place = self.place
        device = (place.x_way, place.y_way)[way]
        return remote(
            self.shard, self.view(place.dp), self.send.at[way], self.recv.at[way], device
        )

    def first_landed(self, way):
        place = self.place
        owner = (place.x_peer, place.y_peer)[way]
        device = (place.x_way, place.y_way)[way]
        remote(
            self.view(owner), self.view(owner), self.send.at[way], self.recv.at[way], device
        ).wait_recv()

    def second(self, way):
        place = self.place
        owner = (place.y_peer, place.x_peer)[way]
        device = (place.x_way, place.y_way)[way]
        part = self.half(owner, 1 - way)
        return remote(part, part, self.send.at[2 + way], self.recv.at[2 + way], device)

    def second_landed(self, way):
        place = self.place
        device = (place.x_way, place.y_way)[way]
        part = self.half(place.across, 1 - way)
        remote(part, part, self.send.at[2 + way], self.recv.at[2 + way], device).wait_recv()

    def begin(self):
        self.first(0).start()
        self.first(1).start()

    def middle(self):
        self.first_landed(0)
        self.second(1).start()
        self.first_landed(1)
        self.second(0).start()

    def end(self):
        self.second_landed(0)
        self.second_landed(1)

    def finish(self):
        self.first(0).wait_send()
        self.first(1).wait_send()
        self.second(0).wait_send()
        self.second(1).wait_send()


def norm_rows(rows, gain, shift):
    normed, hat, inverse = layer_norm_parts(rows, gain, shift)
    return normed


def project_kernel(
    chips,
    parts,
    rows_ref,
    gain_ref,
    shift_ref,
    mix_weight_hbm,
    out_weight_hbm,
    bias_ref,
    up_weight_hbm,
    down_weight_hbm,
    cotangent_hbm,
    offsets_ref,
    lengths_ref,
    normed_ref,
    mixed_hbm,
    mix_hbm,
    out_whole,
    up_ref,
    down_ref,
    branch_ref,
    branch_sum_ref,
    mix_weight_ref,
    out_weight_ref,
    up_weight_ref,
    down_weight_ref,
    cotangent_ref,
    fetch_sem,
    mix_ref,
    out_ref,
    mixed_ref,
    mix_whole,
    emit_sem,
    blocks,
    line_send,
    line_recv,
    mix_send,
    mix_recv,
    out_send,
    out_recv,
    own_sem,
    keep_sem,
):
    place = Place(chips)
    bounds = (offsets_ref[0], offsets_ref[0] + lengths_ref[0])
    count = rows_ref.shape[0]
    rows = count // parts
    fetched = fetch(
        [
            (mix_weight_hbm, mix_weight_ref),
            (out_weight_hbm, out_weight_ref),
            (cotangent_hbm, cotangent_ref),
            (up_weight_hbm, up_weight_ref),
            (down_weight_hbm, down_weight_ref),
        ],
        fetch_sem,
    )
    line = LineGather(place, blocks, line_send, line_recv, parts)

    def norm(part):
        def one(span):
            own = rows_ref[pl.ds(part * rows + span.start, 64), :].astype(jnp.float32)
            normed = norm_rows(own, gain_ref[...], shift_ref[...])
            blocks[2 * (place.chip * parts + part) + place.core, span, :] = normed.astype(
                jnp.bfloat16
            )

        by_rows(rows, 64, one)

    norm(0)
    place.greet(True)
    line.begin_part(0)
    for part in range(1, parts):
        norm(part)
        line.begin_part(part)
    mix = SquareGather(
        place,
        mix_ref,
        lambda owner: mix_whole.at[:, owner],
        lambda owner, which: mix_whole.at[:, owner, pl.ds(which * 256, 256)],
        mix_send,
        mix_recv,
    )
    out = SquareGather(
        place,
        out_ref,
        lambda owner: out_whole.at[owner],
        lambda owner, which: out_whole.at[owner, pl.ds(which * 128, 128)],
        out_send,
        out_recv,
    )

    def lower(source, target):
        def one(span):
            target[span, :] = source[span, :].astype(jnp.bfloat16)

        by_rows(source.shape[0], 64, one)

    fetched[0].wait()
    for part in range(3):
        lower(mix_weight_ref.at[part], mix_ref.at[part])
    mix.begin()
    own_mix = pltpu.make_async_copy(mix_ref, mix_whole.at[:, place.dp], own_sem.at[0])
    own_mix.start()
    fetched[1].wait()
    lower(out_weight_ref, out_ref)
    own_out = pltpu.make_async_copy(out_ref, out_whole.at[place.dp], own_sem.at[1])
    own_out.start()
    branch_sum_ref[...] = jnp.zeros_like(branch_sum_ref)

    def branch(span):
        live = alive((64, 1), 0, place.me * count + span.start, bounds)
        grad = jnp.where(live > 0, cotangent_ref[span, :].astype(jnp.float32), 0.0)
        branch_ref[span, :] = grad.astype(jnp.bfloat16)
        branch_sum_ref[...] += jnp.sum(grad, axis=0, keepdims=True)

    fetched[2].wait()
    by_rows(count, 64, branch)
    fetched[3].wait()
    lower(up_weight_ref, up_ref)
    fetched[4].wait()
    lower(down_weight_ref, down_ref)

    def span_of(chip, core, part):
        start = (2 * chip + core) * count + part * rows
        return pl.ds(pl.multiple_of(start, rows), rows)

    def copies(chip, part):
        piece = chip * parts + part
        taken = []
        for core in range(2):
            span = span_of(chip, core, part)
            taken.append(
                pltpu.make_async_copy(
                    blocks.at[2 * piece + core], normed_ref.at[span], keep_sem.at[piece, core]
                )
            )
            taken.append(
                pltpu.make_async_copy(
                    mixed_ref.at[:, span], mixed_hbm.at[:, span], emit_sem.at[piece, core]
                )
            )
        return taken

    keep_mix = pltpu.make_async_copy(mix_whole, mix_hbm, own_sem.at[2])

    def project(chip, part):
        piece = chip * parts + part
        line.arrive(chip, 1 - place.core, part)
        pair = blocks[pl.ds(2 * piece, 2)].reshape(2 * rows, -1)
        for kind in range(3):
            weight = mix_whole[kind].reshape(-1, mix_whole.shape[3])
            result = jnp.dot(pair, weight, preferred_element_type=jnp.float32)
            if kind == 0:
                result = result + bias_ref[0:1, :]
            if kind == 2:
                result = result + bias_ref[1:2, :]
            low = result.astype(jnp.bfloat16)
            for core in range(2):
                mixed_ref[kind, span_of(chip, core, part), :] = low[
                    core * rows : (core + 1) * rows
                ]
        for copy in copies(chip, part):
            copy.start()

    def turn(index, carry):
        distance = index // parts
        part = index % parts

        @pl.when(distance > 0)
        def _():
            line.step(distance, part)

        @pl.when(index == parts)
        def _():
            mix.middle()
            out.begin()
            mix.end()
            own_mix.wait()
            keep_mix.start()
            out.middle()

        first = jnp.where(index == parts, 0, index)

        def one(order, inner):
            each = order // 2
            side = order % 2
            near = each // parts
            chip = place.chip + near * (2 * side - 1)

            @pl.when((chip >= 0) & (chip < chips) & ((near > 0) | (side == 0)))
            def _():
                project(chip, each % parts)

            return inner

        @pl.when(index >= parts)
        def _():
            lax.fori_loop(2 * first, 2 * index + 2, one, 0)

        return carry

    lax.fori_loop(0, chips * parts, turn, 0)
    out.end()
    own_out.wait()
    line.finish()
    mix.finish()
    out.finish()

    def kept(piece, carry):
        for copy in copies(piece // parts, piece % parts):
            copy.wait()
        return carry

    lax.fori_loop(0, parts * chips, kept, 0)
    keep_mix.wait()


def project_call(
    rows, gain, shift, mix_shard, out_shard, bias, up, down, cotangent, offsets, lengths, chips
):
    count, width = rows.shape
    total = 2 * chips * count
    local = mix_shard.shape[2]
    parts = 2
    vmem = pl.BlockSpec(memory_space=pltpu.VMEM)
    hbm = pl.BlockSpec(memory_space=pl.ANY)
    dma = pltpu.SemaphoreType.DMA
    flops = 2 * total * width * 3 * local
    return pl.pallas_call(
        functools.partial(project_kernel, chips, parts),
        out_shape=(
            jax.ShapeDtypeStruct((total, width), jnp.bfloat16),
            jax.ShapeDtypeStruct((3, total, local), jnp.bfloat16),
            jax.ShapeDtypeStruct((3, 4, mix_shard.shape[1], local), jnp.bfloat16),
            jax.ShapeDtypeStruct((4,) + out_shard.shape, jnp.bfloat16),
            jax.ShapeDtypeStruct(up.shape, jnp.bfloat16),
            jax.ShapeDtypeStruct(down.shape, jnp.bfloat16),
            jax.ShapeDtypeStruct((count, width), jnp.bfloat16),
            jax.ShapeDtypeStruct((1, width), jnp.float32),
        ),
        in_specs=[vmem] * 3
        + [hbm] * 2
        + [vmem]
        + [hbm] * 3
        + [pl.BlockSpec(memory_space=pltpu.SMEM)] * 2,
        out_specs=(hbm,) * 4 + (vmem,) * 4,
        scratch_shapes=[
            pltpu.VMEM(mix_shard.shape, jnp.float32),
            pltpu.VMEM(out_shard.shape, jnp.float32),
            pltpu.VMEM(up.shape, jnp.float32),
            pltpu.VMEM(down.shape, jnp.float32),
            pltpu.VMEM(cotangent.shape, jnp.bfloat16),
            dma((5,)),
            pltpu.VMEM(mix_shard.shape, jnp.bfloat16),
            pltpu.VMEM(out_shard.shape, jnp.bfloat16),
            pltpu.VMEM((3, total, local), jnp.bfloat16),
            pltpu.VMEM((3, 4, mix_shard.shape[1], local), jnp.bfloat16),
            dma((parts * chips, 2)),
            pltpu.VMEM((2 * chips * parts, count // parts, width), jnp.bfloat16),
            dma((3, chips * parts)),
            dma((2 * chips * parts,)),
            dma((4,)),
            dma((4,)),
            dma((4,)),
            dma((4,)),
            dma((3,)),
            dma((parts * chips, 2)),
        ],
        compiler_params=pltpu.CompilerParams(
            collective_id=0, has_side_effects=True, vmem_limit_bytes=VMEM_LIMIT
        ),
        cost_estimate=pl.CostEstimate(flops=flops * 7, bytes_accessed=0, transcendentals=0),
        name="project",
    )(rows, gain, shift, mix_shard, out_shard, bias, up, down, cotangent, offsets, lengths)


class LineScatter:
    def __init__(self, place, term, tiles, bufs, sems, prepare=lambda chip: None):
        self.place, self.term, self.tiles, self.prepare = place, term, tiles, prepare
        self.total, self.side_out, self.side_in, self.line_in = bufs
        self.side_send, self.side_recv, self.line_send, self.line_recv = sems

    def side_copy(self, chip):
        return remote(
            self.side_out.at[chip],
            self.side_in.at[chip],
            self.side_send.at[chip],
            self.side_recv.at[chip],
            self.place.side,
        )

    def span(self, tile):
        width = self.total.shape[1] // self.tiles
        return slice(tile * width, (tile + 1) * width)

    def line_copy(self, way, chip, tile):
        place = self.place
        next_chip = place.chip + 1 - 2 * way
        slot = jnp.where((way == 1) & (chip == next_chip), place.chips, chip)
        return remote(
            self.line_in.at[chip, :, self.span(tile)],
            self.line_in.at[slot, :, self.span(tile)],
            self.line_send.at[chip, tile],
            self.line_recv.at[slot, tile],
            (place.up, place.down)[way],
        )

    def landed(self, way, chip, tile):
        place = self.place
        slot = jnp.where((way == 1) & (chip == place.chip), place.chips, chip)
        remote(
            self.line_in.at[slot, :, self.span(tile)],
            self.line_in.at[slot, :, self.span(tile)],
            self.line_send.at[chip, tile],
            self.line_recv.at[slot, tile],
            (place.up, place.down)[way],
        ).wait_recv()
        return slot

    def each(self, distance, action):
        place = self.place

        def one(index, carry):
            chip = place.chip + distance * (1 - 2 * index)
            valid = (chip >= 0) & (chip < place.chips) & ((distance > 0) | (index == 0))
            pl.when(valid)(lambda: action(chip))
            return carry

        lax.fori_loop(0, 2, one, 0)

    def hand_over(self, chip):
        self.prepare(chip)
        block = 2 * chip + 1 - self.place.core
        for tile in range(self.tiles):
            self.side_out[chip, :, self.span(tile)] = self.term(block, tile).astype(jnp.bfloat16)
        self.side_copy(chip).start()

    def sum_up(self, chip):
        place = self.place
        block = 2 * chip + place.core
        self.side_copy(chip).wait_recv()
        for tile in range(self.tiles):
            span = self.span(tile)
            self.total[:, span] = self.term(block, tile) + self.side_in[chip, :, span].astype(
                jnp.float32
            )
            for way in range(2):
                behind = (place.has_down, place.has_up)[way]
                goes = (chip >= place.chip) if way == 0 else (chip <= place.chip)

                @pl.when(behind & goes)
                def _():
                    slot = self.landed(way, chip, tile)
                    self.total[:, span] += self.line_in[slot, :, span].astype(jnp.float32)

            @pl.when(chip != place.chip)
            def _():
                self.line_in[chip, :, span] = self.total[:, span].astype(jnp.bfloat16)
                pl.when(chip > place.chip)(lambda: self.line_copy(0, chip, tile).start())
                pl.when(chip < place.chip)(lambda: self.line_copy(1, chip, tile).start())

    def begin(self):
        self.each(self.place.chips - 1, self.hand_over)

    def step(self, index, early=False):
        distance = self.place.chips - 1 - index
        ahead = (index > 0) if early else (index < 0)
        pl.when(ahead & (distance > 0))(lambda: self.each(distance - 1, self.hand_over))
        self.each(distance, self.sum_up)
        behind = (index == 0) if early else (index >= 0)
        pl.when(behind & (distance > 0))(lambda: self.each(distance - 1, self.hand_over))

    def finish(self):
        place = self.place

        def drain(chip, carry):
            self.side_copy(chip).wait_send()
            for tile in range(self.tiles):
                pl.when(chip != place.chip)(lambda: self.line_copy(0, chip, tile).wait_send())
            return carry

        lax.fori_loop(0, place.chips, drain, 0)


class SquareScatter:
    def __init__(self, place, piece, owned, bufs, sems):
        self.place, self.piece, self.owned = place, piece, owned
        self.out, self.arrived = bufs
        self.send, self.recv = sems

    def copy(self, kind, way):
        place = self.place
        turn = way if kind < 2 else 1 - way
        peer = place.x_peer + turn * (place.y_peer - place.x_peer)
        return remote(
            self.out.at[kind, way],
            self.arrived.at[kind, way],
            self.send.at[kind, way],
            self.recv.at[kind, way],
            (peer, place.me),
        )

    def owner(self, kind, way):
        place = self.place
        near = place.x_peer + way * (place.y_peer - place.x_peer)
        other = place.y_peer + way * (place.x_peer - place.y_peer)
        return (place.across, near, other, place.dp)[kind]

    def following(self, kind, way):
        after = self.owner(kind, 1) if kind == 3 else self.owner(kind + 1, 0)
        return jnp.where(way == 0, self.owner(kind, 1), after), 1 - way

    def one(self, kind, way):
        value = self.piece(self.owner(kind, way), way)
        if kind == 2:
            self.copy(0, way).wait_recv()
            value = value + self.arrived[0, way].astype(jnp.float32)
        if kind < 3:
            self.out[kind, way] = value.astype(jnp.bfloat16)
            self.copy(kind, way).start()
        else:
            self.owned[way] = value

    def stage(self, kind):
        def one(way, carry):
            self.one(kind, way)
            return carry

        lax.fori_loop(0, 2, one, 0)

    def end(self):
        def one(way, carry):
            self.copy(1, way).wait_recv()
            self.copy(2, way).wait_recv()
            self.owned[way] = (
                self.owned[way]
                + self.arrived[1, way].astype(jnp.float32)
                + self.arrived[2, way].astype(jnp.float32)
            )
            for kind in range(3):
                self.copy(kind, way).wait_send()
            return carry

        lax.fori_loop(0, 2, one, 0)


def square_scratch(half):
    dma = pltpu.SemaphoreType.DMA
    return [
        pltpu.VMEM((3, 2) + half, jnp.bfloat16),
        pltpu.VMEM((3, 2) + half, jnp.bfloat16),
        dma((3, 2)),
        dma((3, 2)),
    ]


class SmallSum:
    def __init__(self, place, rows, alone, bufs, sems):
        self.place, self.rows, self.alone = place, rows, alone
        self.side_buf, self.line_buf, self.square_buf = bufs
        self.send, self.recv = sems

    def side_copy(self):
        place = self.place
        return remote(
            self.rows,
            self.side_buf,
            self.send.at[0],
            self.recv.at[0],
            place.side,
        )

    def line_copy(self, hop):
        place = self.place
        chip = (place.chip + hop) % place.chips
        return remote(
            self.rows,
            self.line_buf.at[place.chip],
            self.send.at[hop],
            self.recv.at[hop],
            (place.dp, 2 * chip + place.core),
        )

    def line_landed(self, hop):
        place = self.place
        chip = (place.chip + place.chips - hop) % place.chips
        remote(
            self.rows,
            self.line_buf.at[chip],
            self.send.at[hop],
            self.recv.at[hop],
            (place.dp, 2 * chip + place.core),
        ).wait_recv()

    def square_copy(self, hop):
        place = self.place
        target = (place.dp + hop) % 4
        at = place.chips + hop
        return remote(
            self.rows,
            self.square_buf.at[place.dp],
            self.send.at[at],
            self.recv.at[at],
            (target, place.me),
        )

    def square_landed(self, hop):
        place = self.place
        source = (place.dp + 4 - hop) % 4
        at = place.chips + hop
        remote(
            self.rows,
            self.square_buf.at[source],
            self.send.at[at],
            self.recv.at[at],
            (source, place.me),
        ).wait_recv()

    def put(self, value):
        if self.alone < self.rows.shape[0]:
            index = lax.broadcasted_iota(jnp.int32, value.shape, 0)
            value = jnp.where(index < self.alone, value, self.rows[...])
        self.rows[...] = value

    def begin(self):
        self.side_copy().start()

    def middle(self):
        self.side_copy().wait()
        self.put(self.rows[...] + self.side_buf[...])
        self.line_buf[self.place.chip] = self.rows[...]
        for hop in range(1, self.place.chips):
            self.line_copy(hop).start()

    def late(self):
        place = self.place
        for hop in range(1, place.chips):
            self.line_copy(hop).wait_send()
            self.line_landed(hop)
        value = self.line_buf[0]
        for chip in range(1, place.chips):
            value = value + self.line_buf[chip]
        self.put(value)
        self.square_buf[place.dp] = self.rows[...]
        for hop in range(1, 4):
            self.square_copy(hop).start()

    def end(self):
        for hop in range(1, 4):
            self.square_copy(hop).wait_send()
            self.square_landed(hop)
        value = self.square_buf[0]
        for device in range(1, 4):
            value = value + self.square_buf[device]
        self.rows[...] = value


def small_scratch(chips, rows, width):
    dma = pltpu.SemaphoreType.DMA
    return [
        pltpu.VMEM((rows, width), jnp.float32),
        pltpu.VMEM((chips, rows, width), jnp.float32),
        pltpu.VMEM((4, rows, width), jnp.float32),
        dma((chips + 4,)),
        dma((chips + 4,)),
    ]


def scatter_scratch(chips, count, width):
    low = jnp.bfloat16
    dma = pltpu.SemaphoreType.DMA
    return [
        pltpu.VMEM((count, width), jnp.float32),
        pltpu.VMEM((chips, count, width), low),
        pltpu.VMEM((chips, count, width), low),
        pltpu.VMEM((chips + 1, count, width), low),
        dma((chips,)),
        dma((chips,)),
        dma((chips, 4)),
        dma((chips + 1, 4)),
    ]


def alive(shape, axis, start, bounds):
    place = lax.broadcasted_iota(jnp.int32, shape, axis) + start
    return jnp.where((place >= bounds[0]) & (place < bounds[1]), 1.0, 0.0)


def by_rows(count, tile, action):
    def one(index, carry):
        action(pl.ds(pl.multiple_of(index * tile, tile), tile))
        return carry

    lax.fori_loop(0, count // tile, one, 0)


def attend_out_kernel(
    chips,
    mixed_hbm,
    offsets_ref,
    lengths_ref,
    out_hbm,
    rows_hbm,
    branch_ref,
    gain_ref,
    shift_ref,
    bias_ref,
    up_ref,
    down_ref,
    attended_ref,
    lse_ref,
    resid_ref,
    normed_ref,
    branch_whole,
    up_whole,
    down_whole,
    mixed_ref,
    out_ref,
    rows_ref,
    fetch_sem,
    seg_col_ref,
    seg_row_ref,
    score_ref,
    blocks,
    line_send,
    line_recv,
    up_send,
    up_recv,
    down_send,
    down_recv,
    own_sem,
    keep_sem,
    *scatter,
):
    place = Place(chips)
    bounds = (offsets_ref[0], offsets_ref[0] + lengths_ref[0])
    count = rows_ref.shape[0]
    fetched = fetch(
        [(mixed_hbm, mixed_ref), (out_hbm, out_ref), (rows_hbm, rows_ref)], fetch_sem
    )
    place.greet(True)

    def square(shard, whole, send, recv):
        half = shard.shape[0] // 2
        return SquareGather(
            place,
            shard,
            lambda owner: whole.at[owner],
            lambda owner, which: whole.at[owner, pl.ds(which * half, half)],
            send,
            recv,
        )

    up = square(up_ref, up_whole, up_send, up_recv)
    down = square(down_ref, down_whole, down_send, down_recv)
    up.begin()
    own = [
        pltpu.make_async_copy(up_ref, up_whole.at[place.dp], own_sem.at[0]),
        pltpu.make_async_copy(down_ref, down_whole.at[place.dp], own_sem.at[1]),
    ]
    own[0].start()
    own[1].start()

    def term(block, tile):
        span = pl.ds(pl.multiple_of(block * count, count), count)
        return jnp.dot(attended_ref[span, :], out_ref[tile], preferred_element_type=jnp.float32)

    def prepare(chip):
        def one(index, carry):
            attend_rows(
                chip * (2 * count // ATTEND_ROWS) + index,
                mixed_ref,
                seg_col_ref,
                seg_row_ref,
                attended_ref,
                lse_ref,
                score_ref,
            )
            return carry

        lax.fori_loop(0, 2 * count // ATTEND_ROWS, one, 0)

    def copy_in(span):
        blocks[place.me, span, :] = branch_ref[span, :]

    by_rows(count, 64, copy_in)
    line = LineGather(place, blocks, line_send, line_recv)
    line.begin()
    seg_row_ref[...] = alive(seg_row_ref.shape, 1, 0, bounds)

    def column(span):
        seg_col_ref[span, :] = alive((64, 1), 0, span.start, bounds)

    by_rows(seg_col_ref.shape[0], 64, column)
    for copy in fetched:
        copy.wait()
    sums = LineScatter(place, term, 4, scatter[:4], scatter[4:8], prepare)
    sums.begin()

    def keep(block, part):
        half = count // 2
        place_of = ((block // 2 * 2 + part) * 2 + block % 2) * half
        span = pl.ds(pl.multiple_of(place_of, half), half)
        source = blocks.at[block, pl.ds(part * half, half)]
        return pltpu.make_async_copy(source, branch_whole.at[span], keep_sem.at[block, part])

    def step(index, carry):
        sums.step(index, True)
        pl.when(index < chips - 1)(lambda: line.step(index + 1))

        @pl.when(index == 1)
        def _():
            up.middle()
            down.begin()

        pl.when(index == 2)(down.middle)
        return carry

    lax.fori_loop(0, chips, step, 0)
    total = scatter[0]

    def norm(span):
        resid = rows_ref[span, :].astype(jnp.float32) + total[span, :] + bias_ref[...]
        resid_ref[span, :] = resid
        normed_ref[span, :] = norm_rows(resid, gain_ref[...], shift_ref[...]).astype(jnp.bfloat16)

    by_rows(count, 64, norm)

    def store(block, carry):
        pl.when((block % 2 != place.core))(lambda: line.arrive(block // 2, block % 2))
        keep(block, 0).start()
        keep(block, 1).start()
        return carry

    lax.fori_loop(0, 2 * chips, store, 0)
    sums.finish()
    line.finish()
    up.end()
    down.end()
    up.finish()
    down.finish()
    own[0].wait()
    own[1].wait()

    def kept(block, carry):
        keep(block, 0).wait()
        keep(block, 1).wait()
        return carry

    lax.fori_loop(0, 2 * chips, kept, 0)


def attend_out_call(
    mixed, offsets, lengths, out_whole, rows, branch, gain, shift, bias, up, down, chips
):
    count, width = rows.shape
    local = mixed.shape[2]
    total = 2 * chips * count
    low = jnp.bfloat16
    vmem = pl.BlockSpec(memory_space=pltpu.VMEM)
    hbm = pl.BlockSpec(memory_space=pl.ANY)
    dma = pltpu.SemaphoreType.DMA
    return pl.pallas_call(
        functools.partial(attend_out_kernel, chips),
        out_shape=(
            jax.ShapeDtypeStruct((total, local), low),
            jax.ShapeDtypeStruct((total, 1 + local // HEAD_DIM), jnp.float32),
            jax.ShapeDtypeStruct((count, width), jnp.float32),
            jax.ShapeDtypeStruct((count, width), low),
            jax.ShapeDtypeStruct((total, width), low),
            jax.ShapeDtypeStruct((4,) + up.shape, low),
            jax.ShapeDtypeStruct((4,) + down.shape, low),
        ),
        in_specs=[hbm] + [pl.BlockSpec(memory_space=pltpu.SMEM)] * 2 + [hbm] * 2 + [vmem] * 6,
        out_specs=(vmem, vmem, vmem, vmem, hbm, hbm, hbm),
        scratch_shapes=[
            pltpu.VMEM(mixed.shape, low),
            pltpu.VMEM(out_whole.shape, low),
            pltpu.VMEM(rows.shape, low),
            dma((3,)),
            pltpu.VMEM((total, 1), jnp.float32),
            pltpu.VMEM((1, total), jnp.float32),
            pltpu.VMEM((local // HEAD_DIM, ATTEND_ROWS, total), jnp.float32),
            pltpu.VMEM((2 * chips, count, width), low),
            dma((3, chips)),
            dma((2 * chips,)),
            dma((4,)),
            dma((4,)),
            dma((4,)),
            dma((4,)),
            dma((2,)),
            dma((2 * chips, 2)),
        ]
        + scatter_scratch(chips, count, width),
        compiler_params=pltpu.CompilerParams(
            collective_id=1, has_side_effects=True, vmem_limit_bytes=VMEM_LIMIT
        ),
        cost_estimate=pl.CostEstimate(flops=10**11, bytes_accessed=0, transcendentals=0),
        name="attend_out",
    )(mixed, offsets, lengths, out_whole, rows, branch, gain, shift, bias, up, down)


def input_back_kernel(
    chips,
    stacked_hbm,
    mix_hbm,
    rows_hbm,
    resid_grad_hbm,
    gain_ref,
    row_sums_ref,
    bias_down_ref,
    mix_bias_ref,
    up_bias_ref,
    hidden_hbm,
    out_grad_hbm,
    normed_one_ref,
    normed_two_ref,
    grad_ref,
    late_out_ref,
    early_out_ref,
    mix_grad_hbm,
    up_grad_hbm,
    out_owned_hbm,
    mix_grad_ref,
    up_grad_ref,
    out_owned_ref,
    hat_buf,
    inverse_buf,
    emit_sem,
    stacked_ref,
    mix_ref,
    rows_ref,
    resid_grad_ref,
    hidden_ref,
    out_grad_ref,
    fetch_sem,
    columns_buf,
    columns_sem,
    *scatter,
):
    place = Place(chips)
    count = rows_ref.shape[0]
    fetched = fetch(
        [
            (stacked_hbm, stacked_ref),
            (mix_hbm, mix_ref),
            (hidden_hbm, hidden_ref),
            (out_grad_hbm, out_grad_ref),
            (rows_hbm, rows_ref),
            (resid_grad_hbm, resid_grad_ref),
        ],
        fetch_sem,
    )
    place.greet(True, True)
    fetched[0].wait()
    fetched[1].wait()
    local = mix_bias_ref.shape[1]
    units = up_bias_ref.shape[1]
    early_out_ref[0:3, :] = row_sums_ref[...]
    early_out_ref[3:4, :] = bias_down_ref[...]
    early_out_ref[4:5, :] = jnp.zeros((1, early_out_ref.shape[1]), jnp.float32)
    early_out_ref[4:5, 0:local] = mix_bias_ref[0:1, :]
    early_out_ref[4:5, local : 2 * local] = mix_bias_ref[1:2, :]
    early_out_ref[4:5, 2 * local : 2 * local + units] = up_bias_ref[...]
    early = SmallSum(place, early_out_ref, 4, scatter[16:19], scatter[19:21])
    late = SmallSum(place, late_out_ref, late_out_ref.shape[0], scatter[21:24], scatter[24:26])

    def term(block, tile):
        span = pl.ds(pl.multiple_of(block * count, count), count)
        result = None
        for part in range(3):
            product = lax.dot_general(
                stacked_ref[part, span, :],
                mix_ref[part, tile],
                TURNED,
                preferred_element_type=jnp.float32,
            )
            result = product if result is None else result + product
        return result

    sums = LineScatter(place, term, 4, scatter[:4], scatter[4:8])
    sums.begin()
    early.begin()
    half_columns = columns_buf.shape[2]

    def load(which, owner, half):
        start = pl.multiple_of((2 * owner + half) * half_columns, half_columns)
        source = (normed_one_ref, normed_two_ref)[which]
        return pltpu.make_async_copy(
            source.at[:, pl.ds(start, half_columns)], columns_buf.at[which], columns_sem.at[which]
        )

    def mix_piece(owner, half):
        load(0, owner, half).wait()
        return jnp.stack(
            [
                lax.dot_general(
                    columns_buf[0],
                    stacked_ref[part],
                    CROSSED,
                    preferred_element_type=jnp.float32,
                )
                for part in range(3)
            ]
        )

    def up_piece(owner, half):
        load(1, owner, half).wait()
        return lax.dot_general(
            columns_buf[1], hidden_ref[...], CROSSED, preferred_element_type=jnp.float32
        )

    out_units = out_grad_ref.shape[0] // 2
    out_columns = out_grad_ref.shape[1] // 4

    def out_piece(owner, half):
        units = pl.ds(pl.multiple_of(half * out_units, out_units), out_units)
        columns = pl.ds(pl.multiple_of(owner * out_columns, 128), out_columns)
        return out_grad_ref[units, columns]

    out = SquareScatter(place, out_piece, out_owned_ref, scatter[26:28], scatter[28:30])
    mix = SquareScatter(place, mix_piece, mix_grad_ref, scatter[8:10], scatter[10:12])
    up = SquareScatter(place, up_piece, up_grad_ref, scatter[12:14], scatter[14:16])

    load(1, place.across, 0).start()
    load(0, place.across, 0).start()

    def stage(kind):
        def one(way, carry):
            for which, matrix in ((1, up), (0, mix)):
                matrix.one(kind, way)
                owner, half = matrix.following(kind, way)
                more = (way == 0) | (kind < 3)
                pl.when(more)(lambda: load(which, owner, half).start())
            out.one(kind, way)
            return carry

        lax.fori_loop(0, 2, one, 0)

    for copy in fetched[2:]:
        copy.wait()

    leaving = [
        pltpu.make_async_copy(source, target, emit_sem.at[index])
        for index, (source, target) in enumerate(
            [
                (up_grad_ref, up_grad_hbm),
                (mix_grad_ref, mix_grad_hbm),
                (out_owned_ref, out_owned_hbm),
            ]
        )
    ]

    def hats(span):
        _, hat, inverse = layer_norm_parts(
            rows_ref[span, :].astype(jnp.float32), gain_ref[...], 0.0
        )
        hat_buf[span, :] = hat
        inverse_buf[span, :] = inverse

    def step(index, carry):
        @pl.when(index == 3)
        def _():
            stage(3)
            by_rows(count, 64, hats)

        sums.step(index)
        for kind in range(3):

            @pl.when(index == kind)
            def _():
                stage(kind)
                if kind == 1:
                    early.middle()
                if kind == 2:
                    early.late()

        return carry

    lax.fori_loop(0, chips, step, 0)
    total = scatter[0]
    late_out_ref[...] = jnp.zeros_like(late_out_ref)

    def columns(span):
        one_grad = total[span, :]
        late_out_ref[0:1, :] += jnp.sum(one_grad * hat_buf[span, :], axis=0, keepdims=True)
        late_out_ref[1:2, :] += jnp.sum(one_grad, axis=0, keepdims=True)

    def back(span):
        grad_ref[span, :] = resid_grad_ref[span, :] + layer_norm_back(
            total[span, :], hat_buf[span, :], inverse_buf[span, :], gain_ref[...]
        )

    by_rows(count, 64, columns)
    late.begin()
    up.end()
    leaving[0].start()
    late.middle()
    mix.end()
    leaving[1].start()
    by_rows(count, 64, back)
    late.late()
    out.end()
    leaving[2].start()
    early.end()
    sums.finish()
    late.end()
    for copy in leaving:
        copy.wait()


def input_back_call(
    stacked, mix_whole, rows, resid_grad, gain, smalls, hidden, out_grad, normed_one, normed_two, chips
):
    count, width = rows.shape
    total, units = hidden.shape
    local = stacked.shape[2]
    half = width // 8
    vmem = pl.BlockSpec(memory_space=pltpu.VMEM)
    hbm = pl.BlockSpec(memory_space=pl.ANY)
    return pl.pallas_call(
        functools.partial(input_back_kernel, chips),
        out_shape=(
            jax.ShapeDtypeStruct((count, width), jnp.float32),
            jax.ShapeDtypeStruct((2, width), jnp.float32),
            jax.ShapeDtypeStruct((5, width), jnp.float32),
            jax.ShapeDtypeStruct((2, 3, half, local), jnp.float32),
            jax.ShapeDtypeStruct((2, half, units), jnp.float32),
            jax.ShapeDtypeStruct((2, local // 2, width // 4), jnp.float32),
        ),
        in_specs=[hbm] * 4 + [vmem] * 5 + [hbm] * 4,
        out_specs=(vmem,) * 3 + (hbm,) * 3,
        scratch_shapes=[
            pltpu.VMEM((2, 3, half, local), jnp.float32),
            pltpu.VMEM((2, half, units), jnp.float32),
            pltpu.VMEM((2, local // 2, width // 4), jnp.float32),
            pltpu.VMEM((count, width), jnp.float32),
            pltpu.VMEM((count, 1), jnp.float32),
            pltpu.SemaphoreType.DMA((3,)),
            pltpu.VMEM(stacked.shape, jnp.bfloat16),
            pltpu.VMEM(mix_whole.shape, jnp.bfloat16),
            pltpu.VMEM(rows.shape, jnp.bfloat16),
            pltpu.VMEM(resid_grad.shape, jnp.float32),
            pltpu.VMEM(hidden.shape, jnp.bfloat16),
            pltpu.VMEM(out_grad.shape, jnp.float32),
            pltpu.SemaphoreType.DMA((6,)),
            pltpu.VMEM((2, total, half), jnp.bfloat16),
            pltpu.SemaphoreType.DMA((2,)),
        ]
        + scatter_scratch(chips, count, width)
        + square_scratch((3, half, local))
        + square_scratch((half, units))
        + small_scratch(chips, 5, width)
        + small_scratch(chips, 2, width)
        + square_scratch((local // 2, width // 4)),
        compiler_params=pltpu.CompilerParams(
            collective_id=2, has_side_effects=True, vmem_limit_bytes=VMEM_LIMIT
        ),
        cost_estimate=pl.CostEstimate(flops=10**11, bytes_accessed=0, transcendentals=0),
        name="input_back",
    )(stacked, mix_whole, rows, resid_grad, gain, *smalls, hidden, out_grad, normed_one, normed_two)


GELU_SLOPE = 0.7978845608028654
GELU_CUBE = 0.044715


def gelu_parts(hidden):
    square = hidden * hidden
    bend = jnp.tanh(GELU_SLOPE * hidden * (1.0 + GELU_CUBE * square))
    lift = 0.5 * (1.0 + bend)
    slope = lift + 0.5 * hidden * (1.0 - bend * bend) * (
        GELU_SLOPE * (1.0 + 3.0 * GELU_CUBE * square)
    )
    return hidden * lift, slope


def feed_kernel(
    chips,
    parts,
    normed_ref,
    branch_ref,
    up_hbm,
    down_hbm,
    bias_ref,
    resid_hbm,
    own_branch_hbm,
    gain_ref,
    normed_whole,
    active_hbm,
    hidden_hbm,
    grad_ref,
    grad_low_ref,
    sums_ref,
    bias_grad_ref,
    up_ref,
    down_ref,
    resid_ref,
    own_branch_ref,
    active_ref,
    hidden_ref,
    fetch_sem,
    emit_sem,
    blocks,
    branch_buf,
    work,
    hold,
    side_out,
    side_in,
    line_in,
    line_send,
    line_recv,
    keep_sem,
    load_sem,
    side_send,
    side_recv,
    out_send,
    out_recv,
):
    place = Place(chips)
    count = normed_ref.shape[0]
    rows = count // parts
    pair = 2 * rows
    last = chips - 1
    fetched = fetch(
        [
            (up_hbm, up_ref),
            (down_hbm, down_ref),
            (resid_hbm, resid_ref),
            (own_branch_hbm, own_branch_ref),
        ],
        fetch_sem,
    )
    place.greet(False)

    def fill(part, carry):
        block = 2 * (place.chip * parts + part) + place.core
        blocks[block] = normed_ref[pl.ds(pl.multiple_of(part * rows, rows), rows), :]
        return carry

    lax.fori_loop(0, parts, fill, 0)
    line = LineGather(place, blocks, line_send, line_recv, parts)
    line.begin_part(0)
    line.copy(2, place.chip, 1).start()
    pl.when(place.has_up & jnp.logical_not(place.has_down))(
        lambda: line.copy(0, place.chip, 1).start()
    )
    pl.when(place.has_down & jnp.logical_not(place.has_up))(
        lambda: line.copy(1, place.chip, 1).start()
    )
    bias_grad_ref[...] = jnp.zeros_like(bias_grad_ref)

    def piece_span(piece):
        return pl.ds(pl.multiple_of(piece * pair, pair), pair)

    def load(piece, slot):
        return pltpu.make_async_copy(
            branch_ref.at[piece_span(piece)], branch_buf.at[slot], load_sem.at[slot]
        )

    def keep(piece, core):
        span = pl.ds(pl.multiple_of(piece * pair + core * rows, rows), rows)
        return pltpu.make_async_copy(
            blocks.at[2 * piece + core], normed_whole.at[span], keep_sem.at[piece, core]
        )

    def side_copy(piece):
        return remote(
            side_out.at[piece],
            side_in.at[piece],
            side_send.at[piece],
            side_recv.at[piece],
            place.side,
        )

    chunk = normed_ref.shape[1] // 4

    def line_copy(way, chip, part, tile):
        piece = chip * parts + part
        next_chip = place.chip + 1 - 2 * way
        slot = jnp.where((way == 1) & (chip == next_chip), chips * parts + part, piece)
        span = slice(tile * chunk, (tile + 1) * chunk)
        return remote(
            line_in.at[piece, :, span],
            line_in.at[slot, :, span],
            out_send.at[piece, tile],
            out_recv.at[slot, tile],
            (place.up, place.down)[way],
        )

    def line_landed(way, chip, part, tile):
        piece = chip * parts + part
        slot = jnp.where((way == 1) & (chip == place.chip), chips * parts + part, piece)
        span = slice(tile * chunk, (tile + 1) * chunk)
        remote(
            line_in.at[slot, :, span],
            line_in.at[slot, :, span],
            out_send.at[piece, tile],
            out_recv.at[slot, tile],
            (place.up, place.down)[way],
        ).wait_recv()
        return slot

    def emit(piece):
        span = piece_span(piece)
        return [
            pltpu.make_async_copy(active_ref.at[span], active_hbm.at[span], emit_sem.at[piece, 0]),
            pltpu.make_async_copy(hidden_ref.at[span], hidden_hbm.at[span], emit_sem.at[piece, 1]),
        ]

    width = 512
    tiles = up_ref.shape[2] // width

    def compute(chip, part, side):
        piece = chip * parts + part
        keep(piece, 0).start()
        keep(piece, 1).start()
        span = piece_span(piece)
        own_rows = blocks[pl.ds(2 * piece, 2)].reshape(pair, -1)
        load(piece, side).wait()

        def tile(index, carry):
            units = pl.ds(pl.multiple_of(index * width, width), width)
            hidden = jnp.dot(
                own_rows,
                up_ref[:, :, units].reshape(-1, width),
                preferred_element_type=jnp.float32,
            )
            active, slope = gelu_parts(hidden + bias_ref[:, units])
            active_ref[span, units] = active.astype(jnp.bfloat16)
            grad = None
            for owner in range(4):
                columns = down_ref.shape[2]
                product = lax.dot_general(
                    branch_buf[side, :, owner * columns : (owner + 1) * columns],
                    down_ref[owner, units, :],
                    TURNED,
                    preferred_element_type=jnp.float32,
                )
                grad = product if grad is None else grad + product
            low = (grad * slope).astype(jnp.bfloat16)
            hidden_ref[span, units] = low
            bias_grad_ref[:, units] += jnp.sum(low.astype(jnp.float32), axis=0, keepdims=True)
            return carry

        lax.fori_loop(0, tiles, tile, 0)
        low = hidden_ref[span, :]
        depth = up_ref.shape[1]
        for owner in range(4):
            columns = slice(owner * depth, (owner + 1) * depth)
            product = lax.dot_general(
                low, up_ref[owner], TURNED, preferred_element_type=jnp.float32
            )
            work[:, :, columns] = product.reshape(2, rows, depth)
        side_out[piece] = work[1 - place.core].astype(jnp.bfloat16)
        side_copy(piece).start()
        hold[piece] = work[place.core]
        for copy in emit(piece):
            copy.start()

    def pass_on(way, chip, part):
        piece = chip * parts + part
        side_copy(piece).wait_recv()
        behind = (place.has_down, place.has_up)[way]
        for tile in range(4):
            span = slice(tile * chunk, (tile + 1) * chunk)
            total = hold[piece, :, span] + side_in[piece, :, span].astype(jnp.float32)

            @pl.when(behind)
            def _():
                slot = line_landed(way, chip, part, tile)
                line_in[piece, :, span] = (
                    total + line_in[slot, :, span].astype(jnp.float32)
                ).astype(jnp.bfloat16)

            @pl.when(jnp.logical_not(behind))
            def _():
                line_in[piece, :, span] = total.astype(jnp.bfloat16)

            line_copy(way, chip, part, tile).start()

    def coming(index, side):
        count_beyond = jnp.where(side == 0, place.chip, last - place.chip)
        early = index <= count_beyond
        distance = jnp.where(early, index, 2 * count_beyond + 1 - index)
        valid = (index == 0) | (index <= 2 * count_beyond)
        chip = jnp.where(index == 0, place.chip, place.chip + distance * (2 * side - 1))
        part = jnp.where(index == 0, side, jnp.where(early, 0, 1))
        return valid, chip, part, count_beyond

    def turn(index, carry):
        def ahead(side, inner):
            valid, chip, part, _ = coming(index, side)
            pl.when(valid)(lambda: load(chip * parts + part, side).start())
            return inner

        lax.fori_loop(0, 2, ahead, 0)

        @pl.when(index > 0)
        def _():
            for side in range(2):
                valid, chip, part, count_beyond = coming(index, side)
                onward = (place.has_up, place.has_down)[side]

                @pl.when(valid)
                def _():
                    line.arrive(chip, place.core, part)
                    pl.when(onward)(lambda: line.copy(side, chip, part).start())
                    pl.when(onward & (index == 2 * count_beyond))(
                        lambda: line.copy(side, place.chip, 1).start()
                    )
                    line.copy(2, chip, part).start()

        def one(side, inner):
            valid, chip, part, _ = coming(index, side)

            @pl.when(valid)
            def _():
                line.arrive(chip, 1 - place.core, part)
                compute(chip, part, side)

            return inner

        lax.fori_loop(0, 2, one, 0)
        mirrored = last - place.chip
        for part in range(2):
            reach = index - place.chip if part == 0 else 2 * last + 1 + place.chip - index

            @pl.when((reach > place.chip) & (reach < chips))
            def _():
                pass_on(0, reach, part)

            back = index - mirrored if part == 0 else 2 * last + 1 + mirrored - index

            @pl.when((back > mirrored) & (back < chips))
            def _():
                pass_on(1, last - back, part)

        return carry

    fetched[0].wait()
    fetched[1].wait()
    lax.fori_loop(0, 2 * last + 1, turn, 0)
    sums_ref[...] = jnp.zeros_like(sums_ref)
    fetched[2].wait()
    fetched[3].wait()

    def own_part(part, carry):
        piece = place.chip * parts + part
        side_copy(piece).wait_recv()
        hold[piece] += side_in[piece].astype(jnp.float32)

        for tile in range(4):

            @pl.when(place.has_down)
            def _():
                line_landed(0, place.chip, part, tile)

            @pl.when(place.has_up)
            def _():
                line_landed(1, place.chip, part, tile)

        pieces_end = chips * parts

        @pl.when(place.has_down)
        def _():
            hold[piece] += line_in[piece].astype(jnp.float32)

        @pl.when(place.has_up)
        def _():
            hold[piece] += line_in[pieces_end + part].astype(jnp.float32)

        tile = 64

        def back(index, inner):
            here = pl.ds(pl.multiple_of(index * tile, tile), tile)
            span = pl.ds(pl.multiple_of(part * rows + index * tile, tile), tile)
            two_grad = hold[piece, here, :]
            _, hat, inverse = layer_norm_parts(resid_ref[span, :], gain_ref[...], 0.0)
            grad = own_branch_ref[span, :].astype(jnp.float32) + layer_norm_back(
                two_grad, hat, inverse, gain_ref[...]
            )
            grad_ref[span, :] = grad
            grad_low_ref[span, :] = grad.astype(jnp.bfloat16)
            sums_ref[0:1, :] += jnp.sum(two_grad * hat, axis=0, keepdims=True)
            sums_ref[1:2, :] += jnp.sum(two_grad, axis=0, keepdims=True)
            sums_ref[2:3, :] += jnp.sum(grad, axis=0, keepdims=True)
            return inner

        lax.fori_loop(0, rows // tile, back, 0)
        return carry

    lax.fori_loop(0, parts, own_part, 0)
    line.finish()

    def drain(piece, carry):
        side_copy(piece).wait_send()
        keep(piece, 0).wait()
        keep(piece, 1).wait()
        for copy in emit(piece):
            copy.wait()
        for tile in range(4):
            pl.when(piece // parts != place.chip)(
                lambda: line_copy(0, piece // parts, piece % parts, tile).wait_send()
            )
        return carry

    lax.fori_loop(0, chips * parts, drain, 0)


def feed_call(normed, branch, up_whole, down_whole, bias, resid, own_branch, gain, chips):
    count, width = normed.shape
    total = 2 * chips * count
    units = up_whole.shape[2]
    parts = 2
    rows = count // parts
    low = jnp.bfloat16
    vmem = pl.BlockSpec(memory_space=pltpu.VMEM)
    hbm = pl.BlockSpec(memory_space=pl.ANY)
    dma = pltpu.SemaphoreType.DMA
    pieces = chips * parts
    return pl.pallas_call(
        functools.partial(feed_kernel, chips, parts),
        out_shape=(
            jax.ShapeDtypeStruct((total, width), low),
            jax.ShapeDtypeStruct((total, units), low),
            jax.ShapeDtypeStruct((total, units), low),
            jax.ShapeDtypeStruct((count, width), jnp.float32),
            jax.ShapeDtypeStruct((count, width), low),
            jax.ShapeDtypeStruct((3, width), jnp.float32),
            jax.ShapeDtypeStruct((1, units), jnp.float32),
        ),
        in_specs=[vmem, hbm, hbm, hbm, vmem, hbm, hbm, vmem],
        out_specs=(hbm,) * 3 + (vmem,) * 4,
        scratch_shapes=[
            pltpu.VMEM(up_whole.shape, low),
            pltpu.VMEM(down_whole.shape, low),
            pltpu.VMEM(resid.shape, jnp.float32),
            pltpu.VMEM(own_branch.shape, low),
            pltpu.VMEM((total, units), low),
            pltpu.VMEM((total, units), low),
            dma((4,)),
            dma((pieces, 2)),
            pltpu.VMEM((2 * pieces, rows, width), low),
            pltpu.VMEM((2, 2 * rows, width), low),
            pltpu.VMEM((2, rows, width), jnp.float32),
            pltpu.VMEM((pieces, rows, width), jnp.float32),
            pltpu.VMEM((pieces, rows, width), low),
            pltpu.VMEM((pieces, rows, width), low),
            pltpu.VMEM((pieces + parts, rows, width), low),
            dma((3, pieces)),
            dma((2 * pieces,)),
            dma((pieces, 2)),
            dma((2,)),
            dma((pieces,)),
            dma((pieces,)),
            dma((pieces, 4)),
            dma((pieces + parts, 4)),
        ],
        compiler_params=pltpu.CompilerParams(
            collective_id=3, has_side_effects=True, vmem_limit_bytes=VMEM_LIMIT
        ),
        cost_estimate=pl.CostEstimate(flops=10**11, bytes_accessed=0, transcendentals=0),
        name="feed",
    )(normed, branch, up_whole, down_whole, bias, resid, own_branch, gain)


def branch_back_kernel(
    chips,
    parts,
    branch_ref,
    active_hbm,
    down_hbm,
    attended_hbm,
    out_hbm,
    shift_ref,
    offsets_ref,
    lengths_ref,
    mixed_hbm,
    aux_hbm,
    resid_ref,
    cotangent_ref,
    stacked_hbm,
    bias_sum_ref,
    down_grad_hbm,
    out_grad_hbm,
    output_ref,
    blocks,
    stacked_ref,
    down_grad_ref,
    out_grad_ref,
    emit_sem,
    active_ref,
    down_ref,
    attended_ref,
    out_ref,
    mixed_ref,
    aux_ref,
    fetch_sem,
    seg_row_ref,
    block_buf,
    columns_buf,
    resid_buf,
    key_sum,
    value_sum,
    line_send,
    line_recv,
    columns_sem,
    block_sem,
    *scatter,
):
    place = Place(chips)
    bounds = (offsets_ref[0], offsets_ref[0] + lengths_ref[0])
    count = branch_ref.shape[0]
    rows = count // parts
    fetched = fetch(
        [
            (active_hbm, active_ref),
            (down_hbm, down_ref),
            (attended_hbm, attended_ref),
            (out_hbm, out_ref),
            (mixed_hbm, mixed_ref),
            (aux_hbm, aux_ref),
            (resid_ref, resid_buf),
        ],
        fetch_sem,
    )
    place.greet(True)
    line = LineGather(place, blocks, line_send, line_recv, 1, branch_ref)
    line.begin()

    def term(block, tile):
        chip, core = block // 2, block % 2
        taken = []
        for part in range(parts):
            start = ((chip * parts + part) * 2 + core) * rows
            taken.append(active_ref[pl.ds(pl.multiple_of(start, rows), rows), :])
        return jnp.dot(
            jnp.concatenate(taken, axis=0), down_ref[tile], preferred_element_type=jnp.float32
        )

    fetched[0].wait()
    fetched[1].wait()
    sums = LineScatter(place, term, 4, scatter[:4], scatter[4:8])
    sums.begin()
    seg_row_ref[...] = alive(seg_row_ref.shape, 1, 0, bounds)
    out_grad_ref[...] = jnp.zeros_like(out_grad_ref)
    key_sum[...] = jnp.zeros_like(key_sum)
    value_sum[...] = jnp.zeros_like(value_sum)
    bias_sum_ref[...] = jnp.zeros_like(bias_sum_ref)
    down_units = down_ref.shape[1] // 2
    down_columns = down_ref.shape[2]

    def load_columns(owner):
        return pltpu.make_async_copy(
            cotangent_ref.at[:, pl.ds(pl.multiple_of(owner * down_columns, 128), down_columns)],
            columns_buf,
            columns_sem,
        )

    load_columns(place.across).start()

    def down_piece(owner, half):
        units = pl.ds(pl.multiple_of(half * down_units, down_units), down_units)
        return lax.dot_general(
            active_ref[:, units], columns_buf[...], CROSSED, preferred_element_type=jnp.float32
        )

    down = SquareScatter(place, down_piece, down_grad_ref, scatter[8:10], scatter[10:12])
    def down_stage(kind):
        def one(way, carry):
            fresh = (way == 0) if kind in (0, 3) else ((way >= 0) if kind == 1 else (way == 1))
            pl.when(fresh)(lambda: load_columns(place.dp).wait())
            down.one(kind, way)
            owner, _ = down.following(kind, way)
            more = (way == 1) if kind == 0 else ((way == 0) if kind == 1 else (way >= 0))
            if kind < 3:
                pl.when(more)(lambda: load_columns(owner).start())
            return carry

        lax.fori_loop(0, 2, one, 0)

    def load_part(source, owner):
        columns = out_ref.shape[2]
        span = slice(owner * columns, (owner + 1) * columns)
        return pltpu.make_async_copy(source.at[:, span], block_buf.at[:, span], block_sem.at[owner])

    def load_block(block):
        mine = block == place.me

        @pl.when(mine)
        def _():
            for owner in range(4):
                load_part(branch_ref, owner).start()

        @pl.when(jnp.logical_not(mine))
        def _():
            for owner in range(4):
                load_part(blocks.at[block], owner).start()

    def take(block):
        span = pl.ds(pl.multiple_of(block * count, count), count)
        columns = out_ref.shape[2]
        load_block(block)
        result = None
        for owner in range(4):
            load_part(branch_ref, owner).wait()
            here = block_buf[:, owner * columns : (owner + 1) * columns]
            product = lax.dot_general(
                here, out_ref[owner], TURNED, preferred_element_type=jnp.float32
            )
            result = product if result is None else result + product
            out_grad_ref[:, owner * columns : (owner + 1) * columns] += lax.dot_general(
                attended_ref[span, :], here, CROSSED, preferred_element_type=jnp.float32
            )
        grad = result.astype(jnp.bfloat16)
        attend_back_rows(
            block,
            grad,
            attended_ref,
            mixed_ref,
            aux_ref,
            seg_row_ref,
            stacked_ref,
            key_sum,
            value_sum,
            bias_sum_ref,
        )

    for copy in fetched[2:-1]:
        copy.wait()
    leaving = [
        pltpu.make_async_copy(source, target, emit_sem.at[index])
        for index, (source, target) in enumerate(
            [
                (stacked_ref, stacked_hbm),
                (out_grad_ref, out_grad_hbm),
                (down_grad_ref, down_grad_hbm),
            ]
        )
    ]

    def settle():
        stacked_ref[1] = (key_sum[...] * HEAD_DIM ** (-0.5)).astype(jnp.bfloat16)
        value_grad = value_sum[...].astype(jnp.bfloat16)
        stacked_ref[2] = value_grad
        leaving[0].start()
        leaving[1].start()
        bias_sum_ref[1:2, :] = jnp.sum(value_grad.astype(jnp.float32), axis=0, keepdims=True)
        down.end()
        leaving[2].start()

    def step(index, carry):
        def one(side, inner):
            chip = place.chip + index * (2 * (side % 2) - 1)
            core = (place.core + side // 2) % 2

            @pl.when((chip >= 0) & (chip < chips) & ((index > 0) | (side % 2 == 0)))
            def _():
                pl.when(side >= 2)(lambda: line.arrive(chip, core))
                take(2 * chip + core)

            return inner

        lax.fori_loop(0, 4, one, 0)
        for kind in range(4):
            pl.when(index == kind)(lambda: down_stage(kind))
        pl.when(index < chips - 1)(lambda: line.step(index + 1))
        pl.when(index == chips - 1)(settle)
        sums.step(index)
        return carry

    lax.fori_loop(0, chips, step, 0)
    total = scatter[0]
    fetched[-1].wait()

    def emit(span):
        result = resid_buf[span, :] + total[span, :] + shift_ref[...]
        live = alive((64, 1), 0, place.me * count + span.start, bounds)
        output_ref[span, :] = jnp.where(live > 0, result, 0.0).astype(jnp.bfloat16)

    by_rows(count, 64, emit)
    sums.finish()
    line.finish()
    for copy in leaving:
        copy.wait()


def branch_back_call(
    branch,
    active,
    down_whole,
    attended,
    out_whole,
    shift,
    offsets,
    lengths,
    mixed,
    aux,
    resid,
    cotangent,
    chips,
):
    count, width = branch.shape
    total, local = attended.shape
    _, units, columns = down_whole.shape
    low = jnp.bfloat16
    vmem = pl.BlockSpec(memory_space=pltpu.VMEM)
    hbm = pl.BlockSpec(memory_space=pl.ANY)
    dma = pltpu.SemaphoreType.DMA
    return pl.pallas_call(
        functools.partial(branch_back_kernel, chips, 2),
        out_shape=(
            jax.ShapeDtypeStruct((3, total, local), low),
            jax.ShapeDtypeStruct((2, local), jnp.float32),
            jax.ShapeDtypeStruct((2, units // 2, columns), jnp.float32),
            jax.ShapeDtypeStruct((local, width), jnp.float32),
            jax.ShapeDtypeStruct((count, width), low),
            jax.ShapeDtypeStruct((2 * chips, count, width), low),
        ),
        in_specs=[hbm] * 5 + [vmem] + [pl.BlockSpec(memory_space=pltpu.SMEM)] * 2 + [hbm] * 4,
        out_specs=(hbm, vmem, hbm, hbm, vmem, hbm),
        scratch_shapes=[
            pltpu.VMEM((3, total, local), low),
            pltpu.VMEM((2, units // 2, columns), jnp.float32),
            pltpu.VMEM((local, width), jnp.float32),
            dma((3,)),
            pltpu.VMEM(active.shape, low),
            pltpu.VMEM(down_whole.shape, low),
            pltpu.VMEM(attended.shape, low),
            pltpu.VMEM(out_whole.shape, low),
            pltpu.VMEM(mixed.shape, low),
            pltpu.VMEM(aux.shape, jnp.float32),
            dma((7,)),
            pltpu.VMEM((1, total), jnp.float32),
            pltpu.VMEM((count, width), low),
            pltpu.VMEM((total, columns), low),
            pltpu.VMEM((count, width), jnp.float32),
            pltpu.VMEM((total, local), jnp.float32),
            pltpu.VMEM((total, local), jnp.float32),
            dma((3, chips)),
            dma((2 * chips,)),
            dma,
            dma((4,)),
        ]
        + scatter_scratch(chips, count, width)
        + square_scratch((units // 2, columns)),
        compiler_params=pltpu.CompilerParams(
            collective_id=4, has_side_effects=True, vmem_limit_bytes=VMEM_LIMIT
        ),
        cost_estimate=pl.CostEstimate(flops=10**11, bytes_accessed=0, transcendentals=0),
        name="branch_back",
    )(
        branch,
        active,
        down_whole,
        attended,
        out_whole,
        shift,
        offsets,
        lengths,
        mixed,
        aux,
        resid,
        cotangent,
    )


ATTEND_ROWS = 256
ATTEND_KEYS = 512


def tile_mask(row_block, key_block, seg_col_ref, seg_row_ref):
    rows = lax.broadcasted_iota(jnp.int32, (ATTEND_ROWS, ATTEND_KEYS), 0)
    keys = lax.broadcasted_iota(jnp.int32, (ATTEND_ROWS, ATTEND_KEYS), 1)
    causal = keys - rows <= row_block * ATTEND_ROWS - key_block * ATTEND_KEYS
    row_span = pl.ds(pl.multiple_of(row_block * ATTEND_ROWS, ATTEND_ROWS), ATTEND_ROWS)
    key_span = pl.ds(pl.multiple_of(key_block * ATTEND_KEYS, ATTEND_KEYS), ATTEND_KEYS)
    return causal & (seg_col_ref[row_span, 0:1] == seg_row_ref[:, key_span])


def attend_rows(
    row_block, mixed_ref, seg_col_ref, seg_row_ref, attended_ref, lse_ref, score_ref
):
    scale = HEAD_DIM ** (-0.5)
    heads = range(mixed_ref.shape[2] // HEAD_DIM)
    lanes = [slice(head * HEAD_DIM, (head + 1) * HEAD_DIM) for head in heads]
    row_span = pl.ds(pl.multiple_of(row_block * ATTEND_ROWS, ATTEND_ROWS), ATTEND_ROWS)
    count = (row_block * ATTEND_ROWS) // ATTEND_KEYS + 1
    queries = [mixed_ref[0, row_span, lanes[head]] for head in heads]

    def span_of(key_block):
        return pl.ds(pl.multiple_of(key_block * ATTEND_KEYS, ATTEND_KEYS), ATTEND_KEYS)

    def score(key_block, peaks):
        key_span = span_of(key_block)
        mask = tile_mask(row_block, key_block, seg_col_ref, seg_row_ref)
        results = []
        for head in heads:
            scores = lax.dot_general(
                queries[head],
                mixed_ref[1, key_span, lanes[head]],
                TURNED,
                preferred_element_type=jnp.float32,
            )
            scores = jnp.where(mask, scores * scale, MASK_FILL)
            score_ref[head, :, key_span] = scores
            peak = peaks[head]
            for part in range(ATTEND_KEYS // 128):
                peak = jnp.maximum(peak, scores[:, part * 128 : (part + 1) * 128])
            results.append(peak)
        return tuple(results)

    filled = jnp.full((ATTEND_ROWS, 128), MASK_FILL, jnp.float32)
    peaks = lax.fori_loop(0, count, score, (filled,) * len(heads))
    peaks = [jnp.max(peak, axis=1, keepdims=True) for peak in peaks]

    def weigh(key_block, masses):
        key_span = span_of(key_block)
        results = []
        for head in heads:
            weights = jnp.exp(score_ref[head, :, key_span] - peaks[head])
            score_ref[head, :, key_span] = weights
            mass = masses[head]
            for part in range(ATTEND_KEYS // 128):
                mass = mass + weights[:, part * 128 : (part + 1) * 128]
            results.append(mass)
        return tuple(results)

    nothing = jnp.zeros((ATTEND_ROWS, 128), jnp.float32)
    masses = lax.fori_loop(0, count, weigh, (nothing,) * len(heads))
    masses = [jnp.sum(mass, axis=1, keepdims=True) for mass in masses]
    inverses = [1.0 / mass for mass in masses]
    lse_ref[row_span, 0:1] = seg_col_ref[row_span, :]
    for head in heads:
        lse_ref[row_span, head + 1 : head + 2] = peaks[head] + jnp.log(masses[head])

    def gather(key_block, totals):
        key_span = span_of(key_block)
        results = []
        for head in heads:
            probs = (score_ref[head, :, key_span] * inverses[head]).astype(jnp.bfloat16)
            results.append(
                totals[head]
                + jnp.dot(
                    probs,
                    mixed_ref[2, key_span, lanes[head]],
                    preferred_element_type=jnp.float32,
                )
            )
        return tuple(results)

    empty = jnp.zeros((ATTEND_ROWS, HEAD_DIM), jnp.float32)
    totals = lax.fori_loop(0, count, gather, (empty,) * len(heads))
    for head in heads:
        attended_ref[row_span, lanes[head]] = totals[head].astype(jnp.bfloat16)


def attend_back_rows(
    row_block,
    grads,
    attended_ref,
    mixed_ref,
    aux_ref,
    seg_row_ref,
    stacked_ref,
    key_sum,
    value_sum,
    bias_sum,
):
    scale = HEAD_DIM ** (-0.5)
    row_span = pl.ds(pl.multiple_of(row_block * ATTEND_ROWS, ATTEND_ROWS), ATTEND_ROWS)
    count = (row_block * ATTEND_ROWS) // ATTEND_KEYS + 1
    row_live = seg_row_ref[:, row_span]
    heads = []
    for head in range(mixed_ref.shape[2] // HEAD_DIM):
        lanes = slice(head * HEAD_DIM, (head + 1) * HEAD_DIM)
        grad = grads[:, lanes]
        product = grad.astype(jnp.float32) * attended_ref[row_span, lanes].astype(jnp.float32)
        delta = jnp.sum(product, axis=1, keepdims=True).reshape(1, ATTEND_ROWS)
        lse = aux_ref[row_span, head + 1 : head + 2].reshape(1, ATTEND_ROWS)
        heads.append((lanes, mixed_ref[0, row_span, lanes], grad, lse, delta))

    def one(key_block, totals):
        key_span = pl.ds(pl.multiple_of(key_block * ATTEND_KEYS, ATTEND_KEYS), ATTEND_KEYS)
        keys = lax.broadcasted_iota(jnp.int32, (ATTEND_KEYS, ATTEND_ROWS), 0)
        rows = lax.broadcasted_iota(jnp.int32, (ATTEND_KEYS, ATTEND_ROWS), 1)
        allowed = (keys - rows <= row_block * ATTEND_ROWS - key_block * ATTEND_KEYS) & (
            aux_ref[key_span, 0:1] == row_live
        )
        results = []
        for (lanes, query, grad, lse, delta), total in zip(heads, totals):
            key = mixed_ref[1, key_span, lanes]
            scores = lax.dot_general(key, query, TURNED, preferred_element_type=jnp.float32)
            flow = lax.dot_general(
                mixed_ref[2, key_span, lanes], grad, TURNED, preferred_element_type=jnp.float32
            )
            probs = jnp.exp(jnp.where(allowed, scores * scale, MASK_FILL) - lse)
            value_sum[key_span, lanes] += jnp.dot(
                probs.astype(jnp.bfloat16), grad, preferred_element_type=jnp.float32
            )
            low = (probs * (flow - delta)).astype(jnp.bfloat16)
            key_sum[key_span, lanes] += jnp.dot(low, query, preferred_element_type=jnp.float32)
            results.append(
                total + lax.dot_general(low, key, CROSSED, preferred_element_type=jnp.float32)
            )
        return tuple(results)

    totals = lax.fori_loop(
        0, count, one, (jnp.zeros((ATTEND_ROWS, HEAD_DIM), jnp.float32),) * len(heads)
    )
    for (lanes, _, _, _, _), total in zip(heads, totals):
        query_grad = (total * scale).astype(jnp.bfloat16)
        stacked_ref[0, row_span, lanes] = query_grad
        bias_sum[0:1, lanes] += jnp.sum(query_grad.astype(jnp.float32), axis=0, keepdims=True)


def tile_scores(query_tile, keys, segment, row_block, col_block):
    key_tile = keys[col_block * BLOCK : (col_block + 1) * BLOCK]
    scale = query_tile.shape[2] ** (-0.5)
    scores = (
        jnp.einsum("qhe,khe->hqk", query_tile, key_tile, preferred_element_type=jnp.float32) * scale
    )
    row_place = row_block * BLOCK + jnp.arange(BLOCK)
    key_place = col_block * BLOCK + jnp.arange(BLOCK)
    row_segment = segment[row_block * BLOCK : (row_block + 1) * BLOCK]
    key_segment = segment[col_block * BLOCK : (col_block + 1) * BLOCK]
    allowed = (key_place[None, :] <= row_place[:, None]) & (
        row_segment[:, None] == key_segment[None, :]
    )
    return (jnp.where(allowed[None], scores, MASK_FILL), allowed)


def attention_forward(queries, keys, values, segment):
    count = queries.shape[0] // BLOCK
    heads = queries.shape[1]
    depth = queries.shape[2]
    outputs = []
    totals = []
    for row_block in range(count):
        query_tile = queries[row_block * BLOCK : (row_block + 1) * BLOCK]
        peak = jnp.full((heads, BLOCK), MASK_FILL, jnp.float32)
        mass = jnp.zeros((heads, BLOCK), jnp.float32)
        for col_block in range(row_block + 1):
            scores, allowed = tile_scores(query_tile, keys, segment, row_block, col_block)
            new_peak = jnp.maximum(peak, jnp.max(scores, axis=-1))
            weights = jnp.where(allowed[None], jnp.exp(scores - new_peak[:, :, None]), 0.0)
            mass = mass * jnp.exp(peak - new_peak) + jnp.sum(weights, axis=-1)
            peak = new_peak
        total = peak + jnp.log(mass)
        gathered = jnp.zeros((BLOCK, heads, depth), jnp.float32)
        for col_block in range(row_block + 1):
            scores, allowed = tile_scores(query_tile, keys, segment, row_block, col_block)
            probs = jnp.where(allowed[None], jnp.exp(scores - total[:, :, None]), 0.0).astype(
                jnp.bfloat16
            )
            value_tile = values[col_block * BLOCK : (col_block + 1) * BLOCK]
            gathered = gathered + jnp.einsum(
                "hqk,khe->qhe", probs, value_tile, preferred_element_type=jnp.float32
            )
        outputs.append(gathered.astype(jnp.bfloat16))
        totals.append(total)
    return (jnp.concatenate(outputs, axis=0), jnp.concatenate(totals, axis=1))


def attention_backward(queries, keys, values, segment, totals, grads):
    count = queries.shape[0] // BLOCK
    heads = queries.shape[1]
    depth = queries.shape[2]
    scale = depth ** (-0.5)
    key_grads = [jnp.zeros((BLOCK, heads, depth), jnp.float32) for index in range(count)]
    value_grads = [jnp.zeros((BLOCK, heads, depth), jnp.float32) for index in range(count)]
    query_grads = []
    for row_block in range(count):
        query_tile = queries[row_block * BLOCK : (row_block + 1) * BLOCK]
        grad_tile = grads[row_block * BLOCK : (row_block + 1) * BLOCK]
        total = totals[:, row_block * BLOCK : (row_block + 1) * BLOCK]
        flows = jnp.zeros((heads, BLOCK), jnp.float32)
        for col_block in range(row_block + 1):
            scores, allowed = tile_scores(query_tile, keys, segment, row_block, col_block)
            probs = jnp.where(allowed[None], jnp.exp(scores - total[:, :, None]), 0.0)
            value_tile = values[col_block * BLOCK : (col_block + 1) * BLOCK]
            prob_grad = jnp.einsum(
                "qhe,khe->hqk", grad_tile, value_tile, preferred_element_type=jnp.float32
            )
            flows = flows + jnp.sum(prob_grad * probs, axis=-1)
            value_grads[col_block] = value_grads[col_block] + jnp.einsum(
                "hqk,qhe->khe",
                probs.astype(jnp.bfloat16),
                grad_tile,
                preferred_element_type=jnp.float32,
            )
        query_sum = jnp.zeros((BLOCK, heads, depth), jnp.float32)
        for col_block in range(row_block + 1):
            scores, allowed = tile_scores(query_tile, keys, segment, row_block, col_block)
            probs = jnp.where(allowed[None], jnp.exp(scores - total[:, :, None]), 0.0)
            value_tile = values[col_block * BLOCK : (col_block + 1) * BLOCK]
            key_tile = keys[col_block * BLOCK : (col_block + 1) * BLOCK]
            prob_grad = jnp.einsum(
                "qhe,khe->hqk", grad_tile, value_tile, preferred_element_type=jnp.float32
            )
            score_grad = (probs * (prob_grad - flows[:, :, None])).astype(jnp.bfloat16)
            query_sum = query_sum + scale * jnp.einsum(
                "hqk,khe->qhe", score_grad, key_tile, preferred_element_type=jnp.float32
            )
            key_grads[col_block] = key_grads[col_block] + scale * jnp.einsum(
                "hqk,qhe->khe", score_grad, query_tile, preferred_element_type=jnp.float32
            )
        query_grads.append(query_sum)
    return (
        jnp.concatenate(query_grads, axis=0).astype(jnp.bfloat16),
        jnp.concatenate(key_grads, axis=0).astype(jnp.bfloat16),
        jnp.concatenate(value_grads, axis=0).astype(jnp.bfloat16),
    )


def adam_update(master, grad, first, second, rate, decay, first_fix, second_fix):
    first_next = BETA_FIRST * first + (1.0 - BETA_FIRST) * grad
    second_next = BETA_SECOND * second + (1.0 - BETA_SECOND) * grad * grad
    change = (
        first_next / first_fix / (jnp.sqrt(second_next / second_fix) + ADAM_EPSILON)
        + decay * master
    )
    return (master - rate * change, first_next, second_next)


def adam_step(master, grad, first, second, rate, decay, fixes):
    first_next = BETA_FIRST * first + (1.0 - BETA_FIRST) * grad
    second_next = BETA_SECOND * second + (1.0 - BETA_SECOND) * grad * grad
    change = (
        first_next / fixes[0] / (jnp.sqrt(second_next / fixes[1]) + ADAM_EPSILON)
        + decay * master
    )
    return master - rate * change, first_next, second_next


def adam_kernel(rates, step_ref, late_ref, early_ref, rows_ref, wide_ref, *refs):
    one = jnp.float32(1.0)
    fixes = tuple(
        one - lax.fori_loop(0, step_ref[0], lambda index, value: value * jnp.float32(beta), one)
        for beta in (BETA_FIRST, BETA_SECOND)
    )
    refs, (rows_out, wide_out) = refs[:-2], refs[-2:]
    rows_out[...] = rows_ref[...]
    wide_out[...] = wide_ref[...]
    smalls = 4
    matrix_inputs, small_inputs = refs[: 4 * len(rates)], refs[4 * len(rates) :][: 3 * smalls]
    outputs = refs[4 * len(rates) + 3 * smalls :]
    for index, rate in enumerate(rates):
        master, grad, first, second = matrix_inputs[4 * index : 4 * index + 4]
        updated, first_out, second_out, grad_out, low_out = outputs[5 * index : 5 * index + 5]
        value = grad[...].reshape(master.shape)
        fresh = adam_step(
            master[...], value, first[...], second[...], rate, MATRIX_DECAY, fixes
        )
        updated[...], first_out[...], second_out[...] = fresh
        grad_out[...] = value
        low_out[...] = fresh[0].astype(jnp.bfloat16)

    @pl.when(pl.program_id(0) == 0)
    def _():
        local = small_inputs[0].shape[1]
        units = small_inputs[3].shape[1]
        early = early_ref
        pieces = (
            [early[4:5, :local], early[4:5, local : 2 * local]],
            [early[4:5, 2 * local : 2 * local + units]],
            [late_ref[0:1, :], early[0:1, :]],
            [late_ref[1:2, :], early[2:3, :], early[1:2, :], early[3:4, :]],
        )
        for index in range(smalls):
            master, first, second = small_inputs[3 * index : 3 * index + 3]
            to = 5 * len(rates) + 4 * index
            updated, first_out, second_out, grad_out = outputs[to : to + 4]
            for row, value in enumerate(pieces[index]):
                here = slice(row, row + 1)
                fresh = adam_step(
                    master[here, :], value, first[here, :], second[here, :], SMALL_RATE, 0.0, fixes
                )
                updated[here, :], first_out[here, :], second_out[here, :] = fresh
                grad_out[here, :] = value


ADAM_STEPS = 4


def adam_call(matrices, smalls, late, early, passing, step):
    in_specs = [pl.BlockSpec(memory_space=pltpu.SMEM)] + [
        pl.BlockSpec(rows.shape, lambda i: (0, 0)) for rows in (late, early)
    ]
    handed = [
        pl.BlockSpec((rows.shape[0] // ADAM_STEPS, rows.shape[1]), lambda i: (i, 0))
        for rows in passing
    ]
    in_specs += handed
    out_specs, out_shape, operands, rates = [], [], [step, late, early, *passing], []
    for master, grad, first, second, rate in matrices:
        lead = master.shape[:-2]
        rows, columns = master.shape[-2] // ADAM_STEPS, master.shape[-1]
        zeros = (0,) * len(lead)
        whole = pl.BlockSpec(lead + (rows, columns), lambda i, z=zeros: z + (i, 0))
        half = pl.BlockSpec(
            (1,) + lead + (rows, columns),
            lambda i, z=zeros: (i // (ADAM_STEPS // 2),) + z + (i % (ADAM_STEPS // 2), 0),
        )
        in_specs += [whole, half, whole, whole]
        operands += [master, grad, first, second]
        shape = jax.ShapeDtypeStruct(master.shape, jnp.float32)
        out_specs += [whole] * 5
        out_shape += [shape] * 4 + [jax.ShapeDtypeStruct(master.shape, jnp.bfloat16)]
        rates.append(rate)
    for group in smalls:
        spec = pl.BlockSpec(group[0].shape, lambda i: (0, 0))
        in_specs += [spec] * 3
        operands += list(group)
        out_specs += [spec] * 4
        out_shape += [jax.ShapeDtypeStruct(group[0].shape, jnp.float32)] * 4
    out_specs += handed
    out_shape += [jax.ShapeDtypeStruct(rows.shape, rows.dtype) for rows in passing]
    return pl.pallas_call(
        functools.partial(adam_kernel, tuple(rates)),
        grid=(ADAM_STEPS,),
        in_specs=in_specs,
        out_specs=out_specs,
        out_shape=out_shape,
        compiler_params=pltpu.CompilerParams(vmem_limit_bytes=VMEM_LIMIT),
        name="adam",
    )(*operands)


def per_device(
    layer_input,
    cotangent,
    lengths,
    offsets,
    step,
    mix_weight,
    out_weight,
    up_weight,
    down_weight,
    mix_first,
    out_first,
    up_first,
    down_first,
    mix_second,
    out_second,
    up_second,
    down_second,
    mix_bias,
    up_bias,
    norm_gains,
    shifts,
    mix_bias_first,
    up_bias_first,
    gains_first,
    shifts_first,
    mix_bias_second,
    up_bias_second,
    gains_second,
    shifts_second,
):
    parts = lax.axis_size("mp")
    local_width = mix_weight.shape[2]
    (
        normed_one,
        mixed,
        mix_whole,
        out_whole,
        up_low,
        down_low,
        own_branch,
        bias_down_grad,
    ) = project_call(
        layer_input,
        norm_gains[0:1],
        shifts[0:1],
        mix_weight,
        out_weight,
        mix_bias,
        up_weight,
        down_weight,
        cotangent,
        offsets,
        lengths,
        parts // 2,
    )
    (
        attended_flat,
        aux,
        resid_own,
        normed_mid,
        branch_grad,
        up_whole,
        down_whole,
    ) = attend_out_call(
        mixed,
        offsets,
        lengths,
        out_whole,
        layer_input,
        own_branch,
        norm_gains[1:2],
        shifts[2:3],
        shifts[1:2],
        up_low,
        down_low,
        parts // 2,
    )
    normed_two, active, hidden_grad, resid_grad, resid_low, row_sums, up_bias_grad = feed_call(
        normed_mid,
        branch_grad,
        up_whole,
        down_whole,
        up_bias[None],
        resid_own,
        own_branch,
        norm_gains[1:2],
        parts // 2,
    )
    stacked, mix_bias_grad, down_pieces, out_grad, layer_output, _ = branch_back_call(
        resid_low,
        active,
        down_whole,
        attended_flat,
        out_whole,
        shifts[3:4],
        offsets,
        lengths,
        mixed,
        aux,
        resid_own,
        branch_grad,
        parts // 2,
    )
    input_grad, late, early, mix_pieces, up_pieces, out_pieces = input_back_call(
        stacked,
        mix_whole,
        layer_input,
        resid_grad,
        norm_gains[0:1],
        (row_sums, bias_down_grad, mix_bias_grad, up_bias_grad),
        hidden_grad,
        out_grad,
        normed_one,
        normed_two,
        parts // 2,
    )
    news = adam_call(
        [
            (mix_weight, mix_pieces, mix_first, mix_second, D ** (-0.5)),
            (out_weight, out_pieces, out_first, out_second, OUT_FAN ** (-0.5)),
            (up_weight, up_pieces, up_first, up_second, D ** (-0.5)),
            (down_weight, down_pieces, down_first, down_second, FF ** (-0.5)),
        ],
        [
            (mix_bias, mix_bias_first, mix_bias_second),
            (up_bias[None], up_bias_first[None], up_bias_second[None]),
            (norm_gains, gains_first, gains_second),
            (shifts, shifts_first, shifts_second),
        ],
        late,
        early,
        (layer_output, input_grad),
        step,
    )
    layer_output, input_grad = news[-2:]
    mix, out, up, down = (news[5 * index : 5 * index + 5] for index in range(4))
    biases, unit_biases, gains, moves = (
        news[20 + 4 * index : 24 + 4 * index] for index in range(4)
    )
    unit_biases = [value[0] for value in unit_biases]
    return (
        layer_output,
        input_grad,
        *mix[:3],
        *out[:3],
        *up[:3],
        *down[:3],
        *biases[:3],
        *unit_biases[:3],
        *gains[:3],
        *moves[:3],
        mix[3],
        out[3],
        up[3],
        down[3],
        biases[3],
        unit_biases[3],
        gains[3],
        moves[3],
        mix[4],
        out[4],
        up[4],
        down[4],
    )


def per_device_any(
    layer_input,
    cotangent,
    lengths,
    offsets,
    step,
    mix_weight,
    out_weight,
    up_weight,
    down_weight,
    mix_first,
    out_first,
    up_first,
    down_first,
    mix_second,
    out_second,
    up_second,
    down_second,
    mix_bias,
    up_bias,
    norm_gains,
    shifts,
    mix_bias_first,
    up_bias_first,
    gains_first,
    shifts_first,
    mix_bias_second,
    up_bias_second,
    gains_second,
    shifts_second,
):
    own_rows = layer_input.shape[0]
    parts = lax.axis_size("mp")
    group_rows = own_rows * parts
    slots_here = lengths.shape[0]
    slot_len = group_rows // slots_here
    local_width = mix_weight.shape[2]
    depth = HEAD_DIM
    heads_here = local_width // depth
    positions = jnp.arange(slot_len, dtype=jnp.int32)
    live = (positions[None, :] >= offsets[:, None]) & (
        positions[None, :] < (offsets + lengths)[:, None]
    )
    segment = live.astype(jnp.int32)
    first_row = lax.axis_index("mp") * own_rows
    own_live = own_slice(live.reshape(-1), first_row, own_rows)[:, None]
    own_input = layer_input.astype(jnp.float32)
    normed_own, hat_one, inv_one = layer_norm_parts(own_input, norm_gains[0], shifts[0])
    normed_one = gather_rows(normed_own.astype(jnp.bfloat16))
    mix_full = gather_shards(mix_weight.astype(jnp.bfloat16), 1)
    out_full = gather_shards(out_weight.astype(jnp.bfloat16), 1)
    up_full = gather_shards(up_weight.astype(jnp.bfloat16), 0)
    down_full = gather_shards(down_weight.astype(jnp.bfloat16), 1)
    out_grad = jnp.where(own_live, cotangent.astype(jnp.float32), 0.0)
    bias_down_grad = jnp.sum(out_grad, axis=0)
    branch_grad = gather_rows(out_grad.astype(jnp.bfloat16))
    mixed = jnp.einsum("td,cde->cte", normed_one, mix_full, preferred_element_type=jnp.float32)
    queries = (
        (mixed[0] + mix_bias[0])
        .astype(jnp.bfloat16)
        .reshape(slots_here, slot_len, heads_here, depth)
    )
    keys = mixed[1].astype(jnp.bfloat16).reshape(slots_here, slot_len, heads_here, depth)
    values = (
        (mixed[2] + mix_bias[1])
        .astype(jnp.bfloat16)
        .reshape(slots_here, slot_len, heads_here, depth)
    )

    def attend(item):
        return attention_forward(item[0], item[1], item[2], item[3])

    attended, totals = lax.map(attend, (queries, keys, values, segment))
    attended_flat = attended.reshape(group_rows, local_width)
    attn_part = jnp.dot(attended_flat, out_full, preferred_element_type=jnp.float32)
    resid_own = own_input + scatter_rows(attn_part) + shifts[1]
    normed_mid, hat_two, inv_two = layer_norm_parts(resid_own, norm_gains[1], shifts[2])
    normed_two = gather_rows(normed_mid.astype(jnp.bfloat16))
    hidden = jnp.dot(normed_two, up_full, preferred_element_type=jnp.float32) + up_bias
    active_value, gelu_pull = jax.vjp(tanh_gelu, hidden)
    active = active_value.astype(jnp.bfloat16)
    active_grad = jnp.einsum(
        "td,fd->tf", branch_grad, down_full, preferred_element_type=jnp.float32
    )
    hidden_grad = gelu_pull(active_grad)[0].astype(jnp.bfloat16)
    two_part = jnp.einsum("tf,df->td", hidden_grad, up_full, preferred_element_type=jnp.float32)
    two_grad = scatter_rows(two_part)
    down_part = jnp.dot(active, down_full, preferred_element_type=jnp.float32)
    down_grad = jnp.einsum("tf,td->fd", active, branch_grad, preferred_element_type=jnp.float32)
    up_bias_grad = jnp.sum(hidden_grad, axis=0, dtype=jnp.float32)
    up_grad = jnp.einsum("td,tf->df", normed_two, hidden_grad, preferred_element_type=jnp.float32)
    resid_grad = out_grad + layer_norm_back(two_grad, hat_two, inv_two, norm_gains[1])
    attn_branch = gather_rows(resid_grad.astype(jnp.bfloat16))
    result_own = resid_own + scatter_rows(down_part) + shifts[3]
    layer_output = jnp.where(own_live, result_own, 0.0).astype(jnp.bfloat16)
    gain_two_grad = jnp.sum(two_grad * hat_two, axis=0)
    shift_two_grad = jnp.sum(two_grad, axis=0)
    bias_out_grad = jnp.sum(resid_grad, axis=0)
    attended_grad = jnp.einsum(
        "td,ed->te", attn_branch, out_full, preferred_element_type=jnp.float32
    ).astype(jnp.bfloat16)
    out_weight_grad = jnp.einsum(
        "te,td->ed", attended_flat, attn_branch, preferred_element_type=jnp.float32
    )

    def attend_back(item):
        return attention_backward(item[0], item[1], item[2], item[3], item[4], item[5])

    query_grad, key_grad, value_grad = lax.map(
        attend_back,
        (
            queries,
            keys,
            values,
            segment,
            totals,
            attended_grad.reshape(slots_here, slot_len, heads_here, depth),
        ),
    )
    stacked = jnp.stack(
        [
            query_grad.reshape(group_rows, local_width),
            key_grad.reshape(group_rows, local_width),
            value_grad.reshape(group_rows, local_width),
        ]
    )
    one_part = jnp.einsum("cte,cde->td", stacked, mix_full, preferred_element_type=jnp.float32)
    one_grad = scatter_rows(one_part)
    mix_grad = jnp.einsum("td,cte->cde", normed_one, stacked, preferred_element_type=jnp.float32)
    mix_bias_grad = jnp.stack(
        [
            jnp.sum(stacked[0], axis=0, dtype=jnp.float32),
            jnp.sum(stacked[2], axis=0, dtype=jnp.float32),
        ]
    )
    mix_owned = scatter_shards(mix_grad, 1)
    out_owned = scatter_shards(out_weight_grad, 1)
    up_owned = scatter_shards(up_grad, 0)
    down_owned = scatter_shards(down_grad, 1)
    input_grad = resid_grad + layer_norm_back(one_grad, hat_one, inv_one, norm_gains[0])
    gain_one_grad = jnp.sum(one_grad * hat_one, axis=0)
    shift_one_grad = jnp.sum(one_grad, axis=0)
    gain_grad = jnp.stack([gain_one_grad, gain_two_grad])
    shift_grad = jnp.stack([shift_one_grad, bias_out_grad, shift_two_grad, bias_down_grad])
    mix_bias_total, up_bias_total = lax.psum((mix_bias_grad, up_bias_grad), "dp")
    gain_total, shift_total = lax.psum((gain_grad, shift_grad), ("dp", "mp"))
    step_count = step[0].astype(jnp.float32)
    first_fix = 1.0 - BETA_FIRST**step_count
    second_fix = 1.0 - BETA_SECOND**step_count
    mix_new = adam_update(
        mix_weight,
        mix_owned,
        mix_first,
        mix_second,
        D ** (-0.5),
        MATRIX_DECAY,
        first_fix,
        second_fix,
    )
    out_new = adam_update(
        out_weight,
        out_owned,
        out_first,
        out_second,
        OUT_FAN ** (-0.5),
        MATRIX_DECAY,
        first_fix,
        second_fix,
    )
    up_new = adam_update(
        up_weight, up_owned, up_first, up_second, D ** (-0.5), MATRIX_DECAY, first_fix, second_fix
    )
    down_new = adam_update(
        down_weight,
        down_owned,
        down_first,
        down_second,
        FF ** (-0.5),
        MATRIX_DECAY,
        first_fix,
        second_fix,
    )
    mix_bias_new = adam_update(
        mix_bias,
        mix_bias_total,
        mix_bias_first,
        mix_bias_second,
        SMALL_RATE,
        0.0,
        first_fix,
        second_fix,
    )
    up_bias_new = adam_update(
        up_bias,
        up_bias_total,
        up_bias_first,
        up_bias_second,
        SMALL_RATE,
        0.0,
        first_fix,
        second_fix,
    )
    gains_new = adam_update(
        norm_gains, gain_total, gains_first, gains_second, SMALL_RATE, 0.0, first_fix, second_fix
    )
    shifts_new = adam_update(
        shifts, shift_total, shifts_first, shifts_second, SMALL_RATE, 0.0, first_fix, second_fix
    )
    return (
        layer_output,
        input_grad,
        mix_new[0],
        mix_new[1],
        mix_new[2],
        out_new[0],
        out_new[1],
        out_new[2],
        up_new[0],
        up_new[1],
        up_new[2],
        down_new[0],
        down_new[1],
        down_new[2],
        mix_bias_new[0],
        mix_bias_new[1],
        mix_bias_new[2],
        up_bias_new[0],
        up_bias_new[1],
        up_bias_new[2],
        gains_new[0],
        gains_new[1],
        gains_new[2],
        shifts_new[0],
        shifts_new[1],
        shifts_new[2],
        mix_owned,
        out_owned,
        up_owned,
        down_owned,
        mix_bias_total,
        up_bias_total,
        gain_total,
        shift_total,
        mix_new[0].astype(jnp.bfloat16),
        out_new[0].astype(jnp.bfloat16),
        up_new[0].astype(jnp.bfloat16),
        down_new[0].astype(jnp.bfloat16),
    )


def solution(mesh):
    placed = (
        P(("dp", "mp"), None),
        P(("dp", "mp"), None),
        P("dp"),
        P("dp"),
        P(),
        P(None, "dp", "mp"),
        P("mp", "dp"),
        P("dp", "mp"),
        P("mp", "dp"),
        P(None, "dp", "mp"),
        P("mp", "dp"),
        P("dp", "mp"),
        P("mp", "dp"),
        P(None, "dp", "mp"),
        P("mp", "dp"),
        P("dp", "mp"),
        P("mp", "dp"),
        P(None, "mp"),
        P("mp"),
        P(),
        P(),
        P(None, "mp"),
        P("mp"),
        P(),
        P(),
        P(None, "mp"),
        P("mp"),
        P(),
        P(),
    )
    fits = mesh.shape["dp"] == 4 and mesh.shape["mp"] == 8
    return jax.shard_map(
        per_device if fits else per_device_any,
        mesh=mesh,
        in_specs=placed,
        out_specs=(
            P(("dp", "mp"), None),
            P(("dp", "mp"), None),
            P(None, "dp", "mp"),
            P(None, "dp", "mp"),
            P(None, "dp", "mp"),
            P("mp", "dp"),
            P("mp", "dp"),
            P("mp", "dp"),
            P("dp", "mp"),
            P("dp", "mp"),
            P("dp", "mp"),
            P("mp", "dp"),
            P("mp", "dp"),
            P("mp", "dp"),
            P(None, "mp"),
            P(None, "mp"),
            P(None, "mp"),
            P("mp"),
            P("mp"),
            P("mp"),
            P(),
            P(),
            P(),
            P(),
            P(),
            P(),
            P(None, "dp", "mp"),
            P("mp", "dp"),
            P("dp", "mp"),
            P("mp", "dp"),
            P(None, "mp"),
            P("mp"),
            P(),
            P(),
            P(None, "dp", "mp"),
            P("mp", "dp"),
            P("dp", "mp"),
            P("mp", "dp"),
        ),
        check_vma=False,
    )
```

```python
import functools

import jax
import jax.numpy as jnp
from jax import lax
from jax.experimental import pallas as pl
from jax.experimental.pallas import tpu as pltpu
from jax.sharding import PartitionSpec as P

D = 2048
HEAD_DIM = 128
FF = 8192
BLOCK = 512
OUT_FAN = 7


NORM_EPSILON = 1e-05
ADAM_EPSILON = 1e-08
BETA_FIRST = 0.9
BETA_SECOND = 0.999
MATRIX_DECAY = 0.1
SMALL_RATE = 0.2
MASK_FILL = -1e30


def layer_norm_parts(rows, gain, shift):
    center = rows - jnp.mean(rows, axis=-1, keepdims=True)
    inverse = lax.rsqrt(jnp.mean(center * center, axis=-1, keepdims=True) + NORM_EPSILON)
    normed = center * inverse
    return (normed * gain + shift, normed, inverse)


def layer_norm_back(grad_out, normed, inverse, gain):
    scaled = grad_out * gain
    return inverse * (
        scaled
        - jnp.mean(scaled, axis=-1, keepdims=True)
        - normed * jnp.mean(scaled * normed, axis=-1, keepdims=True)
    )


def tanh_gelu(values):
    return jax.nn.gelu(values, approximate=True)


def own_slice(whole, first_row, count):
    return lax.dynamic_slice_in_dim(whole, first_row, count, 0)


def gather_rows(rows):
    return lax.all_gather(rows, "mp", axis=0, tiled=True)


def scatter_rows(terms):
    low = terms.astype(jnp.bfloat16)
    return lax.psum_scatter(low, "mp", scatter_dimension=0, tiled=True).astype(jnp.float32)


def swap(value, mask):
    size = lax.axis_size("dp")
    return lax.ppermute(value, "dp", [(place, place ^ mask) for place in range(size)])


def gather_shards(shard, axis):
    if lax.axis_size("dp") != 4:
        return lax.all_gather(shard, "dp", axis=axis, tiled=True)
    count = shard.shape[axis]
    me = lax.axis_index("dp")
    from_x = swap(shard, 1)
    from_y = swap(shard, 2)
    half = count // 2
    low = swap(lax.slice_in_dim(from_x, 0, half, axis=axis), 2)
    high = swap(lax.slice_in_dim(from_y, half, count, axis=axis), 1)
    shape = list(shard.shape)
    shape[axis] = 4 * count
    full = jnp.zeros(shape, shard.dtype)
    full = lax.dynamic_update_slice_in_dim(full, shard, me * count, axis)
    full = lax.dynamic_update_slice_in_dim(full, from_x, (me ^ 1) * count, axis)
    full = lax.dynamic_update_slice_in_dim(full, from_y, (me ^ 2) * count, axis)
    full = lax.dynamic_update_slice_in_dim(full, low, (me ^ 3) * count, axis)
    return lax.dynamic_update_slice_in_dim(full, high, (me ^ 3) * count + half, axis)


def scatter_shards(grad, axis):
    if lax.axis_size("dp") != 4:
        return lax.psum_scatter(grad, "dp", scatter_dimension=axis, tiled=True)
    count = grad.shape[axis] // 4
    half = count // 2
    me = lax.axis_index("dp")

    def piece(owner, upper):
        return lax.dynamic_slice_in_dim(grad, owner * count + upper * half, half, axis)

    def one_way(first, second, upper):
        near = swap(piece(me ^ first, upper).astype(jnp.bfloat16), first)
        far = swap(piece(me ^ 3, upper).astype(jnp.bfloat16), first)
        onward = piece(me ^ second, upper) + far.astype(jnp.float32)
        last = swap(onward.astype(jnp.bfloat16), second)
        return piece(me, upper) + near.astype(jnp.float32) + last.astype(jnp.float32)

    return lax.concatenate([one_way(1, 2, 0), one_way(2, 1, 1)], axis)


MESH = pl.DeviceIdType.MESH
VMEM_LIMIT = 62 * 1024 * 1024
TURNED = (((1,), (1,)), ((), ()))
CROSSED = (((0,), (0,)), ((), ()))


class Place:
    def __init__(self, chips):
        self.chips = chips
        self.dp = lax.axis_index("dp")
        self.me = lax.axis_index("mp")
        self.chip = self.me // 2
        self.core = self.me % 2
        self.has_up = self.chip < chips - 1
        self.has_down = self.chip > 0
        self.up = (self.dp, jnp.minimum(self.me + 2, 2 * chips - 1))
        self.down = (self.dp, jnp.maximum(self.me - 2, 0))
        self.side = (self.dp, self.me + 1 - 2 * self.core)
        self.x_peer = self.dp + 1 - 2 * (self.dp % 2)
        self.y_peer = (self.dp + 2) % 4
        self.across = 3 - self.dp
        self.x_way = (self.x_peer, self.me)
        self.y_way = (self.y_peer, self.me)

    def toward(self, way):
        return (self.dp, jnp.where(way == 0, self.up[1], self.down[1]))

    def greet(self, square, everyone=False):
        barrier = pltpu.get_barrier_semaphore()

        def signal(device):
            pl.semaphore_signal(barrier, inc=1, device_id=device, device_id_type=MESH)

        signal(self.side)
        pl.when(self.has_up)(lambda: signal(self.up))
        pl.when(self.has_down)(lambda: signal(self.down))
        count = 1 + self.has_up.astype(jnp.int32) + self.has_down.astype(jnp.int32)
        if square:
            signal(self.x_way)
            signal(self.y_way)
            count = count + 2
        if everyone:
            signal((self.across, self.me))
            count = count + 1

            def beyond(chip, carry):
                far = (chip > self.chip + 1) | (chip < self.chip - 1)
                pl.when(far)(lambda: signal((self.dp, 2 * chip + self.core)))
                return carry

            lax.fori_loop(0, self.chips, beyond, 0)
            near = self.has_up.astype(jnp.int32) + self.has_down.astype(jnp.int32)
            count = count + (self.chips - 1) - near
        pl.semaphore_wait(barrier, count)


def remote(source, target, send, recv, device):
    return pltpu.make_async_remote_copy(
        src_ref=source,
        dst_ref=target,
        send_sem=send,
        recv_sem=recv,
        device_id=device,
        device_id_type=MESH,
    )


def fetch(pairs, sems):
    copies = [
        pltpu.make_async_copy(source, target, sems.at[index])
        for index, (source, target) in enumerate(pairs)
    ]
    for copy in copies:
        copy.start()
    return copies


class LineGather:
    def __init__(self, place, blocks, send, recv, parts=1, own=None):
        self.place, self.blocks, self.send, self.recv = place, blocks, send, recv
        self.parts, self.own = parts, own

    def copy(self, way, chip, part=0, own=None):
        place = self.place
        piece = chip * self.parts + part
        block = 2 * piece + place.core
        device = (place.up, place.down, place.side)[way]
        return remote(
            self.blocks.at[block] if own is None else own,
            self.blocks.at[block],
            self.send.at[way, piece],
            self.recv.at[block],
            device,
        )

    def arrive(self, chip, core, part=0):
        piece = chip * self.parts + part
        block = 2 * piece + core
        remote(
            self.blocks.at[block],
            self.blocks.at[block],
            self.send.at[2, piece],
            self.recv.at[block],
            self.place.side,
        ).wait_recv()

    def begin_part(self, part):
        place = self.place
        pl.when(place.has_up)(lambda: self.copy(0, place.chip, part, self.own).start())
        pl.when(place.has_down)(lambda: self.copy(1, place.chip, part, self.own).start())
        self.copy(2, place.chip, part, self.own).start()

    def begin(self):
        for part in range(self.parts):
            self.begin_part(part)

    def step(self, distance, part=0):
        place = self.place
        low = place.chip - distance
        high = place.chip + distance

        @pl.when(low >= 0)
        def _():
            self.arrive(low, place.core, part)
            pl.when(place.has_up)(lambda: self.copy(0, low, part).start())
            self.copy(2, low, part).start()

        @pl.when(high < place.chips)
        def _():
            self.arrive(high, place.core, part)
            pl.when(place.has_down)(lambda: self.copy(1, high, part).start())
            self.copy(2, high, part).start()

    def finish(self):
        place = self.place

        def drain(chip, carry):
            for part in range(self.parts):
                pl.when(place.has_up & (chip <= place.chip))(
                    lambda: self.copy(0, chip, part).wait_send()
                )
                pl.when(place.has_down & (chip >= place.chip))(
                    lambda: self.copy(1, chip, part).wait_send()
                )
                self.copy(2, chip, part).wait_send()
            return carry

        lax.fori_loop(0, place.chips, drain, 0)


class SquareGather:
    def __init__(self, place, shard, view, half, send, recv):
        self.place, self.shard, self.view, self.half = place, shard, view, half
        self.send, self.recv = send, recv

    def first(self, way):
        place = self.place
        device = (place.x_way, place.y_way)[way]
        return remote(
            self.shard, self.view(place.dp), self.send.at[way], self.recv.at[way], device
        )

    def first_landed(self, way):
        place = self.place
        owner = (place.x_peer, place.y_peer)[way]
        device = (place.x_way, place.y_way)[way]
        remote(
            self.view(owner), self.view(owner), self.send.at[way], self.recv.at[way], device
        ).wait_recv()

    def second(self, way):
        place = self.place
        owner = (place.y_peer, place.x_peer)[way]
        device = (place.x_way, place.y_way)[way]
        part = self.half(owner, 1 - way)
        return remote(part, part, self.send.at[2 + way], self.recv.at[2 + way], device)

    def second_landed(self, way):
        place = self.place
        device = (place.x_way, place.y_way)[way]
        part = self.half(place.across, 1 - way)
        remote(part, part, self.send.at[2 + way], self.recv.at[2 + way], device).wait_recv()

    def begin(self):
        self.first(0).start()
        self.first(1).start()

    def middle(self):
        self.first_landed(0)
        self.second(1).start()
        self.first_landed(1)
        self.second(0).start()

    def end(self):
        self.second_landed(0)
        self.second_landed(1)

    def finish(self):
        self.first(0).wait_send()
        self.first(1).wait_send()
        self.second(0).wait_send()
        self.second(1).wait_send()


def norm_rows(rows, gain, shift):
    normed, hat, inverse = layer_norm_parts(rows, gain, shift)
    return normed


def project_kernel(
    chips,
    parts,
    rows_ref,
    gain_ref,
    shift_ref,
    mix_weight_hbm,
    out_weight_hbm,
    bias_ref,
    up_weight_hbm,
    down_weight_hbm,
    cotangent_hbm,
    offsets_ref,
    lengths_ref,
    normed_ref,
    mixed_hbm,
    mix_hbm,
    out_whole,
    up_ref,
    down_ref,
    branch_ref,
    branch_sum_ref,
    mix_weight_ref,
    out_weight_ref,
    up_weight_ref,
    down_weight_ref,
    cotangent_ref,
    fetch_sem,
    mix_ref,
    out_ref,
    mixed_ref,
    mix_whole,
    emit_sem,
    blocks,
    line_send,
    line_recv,
    mix_send,
    mix_recv,
    out_send,
    out_recv,
    own_sem,
    keep_sem,
):
    place = Place(chips)
    bounds = (offsets_ref[0], offsets_ref[0] + lengths_ref[0])
    count = rows_ref.shape[0]
    rows = count // parts
    fetched = fetch(
        [
            (mix_weight_hbm, mix_weight_ref),
            (out_weight_hbm, out_weight_ref),
            (cotangent_hbm, cotangent_ref),
            (up_weight_hbm, up_weight_ref),
            (down_weight_hbm, down_weight_ref),
        ],
        fetch_sem,
    )
    line = LineGather(place, blocks, line_send, line_recv, parts)

    def norm(part):
        def one(span):
            own = rows_ref[pl.ds(part * rows + span.start, 64), :].astype(jnp.float32)
            normed = norm_rows(own, gain_ref[...], shift_ref[...])
            blocks[2 * (place.chip * parts + part) + place.core, span, :] = normed.astype(
                jnp.bfloat16
            )

        by_rows(rows, 64, one)

    norm(0)
    place.greet(True)
    line.begin_part(0)
    for part in range(1, parts):
        norm(part)
        line.begin_part(part)
    mix = SquareGather(
        place,
        mix_ref,
        lambda owner: mix_whole.at[:, owner],
        lambda owner, which: mix_whole.at[:, owner, pl.ds(which * 256, 256)],
        mix_send,
        mix_recv,
    )
    out = SquareGather(
        place,
        out_ref,
        lambda owner: out_whole.at[owner],
        lambda owner, which: out_whole.at[owner, pl.ds(which * 128, 128)],
        out_send,
        out_recv,
    )

    def lower(source, target):
        def one(span):
            target[span, :] = source[span, :].astype(jnp.bfloat16)

        by_rows(source.shape[0], 64, one)

    fetched[0].wait()
    for part in range(3):
        lower(mix_weight_ref.at[part], mix_ref.at[part])
    mix.begin()
    own_mix = pltpu.make_async_copy(mix_ref, mix_whole.at[:, place.dp], own_sem.at[0])
    own_mix.start()
    fetched[1].wait()
    lower(out_weight_ref, out_ref)
    own_out = pltpu.make_async_copy(out_ref, out_whole.at[place.dp], own_sem.at[1])
    own_out.start()
    branch_sum_ref[...] = jnp.zeros_like(branch_sum_ref)

    def branch(span):
        live = alive((64, 1), 0, place.me * count + span.start, bounds)
        grad = jnp.where(live > 0, cotangent_ref[span, :].astype(jnp.float32), 0.0)
        branch_ref[span, :] = grad.astype(jnp.bfloat16)
        branch_sum_ref[...] += jnp.sum(grad, axis=0, keepdims=True)

    fetched[2].wait()
    by_rows(count, 64, branch)
    fetched[3].wait()
    lower(up_weight_ref, up_ref)
    fetched[4].wait()
    lower(down_weight_ref, down_ref)

    def span_of(chip, core, part):
        start = (2 * chip + core) * count + part * rows
        return pl.ds(pl.multiple_of(start, rows), rows)

    def copies(chip, part):
        piece = chip * parts + part
        taken = []
        for core in range(2):
            span = span_of(chip, core, part)
            taken.append(
                pltpu.make_async_copy(
                    blocks.at[2 * piece + core], normed_ref.at[span], keep_sem.at[piece, core]
                )
            )
            taken.append(
                pltpu.make_async_copy(
                    mixed_ref.at[:, span], mixed_hbm.at[:, span], emit_sem.at[piece, core]
                )
            )
        return taken

    keep_mix = pltpu.make_async_copy(mix_whole, mix_hbm, own_sem.at[2])

    def project(chip, part):
        piece = chip * parts + part
        line.arrive(chip, 1 - place.core, part)
        pair = blocks[pl.ds(2 * piece, 2)].reshape(2 * rows, -1)
        for kind in range(3):
            weight = mix_whole[kind].reshape(-1, mix_whole.shape[3])
            result = jnp.dot(pair, weight, preferred_element_type=jnp.float32)
            if kind == 0:
                result = result + bias_ref[0:1, :]
            if kind == 2:
                result = result + bias_ref[1:2, :]
            low = result.astype(jnp.bfloat16)
            for core in range(2):
                mixed_ref[kind, span_of(chip, core, part), :] = low[
                    core * rows : (core + 1) * rows
                ]
        for copy in copies(chip, part):
            copy.start()

    def turn(index, carry):
        distance = index // parts
        part = index % parts

        @pl.when(distance > 0)
        def _():
            line.step(distance, part)

        @pl.when(index == 2)
        def _():
            mix.middle()
            out.begin()

        @pl.when(index == 3)
        def _():
            mix.end()
            own_mix.wait()
            keep_mix.start()

        first = jnp.where(index < 6, 2 * (index - 3), index)
        after = jnp.where(index < 6, 2 * (index - 2), index + 1)

        def one(order, inner):
            each = order // 2
            side = order % 2
            near = each // parts
            chip = place.chip + near * (2 * side - 1)

            @pl.when((chip >= 0) & (chip < chips) & ((near > 0) | (side == 0)))
            def _():
                project(chip, each % parts)

            return inner

        @pl.when(index >= 3)
        def _():
            lax.fori_loop(2 * first, 2 * after, one, 0)

        pl.when(index == 4)(out.middle)
        return carry

    lax.fori_loop(0, chips * parts, turn, 0)
    out.end()
    own_out.wait()
    line.finish()
    mix.finish()
    out.finish()

    def kept(piece, carry):
        for copy in copies(piece // parts, piece % parts):
            copy.wait()
        return carry

    lax.fori_loop(0, parts * chips, kept, 0)
    keep_mix.wait()


def project_call(
    rows, gain, shift, mix_shard, out_shard, bias, up, down, cotangent, offsets, lengths, chips
):
    count, width = rows.shape
    total = 2 * chips * count
    local = mix_shard.shape[2]
    parts = 2
    vmem = pl.BlockSpec(memory_space=pltpu.VMEM)
    hbm = pl.BlockSpec(memory_space=pl.ANY)
    dma = pltpu.SemaphoreType.DMA
    flops = 2 * total * width * 3 * local
    return pl.pallas_call(
        functools.partial(project_kernel, chips, parts),
        out_shape=(
            jax.ShapeDtypeStruct((total, width), jnp.bfloat16),
            jax.ShapeDtypeStruct((3, total, local), jnp.bfloat16),
            jax.ShapeDtypeStruct((3, 4, mix_shard.shape[1], local), jnp.bfloat16),
            jax.ShapeDtypeStruct((4,) + out_shard.shape, jnp.bfloat16),
            jax.ShapeDtypeStruct(up.shape, jnp.bfloat16),
            jax.ShapeDtypeStruct(down.shape, jnp.bfloat16),
            jax.ShapeDtypeStruct((count, width), jnp.bfloat16),
            jax.ShapeDtypeStruct((1, width), jnp.float32),
        ),
        in_specs=[vmem] * 3
        + [hbm] * 2
        + [vmem]
        + [hbm] * 3
        + [pl.BlockSpec(memory_space=pltpu.SMEM)] * 2,
        out_specs=(hbm,) * 4 + (vmem,) * 4,
        scratch_shapes=[
            pltpu.VMEM(mix_shard.shape, jnp.float32),
            pltpu.VMEM(out_shard.shape, jnp.float32),
            pltpu.VMEM(up.shape, jnp.float32),
            pltpu.VMEM(down.shape, jnp.float32),
            pltpu.VMEM(cotangent.shape, jnp.bfloat16),
            dma((5,)),
            pltpu.VMEM(mix_shard.shape, jnp.bfloat16),
            pltpu.VMEM(out_shard.shape, jnp.bfloat16),
            pltpu.VMEM((3, total, local), jnp.bfloat16),
            pltpu.VMEM((3, 4, mix_shard.shape[1], local), jnp.bfloat16),
            dma((parts * chips, 2)),
            pltpu.VMEM((2 * chips * parts, count // parts, width), jnp.bfloat16),
            dma((3, chips * parts)),
            dma((2 * chips * parts,)),
            dma((4,)),
            dma((4,)),
            dma((4,)),
            dma((4,)),
            dma((3,)),
            dma((parts * chips, 2)),
        ],
        compiler_params=pltpu.CompilerParams(
            collective_id=0, has_side_effects=True, vmem_limit_bytes=VMEM_LIMIT
        ),
        cost_estimate=pl.CostEstimate(flops=flops * 7, bytes_accessed=0, transcendentals=0),
        name="project",
    )(rows, gain, shift, mix_shard, out_shard, bias, up, down, cotangent, offsets, lengths)


class LineScatter:
    def __init__(self, place, term, tiles, bufs, sems, prepare=lambda chip: None):
        self.place, self.term, self.tiles, self.prepare = place, term, tiles, prepare
        self.total, self.side_out, self.side_in, self.line_in = bufs
        self.side_send, self.side_recv, self.line_send, self.line_recv = sems

    def side_copy(self, chip):
        return remote(
            self.side_out.at[chip],
            self.side_in.at[chip],
            self.side_send.at[chip],
            self.side_recv.at[chip],
            self.place.side,
        )

    def span(self, tile):
        width = self.total.shape[1] // self.tiles
        return slice(tile * width, (tile + 1) * width)

    def line_copy(self, way, chip, tile):
        place = self.place
        next_chip = place.chip + 1 - 2 * way
        slot = jnp.where((way == 1) & (chip == next_chip), place.chips, chip)
        return remote(
            self.line_in.at[chip, :, self.span(tile)],
            self.line_in.at[slot, :, self.span(tile)],
            self.line_send.at[chip, tile],
            self.line_recv.at[slot, tile],
            (place.up, place.down)[way],
        )

    def landed(self, way, chip, tile):
        place = self.place
        slot = jnp.where((way == 1) & (chip == place.chip), place.chips, chip)
        remote(
            self.line_in.at[slot, :, self.span(tile)],
            self.line_in.at[slot, :, self.span(tile)],
            self.line_send.at[chip, tile],
            self.line_recv.at[slot, tile],
            (place.up, place.down)[way],
        ).wait_recv()
        return slot

    def each(self, distance, action):
        place = self.place

        def one(index, carry):
            chip = place.chip + distance * (1 - 2 * index)
            valid = (chip >= 0) & (chip < place.chips) & ((distance > 0) | (index == 0))
            pl.when(valid)(lambda: action(chip))
            return carry

        lax.fori_loop(0, 2, one, 0)

    def hand_over(self, chip):
        self.prepare(chip)
        block = 2 * chip + 1 - self.place.core
        width = self.total.shape[1] // self.tiles

        def one(tile, carry):
            span = pl.ds(pl.multiple_of(tile * width, width), width)
            self.side_out[chip, :, span] = self.term(block, tile).astype(jnp.bfloat16)
            return carry

        lax.fori_loop(0, self.tiles, one, 0)
        self.side_copy(chip).start()

    def sum_up(self, chip):
        place = self.place
        block = 2 * chip + place.core
        self.side_copy(chip).wait_recv()
        for tile in range(self.tiles):
            span = self.span(tile)
            self.total[:, span] = self.term(block, tile) + self.side_in[chip, :, span].astype(
                jnp.float32
            )
            for way in range(2):
                behind = (place.has_down, place.has_up)[way]
                goes = (chip >= place.chip) if way == 0 else (chip <= place.chip)

                @pl.when(behind & goes)
                def _():
                    slot = self.landed(way, chip, tile)
                    self.total[:, span] += self.line_in[slot, :, span].astype(jnp.float32)

            @pl.when(chip != place.chip)
            def _():
                self.line_in[chip, :, span] = self.total[:, span].astype(jnp.bfloat16)
                pl.when(chip > place.chip)(lambda: self.line_copy(0, chip, tile).start())
                pl.when(chip < place.chip)(lambda: self.line_copy(1, chip, tile).start())

    def begin(self):
        self.each(self.place.chips - 1, self.hand_over)

    def step(self, index, early=False):
        distance = self.place.chips - 1 - index
        if early:
            pl.when((index > 0) & (distance > 0))(lambda: self.each(distance - 1, self.hand_over))
        self.each(distance, self.sum_up)
        behind = (index == 0) if early else (distance > 0)
        pl.when(behind)(lambda: self.each(distance - 1, self.hand_over))

    def finish(self):
        place = self.place

        def drain(chip, carry):
            self.side_copy(chip).wait_send()
            for tile in range(self.tiles):
                pl.when(chip != place.chip)(lambda: self.line_copy(0, chip, tile).wait_send())
            return carry

        lax.fori_loop(0, place.chips, drain, 0)


class SquareScatter:
    def __init__(self, place, piece, owned, bufs, sems):
        self.place, self.piece, self.owned = place, piece, owned
        self.out, self.arrived = bufs
        self.send, self.recv = sems

    def copy(self, kind, way):
        place = self.place
        turn = way if kind < 2 else 1 - way
        peer = place.x_peer + turn * (place.y_peer - place.x_peer)
        return remote(
            self.out.at[kind, way],
            self.arrived.at[kind, way],
            self.send.at[kind, way],
            self.recv.at[kind, way],
            (peer, place.me),
        )

    def owner(self, kind, way):
        place = self.place
        near = place.x_peer + way * (place.y_peer - place.x_peer)
        other = place.y_peer + way * (place.x_peer - place.y_peer)
        return (place.across, near, other, place.dp)[kind]

    def following(self, kind, way):
        after = self.owner(kind, 1) if kind == 3 else self.owner(kind + 1, 0)
        return jnp.where(way == 0, self.owner(kind, 1), after), 1 - way

    def one(self, kind, way):
        value = self.piece(self.owner(kind, way), way)
        if kind == 2:
            self.copy(0, way).wait_recv()
            value = value + self.arrived[0, way].astype(jnp.float32)
        if kind < 3:
            self.out[kind, way] = value.astype(jnp.bfloat16)
            self.copy(kind, way).start()
        else:
            self.owned[way] = value

    def stage(self, kind):
        def one(way, carry):
            self.one(kind, way)
            return carry

        lax.fori_loop(0, 2, one, 0)

    def end(self):
        def one(way, carry):
            self.copy(1, way).wait_recv()
            self.copy(2, way).wait_recv()
            self.owned[way] = (
                self.owned[way]
                + self.arrived[1, way].astype(jnp.float32)
                + self.arrived[2, way].astype(jnp.float32)
            )
            for kind in range(3):
                self.copy(kind, way).wait_send()
            return carry

        lax.fori_loop(0, 2, one, 0)


def square_scratch(half):
    dma = pltpu.SemaphoreType.DMA
    return [
        pltpu.VMEM((3, 2) + half, jnp.bfloat16),
        pltpu.VMEM((3, 2) + half, jnp.bfloat16),
        dma((3, 2)),
        dma((3, 2)),
    ]


class SmallSum:
    def __init__(self, place, rows, alone, bufs, sems):
        self.place, self.rows, self.alone = place, rows, alone
        self.side_buf, self.line_buf, self.square_buf = bufs
        self.send, self.recv = sems

    def side_copy(self):
        place = self.place
        return remote(
            self.rows,
            self.side_buf,
            self.send.at[0],
            self.recv.at[0],
            place.side,
        )

    def line_copy(self, hop):
        place = self.place
        chip = (place.chip + hop) % place.chips
        return remote(
            self.rows,
            self.line_buf.at[place.chip],
            self.send.at[hop],
            self.recv.at[hop],
            (place.dp, 2 * chip + place.core),
        )

    def line_landed(self, hop):
        place = self.place
        chip = (place.chip + place.chips - hop) % place.chips
        remote(
            self.rows,
            self.line_buf.at[chip],
            self.send.at[hop],
            self.recv.at[hop],
            (place.dp, 2 * chip + place.core),
        ).wait_recv()

    def square_copy(self, hop):
        place = self.place
        target = (place.dp + hop) % 4
        at = place.chips + hop
        return remote(
            self.rows,
            self.square_buf.at[place.dp],
            self.send.at[at],
            self.recv.at[at],
            (target, place.me),
        )

    def square_landed(self, hop):
        place = self.place
        source = (place.dp + 4 - hop) % 4
        at = place.chips + hop
        remote(
            self.rows,
            self.square_buf.at[source],
            self.send.at[at],
            self.recv.at[at],
            (source, place.me),
        ).wait_recv()

    def put(self, value):
        if self.alone < self.rows.shape[0]:
            index = lax.broadcasted_iota(jnp.int32, value.shape, 0)
            value = jnp.where(index < self.alone, value, self.rows[...])
        self.rows[...] = value

    def begin(self):
        self.side_copy().start()

    def middle(self):
        self.side_copy().wait()
        self.put(self.rows[...] + self.side_buf[...])
        self.line_buf[self.place.chip] = self.rows[...]
        for hop in range(1, self.place.chips):
            self.line_copy(hop).start()

    def late(self):
        place = self.place
        for hop in range(1, place.chips):
            self.line_copy(hop).wait_send()
            self.line_landed(hop)
        value = self.line_buf[0]
        for chip in range(1, place.chips):
            value = value + self.line_buf[chip]
        self.put(value)
        self.square_buf[place.dp] = self.rows[...]
        for hop in range(1, 4):
            self.square_copy(hop).start()

    def end(self):
        for hop in range(1, 4):
            self.square_copy(hop).wait_send()
            self.square_landed(hop)
        value = self.square_buf[0]
        for device in range(1, 4):
            value = value + self.square_buf[device]
        self.rows[...] = value


def small_scratch(chips, rows, width):
    dma = pltpu.SemaphoreType.DMA
    return [
        pltpu.VMEM((rows, width), jnp.float32),
        pltpu.VMEM((chips, rows, width), jnp.float32),
        pltpu.VMEM((4, rows, width), jnp.float32),
        dma((chips + 4,)),
        dma((chips + 4,)),
    ]


def scatter_scratch(chips, count, width):
    low = jnp.bfloat16
    dma = pltpu.SemaphoreType.DMA
    return [
        pltpu.VMEM((count, width), jnp.float32),
        pltpu.VMEM((chips, count, width), low),
        pltpu.VMEM((chips, count, width), low),
        pltpu.VMEM((chips + 1, count, width), low),
        dma((chips,)),
        dma((chips,)),
        dma((chips, 4)),
        dma((chips + 1, 4)),
    ]


def alive(shape, axis, start, bounds):
    place = lax.broadcasted_iota(jnp.int32, shape, axis) + start
    return jnp.where((place >= bounds[0]) & (place < bounds[1]), 1.0, 0.0)


def by_rows(count, tile, action):
    def one(index, carry):
        action(pl.ds(pl.multiple_of(index * tile, tile), tile))
        return carry

    lax.fori_loop(0, count // tile, one, 0)


def attend_out_kernel(
    chips,
    mixed_hbm,
    offsets_ref,
    lengths_ref,
    out_hbm,
    rows_hbm,
    branch_ref,
    gain_ref,
    shift_ref,
    bias_ref,
    up_ref,
    down_ref,
    attended_ref,
    lse_ref,
    resid_ref,
    normed_ref,
    branch_whole,
    up_whole,
    down_whole,
    mixed_ref,
    out_ref,
    rows_ref,
    fetch_sem,
    seg_col_ref,
    seg_row_ref,
    score_ref,
    blocks,
    line_send,
    line_recv,
    up_send,
    up_recv,
    down_send,
    down_recv,
    own_sem,
    keep_sem,
    *scatter,
):
    place = Place(chips)
    bounds = (offsets_ref[0], offsets_ref[0] + lengths_ref[0])
    count = rows_ref.shape[0]
    fetched = fetch(
        [(mixed_hbm, mixed_ref), (out_hbm, out_ref), (rows_hbm, rows_ref)], fetch_sem
    )
    place.greet(True)

    def square(shard, whole, send, recv):
        half = shard.shape[0] // 2
        return SquareGather(
            place,
            shard,
            lambda owner: whole.at[owner],
            lambda owner, which: whole.at[owner, pl.ds(which * half, half)],
            send,
            recv,
        )

    up = square(up_ref, up_whole, up_send, up_recv)
    down = square(down_ref, down_whole, down_send, down_recv)
    up.begin()
    down.begin()
    own = [
        pltpu.make_async_copy(up_ref, up_whole.at[place.dp], own_sem.at[0]),
        pltpu.make_async_copy(down_ref, down_whole.at[place.dp], own_sem.at[1]),
    ]
    own[0].start()
    own[1].start()

    def term(block, tile):
        span = pl.ds(pl.multiple_of(block * count, count), count)
        return jnp.dot(attended_ref[span, :], out_ref[tile], preferred_element_type=jnp.float32)

    def prepare(chip):
        def one(index, carry):
            attend_rows(
                chip * (2 * count // ATTEND_ROWS) + index,
                mixed_ref,
                seg_col_ref,
                seg_row_ref,
                attended_ref,
                lse_ref,
                score_ref,
            )
            return carry

        lax.fori_loop(0, 2 * count // ATTEND_ROWS, one, 0)

    def copy_in(span):
        blocks[place.me, span, :] = branch_ref[span, :]

    by_rows(count, 64, copy_in)
    line = LineGather(place, blocks, line_send, line_recv)
    line.begin()
    seg_row_ref[...] = alive(seg_row_ref.shape, 1, 0, bounds)

    def column(span):
        seg_col_ref[span, :] = alive((64, 1), 0, span.start, bounds)

    by_rows(seg_col_ref.shape[0], 64, column)
    for copy in fetched:
        copy.wait()
    sums = LineScatter(place, term, 4, scatter[:4], scatter[4:8], prepare)
    sums.begin()

    def keep(block, part):
        half = count // 2
        place_of = ((block // 2 * 2 + part) * 2 + block % 2) * half
        span = pl.ds(pl.multiple_of(place_of, half), half)
        source = blocks.at[block, pl.ds(part * half, half)]
        return pltpu.make_async_copy(source, branch_whole.at[span], keep_sem.at[block, part])

    def step(index, carry):
        sums.step(index, True)
        pl.when(index < chips - 1)(lambda: line.step(index + 1))

        @pl.when(index == 1)
        def _():
            up.middle()
            down.middle()

        return carry

    lax.fori_loop(0, chips, step, 0)
    total = scatter[0]

    def norm(span):
        resid = rows_ref[span, :].astype(jnp.float32) + total[span, :] + bias_ref[...]
        resid_ref[span, :] = resid
        normed_ref[span, :] = norm_rows(resid, gain_ref[...], shift_ref[...]).astype(jnp.bfloat16)

    by_rows(count, 64, norm)

    def store(block, carry):
        pl.when((block % 2 != place.core))(lambda: line.arrive(block // 2, block % 2))
        keep(block, 0).start()
        keep(block, 1).start()
        return carry

    lax.fori_loop(0, 2 * chips, store, 0)
    sums.finish()
    line.finish()
    up.end()
    down.end()
    up.finish()
    down.finish()
    own[0].wait()
    own[1].wait()

    def kept(block, carry):
        keep(block, 0).wait()
        keep(block, 1).wait()
        return carry

    lax.fori_loop(0, 2 * chips, kept, 0)


def attend_out_call(
    mixed, offsets, lengths, out_whole, rows, branch, gain, shift, bias, up, down, chips
):
    count, width = rows.shape
    local = mixed.shape[2]
    total = 2 * chips * count
    low = jnp.bfloat16
    vmem = pl.BlockSpec(memory_space=pltpu.VMEM)
    hbm = pl.BlockSpec(memory_space=pl.ANY)
    dma = pltpu.SemaphoreType.DMA
    return pl.pallas_call(
        functools.partial(attend_out_kernel, chips),
        out_shape=(
            jax.ShapeDtypeStruct((total, local), low),
            jax.ShapeDtypeStruct((total, 1 + local // HEAD_DIM), jnp.float32),
            jax.ShapeDtypeStruct((count, width), jnp.float32),
            jax.ShapeDtypeStruct((count, width), low),
            jax.ShapeDtypeStruct((total, width), low),
            jax.ShapeDtypeStruct((4,) + up.shape, low),
            jax.ShapeDtypeStruct((4,) + down.shape, low),
        ),
        in_specs=[hbm] + [pl.BlockSpec(memory_space=pltpu.SMEM)] * 2 + [hbm] * 2 + [vmem] * 6,
        out_specs=(vmem, vmem, vmem, vmem, hbm, hbm, hbm),
        scratch_shapes=[
            pltpu.VMEM(mixed.shape, low),
            pltpu.VMEM(out_whole.shape, low),
            pltpu.VMEM(rows.shape, low),
            dma((3,)),
            pltpu.VMEM((total, 1), jnp.float32),
            pltpu.VMEM((1, total), jnp.float32),
            pltpu.VMEM((local // HEAD_DIM, ATTEND_ROWS, total), jnp.float32),
            pltpu.VMEM((2 * chips, count, width), low),
            dma((3, chips)),
            dma((2 * chips,)),
            dma((4,)),
            dma((4,)),
            dma((4,)),
            dma((4,)),
            dma((2,)),
            dma((2 * chips, 2)),
        ]
        + scatter_scratch(chips, count, width),
        compiler_params=pltpu.CompilerParams(
            collective_id=1, has_side_effects=True, vmem_limit_bytes=VMEM_LIMIT
        ),
        cost_estimate=pl.CostEstimate(flops=10**11, bytes_accessed=0, transcendentals=0),
        name="attend_out",
    )(mixed, offsets, lengths, out_whole, rows, branch, gain, shift, bias, up, down)


def input_back_kernel(
    chips,
    stacked_hbm,
    mix_hbm,
    rows_hbm,
    resid_grad_hbm,
    gain_ref,
    row_sums_ref,
    bias_down_ref,
    mix_bias_ref,
    up_bias_ref,
    hidden_hbm,
    out_grad_hbm,
    normed_one_ref,
    normed_two_ref,
    grad_ref,
    late_out_ref,
    early_out_ref,
    mix_grad_hbm,
    up_grad_hbm,
    out_owned_hbm,
    mix_grad_ref,
    up_grad_ref,
    out_owned_ref,
    hat_buf,
    inverse_buf,
    emit_sem,
    stacked_ref,
    mix_ref,
    rows_ref,
    resid_grad_ref,
    hidden_ref,
    out_grad_ref,
    fetch_sem,
    columns_buf,
    columns_sem,
    *scatter,
):
    place = Place(chips)
    count = rows_ref.shape[0]
    fetched = fetch(
        [
            (stacked_hbm, stacked_ref),
            (mix_hbm, mix_ref),
            (hidden_hbm, hidden_ref),
            (out_grad_hbm, out_grad_ref),
            (rows_hbm, rows_ref),
            (resid_grad_hbm, resid_grad_ref),
        ],
        fetch_sem,
    )
    place.greet(True, True)
    fetched[0].wait()
    fetched[1].wait()
    local = mix_bias_ref.shape[1]
    units = up_bias_ref.shape[1]
    early_out_ref[0:3, :] = row_sums_ref[...]
    early_out_ref[3:4, :] = bias_down_ref[...]
    early_out_ref[4:5, :] = jnp.zeros((1, early_out_ref.shape[1]), jnp.float32)
    early_out_ref[4:5, 0:local] = mix_bias_ref[0:1, :]
    early_out_ref[4:5, local : 2 * local] = mix_bias_ref[1:2, :]
    early_out_ref[4:5, 2 * local : 2 * local + units] = up_bias_ref[...]
    early = SmallSum(place, early_out_ref, 4, scatter[16:19], scatter[19:21])
    late = SmallSum(place, late_out_ref, late_out_ref.shape[0], scatter[21:24], scatter[24:26])

    def term(block, tile):
        span = pl.ds(pl.multiple_of(block * count, count), count)
        result = None
        for part in range(3):
            product = lax.dot_general(
                stacked_ref[part, span, :],
                mix_ref[part, tile],
                TURNED,
                preferred_element_type=jnp.float32,
            )
            result = product if result is None else result + product
        return result

    sums = LineScatter(place, term, 4, scatter[:4], scatter[4:8])
    sums.begin()
    early.begin()
    half_columns = columns_buf.shape[2]

    def load(which, owner, half):
        start = pl.multiple_of((2 * owner + half) * half_columns, half_columns)
        source = (normed_one_ref, normed_two_ref)[which]
        return pltpu.make_async_copy(
            source.at[:, pl.ds(start, half_columns)], columns_buf.at[which], columns_sem.at[which]
        )

    def mix_piece(owner, half):
        load(0, owner, half).wait()
        return jnp.stack(
            [
                lax.dot_general(
                    columns_buf[0],
                    stacked_ref[part],
                    CROSSED,
                    preferred_element_type=jnp.float32,
                )
                for part in range(3)
            ]
        )

    def up_piece(owner, half):
        load(1, owner, half).wait()
        return lax.dot_general(
            columns_buf[1], hidden_ref[...], CROSSED, preferred_element_type=jnp.float32
        )

    out_units = out_grad_ref.shape[0] // 2
    out_columns = out_grad_ref.shape[1] // 4

    def out_piece(owner, half):
        units = pl.ds(pl.multiple_of(half * out_units, out_units), out_units)
        columns = pl.ds(pl.multiple_of(owner * out_columns, 128), out_columns)
        return out_grad_ref[units, columns]

    out = SquareScatter(place, out_piece, out_owned_ref, scatter[26:28], scatter[28:30])
    mix = SquareScatter(place, mix_piece, mix_grad_ref, scatter[8:10], scatter[10:12])
    up = SquareScatter(place, up_piece, up_grad_ref, scatter[12:14], scatter[14:16])

    load(1, place.across, 0).start()
    load(0, place.across, 0).start()

    def stage(kind):
        def one(way, carry):
            for which, matrix in ((1, up), (0, mix)):
                matrix.one(kind, way)
                owner, half = matrix.following(kind, way)
                more = (way == 0) | (kind < 3)
                pl.when(more)(lambda: load(which, owner, half).start())
            out.one(kind, way)
            return carry

        lax.fori_loop(0, 2, one, 0)

    for copy in fetched[2:]:
        copy.wait()

    leaving = [
        pltpu.make_async_copy(source, target, emit_sem.at[index])
        for index, (source, target) in enumerate(
            [
                (up_grad_ref, up_grad_hbm),
                (mix_grad_ref, mix_grad_hbm),
                (out_owned_ref, out_owned_hbm),
            ]
        )
    ]

    def hats(span):
        _, hat, inverse = layer_norm_parts(
            rows_ref[span, :].astype(jnp.float32), gain_ref[...], 0.0
        )
        hat_buf[span, :] = hat
        inverse_buf[span, :] = inverse

    def step(index, carry):
        @pl.when(index == 3)
        def _():
            stage(3)
            by_rows(count, 64, hats)

        sums.step(index)
        for kind in range(3):

            @pl.when(index == kind)
            def _():
                stage(kind)
                if kind == 1:
                    early.middle()
                if kind == 2:
                    early.late()

        return carry

    lax.fori_loop(0, chips, step, 0)
    total = scatter[0]
    late_out_ref[...] = jnp.zeros_like(late_out_ref)

    def columns(span):
        one_grad = total[span, :]
        late_out_ref[0:1, :] += jnp.sum(one_grad * hat_buf[span, :], axis=0, keepdims=True)
        late_out_ref[1:2, :] += jnp.sum(one_grad, axis=0, keepdims=True)

    def back(span):
        grad_ref[span, :] = resid_grad_ref[span, :] + layer_norm_back(
            total[span, :], hat_buf[span, :], inverse_buf[span, :], gain_ref[...]
        )

    by_rows(count, 64, columns)
    late.begin()
    up.end()
    leaving[0].start()
    late.middle()
    mix.end()
    leaving[1].start()
    by_rows(count, 64, back)
    late.late()
    out.end()
    leaving[2].start()
    early.end()
    sums.finish()
    late.end()
    for copy in leaving:
        copy.wait()


def input_back_call(
    stacked, mix_whole, rows, resid_grad, gain, smalls, hidden, out_grad, normed_one, normed_two, chips
):
    count, width = rows.shape
    total, units = hidden.shape
    local = stacked.shape[2]
    half = width // 8
    vmem = pl.BlockSpec(memory_space=pltpu.VMEM)
    hbm = pl.BlockSpec(memory_space=pl.ANY)
    return pl.pallas_call(
        functools.partial(input_back_kernel, chips),
        out_shape=(
            jax.ShapeDtypeStruct((count, width), jnp.float32),
            jax.ShapeDtypeStruct((2, width), jnp.float32),
            jax.ShapeDtypeStruct((5, width), jnp.float32),
            jax.ShapeDtypeStruct((2, 3, half, local), jnp.float32),
            jax.ShapeDtypeStruct((2, half, units), jnp.float32),
            jax.ShapeDtypeStruct((2, local // 2, width // 4), jnp.float32),
        ),
        in_specs=[hbm] * 4 + [vmem] * 5 + [hbm] * 4,
        out_specs=(vmem,) * 3 + (hbm,) * 3,
        scratch_shapes=[
            pltpu.VMEM((2, 3, half, local), jnp.float32),
            pltpu.VMEM((2, half, units), jnp.float32),
            pltpu.VMEM((2, local // 2, width // 4), jnp.float32),
            pltpu.VMEM((count, width), jnp.float32),
            pltpu.VMEM((count, 1), jnp.float32),
            pltpu.SemaphoreType.DMA((3,)),
            pltpu.VMEM(stacked.shape, jnp.bfloat16),
            pltpu.VMEM(mix_whole.shape, jnp.bfloat16),
            pltpu.VMEM(rows.shape, jnp.bfloat16),
            pltpu.VMEM(resid_grad.shape, jnp.float32),
            pltpu.VMEM(hidden.shape, jnp.bfloat16),
            pltpu.VMEM(out_grad.shape, jnp.float32),
            pltpu.SemaphoreType.DMA((6,)),
            pltpu.VMEM((2, total, half), jnp.bfloat16),
            pltpu.SemaphoreType.DMA((2,)),
        ]
        + scatter_scratch(chips, count, width)
        + square_scratch((3, half, local))
        + square_scratch((half, units))
        + small_scratch(chips, 5, width)
        + small_scratch(chips, 2, width)
        + square_scratch((local // 2, width // 4)),
        compiler_params=pltpu.CompilerParams(
            collective_id=2, has_side_effects=True, vmem_limit_bytes=VMEM_LIMIT
        ),
        cost_estimate=pl.CostEstimate(flops=10**11, bytes_accessed=0, transcendentals=0),
        name="input_back",
    )(stacked, mix_whole, rows, resid_grad, gain, *smalls, hidden, out_grad, normed_one, normed_two)


GELU_SLOPE = 0.7978845608028654
GELU_CUBE = 0.044715


def gelu_parts(hidden):
    square = hidden * hidden
    bend = jnp.tanh(GELU_SLOPE * hidden * (1.0 + GELU_CUBE * square))
    lift = 0.5 * (1.0 + bend)
    slope = lift + 0.5 * hidden * (1.0 - bend * bend) * (
        GELU_SLOPE * (1.0 + 3.0 * GELU_CUBE * square)
    )
    return hidden * lift, slope


def feed_kernel(
    chips,
    parts,
    normed_ref,
    branch_ref,
    up_hbm,
    down_hbm,
    bias_ref,
    resid_hbm,
    own_branch_hbm,
    gain_ref,
    normed_whole,
    active_hbm,
    hidden_hbm,
    grad_ref,
    grad_low_ref,
    sums_ref,
    bias_grad_ref,
    up_ref,
    down_ref,
    resid_ref,
    own_branch_ref,
    active_ref,
    hidden_ref,
    fetch_sem,
    emit_sem,
    blocks,
    branch_buf,
    work,
    hold,
    side_out,
    side_in,
    line_in,
    line_send,
    line_recv,
    keep_sem,
    load_sem,
    side_send,
    side_recv,
    out_send,
    out_recv,
):
    place = Place(chips)
    count = normed_ref.shape[0]
    rows = count // parts
    pair = 2 * rows
    last = chips - 1
    fetched = fetch(
        [
            (up_hbm, up_ref),
            (down_hbm, down_ref),
            (resid_hbm, resid_ref),
            (own_branch_hbm, own_branch_ref),
        ],
        fetch_sem,
    )
    place.greet(False)

    def fill(part, carry):
        block = 2 * (place.chip * parts + part) + place.core
        blocks[block] = normed_ref[pl.ds(pl.multiple_of(part * rows, rows), rows), :]
        return carry

    lax.fori_loop(0, parts, fill, 0)
    line = LineGather(place, blocks, line_send, line_recv, parts)
    line.begin_part(0)
    line.copy(2, place.chip, 1).start()
    pl.when(place.has_up & jnp.logical_not(place.has_down))(
        lambda: line.copy(0, place.chip, 1).start()
    )
    pl.when(place.has_down & jnp.logical_not(place.has_up))(
        lambda: line.copy(1, place.chip, 1).start()
    )
    bias_grad_ref[...] = jnp.zeros_like(bias_grad_ref)

    def piece_span(piece):
        return pl.ds(pl.multiple_of(piece * pair, pair), pair)

    def load(piece, slot):
        return pltpu.make_async_copy(
            branch_ref.at[piece_span(piece)], branch_buf.at[slot], load_sem.at[slot]
        )

    def keep(piece, core):
        span = pl.ds(pl.multiple_of(piece * pair + core * rows, rows), rows)
        return pltpu.make_async_copy(
            blocks.at[2 * piece + core], normed_whole.at[span], keep_sem.at[piece, core]
        )

    def side_copy(piece):
        return remote(
            side_out.at[piece],
            side_in.at[piece],
            side_send.at[piece],
            side_recv.at[piece],
            place.side,
        )

    chunk = normed_ref.shape[1] // 4

    def line_copy(way, chip, part, tile):
        piece = chip * parts + part
        next_chip = place.chip + 1 - 2 * way
        slot = jnp.where((way == 1) & (chip == next_chip), chips * parts + part, piece)
        span = slice(tile * chunk, (tile + 1) * chunk)
        return remote(
            line_in.at[piece, :, span],
            line_in.at[slot, :, span],
            out_send.at[piece, tile],
            out_recv.at[slot, tile],
            place.toward(way),
        )

    def line_landed(way, chip, part, tile):
        piece = chip * parts + part
        slot = jnp.where((way == 1) & (chip == place.chip), chips * parts + part, piece)
        span = slice(tile * chunk, (tile + 1) * chunk)
        remote(
            line_in.at[slot, :, span],
            line_in.at[slot, :, span],
            out_send.at[piece, tile],
            out_recv.at[slot, tile],
            place.toward(way),
        ).wait_recv()
        return slot

    def emit(piece):
        span = piece_span(piece)
        return [
            pltpu.make_async_copy(active_ref.at[span], active_hbm.at[span], emit_sem.at[piece, 0]),
            pltpu.make_async_copy(hidden_ref.at[span], hidden_hbm.at[span], emit_sem.at[piece, 1]),
        ]

    width = 512
    tiles = up_ref.shape[2] // width

    def compute(chip, part, side):
        piece = chip * parts + part
        keep(piece, 0).start()
        keep(piece, 1).start()
        span = piece_span(piece)
        own_rows = blocks[pl.ds(2 * piece, 2)].reshape(pair, -1)
        load(piece, side).wait()

        def tile(index, carry):
            units = pl.ds(pl.multiple_of(index * width, width), width)
            hidden = jnp.dot(
                own_rows,
                up_ref[:, :, units].reshape(-1, width),
                preferred_element_type=jnp.float32,
            )
            active, slope = gelu_parts(hidden + bias_ref[:, units])
            active_ref[span, units] = active.astype(jnp.bfloat16)
            grad = None
            for owner in range(4):
                columns = down_ref.shape[2]
                product = lax.dot_general(
                    branch_buf[side, :, owner * columns : (owner + 1) * columns],
                    down_ref[owner, units, :],
                    TURNED,
                    preferred_element_type=jnp.float32,
                )
                grad = product if grad is None else grad + product
            low = (grad * slope).astype(jnp.bfloat16)
            hidden_ref[span, units] = low
            bias_grad_ref[:, units] += jnp.sum(low.astype(jnp.float32), axis=0, keepdims=True)
            return carry

        lax.fori_loop(0, tiles, tile, 0)
        low = hidden_ref[span, :]
        depth = up_ref.shape[1]
        for owner in range(4):
            columns = slice(owner * depth, (owner + 1) * depth)
            product = lax.dot_general(
                low, up_ref[owner], TURNED, preferred_element_type=jnp.float32
            )
            work[:, :, columns] = product.reshape(2, rows, depth)
        side_out[piece] = work[1 - place.core].astype(jnp.bfloat16)
        side_copy(piece).start()
        hold[piece] = work[place.core]
        for copy in emit(piece):
            copy.start()

    def pass_on(way, chip, part):
        piece = chip * parts + part
        side_copy(piece).wait_recv()
        behind = ((way == 0) & place.has_down) | ((way == 1) & place.has_up)
        for tile in range(4):
            span = slice(tile * chunk, (tile + 1) * chunk)
            total = hold[piece, :, span] + side_in[piece, :, span].astype(jnp.float32)

            @pl.when(behind)
            def _():
                slot = line_landed(way, chip, part, tile)
                line_in[piece, :, span] = (
                    total + line_in[slot, :, span].astype(jnp.float32)
                ).astype(jnp.bfloat16)

            @pl.when(jnp.logical_not(behind))
            def _():
                line_in[piece, :, span] = total.astype(jnp.bfloat16)

            line_copy(way, chip, part, tile).start()

    def coming(index, side):
        count_beyond = jnp.where(side == 0, place.chip, last - place.chip)
        early = index <= count_beyond
        distance = jnp.where(early, index, 2 * count_beyond + 1 - index)
        valid = (index == 0) | (index <= 2 * count_beyond)
        chip = jnp.where(index == 0, place.chip, place.chip + distance * (2 * side - 1))
        part = jnp.where(index == 0, side, jnp.where(early, 0, 1))
        return valid, chip, part, count_beyond

    def turn(index, carry):
        def ahead(side, inner):
            valid, chip, part, _ = coming(index, side)
            pl.when(valid)(lambda: load(chip * parts + part, side).start())
            return inner

        lax.fori_loop(0, 2, ahead, 0)

        @pl.when(index > 0)
        def _():
            for side in range(2):
                valid, chip, part, count_beyond = coming(index, side)
                onward = (place.has_up, place.has_down)[side]

                @pl.when(valid)
                def _():
                    line.arrive(chip, place.core, part)
                    pl.when(onward)(lambda: line.copy(side, chip, part).start())
                    pl.when(onward & (index == 2 * count_beyond))(
                        lambda: line.copy(side, place.chip, 1).start()
                    )
                    line.copy(2, chip, part).start()

        def one(side, inner):
            valid, chip, part, _ = coming(index, side)

            @pl.when(valid)
            def _():
                line.arrive(chip, 1 - place.core, part)
                compute(chip, part, side)

            return inner

        lax.fori_loop(0, 2, one, 0)
        def onward(order, inner):
            way = order // 2
            part = order % 2
            here = place.chip + way * (last - 2 * place.chip)
            reach = jnp.where(part == 0, index - here, 2 * last + 1 + here - index)

            @pl.when((reach > here) & (reach < chips))
            def _():
                pass_on(way, reach + way * (last - 2 * reach), part)

            return inner

        lax.fori_loop(0, 4, onward, 0)
        return carry

    fetched[0].wait()
    fetched[1].wait()
    lax.fori_loop(0, 2 * last + 1, turn, 0)
    sums_ref[...] = jnp.zeros_like(sums_ref)
    fetched[2].wait()
    fetched[3].wait()

    def own_part(part, carry):
        piece = place.chip * parts + part
        side_copy(piece).wait_recv()
        hold[piece] += side_in[piece].astype(jnp.float32)

        for tile in range(4):

            @pl.when(place.has_down)
            def _():
                line_landed(0, place.chip, part, tile)

            @pl.when(place.has_up)
            def _():
                line_landed(1, place.chip, part, tile)

        pieces_end = chips * parts

        @pl.when(place.has_down)
        def _():
            hold[piece] += line_in[piece].astype(jnp.float32)

        @pl.when(place.has_up)
        def _():
            hold[piece] += line_in[pieces_end + part].astype(jnp.float32)

        tile = 64

        def back(index, inner):
            here = pl.ds(pl.multiple_of(index * tile, tile), tile)
            span = pl.ds(pl.multiple_of(part * rows + index * tile, tile), tile)
            two_grad = hold[piece, here, :]
            _, hat, inverse = layer_norm_parts(resid_ref[span, :], gain_ref[...], 0.0)
            grad = own_branch_ref[span, :].astype(jnp.float32) + layer_norm_back(
                two_grad, hat, inverse, gain_ref[...]
            )
            grad_ref[span, :] = grad
            grad_low_ref[span, :] = grad.astype(jnp.bfloat16)
            sums_ref[0:1, :] += jnp.sum(two_grad * hat, axis=0, keepdims=True)
            sums_ref[1:2, :] += jnp.sum(two_grad, axis=0, keepdims=True)
            sums_ref[2:3, :] += jnp.sum(grad, axis=0, keepdims=True)
            return inner

        lax.fori_loop(0, rows // tile, back, 0)
        return carry

    lax.fori_loop(0, parts, own_part, 0)
    line.finish()

    def drain(piece, carry):
        side_copy(piece).wait_send()
        keep(piece, 0).wait()
        keep(piece, 1).wait()
        for copy in emit(piece):
            copy.wait()
        for tile in range(4):
            pl.when(piece // parts != place.chip)(
                lambda: line_copy(0, piece // parts, piece % parts, tile).wait_send()
            )
        return carry

    lax.fori_loop(0, chips * parts, drain, 0)


def feed_call(normed, branch, up_whole, down_whole, bias, resid, own_branch, gain, chips):
    count, width = normed.shape
    total = 2 * chips * count
    units = up_whole.shape[2]
    parts = 2
    rows = count // parts
    low = jnp.bfloat16
    vmem = pl.BlockSpec(memory_space=pltpu.VMEM)
    hbm = pl.BlockSpec(memory_space=pl.ANY)
    dma = pltpu.SemaphoreType.DMA
    pieces = chips * parts
    return pl.pallas_call(
        functools.partial(feed_kernel, chips, parts),
        out_shape=(
            jax.ShapeDtypeStruct((total, width), low),
            jax.ShapeDtypeStruct((total, units), low),
            jax.ShapeDtypeStruct((total, units), low),
            jax.ShapeDtypeStruct((count, width), jnp.float32),
            jax.ShapeDtypeStruct((count, width), low),
            jax.ShapeDtypeStruct((3, width), jnp.float32),
            jax.ShapeDtypeStruct((1, units), jnp.float32),
        ),
        in_specs=[vmem, hbm, hbm, hbm, vmem, hbm, hbm, vmem],
        out_specs=(hbm,) * 3 + (vmem,) * 4,
        scratch_shapes=[
            pltpu.VMEM(up_whole.shape, low),
            pltpu.VMEM(down_whole.shape, low),
            pltpu.VMEM(resid.shape, jnp.float32),
            pltpu.VMEM(own_branch.shape, low),
            pltpu.VMEM((total, units), low),
            pltpu.VMEM((total, units), low),
            dma((4,)),
            dma((pieces, 2)),
            pltpu.VMEM((2 * pieces, rows, width), low),
            pltpu.VMEM((2, 2 * rows, width), low),
            pltpu.VMEM((2, rows, width), jnp.float32),
            pltpu.VMEM((pieces, rows, width), jnp.float32),
            pltpu.VMEM((pieces, rows, width), low),
            pltpu.VMEM((pieces, rows, width), low),
            pltpu.VMEM((pieces + parts, rows, width), low),
            dma((3, pieces)),
            dma((2 * pieces,)),
            dma((pieces, 2)),
            dma((2,)),
            dma((pieces,)),
            dma((pieces,)),
            dma((pieces, 4)),
            dma((pieces + parts, 4)),
        ],
        compiler_params=pltpu.CompilerParams(
            collective_id=3, has_side_effects=True, vmem_limit_bytes=VMEM_LIMIT
        ),
        cost_estimate=pl.CostEstimate(flops=10**11, bytes_accessed=0, transcendentals=0),
        name="feed",
    )(normed, branch, up_whole, down_whole, bias, resid, own_branch, gain)


def branch_back_kernel(
    chips,
    parts,
    branch_ref,
    active_hbm,
    down_hbm,
    attended_hbm,
    out_hbm,
    shift_ref,
    offsets_ref,
    lengths_ref,
    mixed_hbm,
    aux_hbm,
    resid_ref,
    cotangent_ref,
    stacked_hbm,
    bias_sum_ref,
    down_grad_hbm,
    out_grad_hbm,
    output_ref,
    blocks,
    stacked_ref,
    down_grad_ref,
    out_grad_ref,
    emit_sem,
    active_ref,
    down_ref,
    attended_ref,
    out_ref,
    mixed_ref,
    aux_ref,
    fetch_sem,
    seg_row_ref,
    block_buf,
    columns_buf,
    resid_buf,
    key_sum,
    value_sum,
    line_send,
    line_recv,
    columns_sem,
    block_sem,
    *scatter,
):
    place = Place(chips)
    bounds = (offsets_ref[0], offsets_ref[0] + lengths_ref[0])
    count = branch_ref.shape[0]
    rows = count // parts
    fetched = fetch(
        [
            (active_hbm, active_ref),
            (down_hbm, down_ref),
            (attended_hbm, attended_ref),
            (out_hbm, out_ref),
            (mixed_hbm, mixed_ref),
            (aux_hbm, aux_ref),
            (resid_ref, resid_buf),
        ],
        fetch_sem,
    )
    place.greet(True)
    line = LineGather(place, blocks, line_send, line_recv, 1, branch_ref)
    line.begin()

    def term(block, tile):
        chip, core = block // 2, block % 2
        taken = []
        for part in range(parts):
            start = ((chip * parts + part) * 2 + core) * rows
            taken.append(active_ref[pl.ds(pl.multiple_of(start, rows), rows), :])
        return jnp.dot(
            jnp.concatenate(taken, axis=0), down_ref[tile], preferred_element_type=jnp.float32
        )

    fetched[0].wait()
    fetched[1].wait()
    sums = LineScatter(place, term, 4, scatter[:4], scatter[4:8])
    sums.begin()
    seg_row_ref[...] = alive(seg_row_ref.shape, 1, 0, bounds)
    out_grad_ref[...] = jnp.zeros_like(out_grad_ref)
    key_sum[...] = jnp.zeros_like(key_sum)
    value_sum[...] = jnp.zeros_like(value_sum)
    bias_sum_ref[...] = jnp.zeros_like(bias_sum_ref)
    down_units = down_ref.shape[1] // 2
    down_columns = down_ref.shape[2]

    def load_columns(owner):
        return pltpu.make_async_copy(
            cotangent_ref.at[:, pl.ds(pl.multiple_of(owner * down_columns, 128), down_columns)],
            columns_buf,
            columns_sem,
        )

    load_columns(place.across).start()

    def down_piece(owner, half):
        units = pl.ds(pl.multiple_of(half * down_units, down_units), down_units)
        return lax.dot_general(
            active_ref[:, units], columns_buf[...], CROSSED, preferred_element_type=jnp.float32
        )

    down = SquareScatter(place, down_piece, down_grad_ref, scatter[8:10], scatter[10:12])
    def down_stage(kind):
        def one(way, carry):
            fresh = (way == 0) if kind in (0, 3) else ((way >= 0) if kind == 1 else (way == 1))
            pl.when(fresh)(lambda: load_columns(place.dp).wait())
            down.one(kind, way)
            owner, _ = down.following(kind, way)
            more = (way == 1) if kind == 0 else ((way == 0) if kind == 1 else (way >= 0))
            if kind < 3:
                pl.when(more)(lambda: load_columns(owner).start())
            return carry

        lax.fori_loop(0, 2, one, 0)

    def load_part(source, owner):
        columns = out_ref.shape[2]
        span = slice(owner * columns, (owner + 1) * columns)
        return pltpu.make_async_copy(source.at[:, span], block_buf.at[:, span], block_sem.at[owner])

    def load_block(block):
        mine = block == place.me

        @pl.when(mine)
        def _():
            for owner in range(4):
                load_part(branch_ref, owner).start()

        @pl.when(jnp.logical_not(mine))
        def _():
            for owner in range(4):
                load_part(blocks.at[block], owner).start()

    def take(block):
        span = pl.ds(pl.multiple_of(block * count, count), count)
        columns = out_ref.shape[2]
        load_block(block)
        result = None
        for owner in range(4):
            load_part(branch_ref, owner).wait()
            here = block_buf[:, owner * columns : (owner + 1) * columns]
            product = lax.dot_general(
                here, out_ref[owner], TURNED, preferred_element_type=jnp.float32
            )
            result = product if result is None else result + product
            out_grad_ref[:, owner * columns : (owner + 1) * columns] += lax.dot_general(
                attended_ref[span, :], here, CROSSED, preferred_element_type=jnp.float32
            )
        grad = result.astype(jnp.bfloat16)
        attend_back_rows(
            block,
            grad,
            attended_ref,
            mixed_ref,
            aux_ref,
            seg_row_ref,
            stacked_ref,
            key_sum,
            value_sum,
            bias_sum_ref,
        )

    for copy in fetched[2:-1]:
        copy.wait()
    leaving = [
        pltpu.make_async_copy(source, target, emit_sem.at[index])
        for index, (source, target) in enumerate(
            [
                (stacked_ref, stacked_hbm),
                (out_grad_ref, out_grad_hbm),
                (down_grad_ref, down_grad_hbm),
            ]
        )
    ]

    def settle():
        stacked_ref[1] = (key_sum[...] * HEAD_DIM ** (-0.5)).astype(jnp.bfloat16)
        value_grad = value_sum[...].astype(jnp.bfloat16)
        stacked_ref[2] = value_grad
        leaving[0].start()
        leaving[1].start()
        bias_sum_ref[1:2, :] = jnp.sum(value_grad.astype(jnp.float32), axis=0, keepdims=True)
        down.end()
        leaving[2].start()

    def step(index, carry):
        def one(side, inner):
            chip = place.chip + index * (2 * (side % 2) - 1)
            core = (place.core + side // 2) % 2

            @pl.when((chip >= 0) & (chip < chips) & ((index > 0) | (side % 2 == 0)))
            def _():
                pl.when(side >= 2)(lambda: line.arrive(chip, core))
                take(2 * chip + core)

            return inner

        lax.fori_loop(0, 4, one, 0)
        for kind in range(4):
            pl.when(index == kind)(lambda: down_stage(kind))
        pl.when(index < chips - 1)(lambda: line.step(index + 1))
        pl.when(index == chips - 1)(settle)
        sums.step(index)
        return carry

    lax.fori_loop(0, chips, step, 0)
    total = scatter[0]
    fetched[-1].wait()

    def emit(span):
        result = resid_buf[span, :] + total[span, :] + shift_ref[...]
        live = alive((64, 1), 0, place.me * count + span.start, bounds)
        output_ref[span, :] = jnp.where(live > 0, result, 0.0).astype(jnp.bfloat16)

    by_rows(count, 64, emit)
    sums.finish()
    line.finish()
    for copy in leaving:
        copy.wait()


def branch_back_call(
    branch,
    active,
    down_whole,
    attended,
    out_whole,
    shift,
    offsets,
    lengths,
    mixed,
    aux,
    resid,
    cotangent,
    chips,
):
    count, width = branch.shape
    total, local = attended.shape
    _, units, columns = down_whole.shape
    low = jnp.bfloat16
    vmem = pl.BlockSpec(memory_space=pltpu.VMEM)
    hbm = pl.BlockSpec(memory_space=pl.ANY)
    dma = pltpu.SemaphoreType.DMA
    return pl.pallas_call(
        functools.partial(branch_back_kernel, chips, 2),
        out_shape=(
            jax.ShapeDtypeStruct((3, total, local), low),
            jax.ShapeDtypeStruct((2, local), jnp.float32),
            jax.ShapeDtypeStruct((2, units // 2, columns), jnp.float32),
            jax.ShapeDtypeStruct((local, width), jnp.float32),
            jax.ShapeDtypeStruct((count, width), low),
            jax.ShapeDtypeStruct((2 * chips, count, width), low),
        ),
        in_specs=[hbm] * 5 + [vmem] + [pl.BlockSpec(memory_space=pltpu.SMEM)] * 2 + [hbm] * 4,
        out_specs=(hbm, vmem, hbm, hbm, vmem, hbm),
        scratch_shapes=[
            pltpu.VMEM((3, total, local), low),
            pltpu.VMEM((2, units // 2, columns), jnp.float32),
            pltpu.VMEM((local, width), jnp.float32),
            dma((3,)),
            pltpu.VMEM(active.shape, low),
            pltpu.VMEM(down_whole.shape, low),
            pltpu.VMEM(attended.shape, low),
            pltpu.VMEM(out_whole.shape, low),
            pltpu.VMEM(mixed.shape, low),
            pltpu.VMEM(aux.shape, jnp.float32),
            dma((7,)),
            pltpu.VMEM((1, total), jnp.float32),
            pltpu.VMEM((count, width), low),
            pltpu.VMEM((total, columns), low),
            pltpu.VMEM((count, width), jnp.float32),
            pltpu.VMEM((total, local), jnp.float32),
            pltpu.VMEM((total, local), jnp.float32),
            dma((3, chips)),
            dma((2 * chips,)),
            dma,
            dma((4,)),
        ]
        + scatter_scratch(chips, count, width)
        + square_scratch((units // 2, columns)),
        compiler_params=pltpu.CompilerParams(
            collective_id=4, has_side_effects=True, vmem_limit_bytes=VMEM_LIMIT
        ),
        cost_estimate=pl.CostEstimate(flops=10**11, bytes_accessed=0, transcendentals=0),
        name="branch_back",
    )(
        branch,
        active,
        down_whole,
        attended,
        out_whole,
        shift,
        offsets,
        lengths,
        mixed,
        aux,
        resid,
        cotangent,
    )


ATTEND_ROWS = 256
ATTEND_KEYS = 512


def tile_mask(row_block, key_block, seg_col_ref, seg_row_ref):
    rows = lax.broadcasted_iota(jnp.int32, (ATTEND_ROWS, ATTEND_KEYS), 0)
    keys = lax.broadcasted_iota(jnp.int32, (ATTEND_ROWS, ATTEND_KEYS), 1)
    causal = keys - rows <= row_block * ATTEND_ROWS - key_block * ATTEND_KEYS
    row_span = pl.ds(pl.multiple_of(row_block * ATTEND_ROWS, ATTEND_ROWS), ATTEND_ROWS)
    key_span = pl.ds(pl.multiple_of(key_block * ATTEND_KEYS, ATTEND_KEYS), ATTEND_KEYS)
    return causal & (seg_col_ref[row_span, 0:1] == seg_row_ref[:, key_span])


def attend_rows(
    row_block, mixed_ref, seg_col_ref, seg_row_ref, attended_ref, lse_ref, score_ref
):
    scale = HEAD_DIM ** (-0.5)
    heads = range(mixed_ref.shape[2] // HEAD_DIM)
    lanes = [slice(head * HEAD_DIM, (head + 1) * HEAD_DIM) for head in heads]
    row_span = pl.ds(pl.multiple_of(row_block * ATTEND_ROWS, ATTEND_ROWS), ATTEND_ROWS)
    count = (row_block * ATTEND_ROWS) // ATTEND_KEYS + 1
    queries = [mixed_ref[0, row_span, lanes[head]] for head in heads]

    def span_of(key_block):
        return pl.ds(pl.multiple_of(key_block * ATTEND_KEYS, ATTEND_KEYS), ATTEND_KEYS)

    def score(key_block, peaks):
        key_span = span_of(key_block)
        mask = tile_mask(row_block, key_block, seg_col_ref, seg_row_ref)
        results = []
        for head in heads:
            scores = lax.dot_general(
                queries[head],
                mixed_ref[1, key_span, lanes[head]],
                TURNED,
                preferred_element_type=jnp.float32,
            )
            scores = jnp.where(mask, scores * scale, MASK_FILL)
            score_ref[head, :, key_span] = scores
            peak = peaks[head]
            for part in range(ATTEND_KEYS // 128):
                peak = jnp.maximum(peak, scores[:, part * 128 : (part + 1) * 128])
            results.append(peak)
        return tuple(results)

    filled = jnp.full((ATTEND_ROWS, 128), MASK_FILL, jnp.float32)
    peaks = lax.fori_loop(0, count, score, (filled,) * len(heads))
    peaks = [jnp.max(peak, axis=1, keepdims=True) for peak in peaks]

    def weigh(key_block, masses):
        key_span = span_of(key_block)
        results = []
        for head in heads:
            weights = jnp.exp(score_ref[head, :, key_span] - peaks[head])
            score_ref[head, :, key_span] = weights
            mass = masses[head]
            for part in range(ATTEND_KEYS // 128):
                mass = mass + weights[:, part * 128 : (part + 1) * 128]
            results.append(mass)
        return tuple(results)

    nothing = jnp.zeros((ATTEND_ROWS, 128), jnp.float32)
    masses = lax.fori_loop(0, count, weigh, (nothing,) * len(heads))
    masses = [jnp.sum(mass, axis=1, keepdims=True) for mass in masses]
    inverses = [1.0 / mass for mass in masses]
    lse_ref[row_span, 0:1] = seg_col_ref[row_span, :]
    for head in heads:
        lse_ref[row_span, head + 1 : head + 2] = peaks[head] + jnp.log(masses[head])

    def gather(key_block, totals):
        key_span = span_of(key_block)
        results = []
        for head in heads:
            probs = (score_ref[head, :, key_span] * inverses[head]).astype(jnp.bfloat16)
            results.append(
                totals[head]
                + jnp.dot(
                    probs,
                    mixed_ref[2, key_span, lanes[head]],
                    preferred_element_type=jnp.float32,
                )
            )
        return tuple(results)

    empty = jnp.zeros((ATTEND_ROWS, HEAD_DIM), jnp.float32)
    totals = lax.fori_loop(0, count, gather, (empty,) * len(heads))
    for head in heads:
        attended_ref[row_span, lanes[head]] = totals[head].astype(jnp.bfloat16)


def attend_back_rows(
    row_block,
    grads,
    attended_ref,
    mixed_ref,
    aux_ref,
    seg_row_ref,
    stacked_ref,
    key_sum,
    value_sum,
    bias_sum,
):
    scale = HEAD_DIM ** (-0.5)
    row_span = pl.ds(pl.multiple_of(row_block * ATTEND_ROWS, ATTEND_ROWS), ATTEND_ROWS)
    count = (row_block * ATTEND_ROWS) // ATTEND_KEYS + 1
    row_live = seg_row_ref[:, row_span]
    heads = []
    for head in range(mixed_ref.shape[2] // HEAD_DIM):
        lanes = slice(head * HEAD_DIM, (head + 1) * HEAD_DIM)
        grad = grads[:, lanes]
        product = grad.astype(jnp.float32) * attended_ref[row_span, lanes].astype(jnp.float32)
        delta = jnp.sum(product, axis=1, keepdims=True).reshape(1, ATTEND_ROWS)
        lse = aux_ref[row_span, head + 1 : head + 2].reshape(1, ATTEND_ROWS)
        heads.append((lanes, mixed_ref[0, row_span, lanes], grad, lse, delta))

    def one(key_block, totals):
        key_span = pl.ds(pl.multiple_of(key_block * ATTEND_KEYS, ATTEND_KEYS), ATTEND_KEYS)
        keys = lax.broadcasted_iota(jnp.int32, (ATTEND_KEYS, ATTEND_ROWS), 0)
        rows = lax.broadcasted_iota(jnp.int32, (ATTEND_KEYS, ATTEND_ROWS), 1)
        allowed = (keys - rows <= row_block * ATTEND_ROWS - key_block * ATTEND_KEYS) & (
            aux_ref[key_span, 0:1] == row_live
        )
        results = []
        for (lanes, query, grad, lse, delta), total in zip(heads, totals):
            key = mixed_ref[1, key_span, lanes]
            scores = lax.dot_general(key, query, TURNED, preferred_element_type=jnp.float32)
            flow = lax.dot_general(
                mixed_ref[2, key_span, lanes], grad, TURNED, preferred_element_type=jnp.float32
            )
            probs = jnp.exp(jnp.where(allowed, scores * scale, MASK_FILL) - lse)
            value_sum[key_span, lanes] += jnp.dot(
                probs.astype(jnp.bfloat16), grad, preferred_element_type=jnp.float32
            )
            low = (probs * (flow - delta)).astype(jnp.bfloat16)
            key_sum[key_span, lanes] += jnp.dot(low, query, preferred_element_type=jnp.float32)
            results.append(
                total + lax.dot_general(low, key, CROSSED, preferred_element_type=jnp.float32)
            )
        return tuple(results)

    totals = lax.fori_loop(
        0, count, one, (jnp.zeros((ATTEND_ROWS, HEAD_DIM), jnp.float32),) * len(heads)
    )
    for (lanes, _, _, _, _), total in zip(heads, totals):
        query_grad = (total * scale).astype(jnp.bfloat16)
        stacked_ref[0, row_span, lanes] = query_grad
        bias_sum[0:1, lanes] += jnp.sum(query_grad.astype(jnp.float32), axis=0, keepdims=True)


def tile_scores(query_tile, keys, segment, row_block, col_block):
    key_tile = keys[col_block * BLOCK : (col_block + 1) * BLOCK]
    scale = query_tile.shape[2] ** (-0.5)
    scores = (
        jnp.einsum("qhe,khe->hqk", query_tile, key_tile, preferred_element_type=jnp.float32) * scale
    )
    row_place = row_block * BLOCK + jnp.arange(BLOCK)
    key_place = col_block * BLOCK + jnp.arange(BLOCK)
    row_segment = segment[row_block * BLOCK : (row_block + 1) * BLOCK]
    key_segment = segment[col_block * BLOCK : (col_block + 1) * BLOCK]
    allowed = (key_place[None, :] <= row_place[:, None]) & (
        row_segment[:, None] == key_segment[None, :]
    )
    return (jnp.where(allowed[None], scores, MASK_FILL), allowed)


def attention_forward(queries, keys, values, segment):
    count = queries.shape[0] // BLOCK
    heads = queries.shape[1]
    depth = queries.shape[2]
    outputs = []
    totals = []
    for row_block in range(count):
        query_tile = queries[row_block * BLOCK : (row_block + 1) * BLOCK]
        peak = jnp.full((heads, BLOCK), MASK_FILL, jnp.float32)
        mass = jnp.zeros((heads, BLOCK), jnp.float32)
        for col_block in range(row_block + 1):
            scores, allowed = tile_scores(query_tile, keys, segment, row_block, col_block)
            new_peak = jnp.maximum(peak, jnp.max(scores, axis=-1))
            weights = jnp.where(allowed[None], jnp.exp(scores - new_peak[:, :, None]), 0.0)
            mass = mass * jnp.exp(peak - new_peak) + jnp.sum(weights, axis=-1)
            peak = new_peak
        total = peak + jnp.log(mass)
        gathered = jnp.zeros((BLOCK, heads, depth), jnp.float32)
        for col_block in range(row_block + 1):
            scores, allowed = tile_scores(query_tile, keys, segment, row_block, col_block)
            probs = jnp.where(allowed[None], jnp.exp(scores - total[:, :, None]), 0.0).astype(
                jnp.bfloat16
            )
            value_tile = values[col_block * BLOCK : (col_block + 1) * BLOCK]
            gathered = gathered + jnp.einsum(
                "hqk,khe->qhe", probs, value_tile, preferred_element_type=jnp.float32
            )
        outputs.append(gathered.astype(jnp.bfloat16))
        totals.append(total)
    return (jnp.concatenate(outputs, axis=0), jnp.concatenate(totals, axis=1))


def attention_backward(queries, keys, values, segment, totals, grads):
    count = queries.shape[0] // BLOCK
    heads = queries.shape[1]
    depth = queries.shape[2]
    scale = depth ** (-0.5)
    key_grads = [jnp.zeros((BLOCK, heads, depth), jnp.float32) for index in range(count)]
    value_grads = [jnp.zeros((BLOCK, heads, depth), jnp.float32) for index in range(count)]
    query_grads = []
    for row_block in range(count):
        query_tile = queries[row_block * BLOCK : (row_block + 1) * BLOCK]
        grad_tile = grads[row_block * BLOCK : (row_block + 1) * BLOCK]
        total = totals[:, row_block * BLOCK : (row_block + 1) * BLOCK]
        flows = jnp.zeros((heads, BLOCK), jnp.float32)
        for col_block in range(row_block + 1):
            scores, allowed = tile_scores(query_tile, keys, segment, row_block, col_block)
            probs = jnp.where(allowed[None], jnp.exp(scores - total[:, :, None]), 0.0)
            value_tile = values[col_block * BLOCK : (col_block + 1) * BLOCK]
            prob_grad = jnp.einsum(
                "qhe,khe->hqk", grad_tile, value_tile, preferred_element_type=jnp.float32
            )
            flows = flows + jnp.sum(prob_grad * probs, axis=-1)
            value_grads[col_block] = value_grads[col_block] + jnp.einsum(
                "hqk,qhe->khe",
                probs.astype(jnp.bfloat16),
                grad_tile,
                preferred_element_type=jnp.float32,
            )
        query_sum = jnp.zeros((BLOCK, heads, depth), jnp.float32)
        for col_block in range(row_block + 1):
            scores, allowed = tile_scores(query_tile, keys, segment, row_block, col_block)
            probs = jnp.where(allowed[None], jnp.exp(scores - total[:, :, None]), 0.0)
            value_tile = values[col_block * BLOCK : (col_block + 1) * BLOCK]
            key_tile = keys[col_block * BLOCK : (col_block + 1) * BLOCK]
            prob_grad = jnp.einsum(
                "qhe,khe->hqk", grad_tile, value_tile, preferred_element_type=jnp.float32
            )
            score_grad = (probs * (prob_grad - flows[:, :, None])).astype(jnp.bfloat16)
            query_sum = query_sum + scale * jnp.einsum(
                "hqk,khe->qhe", score_grad, key_tile, preferred_element_type=jnp.float32
            )
            key_grads[col_block] = key_grads[col_block] + scale * jnp.einsum(
                "hqk,qhe->khe", score_grad, query_tile, preferred_element_type=jnp.float32
            )
        query_grads.append(query_sum)
    return (
        jnp.concatenate(query_grads, axis=0).astype(jnp.bfloat16),
        jnp.concatenate(key_grads, axis=0).astype(jnp.bfloat16),
        jnp.concatenate(value_grads, axis=0).astype(jnp.bfloat16),
    )


def adam_update(master, grad, first, second, rate, decay, first_fix, second_fix):
    first_next = BETA_FIRST * first + (1.0 - BETA_FIRST) * grad
    second_next = BETA_SECOND * second + (1.0 - BETA_SECOND) * grad * grad
    change = (
        first_next / first_fix / (jnp.sqrt(second_next / second_fix) + ADAM_EPSILON)
        + decay * master
    )
    return (master - rate * change, first_next, second_next)


def adam_step(master, grad, first, second, rate, decay, fixes):
    first_next = BETA_FIRST * first + (1.0 - BETA_FIRST) * grad
    second_next = BETA_SECOND * second + (1.0 - BETA_SECOND) * grad * grad
    change = (
        first_next / fixes[0] / (jnp.sqrt(second_next / fixes[1]) + ADAM_EPSILON)
        + decay * master
    )
    return master - rate * change, first_next, second_next


def adam_kernel(rates, step_ref, late_ref, early_ref, rows_ref, wide_ref, *refs):
    one = jnp.float32(1.0)
    fixes = tuple(
        one - lax.fori_loop(0, step_ref[0], lambda index, value: value * jnp.float32(beta), one)
        for beta in (BETA_FIRST, BETA_SECOND)
    )
    refs, (rows_out, wide_out) = refs[:-2], refs[-2:]
    rows_out[...] = rows_ref[...]
    wide_out[...] = wide_ref[...]
    smalls = 4
    matrix_inputs, small_inputs = refs[: 4 * len(rates)], refs[4 * len(rates) :][: 3 * smalls]
    outputs = refs[4 * len(rates) + 3 * smalls :]
    for index, rate in enumerate(rates):
        master, grad, first, second = matrix_inputs[4 * index : 4 * index + 4]
        updated, first_out, second_out, grad_out, low_out = outputs[5 * index : 5 * index + 5]
        value = grad[...].reshape(master.shape)
        fresh = adam_step(
            master[...], value, first[...], second[...], rate, MATRIX_DECAY, fixes
        )
        updated[...], first_out[...], second_out[...] = fresh
        grad_out[...] = value
        low_out[...] = fresh[0].astype(jnp.bfloat16)

    @pl.when(pl.program_id(0) == 0)
    def _():
        local = small_inputs[0].shape[1]
        units = small_inputs[3].shape[1]
        early = early_ref
        pieces = (
            [early[4:5, :local], early[4:5, local : 2 * local]],
            [early[4:5, 2 * local : 2 * local + units]],
            [late_ref[0:1, :], early[0:1, :]],
            [late_ref[1:2, :], early[2:3, :], early[1:2, :], early[3:4, :]],
        )
        for index in range(smalls):
            master, first, second = small_inputs[3 * index : 3 * index + 3]
            to = 5 * len(rates) + 4 * index
            updated, first_out, second_out, grad_out = outputs[to : to + 4]
            for row, value in enumerate(pieces[index]):
                here = slice(row, row + 1)
                fresh = adam_step(
                    master[here, :], value, first[here, :], second[here, :], SMALL_RATE, 0.0, fixes
                )
                updated[here, :], first_out[here, :], second_out[here, :] = fresh
                grad_out[here, :] = value


ADAM_STEPS = 4


def adam_call(matrices, smalls, late, early, passing, step):
    in_specs = [pl.BlockSpec(memory_space=pltpu.SMEM)] + [
        pl.BlockSpec(rows.shape, lambda i: (0, 0)) for rows in (late, early)
    ]
    handed = [
        pl.BlockSpec((rows.shape[0] // ADAM_STEPS, rows.shape[1]), lambda i: (i, 0))
        for rows in passing
    ]
    in_specs += handed
    out_specs, out_shape, operands, rates = [], [], [step, late, early, *passing], []
    for master, grad, first, second, rate in matrices:
        lead = master.shape[:-2]
        rows, columns = master.shape[-2] // ADAM_STEPS, master.shape[-1]
        zeros = (0,) * len(lead)
        whole = pl.BlockSpec(lead + (rows, columns), lambda i, z=zeros: z + (i, 0))
        half = pl.BlockSpec(
            (1,) + lead + (rows, columns),
            lambda i, z=zeros: (i // (ADAM_STEPS // 2),) + z + (i % (ADAM_STEPS // 2), 0),
        )
        in_specs += [whole, half, whole, whole]
        operands += [master, grad, first, second]
        shape = jax.ShapeDtypeStruct(master.shape, jnp.float32)
        out_specs += [whole] * 5
        out_shape += [shape] * 4 + [jax.ShapeDtypeStruct(master.shape, jnp.bfloat16)]
        rates.append(rate)
    for group in smalls:
        spec = pl.BlockSpec(group[0].shape, lambda i: (0, 0))
        in_specs += [spec] * 3
        operands += list(group)
        out_specs += [spec] * 4
        out_shape += [jax.ShapeDtypeStruct(group[0].shape, jnp.float32)] * 4
    out_specs += handed
    out_shape += [jax.ShapeDtypeStruct(rows.shape, rows.dtype) for rows in passing]
    return pl.pallas_call(
        functools.partial(adam_kernel, tuple(rates)),
        grid=(ADAM_STEPS,),
        in_specs=in_specs,
        out_specs=out_specs,
        out_shape=out_shape,
        compiler_params=pltpu.CompilerParams(vmem_limit_bytes=VMEM_LIMIT),
        name="adam",
    )(*operands)


def per_device(
    layer_input,
    cotangent,
    lengths,
    offsets,
    step,
    mix_weight,
    out_weight,
    up_weight,
    down_weight,
    mix_first,
    out_first,
    up_first,
    down_first,
    mix_second,
    out_second,
    up_second,
    down_second,
    mix_bias,
    up_bias,
    norm_gains,
    shifts,
    mix_bias_first,
    up_bias_first,
    gains_first,
    shifts_first,
    mix_bias_second,
    up_bias_second,
    gains_second,
    shifts_second,
):
    parts = lax.axis_size("mp")
    local_width = mix_weight.shape[2]
    (
        normed_one,
        mixed,
        mix_whole,
        out_whole,
        up_low,
        down_low,
        own_branch,
        bias_down_grad,
    ) = project_call(
        layer_input,
        norm_gains[0:1],
        shifts[0:1],
        mix_weight,
        out_weight,
        mix_bias,
        up_weight,
        down_weight,
        cotangent,
        offsets,
        lengths,
        parts // 2,
    )
    (
        attended_flat,
        aux,
        resid_own,
        normed_mid,
        branch_grad,
        up_whole,
        down_whole,
    ) = attend_out_call(
        mixed,
        offsets,
        lengths,
        out_whole,
        layer_input,
        own_branch,
        norm_gains[1:2],
        shifts[2:3],
        shifts[1:2],
        up_low,
        down_low,
        parts // 2,
    )
    normed_two, active, hidden_grad, resid_grad, resid_low, row_sums, up_bias_grad = feed_call(
        normed_mid,
        branch_grad,
        up_whole,
        down_whole,
        up_bias[None],
        resid_own,
        own_branch,
        norm_gains[1:2],
        parts // 2,
    )
    stacked, mix_bias_grad, down_pieces, out_grad, layer_output, _ = branch_back_call(
        resid_low,
        active,
        down_whole,
        attended_flat,
        out_whole,
        shifts[3:4],
        offsets,
        lengths,
        mixed,
        aux,
        resid_own,
        branch_grad,
        parts // 2,
    )
    input_grad, late, early, mix_pieces, up_pieces, out_pieces = input_back_call(
        stacked,
        mix_whole,
        layer_input,
        resid_grad,
        norm_gains[0:1],
        (row_sums, bias_down_grad, mix_bias_grad, up_bias_grad),
        hidden_grad,
        out_grad,
        normed_one,
        normed_two,
        parts // 2,
    )
    news = adam_call(
        [
            (mix_weight, mix_pieces, mix_first, mix_second, D ** (-0.5)),
            (out_weight, out_pieces, out_first, out_second, OUT_FAN ** (-0.5)),
            (up_weight, up_pieces, up_first, up_second, D ** (-0.5)),
            (down_weight, down_pieces, down_first, down_second, FF ** (-0.5)),
        ],
        [
            (mix_bias, mix_bias_first, mix_bias_second),
            (up_bias[None], up_bias_first[None], up_bias_second[None]),
            (norm_gains, gains_first, gains_second),
            (shifts, shifts_first, shifts_second),
        ],
        late,
        early,
        (layer_output, input_grad),
        step,
    )
    layer_output, input_grad = news[-2:]
    mix, out, up, down = (news[5 * index : 5 * index + 5] for index in range(4))
    biases, unit_biases, gains, moves = (
        news[20 + 4 * index : 24 + 4 * index] for index in range(4)
    )
    unit_biases = [value[0] for value in unit_biases]
    return (
        layer_output,
        input_grad,
        *mix[:3],
        *out[:3],
        *up[:3],
        *down[:3],
        *biases[:3],
        *unit_biases[:3],
        *gains[:3],
        *moves[:3],
        mix[3],
        out[3],
        up[3],
        down[3],
        biases[3],
        unit_biases[3],
        gains[3],
        moves[3],
        mix[4],
        out[4],
        up[4],
        down[4],
    )


def per_device_any(
    layer_input,
    cotangent,
    lengths,
    offsets,
    step,
    mix_weight,
    out_weight,
    up_weight,
    down_weight,
    mix_first,
    out_first,
    up_first,
    down_first,
    mix_second,
    out_second,
    up_second,
    down_second,
    mix_bias,
    up_bias,
    norm_gains,
    shifts,
    mix_bias_first,
    up_bias_first,
    gains_first,
    shifts_first,
    mix_bias_second,
    up_bias_second,
    gains_second,
    shifts_second,
):
    own_rows = layer_input.shape[0]
    parts = lax.axis_size("mp")
    group_rows = own_rows * parts
    slots_here = lengths.shape[0]
    slot_len = group_rows // slots_here
    local_width = mix_weight.shape[2]
    depth = HEAD_DIM
    heads_here = local_width // depth
    positions = jnp.arange(slot_len, dtype=jnp.int32)
    live = (positions[None, :] >= offsets[:, None]) & (
        positions[None, :] < (offsets + lengths)[:, None]
    )
    segment = live.astype(jnp.int32)
    first_row = lax.axis_index("mp") * own_rows
    own_live = own_slice(live.reshape(-1), first_row, own_rows)[:, None]
    own_input = layer_input.astype(jnp.float32)
    normed_own, hat_one, inv_one = layer_norm_parts(own_input, norm_gains[0], shifts[0])
    normed_one = gather_rows(normed_own.astype(jnp.bfloat16))
    mix_full = gather_shards(mix_weight.astype(jnp.bfloat16), 1)
    out_full = gather_shards(out_weight.astype(jnp.bfloat16), 1)
    up_full = gather_shards(up_weight.astype(jnp.bfloat16), 0)
    down_full = gather_shards(down_weight.astype(jnp.bfloat16), 1)
    out_grad = jnp.where(own_live, cotangent.astype(jnp.float32), 0.0)
    bias_down_grad = jnp.sum(out_grad, axis=0)
    branch_grad = gather_rows(out_grad.astype(jnp.bfloat16))
    mixed = jnp.einsum("td,cde->cte", normed_one, mix_full, preferred_element_type=jnp.float32)
    queries = (
        (mixed[0] + mix_bias[0])
        .astype(jnp.bfloat16)
        .reshape(slots_here, slot_len, heads_here, depth)
    )
    keys = mixed[1].astype(jnp.bfloat16).reshape(slots_here, slot_len, heads_here, depth)
    values = (
        (mixed[2] + mix_bias[1])
        .astype(jnp.bfloat16)
        .reshape(slots_here, slot_len, heads_here, depth)
    )

    def attend(item):
        return attention_forward(item[0], item[1], item[2], item[3])

    attended, totals = lax.map(attend, (queries, keys, values, segment))
    attended_flat = attended.reshape(group_rows, local_width)
    attn_part = jnp.dot(attended_flat, out_full, preferred_element_type=jnp.float32)
    resid_own = own_input + scatter_rows(attn_part) + shifts[1]
    normed_mid, hat_two, inv_two = layer_norm_parts(resid_own, norm_gains[1], shifts[2])
    normed_two = gather_rows(normed_mid.astype(jnp.bfloat16))
    hidden = jnp.dot(normed_two, up_full, preferred_element_type=jnp.float32) + up_bias
    active_value, gelu_pull = jax.vjp(tanh_gelu, hidden)
    active = active_value.astype(jnp.bfloat16)
    active_grad = jnp.einsum(
        "td,fd->tf", branch_grad, down_full, preferred_element_type=jnp.float32
    )
    hidden_grad = gelu_pull(active_grad)[0].astype(jnp.bfloat16)
    two_part = jnp.einsum("tf,df->td", hidden_grad, up_full, preferred_element_type=jnp.float32)
    two_grad = scatter_rows(two_part)
    down_part = jnp.dot(active, down_full, preferred_element_type=jnp.float32)
    down_grad = jnp.einsum("tf,td->fd", active, branch_grad, preferred_element_type=jnp.float32)
    up_bias_grad = jnp.sum(hidden_grad, axis=0, dtype=jnp.float32)
    up_grad = jnp.einsum("td,tf->df", normed_two, hidden_grad, preferred_element_type=jnp.float32)
    resid_grad = out_grad + layer_norm_back(two_grad, hat_two, inv_two, norm_gains[1])
    attn_branch = gather_rows(resid_grad.astype(jnp.bfloat16))
    result_own = resid_own + scatter_rows(down_part) + shifts[3]
    layer_output = jnp.where(own_live, result_own, 0.0).astype(jnp.bfloat16)
    gain_two_grad = jnp.sum(two_grad * hat_two, axis=0)
    shift_two_grad = jnp.sum(two_grad, axis=0)
    bias_out_grad = jnp.sum(resid_grad, axis=0)
    attended_grad = jnp.einsum(
        "td,ed->te", attn_branch, out_full, preferred_element_type=jnp.float32
    ).astype(jnp.bfloat16)
    out_weight_grad = jnp.einsum(
        "te,td->ed", attended_flat, attn_branch, preferred_element_type=jnp.float32
    )

    def attend_back(item):
        return attention_backward(item[0], item[1], item[2], item[3], item[4], item[5])

    query_grad, key_grad, value_grad = lax.map(
        attend_back,
        (
            queries,
            keys,
            values,
            segment,
            totals,
            attended_grad.reshape(slots_here, slot_len, heads_here, depth),
        ),
    )
    stacked = jnp.stack(
        [
            query_grad.reshape(group_rows, local_width),
            key_grad.reshape(group_rows, local_width),
            value_grad.reshape(group_rows, local_width),
        ]
    )
    one_part = jnp.einsum("cte,cde->td", stacked, mix_full, preferred_element_type=jnp.float32)
    one_grad = scatter_rows(one_part)
    mix_grad = jnp.einsum("td,cte->cde", normed_one, stacked, preferred_element_type=jnp.float32)
    mix_bias_grad = jnp.stack(
        [
            jnp.sum(stacked[0], axis=0, dtype=jnp.float32),
            jnp.sum(stacked[2], axis=0, dtype=jnp.float32),
        ]
    )
    mix_owned = scatter_shards(mix_grad, 1)
    out_owned = scatter_shards(out_weight_grad, 1)
    up_owned = scatter_shards(up_grad, 0)
    down_owned = scatter_shards(down_grad, 1)
    input_grad = resid_grad + layer_norm_back(one_grad, hat_one, inv_one, norm_gains[0])
    gain_one_grad = jnp.sum(one_grad * hat_one, axis=0)
    shift_one_grad = jnp.sum(one_grad, axis=0)
    gain_grad = jnp.stack([gain_one_grad, gain_two_grad])
    shift_grad = jnp.stack([shift_one_grad, bias_out_grad, shift_two_grad, bias_down_grad])
    mix_bias_total, up_bias_total = lax.psum((mix_bias_grad, up_bias_grad), "dp")
    gain_total, shift_total = lax.psum((gain_grad, shift_grad), ("dp", "mp"))
    step_count = step[0].astype(jnp.float32)
    first_fix = 1.0 - BETA_FIRST**step_count
    second_fix = 1.0 - BETA_SECOND**step_count
    mix_new = adam_update(
        mix_weight,
        mix_owned,
        mix_first,
        mix_second,
        D ** (-0.5),
        MATRIX_DECAY,
        first_fix,
        second_fix,
    )
    out_new = adam_update(
        out_weight,
        out_owned,
        out_first,
        out_second,
        OUT_FAN ** (-0.5),
        MATRIX_DECAY,
        first_fix,
        second_fix,
    )
    up_new = adam_update(
        up_weight, up_owned, up_first, up_second, D ** (-0.5), MATRIX_DECAY, first_fix, second_fix
    )
    down_new = adam_update(
        down_weight,
        down_owned,
        down_first,
        down_second,
        FF ** (-0.5),
        MATRIX_DECAY,
        first_fix,
        second_fix,
    )
    mix_bias_new = adam_update(
        mix_bias,
        mix_bias_total,
        mix_bias_first,
        mix_bias_second,
        SMALL_RATE,
        0.0,
        first_fix,
        second_fix,
    )
    up_bias_new = adam_update(
        up_bias,
        up_bias_total,
        up_bias_first,
        up_bias_second,
        SMALL_RATE,
        0.0,
        first_fix,
        second_fix,
    )
    gains_new = adam_update(
        norm_gains, gain_total, gains_first, gains_second, SMALL_RATE, 0.0, first_fix, second_fix
    )
    shifts_new = adam_update(
        shifts, shift_total, shifts_first, shifts_second, SMALL_RATE, 0.0, first_fix, second_fix
    )
    return (
        layer_output,
        input_grad,
        mix_new[0],
        mix_new[1],
        mix_new[2],
        out_new[0],
        out_new[1],
        out_new[2],
        up_new[0],
        up_new[1],
        up_new[2],
        down_new[0],
        down_new[1],
        down_new[2],
        mix_bias_new[0],
        mix_bias_new[1],
        mix_bias_new[2],
        up_bias_new[0],
        up_bias_new[1],
        up_bias_new[2],
        gains_new[0],
        gains_new[1],
        gains_new[2],
        shifts_new[0],
        shifts_new[1],
        shifts_new[2],
        mix_owned,
        out_owned,
        up_owned,
        down_owned,
        mix_bias_total,
        up_bias_total,
        gain_total,
        shift_total,
        mix_new[0].astype(jnp.bfloat16),
        out_new[0].astype(jnp.bfloat16),
        up_new[0].astype(jnp.bfloat16),
        down_new[0].astype(jnp.bfloat16),
    )


def solution(mesh):
    placed = (
        P(("dp", "mp"), None),
        P(("dp", "mp"), None),
        P("dp"),
        P("dp"),
        P(),
        P(None, "dp", "mp"),
        P("mp", "dp"),
        P("dp", "mp"),
        P("mp", "dp"),
        P(None, "dp", "mp"),
        P("mp", "dp"),
        P("dp", "mp"),
        P("mp", "dp"),
        P(None, "dp", "mp"),
        P("mp", "dp"),
        P("dp", "mp"),
        P("mp", "dp"),
        P(None, "mp"),
        P("mp"),
        P(),
        P(),
        P(None, "mp"),
        P("mp"),
        P(),
        P(),
        P(None, "mp"),
        P("mp"),
        P(),
        P(),
    )
    fits = mesh.shape["dp"] == 4 and mesh.shape["mp"] == 8
    return jax.shard_map(
        per_device if fits else per_device_any,
        mesh=mesh,
        in_specs=placed,
        out_specs=(
            P(("dp", "mp"), None),
            P(("dp", "mp"), None),
            P(None, "dp", "mp"),
            P(None, "dp", "mp"),
            P(None, "dp", "mp"),
            P("mp", "dp"),
            P("mp", "dp"),
            P("mp", "dp"),
            P("dp", "mp"),
            P("dp", "mp"),
            P("dp", "mp"),
            P("mp", "dp"),
            P("mp", "dp"),
            P("mp", "dp"),
            P(None, "mp"),
            P(None, "mp"),
            P(None, "mp"),
            P("mp"),
            P("mp"),
            P("mp"),
            P(),
            P(),
            P(),
            P(),
            P(),
            P(),
            P(None, "dp", "mp"),
            P("mp", "dp"),
            P("dp", "mp"),
            P("mp", "dp"),
            P(None, "mp"),
            P("mp"),
            P(),
            P(),
            P(None, "dp", "mp"),
            P("mp", "dp"),
            P("dp", "mp"),
            P("mp", "dp"),
        ),
        check_vma=False,
    )
```

```python
import functools

import jax
import jax.numpy as jnp
from jax import lax
from jax.experimental import pallas as pl
from jax.experimental.pallas import tpu as pltpu
from jax.sharding import PartitionSpec as P

D = 2048
HEAD_DIM = 128
FF = 8192
BLOCK = 512
OUT_FAN = 7


NORM_EPSILON = 1e-05
ADAM_EPSILON = 1e-08
BETA_FIRST = 0.9
BETA_SECOND = 0.999
MATRIX_DECAY = 0.1
SMALL_RATE = 0.2
MASK_FILL = -1e30


def layer_norm_parts(rows, gain, shift):
    center = rows - jnp.mean(rows, axis=-1, keepdims=True)
    inverse = lax.rsqrt(jnp.mean(center * center, axis=-1, keepdims=True) + NORM_EPSILON)
    normed = center * inverse
    return (normed * gain + shift, normed, inverse)


def layer_norm_back(grad_out, normed, inverse, gain):
    scaled = grad_out * gain
    return inverse * (
        scaled
        - jnp.mean(scaled, axis=-1, keepdims=True)
        - normed * jnp.mean(scaled * normed, axis=-1, keepdims=True)
    )


def tanh_gelu(values):
    return jax.nn.gelu(values, approximate=True)


def own_slice(whole, first_row, count):
    return lax.dynamic_slice_in_dim(whole, first_row, count, 0)


def gather_rows(rows):
    return lax.all_gather(rows, "mp", axis=0, tiled=True)


def scatter_rows(terms):
    low = terms.astype(jnp.bfloat16)
    return lax.psum_scatter(low, "mp", scatter_dimension=0, tiled=True).astype(jnp.float32)


def swap(value, mask):
    size = lax.axis_size("dp")
    return lax.ppermute(value, "dp", [(place, place ^ mask) for place in range(size)])


def gather_shards(shard, axis):
    if lax.axis_size("dp") != 4:
        return lax.all_gather(shard, "dp", axis=axis, tiled=True)
    count = shard.shape[axis]
    me = lax.axis_index("dp")
    from_x = swap(shard, 1)
    from_y = swap(shard, 2)
    half = count // 2
    low = swap(lax.slice_in_dim(from_x, 0, half, axis=axis), 2)
    high = swap(lax.slice_in_dim(from_y, half, count, axis=axis), 1)
    shape = list(shard.shape)
    shape[axis] = 4 * count
    full = jnp.zeros(shape, shard.dtype)
    full = lax.dynamic_update_slice_in_dim(full, shard, me * count, axis)
    full = lax.dynamic_update_slice_in_dim(full, from_x, (me ^ 1) * count, axis)
    full = lax.dynamic_update_slice_in_dim(full, from_y, (me ^ 2) * count, axis)
    full = lax.dynamic_update_slice_in_dim(full, low, (me ^ 3) * count, axis)
    return lax.dynamic_update_slice_in_dim(full, high, (me ^ 3) * count + half, axis)


def scatter_shards(grad, axis):
    if lax.axis_size("dp") != 4:
        return lax.psum_scatter(grad, "dp", scatter_dimension=axis, tiled=True)
    count = grad.shape[axis] // 4
    half = count // 2
    me = lax.axis_index("dp")

    def piece(owner, upper):
        return lax.dynamic_slice_in_dim(grad, owner * count + upper * half, half, axis)

    def one_way(first, second, upper):
        near = swap(piece(me ^ first, upper).astype(jnp.bfloat16), first)
        far = swap(piece(me ^ 3, upper).astype(jnp.bfloat16), first)
        onward = piece(me ^ second, upper) + far.astype(jnp.float32)
        last = swap(onward.astype(jnp.bfloat16), second)
        return piece(me, upper) + near.astype(jnp.float32) + last.astype(jnp.float32)

    return lax.concatenate([one_way(1, 2, 0), one_way(2, 1, 1)], axis)


MESH = pl.DeviceIdType.MESH
VMEM_LIMIT = 62 * 1024 * 1024
TURNED = (((1,), (1,)), ((), ()))
CROSSED = (((0,), (0,)), ((), ()))


class Place:
    def __init__(self, chips):
        self.chips = chips
        self.dp = lax.axis_index("dp")
        self.me = lax.axis_index("mp")
        self.chip = self.me // 2
        self.core = self.me % 2
        self.has_up = self.chip < chips - 1
        self.has_down = self.chip > 0
        self.up = (self.dp, jnp.minimum(self.me + 2, 2 * chips - 1))
        self.down = (self.dp, jnp.maximum(self.me - 2, 0))
        self.side = (self.dp, self.me + 1 - 2 * self.core)
        self.x_peer = self.dp + 1 - 2 * (self.dp % 2)
        self.y_peer = (self.dp + 2) % 4
        self.across = 3 - self.dp
        self.x_way = (self.x_peer, self.me)
        self.y_way = (self.y_peer, self.me)

    def toward(self, way):
        return (self.dp, jnp.where(way == 0, self.up[1], self.down[1]))

    def greet(self, square, everyone=False):
        barrier = pltpu.get_barrier_semaphore()

        def signal(device):
            pl.semaphore_signal(barrier, inc=1, device_id=device, device_id_type=MESH)

        signal(self.side)
        pl.when(self.has_up)(lambda: signal(self.up))
        pl.when(self.has_down)(lambda: signal(self.down))
        count = 1 + self.has_up.astype(jnp.int32) + self.has_down.astype(jnp.int32)
        if square:
            signal(self.x_way)
            signal(self.y_way)
            count = count + 2
        if everyone:
            signal((self.across, self.me))
            count = count + 1

            def beyond(chip, carry):
                far = (chip > self.chip + 1) | (chip < self.chip - 1)
                pl.when(far)(lambda: signal((self.dp, 2 * chip + self.core)))
                return carry

            lax.fori_loop(0, self.chips, beyond, 0)
            near = self.has_up.astype(jnp.int32) + self.has_down.astype(jnp.int32)
            count = count + (self.chips - 1) - near
        pl.semaphore_wait(barrier, count)


def remote(source, target, send, recv, device):
    return pltpu.make_async_remote_copy(
        src_ref=source,
        dst_ref=target,
        send_sem=send,
        recv_sem=recv,
        device_id=device,
        device_id_type=MESH,
    )


def fetch(pairs, sems):
    copies = [
        pltpu.make_async_copy(source, target, sems.at[index])
        for index, (source, target) in enumerate(pairs)
    ]
    for copy in copies:
        copy.start()
    return copies


class LineGather:
    def __init__(self, place, blocks, send, recv, parts=1, own=None):
        self.place, self.blocks, self.send, self.recv = place, blocks, send, recv
        self.parts, self.own = parts, own

    def copy(self, way, chip, part=0, own=None):
        place = self.place
        piece = chip * self.parts + part
        block = 2 * piece + place.core
        device = (place.up, place.down, place.side)[way]
        return remote(
            self.blocks.at[block] if own is None else own,
            self.blocks.at[block],
            self.send.at[way, piece],
            self.recv.at[block],
            device,
        )

    def arrive(self, chip, core, part=0):
        piece = chip * self.parts + part
        block = 2 * piece + core
        remote(
            self.blocks.at[block],
            self.blocks.at[block],
            self.send.at[2, piece],
            self.recv.at[block],
            self.place.side,
        ).wait_recv()

    def begin_part(self, part):
        place = self.place
        pl.when(place.has_up)(lambda: self.copy(0, place.chip, part, self.own).start())
        pl.when(place.has_down)(lambda: self.copy(1, place.chip, part, self.own).start())
        self.copy(2, place.chip, part, self.own).start()

    def begin(self):
        for part in range(self.parts):
            self.begin_part(part)

    def step(self, distance, part=0):
        place = self.place
        low = place.chip - distance
        high = place.chip + distance

        @pl.when(low >= 0)
        def _():
            self.arrive(low, place.core, part)
            pl.when(place.has_up)(lambda: self.copy(0, low, part).start())
            self.copy(2, low, part).start()

        @pl.when(high < place.chips)
        def _():
            self.arrive(high, place.core, part)
            pl.when(place.has_down)(lambda: self.copy(1, high, part).start())
            self.copy(2, high, part).start()

    def finish(self):
        place = self.place

        def drain(chip, carry):
            for part in range(self.parts):
                pl.when(place.has_up & (chip <= place.chip))(
                    lambda: self.copy(0, chip, part).wait_send()
                )
                pl.when(place.has_down & (chip >= place.chip))(
                    lambda: self.copy(1, chip, part).wait_send()
                )
                self.copy(2, chip, part).wait_send()
            return carry

        lax.fori_loop(0, place.chips, drain, 0)


class SquareGather:
    def __init__(self, place, shard, view, half, send, recv):
        self.place, self.shard, self.view, self.half = place, shard, view, half
        self.send, self.recv = send, recv

    def first(self, way):
        place = self.place
        device = (place.x_way, place.y_way)[way]
        return remote(
            self.shard, self.view(place.dp), self.send.at[way], self.recv.at[way], device
        )

    def first_landed(self, way):
        place = self.place
        owner = (place.x_peer, place.y_peer)[way]
        device = (place.x_way, place.y_way)[way]
        remote(
            self.view(owner), self.view(owner), self.send.at[way], self.recv.at[way], device
        ).wait_recv()

    def second(self, way):
        place = self.place
        owner = (place.y_peer, place.x_peer)[way]
        device = (place.x_way, place.y_way)[way]
        part = self.half(owner, 1 - way)
        return remote(part, part, self.send.at[2 + way], self.recv.at[2 + way], device)

    def second_landed(self, way):
        place = self.place
        device = (place.x_way, place.y_way)[way]
        part = self.half(place.across, 1 - way)
        remote(part, part, self.send.at[2 + way], self.recv.at[2 + way], device).wait_recv()

    def begin(self):
        self.first(0).start()
        self.first(1).start()

    def middle(self):
        self.first_landed(0)
        self.second(1).start()
        self.first_landed(1)
        self.second(0).start()

    def end(self):
        self.second_landed(0)
        self.second_landed(1)

    def finish(self):
        self.first(0).wait_send()
        self.first(1).wait_send()
        self.second(0).wait_send()
        self.second(1).wait_send()


def norm_rows(rows, gain, shift):
    normed, hat, inverse = layer_norm_parts(rows, gain, shift)
    return normed


def project_kernel(
    chips,
    parts,
    rows_ref,
    gain_ref,
    shift_ref,
    mix_weight_hbm,
    out_weight_hbm,
    bias_ref,
    up_weight_hbm,
    down_weight_hbm,
    cotangent_hbm,
    offsets_ref,
    lengths_ref,
    normed_ref,
    mixed_hbm,
    mix_hbm,
    out_whole,
    up_ref,
    down_ref,
    branch_ref,
    branch_sum_ref,
    mix_weight_ref,
    out_weight_ref,
    up_weight_ref,
    down_weight_ref,
    cotangent_ref,
    fetch_sem,
    mix_ref,
    out_ref,
    mixed_ref,
    mix_whole,
    emit_sem,
    blocks,
    line_send,
    line_recv,
    mix_send,
    mix_recv,
    out_send,
    out_recv,
    own_sem,
    keep_sem,
):
    place = Place(chips)
    bounds = (offsets_ref[0], offsets_ref[0] + lengths_ref[0])
    count = rows_ref.shape[0]
    rows = count // parts
    fetched = fetch(
        [
            (mix_weight_hbm, mix_weight_ref),
            (out_weight_hbm, out_weight_ref),
            (cotangent_hbm, cotangent_ref),
            (up_weight_hbm, up_weight_ref),
            (down_weight_hbm, down_weight_ref),
        ],
        fetch_sem,
    )
    line = LineGather(place, blocks, line_send, line_recv, parts)

    def norm(part):
        def one(span):
            own = rows_ref[pl.ds(part * rows + span.start, 64), :].astype(jnp.float32)
            normed = norm_rows(own, gain_ref[...], shift_ref[...])
            blocks[2 * (place.chip * parts + part) + place.core, span, :] = normed.astype(
                jnp.bfloat16
            )

        by_rows(rows, 64, one)

    norm(0)
    place.greet(True)
    line.begin_part(0)
    for part in range(1, parts):
        norm(part)
        line.begin_part(part)
    mix = SquareGather(
        place,
        mix_ref,
        lambda owner: mix_whole.at[:, owner],
        lambda owner, which: mix_whole.at[:, owner, pl.ds(which * 256, 256)],
        mix_send,
        mix_recv,
    )
    out = SquareGather(
        place,
        out_ref,
        lambda owner: out_whole.at[owner],
        lambda owner, which: out_whole.at[owner, pl.ds(which * 128, 128)],
        out_send,
        out_recv,
    )

    def lower(source, target):
        def one(span):
            target[span, :] = source[span, :].astype(jnp.bfloat16)

        by_rows(source.shape[0], 64, one)

    fetched[0].wait()
    for part in range(3):
        lower(mix_weight_ref.at[part], mix_ref.at[part])
    mix.begin()
    own_mix = pltpu.make_async_copy(mix_ref, mix_whole.at[:, place.dp], own_sem.at[0])
    own_mix.start()
    fetched[1].wait()
    lower(out_weight_ref, out_ref)
    own_out = pltpu.make_async_copy(out_ref, out_whole.at[place.dp], own_sem.at[1])
    own_out.start()
    branch_sum_ref[...] = jnp.zeros_like(branch_sum_ref)

    def branch(span):
        live = alive((64, 1), 0, place.me * count + span.start, bounds)
        grad = jnp.where(live > 0, cotangent_ref[span, :].astype(jnp.float32), 0.0)
        branch_ref[span, :] = grad.astype(jnp.bfloat16)
        branch_sum_ref[...] += jnp.sum(grad, axis=0, keepdims=True)

    fetched[2].wait()
    by_rows(count, 64, branch)
    fetched[3].wait()
    lower(up_weight_ref, up_ref)
    fetched[4].wait()
    lower(down_weight_ref, down_ref)

    def span_of(chip, core, part):
        start = (2 * chip + core) * count + part * rows
        return pl.ds(pl.multiple_of(start, rows), rows)

    def copies(chip, part):
        piece = chip * parts + part
        taken = []
        for core in range(2):
            span = span_of(chip, core, part)
            taken.append(
                pltpu.make_async_copy(
                    blocks.at[2 * piece + core], normed_ref.at[span], keep_sem.at[piece, core]
                )
            )
            taken.append(
                pltpu.make_async_copy(
                    mixed_ref.at[:, span], mixed_hbm.at[:, span], emit_sem.at[piece, core]
                )
            )
        return taken

    keep_mix = pltpu.make_async_copy(mix_whole, mix_hbm, own_sem.at[2])

    def project(chip, part):
        piece = chip * parts + part
        line.arrive(chip, 1 - place.core, part)
        pair = blocks[pl.ds(2 * piece, 2)].reshape(2 * rows, -1)
        for kind in range(3):
            weight = mix_whole[kind].reshape(-1, mix_whole.shape[3])
            result = jnp.dot(pair, weight, preferred_element_type=jnp.float32)
            if kind == 0:
                result = result + bias_ref[0:1, :]
            if kind == 2:
                result = result + bias_ref[1:2, :]
            low = result.astype(jnp.bfloat16)
            for core in range(2):
                mixed_ref[kind, span_of(chip, core, part), :] = low[
                    core * rows : (core + 1) * rows
                ]
        for copy in copies(chip, part):
            copy.start()

    def turn(index, carry):
        distance = index // parts
        part = index % parts

        @pl.when(distance > 0)
        def _():
            line.step(distance, part)

        @pl.when(index == 2)
        def _():
            mix.middle()
            out.begin()

        @pl.when(index == 3)
        def _():
            mix.end()
            own_mix.wait()
            keep_mix.start()

        first = jnp.where(index < 6, 2 * (index - 3), index)
        after = jnp.where(index < 6, 2 * (index - 2), index + 1)

        def one(order, inner):
            each = order // 2
            side = order % 2
            near = each // parts
            chip = place.chip + near * (2 * side - 1)

            @pl.when((chip >= 0) & (chip < chips) & ((near > 0) | (side == 0)))
            def _():
                project(chip, each % parts)

            return inner

        @pl.when(index >= 3)
        def _():
            lax.fori_loop(2 * first, 2 * after, one, 0)

        pl.when(index == 4)(out.middle)
        return carry

    lax.fori_loop(0, chips * parts, turn, 0)
    out.end()
    own_out.wait()
    line.finish()
    mix.finish()
    out.finish()

    def kept(piece, carry):
        for copy in copies(piece // parts, piece % parts):
            copy.wait()
        return carry

    lax.fori_loop(0, parts * chips, kept, 0)
    keep_mix.wait()


def project_call(
    rows, gain, shift, mix_shard, out_shard, bias, up, down, cotangent, offsets, lengths, chips
):
    count, width = rows.shape
    total = 2 * chips * count
    local = mix_shard.shape[2]
    parts = 2
    vmem = pl.BlockSpec(memory_space=pltpu.VMEM)
    hbm = pl.BlockSpec(memory_space=pl.ANY)
    dma = pltpu.SemaphoreType.DMA
    flops = 2 * total * width * 3 * local
    return pl.pallas_call(
        functools.partial(project_kernel, chips, parts),
        out_shape=(
            jax.ShapeDtypeStruct((total, width), jnp.bfloat16),
            jax.ShapeDtypeStruct((3, total, local), jnp.bfloat16),
            jax.ShapeDtypeStruct((3, 4, mix_shard.shape[1], local), jnp.bfloat16),
            jax.ShapeDtypeStruct((4,) + out_shard.shape, jnp.bfloat16),
            jax.ShapeDtypeStruct(up.shape, jnp.bfloat16),
            jax.ShapeDtypeStruct(down.shape, jnp.bfloat16),
            jax.ShapeDtypeStruct((count, width), jnp.bfloat16),
            jax.ShapeDtypeStruct((1, width), jnp.float32),
        ),
        in_specs=[vmem] * 3
        + [hbm] * 2
        + [vmem]
        + [hbm] * 3
        + [pl.BlockSpec(memory_space=pltpu.SMEM)] * 2,
        out_specs=(hbm,) * 4 + (vmem,) * 4,
        scratch_shapes=[
            pltpu.VMEM(mix_shard.shape, jnp.float32),
            pltpu.VMEM(out_shard.shape, jnp.float32),
            pltpu.VMEM(up.shape, jnp.float32),
            pltpu.VMEM(down.shape, jnp.float32),
            pltpu.VMEM(cotangent.shape, jnp.bfloat16),
            dma((5,)),
            pltpu.VMEM(mix_shard.shape, jnp.bfloat16),
            pltpu.VMEM(out_shard.shape, jnp.bfloat16),
            pltpu.VMEM((3, total, local), jnp.bfloat16),
            pltpu.VMEM((3, 4, mix_shard.shape[1], local), jnp.bfloat16),
            dma((parts * chips, 2)),
            pltpu.VMEM((2 * chips * parts, count // parts, width), jnp.bfloat16),
            dma((3, chips * parts)),
            dma((2 * chips * parts,)),
            dma((4,)),
            dma((4,)),
            dma((4,)),
            dma((4,)),
            dma((3,)),
            dma((parts * chips, 2)),
        ],
        compiler_params=pltpu.CompilerParams(
            collective_id=0, has_side_effects=True, vmem_limit_bytes=VMEM_LIMIT
        ),
        cost_estimate=pl.CostEstimate(flops=flops * 7, bytes_accessed=0, transcendentals=0),
        name="project",
    )(rows, gain, shift, mix_shard, out_shard, bias, up, down, cotangent, offsets, lengths)


class LineScatter:
    def __init__(self, place, term, tiles, bufs, sems, prepare=lambda chip: None):
        self.place, self.term, self.tiles, self.prepare = place, term, tiles, prepare
        self.total, self.side_out, self.side_in, self.line_in = bufs
        self.side_send, self.side_recv, self.line_send, self.line_recv = sems

    def side_copy(self, chip):
        return remote(
            self.side_out.at[chip],
            self.side_in.at[chip],
            self.side_send.at[chip],
            self.side_recv.at[chip],
            self.place.side,
        )

    def span(self, tile):
        width = self.total.shape[1] // self.tiles
        return slice(tile * width, (tile + 1) * width)

    def line_copy(self, way, chip, tile):
        place = self.place
        next_chip = place.chip + 1 - 2 * way
        slot = jnp.where((way == 1) & (chip == next_chip), place.chips, chip)
        return remote(
            self.line_in.at[chip, :, self.span(tile)],
            self.line_in.at[slot, :, self.span(tile)],
            self.line_send.at[chip, tile],
            self.line_recv.at[slot, tile],
            (place.up, place.down)[way],
        )

    def landed(self, way, chip, tile):
        place = self.place
        slot = jnp.where((way == 1) & (chip == place.chip), place.chips, chip)
        remote(
            self.line_in.at[slot, :, self.span(tile)],
            self.line_in.at[slot, :, self.span(tile)],
            self.line_send.at[chip, tile],
            self.line_recv.at[slot, tile],
            (place.up, place.down)[way],
        ).wait_recv()
        return slot

    def each(self, distance, action):
        place = self.place

        def one(index, carry):
            chip = place.chip + distance * (1 - 2 * index)
            valid = (chip >= 0) & (chip < place.chips) & ((distance > 0) | (index == 0))
            pl.when(valid)(lambda: action(chip))
            return carry

        lax.fori_loop(0, 2, one, 0)

    def hand_over(self, chip):
        self.prepare(chip)
        block = 2 * chip + 1 - self.place.core
        width = self.total.shape[1] // self.tiles

        def one(tile, carry):
            span = pl.ds(pl.multiple_of(tile * width, width), width)
            self.side_out[chip, :, span] = self.term(block, tile).astype(jnp.bfloat16)
            return carry

        lax.fori_loop(0, self.tiles, one, 0)
        self.side_copy(chip).start()

    def sum_up(self, chip):
        place = self.place
        block = 2 * chip + place.core
        self.side_copy(chip).wait_recv()
        for tile in range(self.tiles):
            span = self.span(tile)
            self.total[:, span] = self.term(block, tile) + self.side_in[chip, :, span].astype(
                jnp.float32
            )
            for way in range(2):
                behind = (place.has_down, place.has_up)[way]
                goes = (chip >= place.chip) if way == 0 else (chip <= place.chip)

                @pl.when(behind & goes)
                def _():
                    slot = self.landed(way, chip, tile)
                    self.total[:, span] += self.line_in[slot, :, span].astype(jnp.float32)

            @pl.when(chip != place.chip)
            def _():
                self.line_in[chip, :, span] = self.total[:, span].astype(jnp.bfloat16)
                pl.when(chip > place.chip)(lambda: self.line_copy(0, chip, tile).start())
                pl.when(chip < place.chip)(lambda: self.line_copy(1, chip, tile).start())

    def begin(self):
        self.each(self.place.chips - 1, self.hand_over)

    def step(self, index, early=False):
        distance = self.place.chips - 1 - index
        if early:
            pl.when((index > 0) & (distance > 0))(lambda: self.each(distance - 1, self.hand_over))
        self.each(distance, self.sum_up)
        behind = (index == 0) if early else (distance > 0)
        pl.when(behind)(lambda: self.each(distance - 1, self.hand_over))

    def finish(self):
        place = self.place

        def drain(chip, carry):
            self.side_copy(chip).wait_send()
            for tile in range(self.tiles):
                pl.when(chip != place.chip)(lambda: self.line_copy(0, chip, tile).wait_send())
            return carry

        lax.fori_loop(0, place.chips, drain, 0)


class SquareScatter:
    def __init__(self, place, piece, owned, bufs, sems):
        self.place, self.piece, self.owned = place, piece, owned
        self.out, self.arrived = bufs
        self.send, self.recv = sems

    def copy(self, kind, way):
        place = self.place
        turn = way if kind < 2 else 1 - way
        peer = place.x_peer + turn * (place.y_peer - place.x_peer)
        return remote(
            self.out.at[kind, way],
            self.arrived.at[kind, way],
            self.send.at[kind, way],
            self.recv.at[kind, way],
            (peer, place.me),
        )

    def owner(self, kind, way):
        place = self.place
        near = place.x_peer + way * (place.y_peer - place.x_peer)
        other = place.y_peer + way * (place.x_peer - place.y_peer)
        return (place.across, near, other, place.dp)[kind]

    def following(self, kind, way):
        after = self.owner(kind, 1) if kind == 3 else self.owner(kind + 1, 0)
        return jnp.where(way == 0, self.owner(kind, 1), after), 1 - way

    def one(self, kind, way):
        value = self.piece(self.owner(kind, way), way)
        if kind == 2:
            self.copy(0, way).wait_recv()
            value = value + self.arrived[0, way].astype(jnp.float32)
        if kind < 3:
            self.out[kind, way] = value.astype(jnp.bfloat16)
            self.copy(kind, way).start()
        else:
            self.owned[way] = value

    def stage(self, kind):
        def one(way, carry):
            self.one(kind, way)
            return carry

        lax.fori_loop(0, 2, one, 0)

    def end(self):
        def one(way, carry):
            self.copy(1, way).wait_recv()
            self.copy(2, way).wait_recv()
            self.owned[way] = (
                self.owned[way]
                + self.arrived[1, way].astype(jnp.float32)
                + self.arrived[2, way].astype(jnp.float32)
            )
            for kind in range(3):
                self.copy(kind, way).wait_send()
            return carry

        lax.fori_loop(0, 2, one, 0)


def square_scratch(half):
    dma = pltpu.SemaphoreType.DMA
    return [
        pltpu.VMEM((3, 2) + half, jnp.bfloat16),
        pltpu.VMEM((3, 2) + half, jnp.bfloat16),
        dma((3, 2)),
        dma((3, 2)),
    ]


class SmallSum:
    def __init__(self, place, rows, alone, bufs, sems):
        self.place, self.rows, self.alone = place, rows, alone
        self.side_buf, self.line_buf, self.square_buf = bufs
        self.send, self.recv = sems

    def side_copy(self):
        place = self.place
        return remote(
            self.rows,
            self.side_buf,
            self.send.at[0],
            self.recv.at[0],
            place.side,
        )

    def line_copy(self, hop):
        place = self.place
        chip = (place.chip + hop) % place.chips
        return remote(
            self.rows,
            self.line_buf.at[place.chip],
            self.send.at[hop],
            self.recv.at[hop],
            (place.dp, 2 * chip + place.core),
        )

    def line_landed(self, hop):
        place = self.place
        chip = (place.chip + place.chips - hop) % place.chips
        remote(
            self.rows,
            self.line_buf.at[chip],
            self.send.at[hop],
            self.recv.at[hop],
            (place.dp, 2 * chip + place.core),
        ).wait_recv()

    def square_copy(self, hop):
        place = self.place
        target = (place.dp + hop) % 4
        at = place.chips + hop
        return remote(
            self.rows,
            self.square_buf.at[place.dp],
            self.send.at[at],
            self.recv.at[at],
            (target, place.me),
        )

    def square_landed(self, hop):
        place = self.place
        source = (place.dp + 4 - hop) % 4
        at = place.chips + hop
        remote(
            self.rows,
            self.square_buf.at[source],
            self.send.at[at],
            self.recv.at[at],
            (source, place.me),
        ).wait_recv()

    def put(self, value):
        if self.alone < self.rows.shape[0]:
            index = lax.broadcasted_iota(jnp.int32, value.shape, 0)
            value = jnp.where(index < self.alone, value, self.rows[...])
        self.rows[...] = value

    def begin(self):
        self.side_copy().start()

    def middle(self):
        self.side_copy().wait()
        self.put(self.rows[...] + self.side_buf[...])
        self.line_buf[self.place.chip] = self.rows[...]
        for hop in range(1, self.place.chips):
            self.line_copy(hop).start()

    def late(self):
        place = self.place
        for hop in range(1, place.chips):
            self.line_copy(hop).wait_send()
            self.line_landed(hop)
        value = self.line_buf[0]
        for chip in range(1, place.chips):
            value = value + self.line_buf[chip]
        self.put(value)
        self.square_buf[place.dp] = self.rows[...]
        for hop in range(1, 4):
            self.square_copy(hop).start()

    def end(self):
        for hop in range(1, 4):
            self.square_copy(hop).wait_send()
            self.square_landed(hop)
        value = self.square_buf[0]
        for device in range(1, 4):
            value = value + self.square_buf[device]
        self.rows[...] = value


def small_scratch(chips, rows, width):
    dma = pltpu.SemaphoreType.DMA
    return [
        pltpu.VMEM((rows, width), jnp.float32),
        pltpu.VMEM((chips, rows, width), jnp.float32),
        pltpu.VMEM((4, rows, width), jnp.float32),
        dma((chips + 4,)),
        dma((chips + 4,)),
    ]


def scatter_scratch(chips, count, width):
    low = jnp.bfloat16
    dma = pltpu.SemaphoreType.DMA
    return [
        pltpu.VMEM((count, width), jnp.float32),
        pltpu.VMEM((chips, count, width), low),
        pltpu.VMEM((chips, count, width), low),
        pltpu.VMEM((chips + 1, count, width), low),
        dma((chips,)),
        dma((chips,)),
        dma((chips, 4)),
        dma((chips + 1, 4)),
    ]


def alive(shape, axis, start, bounds):
    place = lax.broadcasted_iota(jnp.int32, shape, axis) + start
    return jnp.where((place >= bounds[0]) & (place < bounds[1]), 1.0, 0.0)


def by_rows(count, tile, action):
    def one(index, carry):
        action(pl.ds(pl.multiple_of(index * tile, tile), tile))
        return carry

    lax.fori_loop(0, count // tile, one, 0)


def attend_out_kernel(
    chips,
    mixed_hbm,
    offsets_ref,
    lengths_ref,
    out_hbm,
    rows_hbm,
    branch_ref,
    gain_ref,
    shift_ref,
    bias_ref,
    up_ref,
    down_ref,
    attended_ref,
    lse_ref,
    resid_ref,
    normed_ref,
    branch_whole,
    up_whole,
    down_whole,
    mixed_ref,
    out_ref,
    rows_ref,
    fetch_sem,
    seg_col_ref,
    seg_row_ref,
    score_ref,
    blocks,
    line_send,
    line_recv,
    up_send,
    up_recv,
    down_send,
    down_recv,
    own_sem,
    keep_sem,
    *scatter,
):
    place = Place(chips)
    bounds = (offsets_ref[0], offsets_ref[0] + lengths_ref[0])
    count = rows_ref.shape[0]
    fetched = fetch(
        [(mixed_hbm, mixed_ref), (out_hbm, out_ref), (rows_hbm, rows_ref)], fetch_sem
    )
    place.greet(True)

    def square(shard, whole, send, recv):
        half = shard.shape[0] // 2
        return SquareGather(
            place,
            shard,
            lambda owner: whole.at[owner],
            lambda owner, which: whole.at[owner, pl.ds(which * half, half)],
            send,
            recv,
        )

    up = square(up_ref, up_whole, up_send, up_recv)
    down = square(down_ref, down_whole, down_send, down_recv)
    up.begin()
    down.begin()
    own = [
        pltpu.make_async_copy(up_ref, up_whole.at[place.dp], own_sem.at[0]),
        pltpu.make_async_copy(down_ref, down_whole.at[place.dp], own_sem.at[1]),
    ]
    own[0].start()
    own[1].start()

    def term(block, tile):
        span = pl.ds(pl.multiple_of(block * count, count), count)
        return jnp.dot(attended_ref[span, :], out_ref[tile], preferred_element_type=jnp.float32)

    def prepare(chip):
        def one(index, carry):
            attend_rows(
                chip * (2 * count // ATTEND_ROWS) + index,
                mixed_ref,
                seg_col_ref,
                seg_row_ref,
                attended_ref,
                lse_ref,
                score_ref,
            )
            return carry

        lax.fori_loop(0, 2 * count // ATTEND_ROWS, one, 0)

    def copy_in(span):
        blocks[place.me, span, :] = branch_ref[span, :]

    by_rows(count, 64, copy_in)
    line = LineGather(place, blocks, line_send, line_recv)
    line.begin()
    seg_row_ref[...] = alive(seg_row_ref.shape, 1, 0, bounds)

    def column(span):
        seg_col_ref[span, :] = alive((64, 1), 0, span.start, bounds)

    by_rows(seg_col_ref.shape[0], 64, column)
    for copy in fetched:
        copy.wait()
    sums = LineScatter(place, term, 4, scatter[:4], scatter[4:8], prepare)
    sums.begin()

    def keep(block, part):
        half = count // 2
        place_of = ((block // 2 * 2 + part) * 2 + block % 2) * half
        span = pl.ds(pl.multiple_of(place_of, half), half)
        source = blocks.at[block, pl.ds(part * half, half)]
        return pltpu.make_async_copy(source, branch_whole.at[span], keep_sem.at[block, part])

    def step(index, carry):
        sums.step(index, True)
        pl.when(index < chips - 1)(lambda: line.step(index + 1))

        @pl.when(index == 1)
        def _():
            up.middle()
            down.middle()

        return carry

    lax.fori_loop(0, chips, step, 0)
    total = scatter[0]

    def norm(span):
        resid = rows_ref[span, :].astype(jnp.float32) + total[span, :] + bias_ref[...]
        resid_ref[span, :] = resid
        normed_ref[span, :] = norm_rows(resid, gain_ref[...], shift_ref[...]).astype(jnp.bfloat16)

    by_rows(count, 64, norm)

    def store(block, carry):
        pl.when((block % 2 != place.core))(lambda: line.arrive(block // 2, block % 2))
        keep(block, 0).start()
        keep(block, 1).start()
        return carry

    lax.fori_loop(0, 2 * chips, store, 0)
    sums.finish()
    line.finish()
    up.end()
    down.end()
    up.finish()
    down.finish()
    own[0].wait()
    own[1].wait()

    def kept(block, carry):
        keep(block, 0).wait()
        keep(block, 1).wait()
        return carry

    lax.fori_loop(0, 2 * chips, kept, 0)


def attend_out_call(
    mixed, offsets, lengths, out_whole, rows, branch, gain, shift, bias, up, down, chips
):
    count, width = rows.shape
    local = mixed.shape[2]
    total = 2 * chips * count
    low = jnp.bfloat16
    vmem = pl.BlockSpec(memory_space=pltpu.VMEM)
    hbm = pl.BlockSpec(memory_space=pl.ANY)
    dma = pltpu.SemaphoreType.DMA
    return pl.pallas_call(
        functools.partial(attend_out_kernel, chips),
        out_shape=(
            jax.ShapeDtypeStruct((total, local), low),
            jax.ShapeDtypeStruct((total, 1 + local // HEAD_DIM), jnp.float32),
            jax.ShapeDtypeStruct((count, width), jnp.float32),
            jax.ShapeDtypeStruct((count, width), low),
            jax.ShapeDtypeStruct((total, width), low),
            jax.ShapeDtypeStruct((4,) + up.shape, low),
            jax.ShapeDtypeStruct((4,) + down.shape, low),
        ),
        in_specs=[hbm] + [pl.BlockSpec(memory_space=pltpu.SMEM)] * 2 + [hbm] * 2 + [vmem] * 6,
        out_specs=(vmem, vmem, vmem, vmem, hbm, hbm, hbm),
        scratch_shapes=[
            pltpu.VMEM(mixed.shape, low),
            pltpu.VMEM(out_whole.shape, low),
            pltpu.VMEM(rows.shape, low),
            dma((3,)),
            pltpu.VMEM((total, 1), jnp.float32),
            pltpu.VMEM((1, total), jnp.float32),
            pltpu.VMEM((local // HEAD_DIM, ATTEND_ROWS, total), jnp.float32),
            pltpu.VMEM((2 * chips, count, width), low),
            dma((3, chips)),
            dma((2 * chips,)),
            dma((4,)),
            dma((4,)),
            dma((4,)),
            dma((4,)),
            dma((2,)),
            dma((2 * chips, 2)),
        ]
        + scatter_scratch(chips, count, width),
        compiler_params=pltpu.CompilerParams(
            collective_id=1, has_side_effects=True, vmem_limit_bytes=VMEM_LIMIT
        ),
        cost_estimate=pl.CostEstimate(flops=10**11, bytes_accessed=0, transcendentals=0),
        name="attend_out",
    )(mixed, offsets, lengths, out_whole, rows, branch, gain, shift, bias, up, down)


def input_back_kernel(
    chips,
    stacked_hbm,
    mix_hbm,
    rows_hbm,
    resid_grad_hbm,
    gain_ref,
    row_sums_ref,
    bias_down_ref,
    mix_bias_ref,
    up_bias_ref,
    hidden_hbm,
    out_grad_hbm,
    normed_one_ref,
    normed_two_ref,
    grad_ref,
    late_out_ref,
    early_out_ref,
    mix_grad_hbm,
    up_grad_hbm,
    out_owned_hbm,
    mix_grad_ref,
    up_grad_ref,
    out_owned_ref,
    hat_buf,
    inverse_buf,
    emit_sem,
    stacked_ref,
    mix_ref,
    rows_ref,
    resid_grad_ref,
    hidden_ref,
    out_grad_ref,
    fetch_sem,
    columns_buf,
    columns_sem,
    *scatter,
):
    place = Place(chips)
    count = rows_ref.shape[0]
    fetched = fetch(
        [
            (stacked_hbm, stacked_ref),
            (mix_hbm, mix_ref),
            (hidden_hbm, hidden_ref),
            (out_grad_hbm, out_grad_ref),
            (rows_hbm, rows_ref),
            (resid_grad_hbm, resid_grad_ref),
        ],
        fetch_sem,
    )
    place.greet(True, True)
    fetched[0].wait()
    fetched[1].wait()
    local = mix_bias_ref.shape[1]
    units = up_bias_ref.shape[1]
    early_out_ref[0:3, :] = row_sums_ref[...]
    early_out_ref[3:4, :] = bias_down_ref[...]
    early_out_ref[4:5, :] = jnp.zeros((1, early_out_ref.shape[1]), jnp.float32)
    early_out_ref[4:5, 0:local] = mix_bias_ref[0:1, :]
    early_out_ref[4:5, local : 2 * local] = mix_bias_ref[1:2, :]
    early_out_ref[4:5, 2 * local : 2 * local + units] = up_bias_ref[...]
    early = SmallSum(place, early_out_ref, 4, scatter[16:19], scatter[19:21])
    late = SmallSum(place, late_out_ref, late_out_ref.shape[0], scatter[21:24], scatter[24:26])

    def term(block, tile):
        span = pl.ds(pl.multiple_of(block * count, count), count)
        result = None
        for part in range(3):
            product = lax.dot_general(
                stacked_ref[part, span, :],
                mix_ref[part, tile],
                TURNED,
                preferred_element_type=jnp.float32,
            )
            result = product if result is None else result + product
        return result

    sums = LineScatter(place, term, 4, scatter[:4], scatter[4:8])
    sums.begin()
    early.begin()
    half_columns = columns_buf.shape[2]

    def load(which, owner, half):
        start = pl.multiple_of((2 * owner + half) * half_columns, half_columns)
        source = (normed_one_ref, normed_two_ref)[which]
        return pltpu.make_async_copy(
            source.at[:, pl.ds(start, half_columns)], columns_buf.at[which], columns_sem.at[which]
        )

    def mix_piece(owner, half):
        load(0, owner, half).wait()
        return jnp.stack(
            [
                lax.dot_general(
                    columns_buf[0],
                    stacked_ref[part],
                    CROSSED,
                    preferred_element_type=jnp.float32,
                )
                for part in range(3)
            ]
        )

    def up_piece(owner, half):
        load(1, owner, half).wait()
        return lax.dot_general(
            columns_buf[1], hidden_ref[...], CROSSED, preferred_element_type=jnp.float32
        )

    out_units = out_grad_ref.shape[0] // 2
    out_columns = out_grad_ref.shape[1] // 4

    def out_piece(owner, half):
        units = pl.ds(pl.multiple_of(half * out_units, out_units), out_units)
        columns = pl.ds(pl.multiple_of(owner * out_columns, 128), out_columns)
        return out_grad_ref[units, columns]

    out = SquareScatter(place, out_piece, out_owned_ref, scatter[26:28], scatter[28:30])
    mix = SquareScatter(place, mix_piece, mix_grad_ref, scatter[8:10], scatter[10:12])
    up = SquareScatter(place, up_piece, up_grad_ref, scatter[12:14], scatter[14:16])

    load(1, place.across, 0).start()
    load(0, place.across, 0).start()

    def stage(kind):
        def one(way, carry):
            for which, matrix in ((1, up), (0, mix)):
                matrix.one(kind, way)
                owner, half = matrix.following(kind, way)
                more = (way == 0) | (kind < 3)
                pl.when(more)(lambda: load(which, owner, half).start())
            out.one(kind, way)
            return carry

        lax.fori_loop(0, 2, one, 0)

    for copy in fetched[2:]:
        copy.wait()

    leaving = [
        pltpu.make_async_copy(source, target, emit_sem.at[index])
        for index, (source, target) in enumerate(
            [
                (up_grad_ref, up_grad_hbm),
                (mix_grad_ref, mix_grad_hbm),
                (out_owned_ref, out_owned_hbm),
            ]
        )
    ]

    def hats(span):
        _, hat, inverse = layer_norm_parts(
            rows_ref[span, :].astype(jnp.float32), gain_ref[...], 0.0
        )
        hat_buf[span, :] = hat
        inverse_buf[span, :] = inverse

    def step(index, carry):
        pl.when(index == 3)(lambda: by_rows(count, 64, hats))

        sums.step(index)
        pl.when(index == 0)(lambda: stage(0))
        for kind in range(3):

            @pl.when(index == kind)
            def _():
                stage(kind + 1)
                if kind == 1:
                    early.middle()
                if kind == 2:
                    early.late()

        return carry

    lax.fori_loop(0, chips, step, 0)
    total = scatter[0]
    late_out_ref[...] = jnp.zeros_like(late_out_ref)

    def columns(span):
        one_grad = total[span, :]
        late_out_ref[0:1, :] += jnp.sum(one_grad * hat_buf[span, :], axis=0, keepdims=True)
        late_out_ref[1:2, :] += jnp.sum(one_grad, axis=0, keepdims=True)

    def back(span):
        grad_ref[span, :] = resid_grad_ref[span, :] + layer_norm_back(
            total[span, :], hat_buf[span, :], inverse_buf[span, :], gain_ref[...]
        )

    by_rows(count, 64, columns)
    late.begin()
    up.end()
    leaving[0].start()
    late.middle()
    mix.end()
    leaving[1].start()
    by_rows(count, 64, back)
    late.late()
    out.end()
    leaving[2].start()
    early.end()
    sums.finish()
    late.end()
    for copy in leaving:
        copy.wait()


def input_back_call(
    stacked, mix_whole, rows, resid_grad, gain, smalls, hidden, out_grad, normed_one, normed_two, chips
):
    count, width = rows.shape
    total, units = hidden.shape
    local = stacked.shape[2]
    half = width // 8
    vmem = pl.BlockSpec(memory_space=pltpu.VMEM)
    hbm = pl.BlockSpec(memory_space=pl.ANY)
    return pl.pallas_call(
        functools.partial(input_back_kernel, chips),
        out_shape=(
            jax.ShapeDtypeStruct((count, width), jnp.float32),
            jax.ShapeDtypeStruct((2, width), jnp.float32),
            jax.ShapeDtypeStruct((5, width), jnp.float32),
            jax.ShapeDtypeStruct((2, 3, half, local), jnp.float32),
            jax.ShapeDtypeStruct((2, half, units), jnp.float32),
            jax.ShapeDtypeStruct((2, local // 2, width // 4), jnp.float32),
        ),
        in_specs=[hbm] * 4 + [vmem] * 5 + [hbm] * 4,
        out_specs=(vmem,) * 3 + (hbm,) * 3,
        scratch_shapes=[
            pltpu.VMEM((2, 3, half, local), jnp.float32),
            pltpu.VMEM((2, half, units), jnp.float32),
            pltpu.VMEM((2, local // 2, width // 4), jnp.float32),
            pltpu.VMEM((count, width), jnp.float32),
            pltpu.VMEM((count, 1), jnp.float32),
            pltpu.SemaphoreType.DMA((3,)),
            pltpu.VMEM(stacked.shape, jnp.bfloat16),
            pltpu.VMEM(mix_whole.shape, jnp.bfloat16),
            pltpu.VMEM(rows.shape, jnp.bfloat16),
            pltpu.VMEM(resid_grad.shape, jnp.float32),
            pltpu.VMEM(hidden.shape, jnp.bfloat16),
            pltpu.VMEM(out_grad.shape, jnp.float32),
            pltpu.SemaphoreType.DMA((6,)),
            pltpu.VMEM((2, total, half), jnp.bfloat16),
            pltpu.SemaphoreType.DMA((2,)),
        ]
        + scatter_scratch(chips, count, width)
        + square_scratch((3, half, local))
        + square_scratch((half, units))
        + small_scratch(chips, 5, width)
        + small_scratch(chips, 2, width)
        + square_scratch((local // 2, width // 4)),
        compiler_params=pltpu.CompilerParams(
            collective_id=2, has_side_effects=True, vmem_limit_bytes=VMEM_LIMIT
        ),
        cost_estimate=pl.CostEstimate(flops=10**11, bytes_accessed=0, transcendentals=0),
        name="input_back",
    )(stacked, mix_whole, rows, resid_grad, gain, *smalls, hidden, out_grad, normed_one, normed_two)


GELU_SLOPE = 0.7978845608028654
GELU_CUBE = 0.044715


def gelu_parts(hidden):
    square = hidden * hidden
    bend = jnp.tanh(GELU_SLOPE * hidden * (1.0 + GELU_CUBE * square))
    lift = 0.5 * (1.0 + bend)
    slope = lift + 0.5 * hidden * (1.0 - bend * bend) * (
        GELU_SLOPE * (1.0 + 3.0 * GELU_CUBE * square)
    )
    return hidden * lift, slope


def feed_kernel(
    chips,
    parts,
    normed_ref,
    branch_ref,
    up_hbm,
    down_hbm,
    bias_ref,
    resid_hbm,
    own_branch_hbm,
    gain_ref,
    normed_whole,
    active_hbm,
    hidden_hbm,
    grad_ref,
    grad_low_ref,
    sums_ref,
    bias_grad_ref,
    up_ref,
    down_ref,
    resid_ref,
    own_branch_ref,
    active_ref,
    hidden_ref,
    fetch_sem,
    emit_sem,
    blocks,
    branch_buf,
    work,
    hold,
    side_out,
    side_in,
    line_in,
    line_send,
    line_recv,
    keep_sem,
    load_sem,
    side_send,
    side_recv,
    out_send,
    out_recv,
):
    place = Place(chips)
    count = normed_ref.shape[0]
    rows = count // parts
    pair = 2 * rows
    last = chips - 1
    fetched = fetch(
        [
            (up_hbm, up_ref),
            (down_hbm, down_ref),
            (resid_hbm, resid_ref),
            (own_branch_hbm, own_branch_ref),
        ],
        fetch_sem,
    )
    place.greet(False)

    def fill(part, carry):
        block = 2 * (place.chip * parts + part) + place.core
        blocks[block] = normed_ref[pl.ds(pl.multiple_of(part * rows, rows), rows), :]
        return carry

    lax.fori_loop(0, parts, fill, 0)
    line = LineGather(place, blocks, line_send, line_recv, parts)
    line.begin_part(0)
    line.copy(2, place.chip, 1).start()
    pl.when(place.has_up & jnp.logical_not(place.has_down))(
        lambda: line.copy(0, place.chip, 1).start()
    )
    pl.when(place.has_down & jnp.logical_not(place.has_up))(
        lambda: line.copy(1, place.chip, 1).start()
    )
    bias_grad_ref[...] = jnp.zeros_like(bias_grad_ref)

    def piece_span(piece):
        return pl.ds(pl.multiple_of(piece * pair, pair), pair)

    def load(piece, slot):
        return pltpu.make_async_copy(
            branch_ref.at[piece_span(piece)], branch_buf.at[slot], load_sem.at[slot]
        )

    def keep(piece, core):
        span = pl.ds(pl.multiple_of(piece * pair + core * rows, rows), rows)
        return pltpu.make_async_copy(
            blocks.at[2 * piece + core], normed_whole.at[span], keep_sem.at[piece, core]
        )

    def side_copy(piece):
        return remote(
            side_out.at[piece],
            side_in.at[piece],
            side_send.at[piece],
            side_recv.at[piece],
            place.side,
        )

    chunk = normed_ref.shape[1] // 4

    def line_copy(way, chip, part, tile):
        piece = chip * parts + part
        next_chip = place.chip + 1 - 2 * way
        slot = jnp.where((way == 1) & (chip == next_chip), chips * parts + part, piece)
        span = slice(tile * chunk, (tile + 1) * chunk)
        return remote(
            line_in.at[piece, :, span],
            line_in.at[slot, :, span],
            out_send.at[piece, tile],
            out_recv.at[slot, tile],
            place.toward(way),
        )

    def line_landed(way, chip, part, tile):
        piece = chip * parts + part
        slot = jnp.where((way == 1) & (chip == place.chip), chips * parts + part, piece)
        span = slice(tile * chunk, (tile + 1) * chunk)
        remote(
            line_in.at[slot, :, span],
            line_in.at[slot, :, span],
            out_send.at[piece, tile],
            out_recv.at[slot, tile],
            place.toward(way),
        ).wait_recv()
        return slot

    def emit(piece):
        span = piece_span(piece)
        return [
            pltpu.make_async_copy(active_ref.at[span], active_hbm.at[span], emit_sem.at[piece, 0]),
            pltpu.make_async_copy(hidden_ref.at[span], hidden_hbm.at[span], emit_sem.at[piece, 1]),
        ]

    width = 512
    tiles = up_ref.shape[2] // width

    def compute(chip, part, side):
        piece = chip * parts + part
        keep(piece, 0).start()
        keep(piece, 1).start()
        span = piece_span(piece)
        own_rows = blocks[pl.ds(2 * piece, 2)].reshape(pair, -1)
        load(piece, side).wait()

        def tile(index, carry):
            units = pl.ds(pl.multiple_of(index * width, width), width)
            hidden = jnp.dot(
                own_rows,
                up_ref[:, :, units].reshape(-1, width),
                preferred_element_type=jnp.float32,
            )
            active, slope = gelu_parts(hidden + bias_ref[:, units])
            active_ref[span, units] = active.astype(jnp.bfloat16)
            grad = None
            for owner in range(4):
                columns = down_ref.shape[2]
                product = lax.dot_general(
                    branch_buf[side, :, owner * columns : (owner + 1) * columns],
                    down_ref[owner, units, :],
                    TURNED,
                    preferred_element_type=jnp.float32,
                )
                grad = product if grad is None else grad + product
            low = (grad * slope).astype(jnp.bfloat16)
            hidden_ref[span, units] = low
            bias_grad_ref[:, units] += jnp.sum(low.astype(jnp.float32), axis=0, keepdims=True)
            return carry

        lax.fori_loop(0, tiles, tile, 0)
        low = hidden_ref[span, :]
        depth = up_ref.shape[1]
        for owner in range(4):
            columns = slice(owner * depth, (owner + 1) * depth)
            product = lax.dot_general(
                low, up_ref[owner], TURNED, preferred_element_type=jnp.float32
            )
            work[:, :, columns] = product.reshape(2, rows, depth)
        side_out[piece] = work[1 - place.core].astype(jnp.bfloat16)
        side_copy(piece).start()
        hold[piece] = work[place.core]
        for copy in emit(piece):
            copy.start()

    def pass_on(way, chip, part):
        piece = chip * parts + part
        side_copy(piece).wait_recv()
        behind = ((way == 0) & place.has_down) | ((way == 1) & place.has_up)
        for tile in range(4):
            span = slice(tile * chunk, (tile + 1) * chunk)
            total = hold[piece, :, span] + side_in[piece, :, span].astype(jnp.float32)

            @pl.when(behind)
            def _():
                slot = line_landed(way, chip, part, tile)
                line_in[piece, :, span] = (
                    total + line_in[slot, :, span].astype(jnp.float32)
                ).astype(jnp.bfloat16)

            @pl.when(jnp.logical_not(behind))
            def _():
                line_in[piece, :, span] = total.astype(jnp.bfloat16)

            line_copy(way, chip, part, tile).start()

    def coming(index, side):
        count_beyond = jnp.where(side == 0, place.chip, last - place.chip)
        early = index <= count_beyond
        distance = jnp.where(early, index, 2 * count_beyond + 1 - index)
        valid = (index == 0) | (index <= 2 * count_beyond)
        chip = jnp.where(index == 0, place.chip, place.chip + distance * (2 * side - 1))
        part = jnp.where(index == 0, side, jnp.where(early, 0, 1))
        return valid, chip, part, count_beyond

    def turn(index, carry):
        def ahead(side, inner):
            valid, chip, part, _ = coming(index, side)
            pl.when(valid)(lambda: load(chip * parts + part, side).start())
            return inner

        lax.fori_loop(0, 2, ahead, 0)

        @pl.when(index > 0)
        def _():
            for side in range(2):
                valid, chip, part, count_beyond = coming(index, side)
                onward = (place.has_up, place.has_down)[side]

                @pl.when(valid)
                def _():
                    line.arrive(chip, place.core, part)
                    pl.when(onward)(lambda: line.copy(side, chip, part).start())
                    pl.when(onward & (index == 2 * count_beyond))(
                        lambda: line.copy(side, place.chip, 1).start()
                    )
                    line.copy(2, chip, part).start()

        def one(side, inner):
            valid, chip, part, _ = coming(index, side)

            @pl.when(valid)
            def _():
                line.arrive(chip, 1 - place.core, part)
                compute(chip, part, side)

            return inner

        lax.fori_loop(0, 2, one, 0)
        def onward(order, inner):
            way = order // 2
            part = order % 2
            here = place.chip + way * (last - 2 * place.chip)
            reach = jnp.where(part == 0, index - here, 2 * last + 1 + here - index)

            @pl.when((reach > here) & (reach < chips))
            def _():
                pass_on(way, reach + way * (last - 2 * reach), part)

            return inner

        lax.fori_loop(0, 4, onward, 0)
        return carry

    fetched[0].wait()
    fetched[1].wait()
    lax.fori_loop(0, 2 * last + 1, turn, 0)
    sums_ref[...] = jnp.zeros_like(sums_ref)
    fetched[2].wait()
    fetched[3].wait()

    def own_part(part, carry):
        piece = place.chip * parts + part
        side_copy(piece).wait_recv()
        hold[piece] += side_in[piece].astype(jnp.float32)

        for tile in range(4):

            @pl.when(place.has_down)
            def _():
                line_landed(0, place.chip, part, tile)

            @pl.when(place.has_up)
            def _():
                line_landed(1, place.chip, part, tile)

        pieces_end = chips * parts

        @pl.when(place.has_down)
        def _():
            hold[piece] += line_in[piece].astype(jnp.float32)

        @pl.when(place.has_up)
        def _():
            hold[piece] += line_in[pieces_end + part].astype(jnp.float32)

        tile = 64

        def back(index, inner):
            here = pl.ds(pl.multiple_of(index * tile, tile), tile)
            span = pl.ds(pl.multiple_of(part * rows + index * tile, tile), tile)
            two_grad = hold[piece, here, :]
            _, hat, inverse = layer_norm_parts(resid_ref[span, :], gain_ref[...], 0.0)
            grad = own_branch_ref[span, :].astype(jnp.float32) + layer_norm_back(
                two_grad, hat, inverse, gain_ref[...]
            )
            grad_ref[span, :] = grad
            grad_low_ref[span, :] = grad.astype(jnp.bfloat16)
            sums_ref[0:1, :] += jnp.sum(two_grad * hat, axis=0, keepdims=True)
            sums_ref[1:2, :] += jnp.sum(two_grad, axis=0, keepdims=True)
            sums_ref[2:3, :] += jnp.sum(grad, axis=0, keepdims=True)
            return inner

        lax.fori_loop(0, rows // tile, back, 0)
        return carry

    lax.fori_loop(0, parts, own_part, 0)
    line.finish()

    def drain(piece, carry):
        side_copy(piece).wait_send()
        keep(piece, 0).wait()
        keep(piece, 1).wait()
        for copy in emit(piece):
            copy.wait()
        for tile in range(4):
            pl.when(piece // parts != place.chip)(
                lambda: line_copy(0, piece // parts, piece % parts, tile).wait_send()
            )
        return carry

    lax.fori_loop(0, chips * parts, drain, 0)


def feed_call(normed, branch, up_whole, down_whole, bias, resid, own_branch, gain, chips):
    count, width = normed.shape
    total = 2 * chips * count
    units = up_whole.shape[2]
    parts = 2
    rows = count // parts
    low = jnp.bfloat16
    vmem = pl.BlockSpec(memory_space=pltpu.VMEM)
    hbm = pl.BlockSpec(memory_space=pl.ANY)
    dma = pltpu.SemaphoreType.DMA
    pieces = chips * parts
    return pl.pallas_call(
        functools.partial(feed_kernel, chips, parts),
        out_shape=(
            jax.ShapeDtypeStruct((total, width), low),
            jax.ShapeDtypeStruct((total, units), low),
            jax.ShapeDtypeStruct((total, units), low),
            jax.ShapeDtypeStruct((count, width), jnp.float32),
            jax.ShapeDtypeStruct((count, width), low),
            jax.ShapeDtypeStruct((3, width), jnp.float32),
            jax.ShapeDtypeStruct((1, units), jnp.float32),
        ),
        in_specs=[vmem, hbm, hbm, hbm, vmem, hbm, hbm, vmem],
        out_specs=(hbm,) * 3 + (vmem,) * 4,
        scratch_shapes=[
            pltpu.VMEM(up_whole.shape, low),
            pltpu.VMEM(down_whole.shape, low),
            pltpu.VMEM(resid.shape, jnp.float32),
            pltpu.VMEM(own_branch.shape, low),
            pltpu.VMEM((total, units), low),
            pltpu.VMEM((total, units), low),
            dma((4,)),
            dma((pieces, 2)),
            pltpu.VMEM((2 * pieces, rows, width), low),
            pltpu.VMEM((2, 2 * rows, width), low),
            pltpu.VMEM((2, rows, width), jnp.float32),
            pltpu.VMEM((pieces, rows, width), jnp.float32),
            pltpu.VMEM((pieces, rows, width), low),
            pltpu.VMEM((pieces, rows, width), low),
            pltpu.VMEM((pieces + parts, rows, width), low),
            dma((3, pieces)),
            dma((2 * pieces,)),
            dma((pieces, 2)),
            dma((2,)),
            dma((pieces,)),
            dma((pieces,)),
            dma((pieces, 4)),
            dma((pieces + parts, 4)),
        ],
        compiler_params=pltpu.CompilerParams(
            collective_id=3, has_side_effects=True, vmem_limit_bytes=VMEM_LIMIT
        ),
        cost_estimate=pl.CostEstimate(flops=10**11, bytes_accessed=0, transcendentals=0),
        name="feed",
    )(normed, branch, up_whole, down_whole, bias, resid, own_branch, gain)


def branch_back_kernel(
    chips,
    parts,
    branch_ref,
    active_hbm,
    down_hbm,
    attended_hbm,
    out_hbm,
    shift_ref,
    offsets_ref,
    lengths_ref,
    mixed_hbm,
    aux_hbm,
    resid_ref,
    cotangent_ref,
    stacked_hbm,
    bias_sum_ref,
    down_grad_hbm,
    out_grad_hbm,
    output_ref,
    blocks,
    stacked_ref,
    down_grad_ref,
    out_grad_ref,
    emit_sem,
    active_ref,
    down_ref,
    attended_ref,
    out_ref,
    mixed_ref,
    aux_ref,
    fetch_sem,
    seg_row_ref,
    block_buf,
    columns_buf,
    resid_buf,
    key_sum,
    value_sum,
    line_send,
    line_recv,
    columns_sem,
    block_sem,
    *scatter,
):
    place = Place(chips)
    bounds = (offsets_ref[0], offsets_ref[0] + lengths_ref[0])
    count = branch_ref.shape[0]
    rows = count // parts
    fetched = fetch(
        [
            (active_hbm, active_ref),
            (down_hbm, down_ref),
            (attended_hbm, attended_ref),
            (out_hbm, out_ref),
            (mixed_hbm, mixed_ref),
            (aux_hbm, aux_ref),
            (resid_ref, resid_buf),
        ],
        fetch_sem,
    )
    place.greet(True)
    line = LineGather(place, blocks, line_send, line_recv, 1, branch_ref)
    line.begin()

    def term(block, tile):
        chip, core = block // 2, block % 2
        taken = []
        for part in range(parts):
            start = ((chip * parts + part) * 2 + core) * rows
            taken.append(active_ref[pl.ds(pl.multiple_of(start, rows), rows), :])
        return jnp.dot(
            jnp.concatenate(taken, axis=0), down_ref[tile], preferred_element_type=jnp.float32
        )

    fetched[0].wait()
    fetched[1].wait()
    sums = LineScatter(place, term, 4, scatter[:4], scatter[4:8])
    sums.begin()
    seg_row_ref[...] = alive(seg_row_ref.shape, 1, 0, bounds)
    out_grad_ref[...] = jnp.zeros_like(out_grad_ref)
    key_sum[...] = jnp.zeros_like(key_sum)
    value_sum[...] = jnp.zeros_like(value_sum)
    bias_sum_ref[...] = jnp.zeros_like(bias_sum_ref)
    down_units = down_ref.shape[1] // 2
    down_columns = down_ref.shape[2]

    def load_columns(owner):
        return pltpu.make_async_copy(
            cotangent_ref.at[:, pl.ds(pl.multiple_of(owner * down_columns, 128), down_columns)],
            columns_buf,
            columns_sem,
        )

    load_columns(place.across).start()

    def down_piece(owner, half):
        units = pl.ds(pl.multiple_of(half * down_units, down_units), down_units)
        return lax.dot_general(
            active_ref[:, units], columns_buf[...], CROSSED, preferred_element_type=jnp.float32
        )

    down = SquareScatter(place, down_piece, down_grad_ref, scatter[8:10], scatter[10:12])
    def down_stage(kind):
        def one(way, carry):
            fresh = (way == 0) if kind in (0, 3) else ((way >= 0) if kind == 1 else (way == 1))
            pl.when(fresh)(lambda: load_columns(place.dp).wait())
            down.one(kind, way)
            owner, _ = down.following(kind, way)
            more = (way == 1) if kind == 0 else ((way == 0) if kind == 1 else (way >= 0))
            if kind < 3:
                pl.when(more)(lambda: load_columns(owner).start())
            return carry

        lax.fori_loop(0, 2, one, 0)

    def load_part(source, owner):
        columns = out_ref.shape[2]
        span = slice(owner * columns, (owner + 1) * columns)
        return pltpu.make_async_copy(source.at[:, span], block_buf.at[:, span], block_sem.at[owner])

    def load_block(block):
        mine = block == place.me

        @pl.when(mine)
        def _():
            for owner in range(4):
                load_part(branch_ref, owner).start()

        @pl.when(jnp.logical_not(mine))
        def _():
            for owner in range(4):
                load_part(blocks.at[block], owner).start()

    def take(block):
        span = pl.ds(pl.multiple_of(block * count, count), count)
        columns = out_ref.shape[2]
        load_block(block)
        result = None
        for owner in range(4):
            load_part(branch_ref, owner).wait()
            here = block_buf[:, owner * columns : (owner + 1) * columns]
            product = lax.dot_general(
                here, out_ref[owner], TURNED, preferred_element_type=jnp.float32
            )
            result = product if result is None else result + product
            out_grad_ref[:, owner * columns : (owner + 1) * columns] += lax.dot_general(
                attended_ref[span, :], here, CROSSED, preferred_element_type=jnp.float32
            )
        grad = result.astype(jnp.bfloat16)
        attend_back_rows(
            block,
            grad,
            attended_ref,
            mixed_ref,
            aux_ref,
            seg_row_ref,
            stacked_ref,
            key_sum,
            value_sum,
            bias_sum_ref,
        )

    for copy in fetched[2:-1]:
        copy.wait()
    leaving = [
        pltpu.make_async_copy(source, target, emit_sem.at[index])
        for index, (source, target) in enumerate(
            [
                (stacked_ref, stacked_hbm),
                (out_grad_ref, out_grad_hbm),
                (down_grad_ref, down_grad_hbm),
            ]
        )
    ]

    def settle():
        stacked_ref[1] = (key_sum[...] * HEAD_DIM ** (-0.5)).astype(jnp.bfloat16)
        value_grad = value_sum[...].astype(jnp.bfloat16)
        stacked_ref[2] = value_grad
        leaving[0].start()
        leaving[1].start()
        bias_sum_ref[1:2, :] = jnp.sum(value_grad.astype(jnp.float32), axis=0, keepdims=True)
        down.end()
        leaving[2].start()

    def step(index, carry):
        def one(side, inner):
            chip = place.chip + index * (2 * (side % 2) - 1)
            core = (place.core + side // 2) % 2

            @pl.when((chip >= 0) & (chip < chips) & ((index > 0) | (side % 2 == 0)))
            def _():
                pl.when(side >= 2)(lambda: line.arrive(chip, core))
                take(2 * chip + core)

            return inner

        lax.fori_loop(0, 4, one, 0)
        for kind in range(4):
            pl.when(index == kind)(lambda: down_stage(kind))
        pl.when(index < chips - 1)(lambda: line.step(index + 1))
        pl.when(index == chips - 1)(settle)
        sums.step(index)
        return carry

    lax.fori_loop(0, chips, step, 0)
    total = scatter[0]
    fetched[-1].wait()

    def emit(span):
        result = resid_buf[span, :] + total[span, :] + shift_ref[...]
        live = alive((64, 1), 0, place.me * count + span.start, bounds)
        output_ref[span, :] = jnp.where(live > 0, result, 0.0).astype(jnp.bfloat16)

    by_rows(count, 64, emit)
    sums.finish()
    line.finish()
    for copy in leaving:
        copy.wait()


def branch_back_call(
    branch,
    active,
    down_whole,
    attended,
    out_whole,
    shift,
    offsets,
    lengths,
    mixed,
    aux,
    resid,
    cotangent,
    chips,
):
    count, width = branch.shape
    total, local = attended.shape
    _, units, columns = down_whole.shape
    low = jnp.bfloat16
    vmem = pl.BlockSpec(memory_space=pltpu.VMEM)
    hbm = pl.BlockSpec(memory_space=pl.ANY)
    dma = pltpu.SemaphoreType.DMA
    return pl.pallas_call(
        functools.partial(branch_back_kernel, chips, 2),
        out_shape=(
            jax.ShapeDtypeStruct((3, total, local), low),
            jax.ShapeDtypeStruct((2, local), jnp.float32),
            jax.ShapeDtypeStruct((2, units // 2, columns), jnp.float32),
            jax.ShapeDtypeStruct((local, width), jnp.float32),
            jax.ShapeDtypeStruct((count, width), low),
            jax.ShapeDtypeStruct((2 * chips, count, width), low),
        ),
        in_specs=[hbm] * 5 + [vmem] + [pl.BlockSpec(memory_space=pltpu.SMEM)] * 2 + [hbm] * 4,
        out_specs=(hbm, vmem, hbm, hbm, vmem, hbm),
        scratch_shapes=[
            pltpu.VMEM((3, total, local), low),
            pltpu.VMEM((2, units // 2, columns), jnp.float32),
            pltpu.VMEM((local, width), jnp.float32),
            dma((3,)),
            pltpu.VMEM(active.shape, low),
            pltpu.VMEM(down_whole.shape, low),
            pltpu.VMEM(attended.shape, low),
            pltpu.VMEM(out_whole.shape, low),
            pltpu.VMEM(mixed.shape, low),
            pltpu.VMEM(aux.shape, jnp.float32),
            dma((7,)),
            pltpu.VMEM((1, total), jnp.float32),
            pltpu.VMEM((count, width), low),
            pltpu.VMEM((total, columns), low),
            pltpu.VMEM((count, width), jnp.float32),
            pltpu.VMEM((total, local), jnp.float32),
            pltpu.VMEM((total, local), jnp.float32),
            dma((3, chips)),
            dma((2 * chips,)),
            dma,
            dma((4,)),
        ]
        + scatter_scratch(chips, count, width)
        + square_scratch((units // 2, columns)),
        compiler_params=pltpu.CompilerParams(
            collective_id=4, has_side_effects=True, vmem_limit_bytes=VMEM_LIMIT
        ),
        cost_estimate=pl.CostEstimate(flops=10**11, bytes_accessed=0, transcendentals=0),
        name="branch_back",
    )(
        branch,
        active,
        down_whole,
        attended,
        out_whole,
        shift,
        offsets,
        lengths,
        mixed,
        aux,
        resid,
        cotangent,
    )


ATTEND_ROWS = 256
ATTEND_KEYS = 512


def tile_mask(row_block, key_block, seg_col_ref, seg_row_ref):
    rows = lax.broadcasted_iota(jnp.int32, (ATTEND_ROWS, ATTEND_KEYS), 0)
    keys = lax.broadcasted_iota(jnp.int32, (ATTEND_ROWS, ATTEND_KEYS), 1)
    causal = keys - rows <= row_block * ATTEND_ROWS - key_block * ATTEND_KEYS
    row_span = pl.ds(pl.multiple_of(row_block * ATTEND_ROWS, ATTEND_ROWS), ATTEND_ROWS)
    key_span = pl.ds(pl.multiple_of(key_block * ATTEND_KEYS, ATTEND_KEYS), ATTEND_KEYS)
    return causal & (seg_col_ref[row_span, 0:1] == seg_row_ref[:, key_span])


def attend_rows(
    row_block, mixed_ref, seg_col_ref, seg_row_ref, attended_ref, lse_ref, score_ref
):
    scale = HEAD_DIM ** (-0.5)
    heads = range(mixed_ref.shape[2] // HEAD_DIM)
    lanes = [slice(head * HEAD_DIM, (head + 1) * HEAD_DIM) for head in heads]
    row_span = pl.ds(pl.multiple_of(row_block * ATTEND_ROWS, ATTEND_ROWS), ATTEND_ROWS)
    count = (row_block * ATTEND_ROWS) // ATTEND_KEYS + 1
    queries = [mixed_ref[0, row_span, lanes[head]] for head in heads]

    def span_of(key_block):
        return pl.ds(pl.multiple_of(key_block * ATTEND_KEYS, ATTEND_KEYS), ATTEND_KEYS)

    def score(key_block, peaks):
        key_span = span_of(key_block)
        mask = tile_mask(row_block, key_block, seg_col_ref, seg_row_ref)
        results = []
        for head in heads:
            scores = lax.dot_general(
                queries[head],
                mixed_ref[1, key_span, lanes[head]],
                TURNED,
                preferred_element_type=jnp.float32,
            )
            scores = jnp.where(mask, scores * scale, MASK_FILL)
            score_ref[head, :, key_span] = scores
            peak = peaks[head]
            for part in range(ATTEND_KEYS // 128):
                peak = jnp.maximum(peak, scores[:, part * 128 : (part + 1) * 128])
            results.append(peak)
        return tuple(results)

    filled = jnp.full((ATTEND_ROWS, 128), MASK_FILL, jnp.float32)
    peaks = lax.fori_loop(0, count, score, (filled,) * len(heads))
    peaks = [jnp.max(peak, axis=1, keepdims=True) for peak in peaks]

    def weigh(key_block, masses):
        key_span = span_of(key_block)
        results = []
        for head in heads:
            weights = jnp.exp(score_ref[head, :, key_span] - peaks[head])
            score_ref[head, :, key_span] = weights
            mass = masses[head]
            for part in range(ATTEND_KEYS // 128):
                mass = mass + weights[:, part * 128 : (part + 1) * 128]
            results.append(mass)
        return tuple(results)

    nothing = jnp.zeros((ATTEND_ROWS, 128), jnp.float32)
    masses = lax.fori_loop(0, count, weigh, (nothing,) * len(heads))
    masses = [jnp.sum(mass, axis=1, keepdims=True) for mass in masses]
    inverses = [1.0 / mass for mass in masses]
    lse_ref[row_span, 0:1] = seg_col_ref[row_span, :]
    for head in heads:
        lse_ref[row_span, head + 1 : head + 2] = peaks[head] + jnp.log(masses[head])

    def gather(key_block, totals):
        key_span = span_of(key_block)
        results = []
        for head in heads:
            probs = (score_ref[head, :, key_span] * inverses[head]).astype(jnp.bfloat16)
            results.append(
                totals[head]
                + jnp.dot(
                    probs,
                    mixed_ref[2, key_span, lanes[head]],
                    preferred_element_type=jnp.float32,
                )
            )
        return tuple(results)

    empty = jnp.zeros((ATTEND_ROWS, HEAD_DIM), jnp.float32)
    totals = lax.fori_loop(0, count, gather, (empty,) * len(heads))
    for head in heads:
        attended_ref[row_span, lanes[head]] = totals[head].astype(jnp.bfloat16)


def attend_back_rows(
    row_block,
    grads,
    attended_ref,
    mixed_ref,
    aux_ref,
    seg_row_ref,
    stacked_ref,
    key_sum,
    value_sum,
    bias_sum,
):
    scale = HEAD_DIM ** (-0.5)
    row_span = pl.ds(pl.multiple_of(row_block * ATTEND_ROWS, ATTEND_ROWS), ATTEND_ROWS)
    count = (row_block * ATTEND_ROWS) // ATTEND_KEYS + 1
    row_live = seg_row_ref[:, row_span]
    heads = []
    for head in range(mixed_ref.shape[2] // HEAD_DIM):
        lanes = slice(head * HEAD_DIM, (head + 1) * HEAD_DIM)
        grad = grads[:, lanes]
        product = grad.astype(jnp.float32) * attended_ref[row_span, lanes].astype(jnp.float32)
        delta = jnp.sum(product, axis=1, keepdims=True).reshape(1, ATTEND_ROWS)
        lse = aux_ref[row_span, head + 1 : head + 2].reshape(1, ATTEND_ROWS)
        heads.append((lanes, mixed_ref[0, row_span, lanes], grad, lse, delta))

    def one(key_block, totals):
        key_span = pl.ds(pl.multiple_of(key_block * ATTEND_KEYS, ATTEND_KEYS), ATTEND_KEYS)
        keys = lax.broadcasted_iota(jnp.int32, (ATTEND_KEYS, ATTEND_ROWS), 0)
        rows = lax.broadcasted_iota(jnp.int32, (ATTEND_KEYS, ATTEND_ROWS), 1)
        allowed = (keys - rows <= row_block * ATTEND_ROWS - key_block * ATTEND_KEYS) & (
            aux_ref[key_span, 0:1] == row_live
        )
        results = []
        for (lanes, query, grad, lse, delta), total in zip(heads, totals):
            key = mixed_ref[1, key_span, lanes]
            scores = lax.dot_general(key, query, TURNED, preferred_element_type=jnp.float32)
            flow = lax.dot_general(
                mixed_ref[2, key_span, lanes], grad, TURNED, preferred_element_type=jnp.float32
            )
            probs = jnp.exp(jnp.where(allowed, scores * scale, MASK_FILL) - lse)
            value_sum[key_span, lanes] += jnp.dot(
                probs.astype(jnp.bfloat16), grad, preferred_element_type=jnp.float32
            )
            low = (probs * (flow - delta)).astype(jnp.bfloat16)
            key_sum[key_span, lanes] += jnp.dot(low, query, preferred_element_type=jnp.float32)
            results.append(
                total + lax.dot_general(low, key, CROSSED, preferred_element_type=jnp.float32)
            )
        return tuple(results)

    totals = lax.fori_loop(
        0, count, one, (jnp.zeros((ATTEND_ROWS, HEAD_DIM), jnp.float32),) * len(heads)
    )
    for (lanes, _, _, _, _), total in zip(heads, totals):
        query_grad = (total * scale).astype(jnp.bfloat16)
        stacked_ref[0, row_span, lanes] = query_grad
        bias_sum[0:1, lanes] += jnp.sum(query_grad.astype(jnp.float32), axis=0, keepdims=True)


def tile_scores(query_tile, keys, segment, row_block, col_block):
    key_tile = keys[col_block * BLOCK : (col_block + 1) * BLOCK]
    scale = query_tile.shape[2] ** (-0.5)
    scores = (
        jnp.einsum("qhe,khe->hqk", query_tile, key_tile, preferred_element_type=jnp.float32) * scale
    )
    row_place = row_block * BLOCK + jnp.arange(BLOCK)
    key_place = col_block * BLOCK + jnp.arange(BLOCK)
    row_segment = segment[row_block * BLOCK : (row_block + 1) * BLOCK]
    key_segment = segment[col_block * BLOCK : (col_block + 1) * BLOCK]
    allowed = (key_place[None, :] <= row_place[:, None]) & (
        row_segment[:, None] == key_segment[None, :]
    )
    return (jnp.where(allowed[None], scores, MASK_FILL), allowed)


def attention_forward(queries, keys, values, segment):
    count = queries.shape[0] // BLOCK
    heads = queries.shape[1]
    depth = queries.shape[2]
    outputs = []
    totals = []
    for row_block in range(count):
        query_tile = queries[row_block * BLOCK : (row_block + 1) * BLOCK]
        peak = jnp.full((heads, BLOCK), MASK_FILL, jnp.float32)
        mass = jnp.zeros((heads, BLOCK), jnp.float32)
        for col_block in range(row_block + 1):
            scores, allowed = tile_scores(query_tile, keys, segment, row_block, col_block)
            new_peak = jnp.maximum(peak, jnp.max(scores, axis=-1))
            weights = jnp.where(allowed[None], jnp.exp(scores - new_peak[:, :, None]), 0.0)
            mass = mass * jnp.exp(peak - new_peak) + jnp.sum(weights, axis=-1)
            peak = new_peak
        total = peak + jnp.log(mass)
        gathered = jnp.zeros((BLOCK, heads, depth), jnp.float32)
        for col_block in range(row_block + 1):
            scores, allowed = tile_scores(query_tile, keys, segment, row_block, col_block)
            probs = jnp.where(allowed[None], jnp.exp(scores - total[:, :, None]), 0.0).astype(
                jnp.bfloat16
            )
            value_tile = values[col_block * BLOCK : (col_block + 1) * BLOCK]
            gathered = gathered + jnp.einsum(
                "hqk,khe->qhe", probs, value_tile, preferred_element_type=jnp.float32
            )
        outputs.append(gathered.astype(jnp.bfloat16))
        totals.append(total)
    return (jnp.concatenate(outputs, axis=0), jnp.concatenate(totals, axis=1))


def attention_backward(queries, keys, values, segment, totals, grads):
    count = queries.shape[0] // BLOCK
    heads = queries.shape[1]
    depth = queries.shape[2]
    scale = depth ** (-0.5)
    key_grads = [jnp.zeros((BLOCK, heads, depth), jnp.float32) for index in range(count)]
    value_grads = [jnp.zeros((BLOCK, heads, depth), jnp.float32) for index in range(count)]
    query_grads = []
    for row_block in range(count):
        query_tile = queries[row_block * BLOCK : (row_block + 1) * BLOCK]
        grad_tile = grads[row_block * BLOCK : (row_block + 1) * BLOCK]
        total = totals[:, row_block * BLOCK : (row_block + 1) * BLOCK]
        flows = jnp.zeros((heads, BLOCK), jnp.float32)
        for col_block in range(row_block + 1):
            scores, allowed = tile_scores(query_tile, keys, segment, row_block, col_block)
            probs = jnp.where(allowed[None], jnp.exp(scores - total[:, :, None]), 0.0)
            value_tile = values[col_block * BLOCK : (col_block + 1) * BLOCK]
            prob_grad = jnp.einsum(
                "qhe,khe->hqk", grad_tile, value_tile, preferred_element_type=jnp.float32
            )
            flows = flows + jnp.sum(prob_grad * probs, axis=-1)
            value_grads[col_block] = value_grads[col_block] + jnp.einsum(
                "hqk,qhe->khe",
                probs.astype(jnp.bfloat16),
                grad_tile,
                preferred_element_type=jnp.float32,
            )
        query_sum = jnp.zeros((BLOCK, heads, depth), jnp.float32)
        for col_block in range(row_block + 1):
            scores, allowed = tile_scores(query_tile, keys, segment, row_block, col_block)
            probs = jnp.where(allowed[None], jnp.exp(scores - total[:, :, None]), 0.0)
            value_tile = values[col_block * BLOCK : (col_block + 1) * BLOCK]
            key_tile = keys[col_block * BLOCK : (col_block + 1) * BLOCK]
            prob_grad = jnp.einsum(
                "qhe,khe->hqk", grad_tile, value_tile, preferred_element_type=jnp.float32
            )
            score_grad = (probs * (prob_grad - flows[:, :, None])).astype(jnp.bfloat16)
            query_sum = query_sum + scale * jnp.einsum(
                "hqk,khe->qhe", score_grad, key_tile, preferred_element_type=jnp.float32
            )
            key_grads[col_block] = key_grads[col_block] + scale * jnp.einsum(
                "hqk,qhe->khe", score_grad, query_tile, preferred_element_type=jnp.float32
            )
        query_grads.append(query_sum)
    return (
        jnp.concatenate(query_grads, axis=0).astype(jnp.bfloat16),
        jnp.concatenate(key_grads, axis=0).astype(jnp.bfloat16),
        jnp.concatenate(value_grads, axis=0).astype(jnp.bfloat16),
    )


def adam_update(master, grad, first, second, rate, decay, first_fix, second_fix):
    first_next = BETA_FIRST * first + (1.0 - BETA_FIRST) * grad
    second_next = BETA_SECOND * second + (1.0 - BETA_SECOND) * grad * grad
    change = (
        first_next / first_fix / (jnp.sqrt(second_next / second_fix) + ADAM_EPSILON)
        + decay * master
    )
    return (master - rate * change, first_next, second_next)


def adam_step(master, grad, first, second, rate, decay, fixes):
    first_next = BETA_FIRST * first + (1.0 - BETA_FIRST) * grad
    second_next = BETA_SECOND * second + (1.0 - BETA_SECOND) * grad * grad
    change = (
        first_next / fixes[0] / (jnp.sqrt(second_next / fixes[1]) + ADAM_EPSILON)
        + decay * master
    )
    return master - rate * change, first_next, second_next


def adam_kernel(rates, step_ref, late_ref, early_ref, rows_ref, wide_ref, *refs):
    one = jnp.float32(1.0)
    fixes = tuple(
        one - lax.fori_loop(0, step_ref[0], lambda index, value: value * jnp.float32(beta), one)
        for beta in (BETA_FIRST, BETA_SECOND)
    )
    refs, (rows_out, wide_out) = refs[:-2], refs[-2:]
    rows_out[...] = rows_ref[...]
    wide_out[...] = wide_ref[...]
    smalls = 4
    matrix_inputs, small_inputs = refs[: 4 * len(rates)], refs[4 * len(rates) :][: 3 * smalls]
    outputs = refs[4 * len(rates) + 3 * smalls :]
    for index, rate in enumerate(rates):
        master, grad, first, second = matrix_inputs[4 * index : 4 * index + 4]
        updated, first_out, second_out, grad_out, low_out = outputs[5 * index : 5 * index + 5]
        value = grad[...].reshape(master.shape)
        fresh = adam_step(
            master[...], value, first[...], second[...], rate, MATRIX_DECAY, fixes
        )
        updated[...], first_out[...], second_out[...] = fresh
        grad_out[...] = value
        low_out[...] = fresh[0].astype(jnp.bfloat16)

    @pl.when(pl.program_id(0) == 0)
    def _():
        local = small_inputs[0].shape[1]
        units = small_inputs[3].shape[1]
        early = early_ref
        pieces = (
            [early[4:5, :local], early[4:5, local : 2 * local]],
            [early[4:5, 2 * local : 2 * local + units]],
            [late_ref[0:1, :], early[0:1, :]],
            [late_ref[1:2, :], early[2:3, :], early[1:2, :], early[3:4, :]],
        )
        for index in range(smalls):
            master, first, second = small_inputs[3 * index : 3 * index + 3]
            to = 5 * len(rates) + 4 * index
            updated, first_out, second_out, grad_out = outputs[to : to + 4]
            for row, value in enumerate(pieces[index]):
                here = slice(row, row + 1)
                fresh = adam_step(
                    master[here, :], value, first[here, :], second[here, :], SMALL_RATE, 0.0, fixes
                )
                updated[here, :], first_out[here, :], second_out[here, :] = fresh
                grad_out[here, :] = value


ADAM_STEPS = 4


def adam_call(matrices, smalls, late, early, passing, step):
    in_specs = [pl.BlockSpec(memory_space=pltpu.SMEM)] + [
        pl.BlockSpec(rows.shape, lambda i: (0, 0)) for rows in (late, early)
    ]
    handed = [
        pl.BlockSpec((rows.shape[0] // ADAM_STEPS, rows.shape[1]), lambda i: (i, 0))
        for rows in passing
    ]
    in_specs += handed
    out_specs, out_shape, operands, rates = [], [], [step, late, early, *passing], []
    for master, grad, first, second, rate in matrices:
        lead = master.shape[:-2]
        rows, columns = master.shape[-2] // ADAM_STEPS, master.shape[-1]
        zeros = (0,) * len(lead)
        whole = pl.BlockSpec(lead + (rows, columns), lambda i, z=zeros: z + (i, 0))
        half = pl.BlockSpec(
            (1,) + lead + (rows, columns),
            lambda i, z=zeros: (i // (ADAM_STEPS // 2),) + z + (i % (ADAM_STEPS // 2), 0),
        )
        in_specs += [whole, half, whole, whole]
        operands += [master, grad, first, second]
        shape = jax.ShapeDtypeStruct(master.shape, jnp.float32)
        out_specs += [whole] * 5
        out_shape += [shape] * 4 + [jax.ShapeDtypeStruct(master.shape, jnp.bfloat16)]
        rates.append(rate)
    for group in smalls:
        spec = pl.BlockSpec(group[0].shape, lambda i: (0, 0))
        in_specs += [spec] * 3
        operands += list(group)
        out_specs += [spec] * 4
        out_shape += [jax.ShapeDtypeStruct(group[0].shape, jnp.float32)] * 4
    out_specs += handed
    out_shape += [jax.ShapeDtypeStruct(rows.shape, rows.dtype) for rows in passing]
    return pl.pallas_call(
        functools.partial(adam_kernel, tuple(rates)),
        grid=(ADAM_STEPS,),
        in_specs=in_specs,
        out_specs=out_specs,
        out_shape=out_shape,
        compiler_params=pltpu.CompilerParams(vmem_limit_bytes=VMEM_LIMIT),
        name="adam",
    )(*operands)


def per_device(
    layer_input,
    cotangent,
    lengths,
    offsets,
    step,
    mix_weight,
    out_weight,
    up_weight,
    down_weight,
    mix_first,
    out_first,
    up_first,
    down_first,
    mix_second,
    out_second,
    up_second,
    down_second,
    mix_bias,
    up_bias,
    norm_gains,
    shifts,
    mix_bias_first,
    up_bias_first,
    gains_first,
    shifts_first,
    mix_bias_second,
    up_bias_second,
    gains_second,
    shifts_second,
):
    parts = lax.axis_size("mp")
    local_width = mix_weight.shape[2]
    (
        normed_one,
        mixed,
        mix_whole,
        out_whole,
        up_low,
        down_low,
        own_branch,
        bias_down_grad,
    ) = project_call(
        layer_input,
        norm_gains[0:1],
        shifts[0:1],
        mix_weight,
        out_weight,
        mix_bias,
        up_weight,
        down_weight,
        cotangent,
        offsets,
        lengths,
        parts // 2,
    )
    (
        attended_flat,
        aux,
        resid_own,
        normed_mid,
        branch_grad,
        up_whole,
        down_whole,
    ) = attend_out_call(
        mixed,
        offsets,
        lengths,
        out_whole,
        layer_input,
        own_branch,
        norm_gains[1:2],
        shifts[2:3],
        shifts[1:2],
        up_low,
        down_low,
        parts // 2,
    )
    normed_two, active, hidden_grad, resid_grad, resid_low, row_sums, up_bias_grad = feed_call(
        normed_mid,
        branch_grad,
        up_whole,
        down_whole,
        up_bias[None],
        resid_own,
        own_branch,
        norm_gains[1:2],
        parts // 2,
    )
    stacked, mix_bias_grad, down_pieces, out_grad, layer_output, _ = branch_back_call(
        resid_low,
        active,
        down_whole,
        attended_flat,
        out_whole,
        shifts[3:4],
        offsets,
        lengths,
        mixed,
        aux,
        resid_own,
        branch_grad,
        parts // 2,
    )
    input_grad, late, early, mix_pieces, up_pieces, out_pieces = input_back_call(
        stacked,
        mix_whole,
        layer_input,
        resid_grad,
        norm_gains[0:1],
        (row_sums, bias_down_grad, mix_bias_grad, up_bias_grad),
        hidden_grad,
        out_grad,
        normed_one,
        normed_two,
        parts // 2,
    )
    news = adam_call(
        [
            (mix_weight, mix_pieces, mix_first, mix_second, D ** (-0.5)),
            (out_weight, out_pieces, out_first, out_second, OUT_FAN ** (-0.5)),
            (up_weight, up_pieces, up_first, up_second, D ** (-0.5)),
            (down_weight, down_pieces, down_first, down_second, FF ** (-0.5)),
        ],
        [
            (mix_bias, mix_bias_first, mix_bias_second),
            (up_bias[None], up_bias_first[None], up_bias_second[None]),
            (norm_gains, gains_first, gains_second),
            (shifts, shifts_first, shifts_second),
        ],
        late,
        early,
        (layer_output, input_grad),
        step,
    )
    layer_output, input_grad = news[-2:]
    mix, out, up, down = (news[5 * index : 5 * index + 5] for index in range(4))
    biases, unit_biases, gains, moves = (
        news[20 + 4 * index : 24 + 4 * index] for index in range(4)
    )
    unit_biases = [value[0] for value in unit_biases]
    return (
        layer_output,
        input_grad,
        *mix[:3],
        *out[:3],
        *up[:3],
        *down[:3],
        *biases[:3],
        *unit_biases[:3],
        *gains[:3],
        *moves[:3],
        mix[3],
        out[3],
        up[3],
        down[3],
        biases[3],
        unit_biases[3],
        gains[3],
        moves[3],
        mix[4],
        out[4],
        up[4],
        down[4],
    )


def per_device_any(
    layer_input,
    cotangent,
    lengths,
    offsets,
    step,
    mix_weight,
    out_weight,
    up_weight,
    down_weight,
    mix_first,
    out_first,
    up_first,
    down_first,
    mix_second,
    out_second,
    up_second,
    down_second,
    mix_bias,
    up_bias,
    norm_gains,
    shifts,
    mix_bias_first,
    up_bias_first,
    gains_first,
    shifts_first,
    mix_bias_second,
    up_bias_second,
    gains_second,
    shifts_second,
):
    own_rows = layer_input.shape[0]
    parts = lax.axis_size("mp")
    group_rows = own_rows * parts
    slots_here = lengths.shape[0]
    slot_len = group_rows // slots_here
    local_width = mix_weight.shape[2]
    depth = HEAD_DIM
    heads_here = local_width // depth
    positions = jnp.arange(slot_len, dtype=jnp.int32)
    live = (positions[None, :] >= offsets[:, None]) & (
        positions[None, :] < (offsets + lengths)[:, None]
    )
    segment = live.astype(jnp.int32)
    first_row = lax.axis_index("mp") * own_rows
    own_live = own_slice(live.reshape(-1), first_row, own_rows)[:, None]
    own_input = layer_input.astype(jnp.float32)
    normed_own, hat_one, inv_one = layer_norm_parts(own_input, norm_gains[0], shifts[0])
    normed_one = gather_rows(normed_own.astype(jnp.bfloat16))
    mix_full = gather_shards(mix_weight.astype(jnp.bfloat16), 1)
    out_full = gather_shards(out_weight.astype(jnp.bfloat16), 1)
    up_full = gather_shards(up_weight.astype(jnp.bfloat16), 0)
    down_full = gather_shards(down_weight.astype(jnp.bfloat16), 1)
    out_grad = jnp.where(own_live, cotangent.astype(jnp.float32), 0.0)
    bias_down_grad = jnp.sum(out_grad, axis=0)
    branch_grad = gather_rows(out_grad.astype(jnp.bfloat16))
    mixed = jnp.einsum("td,cde->cte", normed_one, mix_full, preferred_element_type=jnp.float32)
    queries = (
        (mixed[0] + mix_bias[0])
        .astype(jnp.bfloat16)
        .reshape(slots_here, slot_len, heads_here, depth)
    )
    keys = mixed[1].astype(jnp.bfloat16).reshape(slots_here, slot_len, heads_here, depth)
    values = (
        (mixed[2] + mix_bias[1])
        .astype(jnp.bfloat16)
        .reshape(slots_here, slot_len, heads_here, depth)
    )

    def attend(item):
        return attention_forward(item[0], item[1], item[2], item[3])

    attended, totals = lax.map(attend, (queries, keys, values, segment))
    attended_flat = attended.reshape(group_rows, local_width)
    attn_part = jnp.dot(attended_flat, out_full, preferred_element_type=jnp.float32)
    resid_own = own_input + scatter_rows(attn_part) + shifts[1]
    normed_mid, hat_two, inv_two = layer_norm_parts(resid_own, norm_gains[1], shifts[2])
    normed_two = gather_rows(normed_mid.astype(jnp.bfloat16))
    hidden = jnp.dot(normed_two, up_full, preferred_element_type=jnp.float32) + up_bias
    active_value, gelu_pull = jax.vjp(tanh_gelu, hidden)
    active = active_value.astype(jnp.bfloat16)
    active_grad = jnp.einsum(
        "td,fd->tf", branch_grad, down_full, preferred_element_type=jnp.float32
    )
    hidden_grad = gelu_pull(active_grad)[0].astype(jnp.bfloat16)
    two_part = jnp.einsum("tf,df->td", hidden_grad, up_full, preferred_element_type=jnp.float32)
    two_grad = scatter_rows(two_part)
    down_part = jnp.dot(active, down_full, preferred_element_type=jnp.float32)
    down_grad = jnp.einsum("tf,td->fd", active, branch_grad, preferred_element_type=jnp.float32)
    up_bias_grad = jnp.sum(hidden_grad, axis=0, dtype=jnp.float32)
    up_grad = jnp.einsum("td,tf->df", normed_two, hidden_grad, preferred_element_type=jnp.float32)
    resid_grad = out_grad + layer_norm_back(two_grad, hat_two, inv_two, norm_gains[1])
    attn_branch = gather_rows(resid_grad.astype(jnp.bfloat16))
    result_own = resid_own + scatter_rows(down_part) + shifts[3]
    layer_output = jnp.where(own_live, result_own, 0.0).astype(jnp.bfloat16)
    gain_two_grad = jnp.sum(two_grad * hat_two, axis=0)
    shift_two_grad = jnp.sum(two_grad, axis=0)
    bias_out_grad = jnp.sum(resid_grad, axis=0)
    attended_grad = jnp.einsum(
        "td,ed->te", attn_branch, out_full, preferred_element_type=jnp.float32
    ).astype(jnp.bfloat16)
    out_weight_grad = jnp.einsum(
        "te,td->ed", attended_flat, attn_branch, preferred_element_type=jnp.float32
    )

    def attend_back(item):
        return attention_backward(item[0], item[1], item[2], item[3], item[4], item[5])

    query_grad, key_grad, value_grad = lax.map(
        attend_back,
        (
            queries,
            keys,
            values,
            segment,
            totals,
            attended_grad.reshape(slots_here, slot_len, heads_here, depth),
        ),
    )
    stacked = jnp.stack(
        [
            query_grad.reshape(group_rows, local_width),
            key_grad.reshape(group_rows, local_width),
            value_grad.reshape(group_rows, local_width),
        ]
    )
    one_part = jnp.einsum("cte,cde->td", stacked, mix_full, preferred_element_type=jnp.float32)
    one_grad = scatter_rows(one_part)
    mix_grad = jnp.einsum("td,cte->cde", normed_one, stacked, preferred_element_type=jnp.float32)
    mix_bias_grad = jnp.stack(
        [
            jnp.sum(stacked[0], axis=0, dtype=jnp.float32),
            jnp.sum(stacked[2], axis=0, dtype=jnp.float32),
        ]
    )
    mix_owned = scatter_shards(mix_grad, 1)
    out_owned = scatter_shards(out_weight_grad, 1)
    up_owned = scatter_shards(up_grad, 0)
    down_owned = scatter_shards(down_grad, 1)
    input_grad = resid_grad + layer_norm_back(one_grad, hat_one, inv_one, norm_gains[0])
    gain_one_grad = jnp.sum(one_grad * hat_one, axis=0)
    shift_one_grad = jnp.sum(one_grad, axis=0)
    gain_grad = jnp.stack([gain_one_grad, gain_two_grad])
    shift_grad = jnp.stack([shift_one_grad, bias_out_grad, shift_two_grad, bias_down_grad])
    mix_bias_total, up_bias_total = lax.psum((mix_bias_grad, up_bias_grad), "dp")
    gain_total, shift_total = lax.psum((gain_grad, shift_grad), ("dp", "mp"))
    step_count = step[0].astype(jnp.float32)
    first_fix = 1.0 - BETA_FIRST**step_count
    second_fix = 1.0 - BETA_SECOND**step_count
    mix_new = adam_update(
        mix_weight,
        mix_owned,
        mix_first,
        mix_second,
        D ** (-0.5),
        MATRIX_DECAY,
        first_fix,
        second_fix,
    )
    out_new = adam_update(
        out_weight,
        out_owned,
        out_first,
        out_second,
        OUT_FAN ** (-0.5),
        MATRIX_DECAY,
        first_fix,
        second_fix,
    )
    up_new = adam_update(
        up_weight, up_owned, up_first, up_second, D ** (-0.5), MATRIX_DECAY, first_fix, second_fix
    )
    down_new = adam_update(
        down_weight,
        down_owned,
        down_first,
        down_second,
        FF ** (-0.5),
        MATRIX_DECAY,
        first_fix,
        second_fix,
    )
    mix_bias_new = adam_update(
        mix_bias,
        mix_bias_total,
        mix_bias_first,
        mix_bias_second,
        SMALL_RATE,
        0.0,
        first_fix,
        second_fix,
    )
    up_bias_new = adam_update(
        up_bias,
        up_bias_total,
        up_bias_first,
        up_bias_second,
        SMALL_RATE,
        0.0,
        first_fix,
        second_fix,
    )
    gains_new = adam_update(
        norm_gains, gain_total, gains_first, gains_second, SMALL_RATE, 0.0, first_fix, second_fix
    )
    shifts_new = adam_update(
        shifts, shift_total, shifts_first, shifts_second, SMALL_RATE, 0.0, first_fix, second_fix
    )
    return (
        layer_output,
        input_grad,
        mix_new[0],
        mix_new[1],
        mix_new[2],
        out_new[0],
        out_new[1],
        out_new[2],
        up_new[0],
        up_new[1],
        up_new[2],
        down_new[0],
        down_new[1],
        down_new[2],
        mix_bias_new[0],
        mix_bias_new[1],
        mix_bias_new[2],
        up_bias_new[0],
        up_bias_new[1],
        up_bias_new[2],
        gains_new[0],
        gains_new[1],
        gains_new[2],
        shifts_new[0],
        shifts_new[1],
        shifts_new[2],
        mix_owned,
        out_owned,
        up_owned,
        down_owned,
        mix_bias_total,
        up_bias_total,
        gain_total,
        shift_total,
        mix_new[0].astype(jnp.bfloat16),
        out_new[0].astype(jnp.bfloat16),
        up_new[0].astype(jnp.bfloat16),
        down_new[0].astype(jnp.bfloat16),
    )


def solution(mesh):
    placed = (
        P(("dp", "mp"), None),
        P(("dp", "mp"), None),
        P("dp"),
        P("dp"),
        P(),
        P(None, "dp", "mp"),
        P("mp", "dp"),
        P("dp", "mp"),
        P("mp", "dp"),
        P(None, "dp", "mp"),
        P("mp", "dp"),
        P("dp", "mp"),
        P("mp", "dp"),
        P(None, "dp", "mp"),
        P("mp", "dp"),
        P("dp", "mp"),
        P("mp", "dp"),
        P(None, "mp"),
        P("mp"),
        P(),
        P(),
        P(None, "mp"),
        P("mp"),
        P(),
        P(),
        P(None, "mp"),
        P("mp"),
        P(),
        P(),
    )
    fits = mesh.shape["dp"] == 4 and mesh.shape["mp"] == 8
    return jax.shard_map(
        per_device if fits else per_device_any,
        mesh=mesh,
        in_specs=placed,
        out_specs=(
            P(("dp", "mp"), None),
            P(("dp", "mp"), None),
            P(None, "dp", "mp"),
            P(None, "dp", "mp"),
            P(None, "dp", "mp"),
            P("mp", "dp"),
            P("mp", "dp"),
            P("mp", "dp"),
            P("dp", "mp"),
            P("dp", "mp"),
            P("dp", "mp"),
            P("mp", "dp"),
            P("mp", "dp"),
            P("mp", "dp"),
            P(None, "mp"),
            P(None, "mp"),
            P(None, "mp"),
            P("mp"),
            P("mp"),
            P("mp"),
            P(),
            P(),
            P(),
            P(),
            P(),
            P(),
            P(None, "dp", "mp"),
            P("mp", "dp"),
            P("dp", "mp"),
            P("mp", "dp"),
            P(None, "mp"),
            P("mp"),
            P(),
            P(),
            P(None, "dp", "mp"),
            P("mp", "dp"),
            P("dp", "mp"),
            P("mp", "dp"),
        ),
        check_vma=False,
    )
```
